32 devices in a mesh: ctx: 8 (over z, x), wt: 4 (over y, core).
Axes of the slice: x: 2, y: 2, z: 4, core: 2. Of those that a mesh axis runs over, the one named last changes fastest.
Arguments:
- tokens: bfloat16 [8192, 768], P(('ctx', 'wt')), may hold values from -6 to 6
- doc_start: int32 [8192], replicated, may hold values from 0 to 8191, as said below
- cotangent: bfloat16 [8192, 768], P(('ctx', 'wt')), may hold values from -6 to 6
- query_weight: bfloat16 [768, 768], P('wt'), may hold values from -0.3125 to 0.3125
- key_weight: bfloat16 [768, 768], P('wt'), may hold values from -0.3125 to 0.3125
- value_weight: bfloat16 [768, 768], P('wt'), may hold values from -0.21875 to 0.21875
- out_weight: bfloat16 [768, 768], P('wt'), may hold values from -0.875 to 0.875
- query_bias: bfloat16 [768], P('wt'), may hold values from -1.5 to 1.5
- value_bias: bfloat16 [768], P('wt'), may hold values from -1 to 1
- out_bias: bfloat16 [768], P('wt'), may hold values from -1.5 to 1.5
- first_gain: bfloat16 [768], P('wt'), may hold values from 0.5 to 1.5
- first_shift: bfloat16 [768], P('wt'), may hold values from -1.5 to 1.5
- inner_weight: bfloat16 [768, 3072], P('wt'), may hold values from -0.21875 to 0.21875
- inner_bias: bfloat16 [3072], P('wt'), may hold values from -1.5 to 1.5
- outer_weight: bfloat16 [3072, 768], P('wt'), may hold values from -0.109375 to 0.109375
- outer_bias: bfloat16 [768], P('wt'), may hold values from -1 to 1
- second_gain: bfloat16 [768], P('wt'), may hold values from 0.5 to 1.5
- second_shift: bfloat16 [768], P('wt'), may hold values from -1.5 to 1.5
Outputs:
- layer_out: bfloat16 [8192, 768], P(('ctx', 'wt'))
- tokens_gradient: float32 [8192, 768], P(('ctx', 'wt'))
- query_weight_gradient: float32 [768, 768], P('wt')
- key_weight_gradient: float32 [768, 768], P('wt')
- value_weight_gradient: float32 [768, 768], P('wt')
- out_weight_gradient: float32 [768, 768], P('wt')
- query_bias_gradient: float32 [768], P('wt')
- value_bias_gradient: float32 [768], P('wt')
- out_bias_gradient: float32 [768], P('wt')
- first_gain_gradient: float32 [768], P('wt')
- first_shift_gradient: float32 [768], P('wt')
- inner_weight_gradient: float32 [768, 3072], P('wt')
- inner_bias_gradient: float32 [3072], P('wt')
- outer_weight_gradient: float32 [3072, 768], P('wt')
- outer_bias_gradient: float32 [768], P('wt')
- second_gain_gradient: float32 [768], P('wt')
- second_shift_gradient: float32 [768], P('wt')
The draws below stay inside these ranges and needn't reach their ends.
Inputs may be any that keep to these rules, and one draw needn't show every extreme that they name: `doc_start`: each position holds the first position of its document; documents are runs of consecutive positions, each 1 to 2048 long, at least one is exactly 2048 long, and the last position starts a document of its own.
All inputs are finite; a program needn't handle non-finite values.
Results may differ from the reference program's by a relative error of at most 0.02.
The reference program's roundings to bfloat16 on the way count: a program that leaves them out, or rounds other values in their place, can miss the bound.
Values may be sent and summed in bfloat16 or wider, within the bound.
No kernel may reach another device: no remote copies, remote signals or barrier semaphores. Data moves between devices by JAX's collectives and lax.ppermute only.
A program may use at most 256 MiB of HBM per device.

```python
import jax
import jax.numpy as jnp
from jax import lax

D = 768
HEADS = 12
HEAD_DIM = 64
FF = 3072
MAXDOC = 2048
TOKENS = 8192


def draw_doc_start(key, part):
    positions = jnp.arange(TOKENS, dtype=jnp.int32)
    offset = jax.random.randint(jax.random.fold_in(key, 1), (), 0, MAXDOC, dtype=jnp.int32)
    chosen = jax.random.randint(jax.random.fold_in(key, 2), (), 0, TOKENS // MAXDOC - 1, dtype=jnp.int32)
    lower_edge = offset + chosen * MAXDOC
    upper_edge = lower_edge + MAXDOC
    inside = (positions > lower_edge) & (positions < upper_edge)
    random_cuts = jax.random.randint(jax.random.fold_in(key, 3), (TOKENS,), 0, MAXDOC, dtype=jnp.int32) < 3
    forced = (positions == 0) | (positions == TOKENS - 1) | ((positions - offset) % MAXDOC == 0)
    begins = forced | random_cuts & jnp.logical_not(inside)
    return lax.cummax(jnp.where(begins, positions, 0), axis=0)


def with_spikes(entries, stream_key, source, target, blocks, factor):
    def block_of(position):
        return (jnp.arange(entries.shape[position]) // (entries.shape[position] // blocks)).reshape((-1,) + (1,) * (entries.ndim - 1 - position))

    near = jax.random.permutation(stream_key, blocks)[block_of(target)]
    other_side = (block_of(target) + blocks // 2) % blocks
    return jnp.where((block_of(source) == near) | (block_of(source) == other_side), factor * entries, entries)


def shard_levels(key, dims, shards, least, top_value):
    def one(position, blocks):
        steps = jax.random.uniform(jax.random.fold_in(jax.random.fold_in(key, 6), position), (blocks,), jnp.float32, least / len(shards), top_value / len(shards))
        return jnp.repeat(jnp.exp(steps), dims[position] // blocks).reshape((-1,) + (1,) * (len(dims) - position - 1))

    loudness = one(*shards[0])
    for cut in shards[1:]:
        loudness = loudness * one(*cut)
    return loudness


def centred(own_key, extent, deviation, limit, shards=(), kind=jnp.bfloat16):
    values = deviation * jax.random.normal(own_key, extent, jnp.float32)
    if shards:
        values = values * shard_levels(own_key, extent, shards, -0.22, 0.18)
    return jnp.clip(values, -limit, limit).astype(kind)


def heavy_noise(key, shape, deviation, limit, pieces, heavy, held_as=jnp.bfloat16):
    drawn = deviation * jax.random.normal(key, shape, jnp.float32)
    if pieces:
        drawn = drawn * shard_levels(key, shape, pieces, -0.22, 0.18)
    return jnp.clip(with_spikes(drawn, jax.random.fold_in(key, 3), *heavy), -limit, limit).astype(held_as)


def setup_inputs(seed: int = 0) -> dict:
    key_list = jax.random.split(jax.random.key(seed), 19)
    tokens = centred(key_list[0], (TOKENS, D), 1.0, 6.0, ((0, 32),))
    doc_start = draw_doc_start(jax.random.fold_in(key_list[18], 71), 0)
    cotangent = heavy_noise(key_list[2], (TOKENS, D), 1.0, 6.0, ((0, 32),), (0, 1, 32, 2.75))
    query_weight = centred(key_list[3], (D, D), (D // 2) ** -0.5, 0.3125, ((0, 4),))
    key_weight = centred(key_list[4], (D, D), (D // 2) ** -0.5, 0.3125, ((0, 4),))
    value_weight = centred(key_list[5], (D, D), D ** -0.5, 0.21875, ((0, 4),))
    out_weight = centred(key_list[6], (D, D), (D // 16) ** -0.5, 0.875, ((0, 4),))
    query_bias = centred(key_list[7], (D,), 0.3, 1.5, ((0, 4),))
    value_bias = centred(key_list[8], (D,), 0.2, 1.0, ((0, 4),))
    out_bias = centred(key_list[9], (D,), 0.3, 1.5, ((0, 4),))
    first_gain = jnp.clip(1.0 + 0.1 * jax.random.normal(key_list[10], (D,), jnp.float32), 0.5, 1.5).astype(jnp.bfloat16)
    first_shift = centred(key_list[11], (D,), 0.3, 1.5, ((0, 4),))
    inner_weight = centred(key_list[12], (D, FF), D ** -0.5, 0.21875, ((0, 4),))
    inner_bias = centred(key_list[13], (FF,), 0.3, 1.5, ((0, 4),))
    outer_weight = centred(key_list[14], (FF, D), FF ** -0.5, 0.109375, ((0, 4),))
    outer_bias = centred(key_list[15], (D,), 0.2, 1.0, ((0, 4),))
    second_gain = jnp.clip(1.0 + 0.1 * jax.random.normal(key_list[16], (D,), jnp.float32), 0.5, 1.5).astype(jnp.bfloat16)
    second_shift = centred(key_list[17], (D,), 0.3, 1.5, ((0, 4),))
    return {"tokens": tokens, "doc_start": doc_start, "cotangent": cotangent, "query_weight": query_weight, "key_weight": key_weight, "value_weight": value_weight, "out_weight": out_weight, "query_bias": query_bias, "value_bias": value_bias, "out_bias": out_bias, "first_gain": first_gain, "first_shift": first_shift, "inner_weight": inner_weight, "inner_bias": inner_bias, "outer_weight": outer_weight, "outer_bias": outer_bias, "second_gain": second_gain, "second_shift": second_shift}


masked_score = -1e+30
epsilon = 1e-06
highest = lax.Precision.HIGHEST

@jax.custom_vjp
def low(v):
    return lax.optimization_barrier(v.astype(jnp.bfloat16)).astype(jnp.float32)

@jax.custom_vjp
def low_back(v):
    return v

def low_keep(v):
    return (low(v), None)

def low_pass(kept, grad):
    return (grad,)

def back_keep(v):
    return (v, None)

def back_low(kept, grad):
    return (low(grad),)
low.defvjp(low_keep, low_pass)
low_back.defvjp(back_keep, back_low)

def layer_norm(values, gain, shift):
    center = values - lax.optimization_barrier(jnp.mean(values, axis=-1, keepdims=True))
    spread = lax.optimization_barrier(jnp.mean(center * center, axis=-1, keepdims=True))
    return center * lax.rsqrt(spread + epsilon) * gain + shift

def attention(queries, keyset, valueset, marks):
    query_block = MAXDOC // 4
    span = query_block + 2 * MAXDOC
    key_pad = jnp.pad(keyset, ((MAXDOC, MAXDOC), (0, 0)))
    value_pad = jnp.pad(valueset, ((MAXDOC, MAXDOC), (0, 0)))
    mark_pad = jnp.pad(marks, (MAXDOC, MAXDOC))

    def one_block(index):
        start = (index * query_block).astype(jnp.int32)
        query_part = lax.dynamic_slice_in_dim(queries, start, query_block, 0).reshape(query_block, HEADS, HEAD_DIM)
        key_part = lax.dynamic_slice_in_dim(key_pad, start, span, 0).reshape(span, HEADS, HEAD_DIM)
        value_part = lax.dynamic_slice_in_dim(value_pad, start, span, 0).reshape(span, HEADS, HEAD_DIM)
        query_marks = lax.dynamic_slice_in_dim(marks, start, query_block, 0)
        key_marks = lax.dynamic_slice_in_dim(mark_pad, start, span, 0)
        scores = low_back(jnp.einsum('qhd,khd->hqk', query_part, key_part, precision=highest) * 0.125)
        allowed = (query_marks[:, None] == key_marks[None, :])[None]
        masked = jnp.where(allowed, scores, masked_score)
        largest = lax.optimization_barrier(jnp.max(masked, axis=-1, keepdims=True))
        raised = jnp.where(allowed, jnp.exp(masked - largest), 0.0)
        chances = raised / lax.optimization_barrier(jnp.sum(raised, axis=-1, keepdims=True))
        mixed = jnp.einsum('hqk,khd->qhd', low(chances), value_part, precision=highest)
        return mixed.reshape(query_block, HEADS * HEAD_DIM)
    count = TOKENS // query_block
    blocks = lax.map(jax.checkpoint(one_block), jnp.arange(count, dtype=jnp.int32))
    return blocks.reshape(TOKENS, HEADS * HEAD_DIM)

def reference(tokens, doc_start, cotangent, query_weight, key_weight, value_weight, out_weight, query_bias, value_bias, out_bias, first_gain, first_shift, inner_weight, inner_bias, outer_weight, outer_bias, second_gain, second_shift):
    marks = (doc_start + 1).astype(jnp.int32)
    params = (query_weight, key_weight, value_weight, out_weight, query_bias, value_bias, out_bias, first_gain, first_shift, inner_weight, inner_bias, outer_weight, outer_bias, second_gain, second_shift)
    floats = tuple((member.astype(jnp.float32) for member in params))

    def forward(inputs, full_query, full_key, full_value, full_out, bias_query, bias_value, bias_out, gain_first, shift_first, full_inner, bias_inner, full_outer, bias_outer, gain_second, shift_second):
        queries = low_back(low(jnp.dot(inputs, full_query, precision=highest) + bias_query))
        keyset = low_back(low(jnp.dot(inputs, full_key, precision=highest)))
        valueset = low_back(low(jnp.dot(inputs, full_value, precision=highest) + bias_value))
        mixed = low_back(low(attention(queries, keyset, valueset, marks)))
        branch = low_back(jnp.dot(mixed, full_out, precision=highest) + bias_out)
        first = layer_norm(inputs + branch, gain_first, shift_first)
        hidden = low_back(jnp.dot(low(first), full_inner, precision=highest) + bias_inner)
        activated = low(jax.nn.gelu(hidden, approximate=False))
        outer = low_back(jnp.dot(activated, full_outer, precision=highest) + bias_outer)
        return layer_norm(first + outer, gain_second, shift_second)
    output, pullback = jax.vjp(forward, tokens.astype(jnp.float32), *floats)
    grads = pullback(cotangent.astype(jnp.float32))
    return (output.astype(jnp.bfloat16), grads[0], grads[1], grads[2], grads[3], grads[4], grads[5], grads[6], grads[7], grads[8], grads[9], grads[10], grads[11], grads[12], grads[13], grads[14], grads[15])
```

```python
import functools

import jax
import jax.numpy as jnp
from jax import lax
from jax.experimental import pallas as pl
from jax.experimental.pallas import tpu as pltpu
from jax.sharding import PartitionSpec as P

HEADS = 12
HEAD_DIM = 64
MAXDOC = 2048
TILE = 256

masked_score = -1e30
epsilon = 1e-06
bf16 = jnp.bfloat16
f32 = jnp.float32


def swapped(block, axis, bit):
    count = lax.axis_size(axis)
    return lax.ppermute(block, axis, [(i, i ^ bit) for i in range(count)])


def shifted(block, axis, distance):
    count = lax.axis_size(axis)
    route = [(i, i + distance) for i in range(count) if 0 <= i + distance < count]
    return lax.ppermute(block, axis, route)


def matmul(left, right):
    return jnp.dot(left, right, preferred_element_type=f32)


def left_transposed(left, right):
    return jnp.einsum("td,te->de", left, right, preferred_element_type=f32)


def right_transposed(left, right):
    return jnp.einsum("te,de->td", left, right, preferred_element_type=f32)


def column_sums(values):
    return jnp.sum(values.astype(f32), axis=0)


def rows_nt(left, right):
    return lax.dot_general(left, right, (((1,), (1,)), ((), ())), preferred_element_type=f32)


def rows_nn(left, right):
    return lax.dot_general(left, right, (((1,), (0,)), ((), ())), preferred_element_type=f32)


def load_window(pieces, target, sem, block):
    copies = [
        pltpu.make_async_copy(piece, target.at[pl.ds(i * block, block), :], sem.at[i])
        for i, piece in enumerate(pieces)
    ]
    for copy in copies:
        copy.start()
    return copies


def tile_loops(bounds, step, run):
    low, full_low, full_high, high = (bounds[4 * step + i] for i in range(4))
    front = full_low - low

    def edge(i, carry):
        tile = jnp.where(i < front, low + i, full_high + i - front)
        run(tile, True)
        return carry

    def inner(i, carry):
        run(i, False)
        return carry

    lax.fori_loop(0, front + high - full_high, edge, 0)
    lax.fori_loop(full_low, full_high, inner, 0)


def allowed_rows(span_ref, first, tile):
    keys = tile * TILE + lax.broadcasted_iota(jnp.int32, (TILE, TILE), 1)
    start = span_ref[pl.ds(first, TILE), 0:1]
    stop = span_ref[pl.ds(first, TILE), 1:2]
    return (keys >= start) & (keys < stop)


def head_of(tile0, tile1, head):
    lane = lax.broadcasted_iota(jnp.int32, tile0.shape, 1)
    if head == 0:
        return jnp.where(lane < HEAD_DIM, tile0, jnp.zeros_like(tile0))
    if head == 1:
        return jnp.where(lane >= HEAD_DIM, tile0, jnp.zeros_like(tile0))
    return tile1


def forward_kernel(bounds, q_ref, span_ref, *rest):
    pieces, (out_ref, wide_ref, stat_ref, kv, top, total, accum, sem) = rest[:-8], rest[-8:]
    step = pl.program_id(0)
    block = pieces[0].shape[0]

    @pl.when(step == 0)
    def _():
        for copy in load_window(pieces, kv, sem, block):
            copy.wait()

    first = pl.multiple_of(step * TILE, TILE)
    top[...] = jnp.full_like(top, masked_score)
    total[...] = jnp.zeros_like(total)
    accum[...] = jnp.zeros_like(accum)
    q_tile = q_ref[pl.ds(first, TILE), :]
    heads = [head_of(q_tile[:, :128], q_tile[:, 128:], h) for h in range(3)]

    def run(tile, edge):
        rows = pl.ds(pl.multiple_of(tile * TILE, TILE), TILE)
        allowed = allowed_rows(span_ref, first, tile) if edge else None
        for h in range(3):
            keys = kv[rows, 0:128] if h < 2 else kv[rows, 128:192]
            values = kv[rows, 128:256] if h == 0 else kv[rows, 256:384]
            score = rows_nt(heads[h], keys)
            if edge:
                score = jnp.where(allowed, score, masked_score)
            before = top[h]
            newest = jnp.maximum(before, jnp.max(score, axis=1, keepdims=True))
            factor = jnp.exp(before - newest)
            weight = jnp.exp(score - jnp.tile(newest, (1, TILE // 128)))
            if edge:
                weight = jnp.where(allowed, weight, 0.0)
            part = weight[:, 0:128]
            for i in range(1, TILE // 128):
                part = part + weight[:, 128 * i : 128 * i + 128]
            total[h] = total[h] * factor + part
            accum[h] = accum[h] * factor + rows_nn(weight.astype(bf16), values)
            top[h] = newest

    tile_loops(bounds, step, run)
    lane = lax.broadcasted_iota(jnp.int32, (TILE, 128), 1)
    mixed, stats = [], jnp.zeros((TILE, 128), f32)
    for h in range(3):
        mass = jnp.sum(total[h], axis=1, keepdims=True)
        mixed.append(pltpu.roll(accum[h] / mass, HEAD_DIM, 1))
        stats = jnp.where(lane == h, top[h] + jnp.log(mass), stats)
    here = pl.ds(first, TILE)
    pair = jnp.where(lane < HEAD_DIM, mixed[0], mixed[1])
    wide_ref[here, 0:128] = pair
    wide_ref[here, 128:192] = mixed[2][:, :HEAD_DIM]
    out_ref[here, 0:128] = pair.astype(bf16)
    out_ref[here, 128:192] = mixed[2][:, :HEAD_DIM].astype(bf16)
    stat_ref[here, :] = stats


def whole_spec(shape):
    return pl.BlockSpec(shape, lambda i, *_: (0,) * len(shape))


def attention_forward(bounds, queries, spans, pieces):
    block = queries.shape[0]
    window = len(pieces) * block
    return pl.pallas_call(
        forward_kernel,
        grid_spec=pltpu.PrefetchScalarGridSpec(
            num_scalar_prefetch=1,
            grid=(block // TILE,),
            in_specs=[whole_spec(queries.shape), whole_spec(spans.shape)]
            + [pl.BlockSpec(memory_space=pl.ANY)] * len(pieces),
            out_specs=[
                whole_spec((block, 192)),
                whole_spec((block, 192)),
                whole_spec((block, 128)),
            ],
            scratch_shapes=[
                pltpu.VMEM((window, 384), bf16),
                pltpu.VMEM((3, TILE, 128), f32),
                pltpu.VMEM((3, TILE, 128), f32),
                pltpu.VMEM((3, TILE, 128), f32),
                pltpu.SemaphoreType.DMA((len(pieces),)),
            ],
        ),
        out_shape=[
            jax.ShapeDtypeStruct((block, 192), bf16),
            jax.ShapeDtypeStruct((block, 192), f32),
            jax.ShapeDtypeStruct((block, 128), f32),
        ],
        compiler_params=pltpu.CompilerParams(vmem_limit_bytes=40 * 2**20),
        cost_estimate=pl.CostEstimate(
            flops=4 * block * 2304 * 192, bytes_accessed=6 * 2**20, transcendentals=block * 2304 * 3
        ),
        name="attention_forward",
    )(bounds, queries, spans, *pieces)


def query_kernel(bounds, q_ref, span_ref, grad_ref, wide_ref, stat_ref, *rest):
    pieces, (out_ref, kv, accum, sem) = rest[:-4], rest[-4:]
    step = pl.program_id(0)
    block = pieces[0].shape[0]

    @pl.when(step == 0)
    def _():
        for copy in load_window(pieces, kv, sem, block):
            copy.wait()

    first = pl.multiple_of(step * TILE, TILE)
    here = pl.ds(first, TILE)
    accum[...] = jnp.zeros_like(accum)
    q_tile = q_ref[here, :]
    heads = [head_of(q_tile[:, :128], q_tile[:, 128:], h) for h in range(3)]
    g_tile = grad_ref[here, :]
    lane = lax.broadcasted_iota(jnp.int32, (TILE, 128), 1)
    g_pair = g_tile[:, :128]
    g_last = jnp.concatenate([g_tile[:, 128:], jnp.zeros((TILE, HEAD_DIM), bf16)], axis=1)
    none = jnp.zeros((TILE, 128), bf16)
    r_pair = pltpu.roll(g_pair.astype(f32), HEAD_DIM, 1).astype(bf16)
    r_last = pltpu.roll(g_last.astype(f32), HEAD_DIM, 1).astype(bf16)
    grads = [
        jnp.where(lane >= HEAD_DIM, r_pair, none),
        jnp.where(lane < HEAD_DIM, r_pair, none),
        jnp.where(lane >= HEAD_DIM, r_last, none),
    ]
    product_pair = g_pair.astype(f32) * wide_ref[here, 0:128]
    product_last = g_tile[:, 128:].astype(f32) * wide_ref[here, 128:192]
    deltas = [
        jnp.sum(jnp.where(lane < HEAD_DIM, product_pair, 0.0), axis=1, keepdims=True),
        jnp.sum(jnp.where(lane < HEAD_DIM, 0.0, product_pair), axis=1, keepdims=True),
        jnp.sum(product_last, axis=1, keepdims=True),
    ]
    logs = [stat_ref[here, h : h + 1] for h in range(3)]
    deltas = [jnp.broadcast_to(d, (TILE, 128)) for d in deltas]
    logs = [jnp.broadcast_to(d, (TILE, 128)) for d in logs]

    def run(tile, edge):
        rows = pl.ds(pl.multiple_of(tile * TILE, TILE), TILE)
        allowed = allowed_rows(span_ref, first, tile) if edge else None
        for h in range(3):
            keys = kv[rows, 0:128] if h < 2 else kv[rows, 128:192]
            values = kv[rows, 128:256] if h == 0 else kv[rows, 256:384]
            score = rows_nt(heads[h], keys) - jnp.tile(logs[h], (1, TILE // 128))
            if edge:
                score = jnp.where(allowed, score, masked_score)
            chance = jnp.exp(score)
            back = rows_nt(grads[h], values) - jnp.tile(deltas[h], (1, TILE // 128))
            change = (chance * back).astype(bf16)
            accum[h] += rows_nn(change, kv[rows, 0:128] if h < 2 else kv[rows, 128:256])

    tile_loops(bounds, step, run)
    out_ref[here, 0:128] = (jnp.where(lane < HEAD_DIM, accum[0], accum[1]) * 0.125).astype(bf16)
    out_ref[here, 128:192] = (accum[2][:, :HEAD_DIM] * 0.125).astype(bf16)


def attention_queries(bounds, queries, spans, grads, wide, stats, pieces):
    block = queries.shape[0]
    window = len(pieces) * block
    return pl.pallas_call(
        query_kernel,
        grid_spec=pltpu.PrefetchScalarGridSpec(
            num_scalar_prefetch=1,
            grid=(block // TILE,),
            in_specs=[whole_spec(x.shape) for x in (queries, spans, grads, wide, stats)]
            + [pl.BlockSpec(memory_space=pl.ANY)] * len(pieces),
            out_specs=whole_spec((block, 192)),
            scratch_shapes=[
                pltpu.VMEM((window, 384), bf16),
                pltpu.VMEM((3, TILE, 128), f32),
                pltpu.SemaphoreType.DMA((len(pieces),)),
            ],
        ),
        out_shape=jax.ShapeDtypeStruct((block, 192), bf16),
        compiler_params=pltpu.CompilerParams(vmem_limit_bytes=40 * 2**20),
        cost_estimate=pl.CostEstimate(
            flops=6 * block * 2304 * 192, bytes_accessed=6 * 2**20, transcendentals=block * 2304 * 3
        ),
        name="attention_queries",
    )(bounds, queries, spans, grads, wide, stats, *pieces)


def key_kernel(reach, bounds, kv_ref, span_ref, stat_ref, *rest):
    window = 2 * reach + 1
    q_pieces, g_pieces = rest[:window], rest[window : 2 * window]
    out_ref, qs, gs, key_sum, value_sum, sem = rest[2 * window :]
    step = pl.program_id(0)
    block = q_pieces[0].shape[0]

    @pl.when(step == 0)
    def _():
        copies = load_window(q_pieces, qs, sem.at[0], block)
        copies += load_window(g_pieces, gs, sem.at[1], block)
        for copy in copies:
            copy.wait()

    first = pl.multiple_of(step * TILE, TILE)
    here = pl.ds(first, TILE)
    key_sum[...] = jnp.zeros_like(key_sum)
    value_sum[...] = jnp.zeros_like(value_sum)
    keys_pair = kv_ref[here, 0:128]
    keys = [head_of(keys_pair, kv_ref[here, 128:192], h) for h in range(3)]
    lane = lax.broadcasted_iota(jnp.int32, (TILE, 128), 1)
    zero = jnp.zeros((TILE, 128), f32)
    v_one = pltpu.roll(kv_ref[here, 128:256].astype(f32), HEAD_DIM, 1)
    v_two = pltpu.roll(kv_ref[here, 256:384].astype(f32), HEAD_DIM, 1)
    values = [
        jnp.where(lane < HEAD_DIM, v_one, zero).astype(bf16),
        jnp.where(lane < HEAD_DIM, zero, v_two).astype(bf16),
        v_two.astype(bf16)[:, :HEAD_DIM],
    ]

    def run(tile, edge):
        columns = pl.ds(pl.multiple_of(tile * TILE, TILE), TILE)
        if edge:
            place = reach * block + first + lax.broadcasted_iota(jnp.int32, (TILE, TILE), 0)
            allowed = (place >= span_ref[0:1, columns]) & (place < span_ref[1:2, columns])
        for h in range(3):
            lanes = slice(0, 128) if h < 2 else slice(128, 192)
            q_tile, g_tile = qs[columns, lanes], gs[columns, lanes]
            score = rows_nt(keys[h], q_tile) - stat_ref[h : h + 1, columns]
            if edge:
                score = jnp.where(allowed, score, masked_score)
            chance = jnp.exp(score)
            back = rows_nt(values[h], g_tile) - stat_ref[h + 3 : h + 4, columns]
            change = (chance * back).astype(bf16)
            size = 128 if h < 2 else HEAD_DIM
            key_sum[h, :, 0:size] += rows_nn(change, q_tile)
            value_sum[h, :, 0:size] += rows_nn(chance.astype(bf16), g_tile)

    tile_loops(bounds, step, run)
    k_pair = jnp.where(lane < HEAD_DIM, key_sum[0], key_sum[1])
    v_pair = jnp.where(lane < HEAD_DIM, value_sum[0], value_sum[1])
    k_last = key_sum[2]
    v_last = value_sum[2]
    v_turn = pltpu.roll(v_pair, HEAD_DIM, 1)
    last_turn = pltpu.roll(v_last, HEAD_DIM, 1)
    out_ref[here, 0:128] = k_pair.astype(bf16)
    out_ref[here, 128:256] = jnp.where(lane < HEAD_DIM, k_last, v_turn).astype(bf16)
    out_ref[here, 256:384] = jnp.where(lane < HEAD_DIM, v_turn, last_turn).astype(bf16)


def attention_keys(bounds, pair, spans, stats, q_pieces, g_pieces):
    block = pair.shape[0]
    count = len(q_pieces)
    return pl.pallas_call(
        functools.partial(key_kernel, count // 2),
        grid_spec=pltpu.PrefetchScalarGridSpec(
            num_scalar_prefetch=1,
            grid=(block // TILE,),
            in_specs=[whole_spec(x.shape) for x in (pair, spans, stats)]
            + [pl.BlockSpec(memory_space=pl.ANY)] * (2 * count),
            out_specs=whole_spec((block, 384)),
            scratch_shapes=[
                pltpu.VMEM((count * block, 192), bf16),
                pltpu.VMEM((count * block, 192), bf16),
                pltpu.VMEM((3, TILE, 128), f32),
                pltpu.VMEM((3, TILE, 128), f32),
                pltpu.SemaphoreType.DMA((2, count)),
            ],
        ),
        out_shape=jax.ShapeDtypeStruct((block, 384), bf16),
        compiler_params=pltpu.CompilerParams(vmem_limit_bytes=40 * 2**20),
        cost_estimate=pl.CostEstimate(
            flops=8 * block * 2304 * 192, bytes_accessed=8 * 2**20, transcendentals=block * 2304 * 3
        ),
        name="attention_keys",
    )(bounds, pair, spans, stats, *q_pieces, *g_pieces)


def norm_parts(values):
    center = values - jnp.mean(values, axis=-1, keepdims=True)
    inverse = lax.rsqrt(jnp.mean(center * center, axis=-1, keepdims=True) + epsilon)
    return center * inverse, inverse


def norm_back(upstream, normal, inverse, gain):
    scaled = upstream * gain
    mean_scaled = jnp.mean(scaled, axis=-1, keepdims=True)
    mean_product = jnp.mean(scaled * normal, axis=-1, keepdims=True)
    grad = (scaled - mean_scaled - normal * mean_product) * inverse
    return grad, jnp.sum(upstream * normal, axis=0), jnp.sum(upstream, axis=0)


def both(left, right):
    return (left.astype(f32) + right.astype(f32)).astype(bf16)


def halves(block, bit, axis):
    size = block.shape[axis] // 2
    kept = lax.dynamic_slice_in_dim(block, bit * size, size, axis)
    sent = lax.dynamic_slice_in_dim(block, (1 - bit) * size, size, axis)
    return kept, sent


def scatter_sum(block, axis_name, order, axis):
    index = lax.axis_index(axis_name)
    for step in order:
        kept, sent = halves(block, (index // step) % 2, axis)
        block = both(kept, swapped(sent, axis_name, step))
    return block


def gather_back(block, axis_name, order, axis):
    index = lax.axis_index(axis_name)
    for step in reversed(order):
        other = swapped(block, axis_name, step)
        late = (index // step) % 2 == 1
        block = jnp.where(
            late,
            jnp.concatenate([other, block], axis),
            jnp.concatenate([block, other], axis),
        )
    return block


def on_device(
    tokens,
    doc_start,
    cotangent,
    query_weight,
    key_weight,
    value_weight,
    out_weight,
    query_bias,
    value_bias,
    out_bias,
    first_gain,
    first_shift,
    inner_weight,
    inner_bias,
    outer_weight,
    outer_bias,
    second_gain,
    second_shift,
):
    rows, width = tokens.shape
    cycle = lax.axis_size("ctx")
    shards = lax.axis_size("wt")
    block = rows * shards
    reach = (MAXDOC + block - 2) // block
    window = (2 * reach + 1) * block
    c = lax.axis_index("ctx")
    w = lax.axis_index("wt")
    part = width // shards
    hidden_size = inner_weight.shape[1]
    others = [w ^ r for r in range(shards)]

    def placed(pieces):
        buffer = jnp.zeros((shards,) + pieces[0].shape, pieces[0].dtype)
        for r, piece in enumerate(pieces):
            buffer = lax.dynamic_update_slice_in_dim(buffer, piece[None], others[r], 0)
        return buffer

    def spread(own):
        far = swapped(own, "wt", 2)
        near = swapped(jnp.stack((own, far)), "wt", 1)
        return [own, near[0], far, near[1]]

    token_pieces = spread(tokens)

    def columns(r):
        start = others[r] * part
        return jnp.concatenate(
            [
                lax.dynamic_slice_in_dim(x, start, part, 1)
                for x in (query_weight, key_weight, value_weight)
            ],
            axis=1,
        )

    projection = placed(
        [columns(0)] + [swapped(columns(r), "wt", r) for r in range(1, shards)]
    ).reshape(width, 3 * part)
    block_tokens = placed(token_pieces).reshape(block, width)

    small_own = jnp.concatenate(
        [out_bias, first_gain, first_shift, outer_bias, second_gain, second_shift, inner_bias]
    ).reshape(-1, part)
    small = lax.all_gather(small_own, "wt", axis=0)
    out_bias_row, gain_one, shift_one, outer_bias_row, gain_two, shift_two = (
        small[:, i].reshape(width).astype(f32) for i in range(6)
    )
    inner_bias_row = small[:, 6:].reshape(hidden_size).astype(f32)

    pad = reach * block
    padded = jnp.pad(doc_start, (pad, pad), constant_values=-1)
    base = c * block - pad
    marks = lax.dynamic_slice_in_dim(padded, c * block, window)
    place = jnp.arange(window, dtype=jnp.int32)
    begins = jnp.where((marks == base + place) | (marks < 0), place, window)
    next_begin = lax.cummin(begins, axis=0, reverse=True)
    stops = jnp.concatenate([next_begin[1:], jnp.full((1,), window, jnp.int32)])
    starts = marks - base
    spans_row = jnp.stack([starts, stops] + [jnp.zeros_like(starts)] * 6)
    spans_column = spans_row[:, pad : pad + block].T
    own_starts = starts[pad : pad + block].reshape(-1, TILE)
    own_stops = stops[pad : pad + block].reshape(-1, TILE)
    lowest, highest = own_starts[:, 0], own_stops[:, -1]
    low, high = lowest // TILE, (highest + TILE - 1) // TILE
    full_low, full_high = (lowest + TILE - 1) // TILE, highest // TILE
    single = (own_starts[:, -1] == lowest) & (full_low < full_high)
    full_low = jnp.where(single, full_low, low)
    full_high = jnp.where(single, full_high, low)
    bounds = jnp.stack([low, full_low, full_high, high], axis=1).reshape(-1)

    projected = matmul(block_tokens, projection)
    own_query_bias = query_bias.astype(f32)
    own_value_bias = value_bias.astype(f32)
    queries = (
        (projected[:, :part] + own_query_bias).astype(bf16).astype(f32) * 0.125
    ).astype(bf16)
    pair = jnp.concatenate(
        [projected[:, part : 2 * part], projected[:, 2 * part :] + own_value_bias], axis=1
    ).astype(bf16)

    distances = [d for d in range(reach, -reach - 1, -1)]

    def halo(own):
        return [own if d == 0 else shifted(own, "ctx", d) for d in distances]

    pairs = halo(pair)
    inner_pieces = spread(inner_weight)
    outer_pieces = spread(jnp.concatenate([outer_weight, out_weight], axis=0))
    out_pieces = [x[hidden_size // shards :] for x in outer_pieces]
    full_inner = placed(inner_pieces).reshape(width, hidden_size)
    full_outer = placed([x[: hidden_size // shards] for x in outer_pieces]).reshape(
        hidden_size, width
    )

    mixed, mixed_wide, stat_columns = attention_forward(bounds, queries, spans_column, pairs)
    query_halo = halo(queries)

    mixed_rows = mixed.reshape(shards, rows, part)
    mixed_pieces = [
        lax.dynamic_index_in_dim(mixed_rows, others[r], 0, keepdims=False) for r in range(shards)
    ]
    mixed_pieces = [mixed_pieces[0]] + [
        swapped(mixed_pieces[r], "wt", r) for r in range(1, shards)
    ]
    branch = sum(matmul(mixed_pieces[r], out_pieces[r]) for r in range(shards))
    residual_one = tokens.astype(f32) + branch + out_bias_row
    normal_one, inverse_one = norm_parts(residual_one)
    first = normal_one * gain_one + shift_one
    first_low = first.astype(bf16)
    hidden = matmul(first_low, full_inner) + inner_bias_row
    cdf = 0.5 * (1.0 + lax.erf(hidden * (2.0**-0.5)))
    slope = cdf + hidden * jnp.exp(-0.5 * hidden * hidden) * ((2.0 * jnp.pi) ** -0.5)
    activated = (hidden * cdf).astype(bf16)
    residual_two = first + matmul(activated, full_outer) + outer_bias_row
    normal_two, inverse_two = norm_parts(residual_two)
    layer_out = (normal_two * gain_two + shift_two).astype(bf16)

    upstream = cotangent.astype(f32)
    grad_two, gain_two_grad, shift_two_grad = norm_back(
        upstream, normal_two, inverse_two, gain_two
    )
    grad_two_low = grad_two.astype(bf16)
    outer_bias_grad = column_sums(grad_two_low)
    outer_grad = left_transposed(activated, grad_two_low).astype(bf16)
    grad_hidden = (right_transposed(grad_two_low, full_outer) * slope).astype(bf16)
    inner_bias_grad = column_sums(grad_hidden)
    inner_grad = left_transposed(first_low, grad_hidden).astype(bf16)
    grad_first = grad_two + right_transposed(grad_hidden, full_inner)
    grad_one, gain_one_grad, shift_one_grad = norm_back(
        grad_first, normal_one, inverse_one, gain_one
    )
    grad_one_low = grad_one.astype(bf16)
    out_bias_grad = column_sums(grad_one_low)

    back_pieces = [right_transposed(grad_one_low, out_pieces[r]).astype(bf16) for r in range(shards)]
    back_pieces = [back_pieces[0]] + [swapped(back_pieces[r], "wt", r) for r in range(1, shards)]
    grad_mixed = placed(back_pieces).reshape(block, part)

    selector = (
        jnp.arange(part)[:, None] // HEAD_DIM == jnp.arange(3)[None, :]
    ).astype(f32)
    delta = jnp.einsum(
        "ij,jh->hi",
        grad_mixed.astype(f32) * mixed_wide,
        selector,
        precision=lax.Precision.HIGHEST,
    )
    stat_rows = jnp.concatenate([stat_columns[:, :3].T, delta], axis=0)
    parts, rest = [], stat_rows
    for _ in range(3):
        piece = lax.reduce_precision(rest, 8, 7)
        parts.append(piece.astype(bf16))
        rest = rest - piece
    packed = jnp.concatenate(parts, axis=0).reshape(-1, part)
    grad_halo = halo(jnp.concatenate([grad_mixed, packed], axis=0))
    grad_blocks = [x[:block] for x in grad_halo]
    stat_parts = jnp.concatenate(
        [x[block:].reshape(3, -1, block) for x in grad_halo], axis=2
    ).astype(f32)
    stat_window = stat_parts[0] + stat_parts[1] + stat_parts[2]
    stat_window = jnp.concatenate([stat_window, jnp.zeros((2, window), f32)], axis=0)

    def shard_sum(grad):
        kept, sent = halves(grad.reshape((2, 2) + grad.shape[1:]), w % 2, 1)
        grad = both(kept, swapped(sent, "wt", 1))
        kept, sent = halves(grad, w // 2, 0)
        return both(kept, swapped(sent, "wt", 2))[0, 0]

    near_first = [1 << i for i in range(cycle.bit_length() - 1)]
    far_first = [2, 1] + near_first[2:]
    outer_shard = shard_sum(outer_grad.reshape(shards, -1, width))
    outer_total = gather_back(scatter_sum(outer_shard, "ctx", near_first, 0), "ctx", near_first, 0)
    inner_shard = shard_sum(inner_grad.reshape(shards, part, hidden_size))
    inner_total = gather_back(scatter_sum(inner_shard, "ctx", far_first, 0), "ctx", far_first, 0)

    grad_query = attention_queries(
        bounds, queries, spans_column, grad_mixed, mixed_wide, stat_columns, pairs
    )
    grad_pair = attention_keys(bounds, pair, spans_row, stat_window, query_halo, grad_blocks)

    grad_one_block = placed(spread(grad_one_low)).reshape(block, width)
    out_grad = left_transposed(mixed, grad_one_block).astype(bf16)
    query_grad = left_transposed(block_tokens, grad_query).astype(bf16)
    pair_grad = left_transposed(block_tokens, grad_pair).astype(bf16)
    early = jnp.concatenate([query_grad.reshape(shards, part, part)], axis=2)
    late = pair_grad.reshape(shards, part, 2 * part)

    def head_sum(grad, order):
        grad = scatter_sum(grad, "ctx", order, 1)
        pieces = [
            lax.dynamic_index_in_dim(grad, others[r], 0, keepdims=False) for r in range(shards)
        ]
        pieces = [pieces[0]] + [swapped(pieces[r], "wt", r) for r in range(1, shards)]
        return gather_back(placed(pieces), "ctx", order, 1)

    out_total = gather_back(scatter_sum(out_grad, "ctx", far_first, 0), "ctx", far_first, 0)
    query_total = head_sum(early, near_first)
    pair_total = head_sum(late, near_first)

    def columns_joined(grad):
        return jnp.transpose(grad, (1, 0, 2)).reshape(part, width).astype(f32)

    token_partial = (
        right_transposed(grad_query, projection[:, :part])
        + right_transposed(grad_pair, projection[:, part:])
    ).astype(bf16)
    token_sum = shard_sum(token_partial.reshape(shards, rows, width))
    tokens_gradient = grad_one + token_sum.astype(f32)

    query_bias_grad = column_sums(grad_query)
    value_bias_grad = column_sums(grad_pair[:, part:])
    own_bias = jnp.stack([query_bias_grad, value_bias_grad])
    small_grads = jnp.concatenate(
        [
            jnp.stack(
                [
                    x.reshape(shards, part)
                    for x in (
                        out_bias_grad,
                        gain_one_grad,
                        shift_one_grad,
                        outer_bias_grad,
                        gain_two_grad,
                        shift_two_grad,
                    )
                ],
                axis=1,
            ),
            inner_bias_grad.reshape(shards, -1, part),
            jnp.where((jnp.arange(shards) == w)[:, None, None], own_bias[None], 0.0),
        ],
        axis=1,
    )
    small_sums = lax.psum(small_grads, ("ctx", "wt"))
    mine = lax.dynamic_index_in_dim(small_sums, w, 0, keepdims=False)

    return (
        layer_out,
        tokens_gradient,
        columns_joined(query_total),
        columns_joined(pair_total[:, :, :part]),
        columns_joined(pair_total[:, :, part:]),
        out_total.astype(f32),
        mine[-2],
        mine[-1],
        mine[0],
        mine[1],
        mine[2],
        inner_total.astype(f32),
        mine[6:-2].reshape(-1),
        outer_total.astype(f32),
        mine[3],
        mine[4],
        mine[5],
    )


def solution(mesh):
    matrix, vector = P("wt", None), P("wt")
    stream = P(("ctx", "wt"), None)
    in_specs = (stream, P(), stream) + (matrix,) * 4 + (vector,) * 5
    in_specs += (matrix, vector, matrix, vector, vector, vector)
    out_specs = (stream, stream) + (matrix,) * 4 + (vector,) * 5
    out_specs += (matrix, vector, matrix, vector, vector, vector)
    return jax.shard_map(
        on_device, mesh=mesh, in_specs=in_specs, out_specs=out_specs, check_vma=False
    )
```

```python
import functools

import jax
import jax.numpy as jnp
from jax import lax
from jax.experimental import pallas as pl
from jax.experimental.pallas import tpu as pltpu
from jax.sharding import PartitionSpec as P

HEADS = 12
HEAD_DIM = 64
MAXDOC = 2048
TILE_Q = 256
SPAN_K = 768
TILE_K = 256
SPAN_Q = 768

masked_score = -1e30
epsilon = 1e-06
bf16 = jnp.bfloat16
f32 = jnp.float32


def swapped(block, axis, bit):
    count = lax.axis_size(axis)
    return lax.ppermute(block, axis, [(i, i ^ bit) for i in range(count)])


def shifted(block, axis, distance):
    count = lax.axis_size(axis)
    route = [(i, i + distance) for i in range(count) if 0 <= i + distance < count]
    return lax.ppermute(block, axis, route)


def rows_nt(left, right):
    return lax.dot_general(left, right, (((1,), (1,)), ((), ())), preferred_element_type=f32)


def rows_nn(left, right):
    return lax.dot_general(left, right, (((1,), (0,)), ((), ())), preferred_element_type=f32)


def load_window(pieces, target, sem, block):
    copies = [
        pltpu.make_async_copy(piece, target.at[pl.ds(i * block, block), :], sem.at[i])
        for i, piece in enumerate(pieces)
    ]
    for copy in copies:
        copy.start()
    return copies


def lanes_of(values, size):
    return jnp.tile(values, (1, size // 128))


def head_of(tile0, tile1, head):
    lane = lax.broadcasted_iota(jnp.int32, tile0.shape, 1)
    if head == 0:
        return jnp.where(lane < HEAD_DIM, tile0, jnp.zeros_like(tile0))
    if head == 1:
        return jnp.where(lane >= HEAD_DIM, tile0, jnp.zeros_like(tile0))
    return tile1


def forward_kernel(bounds, q_ref, span_ref, *rest):
    pieces, (out_ref, wide_ref, stat_ref, kv, top, total, accum, sem) = rest[:-8], rest[-8:]
    step = pl.program_id(0)
    block = pieces[0].shape[0]

    @pl.when(step == 0)
    def _():
        for copy in load_window(pieces, kv, sem, block):
            copy.wait()

    first = pl.multiple_of(step * TILE_Q, TILE_Q)
    here = pl.ds(first, TILE_Q)
    top[...] = jnp.full_like(top, masked_score)
    total[...] = jnp.zeros_like(total)
    accum[...] = jnp.zeros_like(accum)
    q_tile = q_ref[here, :]
    heads = [head_of(q_tile[:, :128], q_tile[:, 128:], h) for h in range(3)]
    lower, count = bounds[2 * step], bounds[2 * step + 1]

    def run(i, carry):
        begin = pl.multiple_of(lower + i * SPAN_K, 128)
        rows = pl.ds(begin, SPAN_K)
        keys = lax.broadcasted_iota(jnp.int32, (TILE_Q, SPAN_K), 1)
        allowed = (keys >= span_ref[here, 0:1] - begin) & (keys < span_ref[here, 1:2] - begin)
        scores = [rows_nt(heads[h], kv[rows, 0:128] if h < 2 else kv[rows, 128:192]) for h in range(3)]
        for h in range(3):
            score = scores[h]
            score = jnp.where(allowed, score, masked_score)
            before = top[h]
            newest = jnp.maximum(before, jnp.max(score, axis=1, keepdims=True))
            factor = jnp.exp(before - newest)
            weight = jnp.exp(score - lanes_of(newest, SPAN_K))
            part = weight[:, 0:128]
            for j in range(1, SPAN_K // 128):
                part = part + weight[:, 128 * j : 128 * j + 128]
            total[h] = total[h] * factor + part
            values = kv[rows, 128:256] if h == 0 else kv[rows, 256:384]
            accum[h] = accum[h] * factor + rows_nn(weight.astype(bf16), values)
            top[h] = newest
        return carry

    lax.fori_loop(0, count, run, 0)
    lane = lax.broadcasted_iota(jnp.int32, (TILE_Q, 128), 1)
    mixed, stats = [], jnp.zeros((TILE_Q, 128), f32)
    for h in range(3):
        mass = jnp.sum(total[h], axis=1, keepdims=True)
        mixed.append(pltpu.roll(accum[h] / mass, HEAD_DIM, 1))
        stats = jnp.where(lane == h, top[h] + jnp.log(mass), stats)
    pair = jnp.where(lane < HEAD_DIM, mixed[0], mixed[1])
    wide_ref[here, 0:128] = pair
    wide_ref[here, 128:192] = mixed[2][:, :HEAD_DIM]
    out_ref[here, 0:128] = pair.astype(bf16)
    out_ref[here, 128:192] = mixed[2][:, :HEAD_DIM].astype(bf16)
    stat_ref[here, :] = stats


def whole_spec(shape):
    return pl.BlockSpec(shape, lambda i, *_: (0,) * len(shape))


def attention_forward(bounds, queries, spans, pieces):
    block = queries.shape[0]
    window = len(pieces) * block
    return pl.pallas_call(
        forward_kernel,
        grid_spec=pltpu.PrefetchScalarGridSpec(
            num_scalar_prefetch=1,
            grid=(block // TILE_Q,),
            in_specs=[whole_spec(queries.shape), whole_spec(spans.shape)]
            + [pl.BlockSpec(memory_space=pl.ANY)] * len(pieces),
            out_specs=[
                whole_spec((block, 192)),
                whole_spec((block, 192)),
                whole_spec((block, 128)),
            ],
            scratch_shapes=[
                pltpu.VMEM((window, 384), bf16),
                pltpu.VMEM((3, TILE_Q, 128), f32),
                pltpu.VMEM((3, TILE_Q, 128), f32),
                pltpu.VMEM((3, TILE_Q, 128), f32),
                pltpu.SemaphoreType.DMA((len(pieces),)),
            ],
        ),
        out_shape=[
            jax.ShapeDtypeStruct((block, 192), bf16),
            jax.ShapeDtypeStruct((block, 192), f32),
            jax.ShapeDtypeStruct((block, 128), f32),
        ],
        compiler_params=pltpu.CompilerParams(vmem_limit_bytes=40 * 2**20),
        cost_estimate=pl.CostEstimate(
            flops=4 * block * 2304 * 192, bytes_accessed=6 * 2**20, transcendentals=block * 2304 * 3
        ),
        name="attention_forward",
    )(bounds, queries, spans, *pieces)


def query_kernel(bounds, q_ref, span_ref, grad_ref, wide_ref, stat_ref, *rest):
    pieces, (out_ref, kv, accum, sem) = rest[:-4], rest[-4:]
    step = pl.program_id(0)
    block = pieces[0].shape[0]

    @pl.when(step == 0)
    def _():
        for copy in load_window(pieces, kv, sem, block):
            copy.wait()

    first = pl.multiple_of(step * TILE_Q, TILE_Q)
    here = pl.ds(first, TILE_Q)
    accum[...] = jnp.zeros_like(accum)
    q_tile = q_ref[here, :]
    heads = [head_of(q_tile[:, :128], q_tile[:, 128:], h) for h in range(3)]
    g_tile = grad_ref[here, :]
    lane = lax.broadcasted_iota(jnp.int32, (TILE_Q, 128), 1)
    g_pair = g_tile[:, :128]
    g_last = g_tile[:, 128:256]
    none = jnp.zeros((TILE_Q, 128), bf16)
    r_pair = pltpu.roll(g_pair.astype(f32), HEAD_DIM, 1).astype(bf16)
    r_last = pltpu.roll(g_last.astype(f32), HEAD_DIM, 1).astype(bf16)
    grads = [
        jnp.where(lane >= HEAD_DIM, r_pair, none),
        jnp.where(lane < HEAD_DIM, r_pair, none),
        jnp.where(lane >= HEAD_DIM, r_last, none),
    ]
    product_pair = g_pair.astype(f32) * wide_ref[here, 0:128]
    product_last = g_tile[:, 128:192].astype(f32) * wide_ref[here, 128:192]
    deltas = [
        jnp.sum(jnp.where(lane < HEAD_DIM, product_pair, 0.0), axis=1, keepdims=True),
        jnp.sum(jnp.where(lane < HEAD_DIM, 0.0, product_pair), axis=1, keepdims=True),
        jnp.sum(product_last, axis=1, keepdims=True),
    ]
    logs = [stat_ref[here, h : h + 1] for h in range(3)]
    lower, count = bounds[2 * step], bounds[2 * step + 1]

    def run(i, carry):
        begin = pl.multiple_of(lower + i * SPAN_K, 128)
        rows = pl.ds(begin, SPAN_K)
        keys = lax.broadcasted_iota(jnp.int32, (TILE_Q, SPAN_K), 1)
        allowed = (keys >= span_ref[here, 0:1] - begin) & (keys < span_ref[here, 1:2] - begin)
        S = [rows_nt(heads[h], kv[rows, 0:128] if h < 2 else kv[rows, 128:192]) for h in range(3)]
        B = [rows_nt(grads[h], kv[rows, 128:256] if h == 0 else kv[rows, 256:384]) for h in range(3)]
        for h in range(3):
            chance = jnp.exp(jnp.where(allowed, S[h] - logs[h], masked_score))
            change = (chance * (B[h] - deltas[h])).astype(bf16)
            accum[h] += rows_nn(change, kv[rows, 0:128] if h < 2 else kv[rows, 128:256])
        return carry

    lax.fori_loop(0, count, run, 0)
    out_ref[here, 0:128] = (jnp.where(lane < HEAD_DIM, accum[0], accum[1]) * 0.125).astype(bf16)
    out_ref[here, 128:192] = (accum[2][:, :HEAD_DIM] * 0.125).astype(bf16)


def attention_queries(bounds, queries, spans, grads, wide, stats, pieces):
    block = queries.shape[0]
    window = len(pieces) * block
    return pl.pallas_call(
        query_kernel,
        grid_spec=pltpu.PrefetchScalarGridSpec(
            num_scalar_prefetch=1,
            grid=(block // TILE_Q,),
            in_specs=[whole_spec(x.shape) for x in (queries, spans, grads, wide, stats)]
            + [pl.BlockSpec(memory_space=pl.ANY)] * len(pieces),
            out_specs=whole_spec((block, 192)),
            scratch_shapes=[
                pltpu.VMEM((window, 384), bf16),
                pltpu.VMEM((3, TILE_Q, 128), f32),
                pltpu.SemaphoreType.DMA((len(pieces),)),
            ],
        ),
        out_shape=jax.ShapeDtypeStruct((block, 192), bf16),
        compiler_params=pltpu.CompilerParams(vmem_limit_bytes=40 * 2**20),
        cost_estimate=pl.CostEstimate(
            flops=6 * block * 2304 * 192, bytes_accessed=6 * 2**20, transcendentals=block * 2304 * 3
        ),
        name="attention_queries",
    )(bounds, queries, spans, grads, wide, stats, *pieces)


def key_kernel(reach, bounds, kv_ref, span_ref, *rest):
    window = 2 * reach + 1
    q_pieces, g_pieces = rest[:window], rest[window : 2 * window]
    out_ref, qs, gs, key_sum, value_sum, sem = rest[2 * window :]
    step = pl.program_id(0)
    block = q_pieces[0].shape[0]

    @pl.when(step == 0)
    def _():
        copies = load_window(q_pieces, qs, sem.at[0], block)
        copies += load_window(g_pieces, gs, sem.at[1], block)
        for copy in copies:
            copy.wait()

    first = pl.multiple_of(step * TILE_K, TILE_K)
    here = pl.ds(first, TILE_K)
    key_sum[...] = jnp.zeros_like(key_sum)
    value_sum[...] = jnp.zeros_like(value_sum)
    keys_pair = kv_ref[here, 0:128]
    keys = [head_of(keys_pair, kv_ref[here, 128:192], h) for h in range(3)]
    lane = lax.broadcasted_iota(jnp.int32, (TILE_K, 128), 1)
    zero = jnp.zeros((TILE_K, 128), f32)
    v_one = pltpu.roll(kv_ref[here, 128:256].astype(f32), HEAD_DIM, 1)
    v_two = pltpu.roll(kv_ref[here, 256:384].astype(f32), HEAD_DIM, 1)
    values = [
        jnp.where(lane < HEAD_DIM, v_one, zero).astype(bf16),
        jnp.where(lane < HEAD_DIM, zero, v_two).astype(bf16),
        v_two.astype(bf16)[:, :HEAD_DIM],
    ]
    line = lax.broadcasted_iota(jnp.int32, (16, HEAD_DIM), 0)
    slot = lax.broadcasted_iota(jnp.int32, (16, HEAD_DIM), 1)
    selector = jnp.where((slot // 3 == line) & (slot < 18), 1.0, 0.0).astype(bf16)
    lower, count = bounds[2 * step], bounds[2 * step + 1]

    def run(i, carry):
        begin = pl.multiple_of(lower + i * SPAN_Q, 128)
        columns = pl.ds(begin, SPAN_Q)
        place = reach * block + first + lax.broadcasted_iota(jnp.int32, (TILE_K, SPAN_Q), 0)
        allowed = (place >= span_ref[0:1, columns]) & (place < span_ref[1:2, columns])
        lanes = [slice(0, 128), slice(0, 128), slice(128, 192)]
        parts = gs[columns, 192:256]
        stats = rows_nt(selector, parts)
        S = [rows_nt(keys[h], qs[columns, lanes[h]]) for h in range(3)]
        B = [rows_nt(values[h], gs[columns, lanes[h]]) for h in range(3)]
        for h in range(3):
            score = S[h] - stats[h : h + 1, :]
            chance = jnp.exp(jnp.where(allowed, score, masked_score))
            change = (chance * (B[h] - stats[h + 3 : h + 4, :])).astype(bf16)
            size = 128 if h < 2 else HEAD_DIM
            key_sum[h, :, 0:size] += rows_nn(change, qs[columns, lanes[h]])
            value_sum[h, :, 0:size] += rows_nn(chance.astype(bf16), gs[columns, lanes[h]])
        return carry

    lax.fori_loop(0, count, run, 0)
    k_pair = jnp.where(lane < HEAD_DIM, key_sum[0], key_sum[1])
    v_pair = jnp.where(lane < HEAD_DIM, value_sum[0], value_sum[1])
    v_turn = pltpu.roll(v_pair, HEAD_DIM, 1)
    last_turn = pltpu.roll(value_sum[2], HEAD_DIM, 1)
    out_ref[here, 0:128] = k_pair.astype(bf16)
    out_ref[here, 128:256] = jnp.where(lane < HEAD_DIM, key_sum[2], v_turn).astype(bf16)
    out_ref[here, 256:384] = jnp.where(lane < HEAD_DIM, v_turn, last_turn).astype(bf16)


def attention_keys(bounds, pair, spans, q_pieces, g_pieces):
    block = pair.shape[0]
    count = len(q_pieces)
    return pl.pallas_call(
        functools.partial(key_kernel, count // 2),
        grid_spec=pltpu.PrefetchScalarGridSpec(
            num_scalar_prefetch=1,
            grid=(block // TILE_K,),
            in_specs=[whole_spec(x.shape) for x in (pair, spans)]
            + [pl.BlockSpec(memory_space=pl.ANY)] * (2 * count),
            out_specs=whole_spec((block, 384)),
            scratch_shapes=[
                pltpu.VMEM((count * block, 192), bf16),
                pltpu.VMEM((count * block, 256), bf16),
                pltpu.VMEM((3, TILE_K, 128), f32),
                pltpu.VMEM((3, TILE_K, 128), f32),
                pltpu.SemaphoreType.DMA((2, count)),
            ],
        ),
        out_shape=jax.ShapeDtypeStruct((block, 384), bf16),
        compiler_params=pltpu.CompilerParams(vmem_limit_bytes=40 * 2**20),
        cost_estimate=pl.CostEstimate(
            flops=8 * block * 2304 * 192, bytes_accessed=8 * 2**20, transcendentals=block * 2304 * 3
        ),
        name="attention_keys",
    )(bounds, pair, spans, *q_pieces, *g_pieces)


def projection_kernel(place_ref, own, near, far, corner, w_own, w_near, w_far, w_corner, bias_ref, *rest):
    tokens_ref, query_ref, pair_ref, weight, sem = rest
    rows, part = own.shape[0], w_own.shape[0]
    pieces = (w_own, w_near, w_far, w_corner)
    copies = []
    for r, piece in enumerate(pieces):
        where = pl.multiple_of(place_ref[r] * part, part)
        copies.append(pltpu.make_async_copy(piece, weight.at[pl.ds(where, part), :], sem.at[r]))
        copies[-1].start()
    for copy in copies:
        copy.wait()
    for r, piece in enumerate((own, near, far, corner)):
        here = pl.ds(pl.multiple_of(place_ref[r] * rows, rows), rows)
        tile = piece[...]
        tokens_ref[here, :] = tile
        made = rows_nn(tile, weight[...]) + bias_ref[0:1, :]
        pair_ref[here, :] = made[:, : 2 * part].astype(bf16)
        query_ref[here, :] = (made[:, 2 * part :].astype(bf16).astype(f32) * 0.125).astype(bf16)


def project(places, token_pieces, weight_pieces, bias):
    rows, width = token_pieces[0].shape
    part = weight_pieces[0].shape[0]
    block = rows * len(token_pieces)
    vmem = pl.BlockSpec(memory_space=pltpu.VMEM)
    return pl.pallas_call(
        projection_kernel,
        in_specs=[pl.BlockSpec(memory_space=pltpu.SMEM)]
        + [vmem] * 4
        + [pl.BlockSpec(memory_space=pl.ANY)] * 4
        + [vmem],
        out_specs=[vmem] * 3,
        out_shape=[
            jax.ShapeDtypeStruct((block, width), bf16),
            jax.ShapeDtypeStruct((block, part), bf16),
            jax.ShapeDtypeStruct((block, 2 * part), bf16),
        ],
        scratch_shapes=[pltpu.VMEM((width, 3 * part), bf16), pltpu.SemaphoreType.DMA((4,))],
        compiler_params=pltpu.CompilerParams(vmem_limit_bytes=32 * 2**20),
        cost_estimate=pl.CostEstimate(
            flops=2 * block * width * 3 * part, bytes_accessed=5 * 2**20, transcendentals=0
        ),
        name="layer_projection",
    )(places, *token_pieces, *weight_pieces, bias)


def normal_of(values):
    center = values - jnp.mean(values, axis=1, keepdims=True)
    inverse = lax.rsqrt(jnp.mean(center * center, axis=1, keepdims=True) + epsilon)
    return center * inverse, inverse


def normal_back(upstream, normal, inverse, gain):
    scaled = upstream * gain
    mean_scaled = jnp.mean(scaled, axis=1, keepdims=True)
    mean_product = jnp.mean(scaled * normal, axis=1, keepdims=True)
    return (scaled - mean_scaled - normal * mean_product) * inverse


def rows_tn(left, right):
    return lax.dot_general(left, right, (((0,), (0,)), ((), ())), preferred_element_type=f32)


def dense_kernel(place_ref, *refs):
    mixed = refs[0:4]
    tokens_ref, up_ref, small_ref, inner_bias_ref = refs[4:8]
    inner_pieces, outer_pieces = refs[8:12], refs[12:16]
    out_ref, grad_ref, back_ref, outer_grad, inner_grad = refs[16:21]
    w_out, w_inner, w_outer, hidden, activated, slopes, sem = refs[21:]
    rows, width = tokens_ref.shape
    groups = w_inner.shape[0]
    part = width // groups
    copies = []
    for r in range(groups):
        copies.append(
            pltpu.make_async_copy(outer_pieces[r].at[pl.ds(width, part), :], w_out.at[r], sem.at[0, r])
        )
    for r in range(groups):
        here = pl.ds(pl.multiple_of(place_ref[r] * part, part), part)
        for g in range(groups):
            copies.append(
                pltpu.make_async_copy(
                    inner_pieces[r].at[:, pl.ds(g * width, width)],
                    w_inner.at[g, here, :],
                    sem.at[1 + g, r],
                )
            )
    for r in range(groups):
        copies.append(
            pltpu.make_async_copy(
                outer_pieces[r].at[pl.ds(0, width), :], w_outer.at[place_ref[r]], sem.at[1 + groups, r]
            )
        )
    for copy in copies:
        copy.start()

    out_bias, gain_one, shift_one = small_ref[0:1], small_ref[1:2], small_ref[2:3]
    outer_bias, gain_two, shift_two = small_ref[3:4], small_ref[4:5], small_ref[5:6]

    for copy in copies[:groups]:
        copy.wait()
    residual = tokens_ref[...].astype(f32) + out_bias
    for r in range(groups):
        residual = residual + rows_nn(mixed[r][...], w_out[r])
    normal_one, inverse_one = normal_of(residual)
    first = normal_one * gain_one + shift_one
    first_low = first.astype(bf16)
    for copy in copies[groups:]:
        copy.wait()

    def ahead(g, total):
        value = rows_nn(first_low, w_inner[g]) + inner_bias_ref[pl.ds(g, 1), :]
        chance = 0.5 * (1.0 + lax.erf(value * (2.0**-0.5)))
        density = jnp.exp(-0.5 * value * value) * (2.0 * jnp.pi) ** -0.5
        slopes[g] = chance + value * density
        low = (value * chance).astype(bf16)
        activated[g] = low
        return total + rows_nn(low, w_outer[g])

    residual = lax.fori_loop(0, groups, ahead, first + outer_bias)
    normal_two, inverse_two = normal_of(residual)
    out_ref[...] = (normal_two * gain_two + shift_two).astype(bf16)
    upstream = up_ref[...].astype(f32)
    grad_two = normal_back(upstream, normal_two, inverse_two, gain_two)
    grad_two_low = grad_two.astype(bf16)
    shift_two_sum = jnp.sum(upstream, axis=0, keepdims=True)
    gain_two_sum = jnp.sum(upstream * normal_two, axis=0, keepdims=True)
    outer_bias_sum = jnp.sum(grad_two_low.astype(f32), axis=0, keepdims=True)

    def behind(g, total):
        outer_grad[g] = rows_tn(activated[g], grad_two_low).astype(bf16)
        value = (rows_nt(grad_two_low, w_outer[g]) * slopes[g]).astype(bf16)
        hidden[g] = value
        return total + rows_nt(value, w_inner[g])

    grad_first = lax.fori_loop(0, groups, behind, grad_two)
    grad_one = normal_back(grad_first, normal_one, inverse_one, gain_one)
    grad_ref[...] = grad_one
    grad_one_low = grad_one.astype(bf16)
    for r in range(groups):
        back_ref[r] = rows_nt(grad_one_low, w_out[r]).astype(bf16)

    for g in range(groups):
        made = rows_tn(first_low, hidden[g]).astype(bf16)
        for k in range(groups):
            inner_grad[k, g * part : (g + 1) * part, :] = made[k * part : (k + 1) * part, :]
    for r in range(groups):
        made = rows_tn(mixed[r][...], grad_one_low).astype(bf16)
        inner_grad[place_ref[r], width : width + part, :] = made

    sums = [
        jnp.sum(grad_one_low.astype(f32), axis=0, keepdims=True),
        jnp.sum(grad_first * normal_one, axis=0, keepdims=True),
        jnp.sum(grad_first, axis=0, keepdims=True),
        outer_bias_sum,
        gain_two_sum,
        shift_two_sum,
    ]
    line = lax.broadcasted_iota(jnp.int32, (16, part), 0)
    inner_grad[:, width + part : width + part + 64, :] = jnp.zeros((groups, 64, width), bf16)
    for k in range(groups):
        tail = jnp.zeros((16, part), f32)
        for i, line_sum in enumerate(sums):
            tail = jnp.where(line == i, line_sum[:, k * part : (k + 1) * part], tail)
        bias_sum = jnp.sum(hidden[k].astype(f32), axis=0, keepdims=True)
        for i in range(groups):
            tail = jnp.where(
                line == len(sums) + i, bias_sum[:, i * part : (i + 1) * part], tail
            )
        inner_grad[k, width + part : width + part + 16, 0:part] = tail.astype(bf16)


def dense(places, mixed_pieces, tokens, cotangent, small, inner_bias, inner_pieces, outer_pieces):
    rows, width = tokens.shape
    groups = len(inner_pieces)
    part = width // groups
    vmem = pl.BlockSpec(memory_space=pltpu.VMEM)
    hbm = pl.BlockSpec(memory_space=pl.ANY)
    return pl.pallas_call(
        dense_kernel,
        in_specs=[pl.BlockSpec(memory_space=pltpu.SMEM)] + [vmem] * (groups + 4) + [hbm] * (2 * groups),
        out_specs=[vmem] * 5,
        out_shape=[
            jax.ShapeDtypeStruct((rows, width), bf16),
            jax.ShapeDtypeStruct((rows, width), f32),
            jax.ShapeDtypeStruct((groups, rows, part), bf16),
            jax.ShapeDtypeStruct((groups, width, width), bf16),
            jax.ShapeDtypeStruct((groups, width + part + 64, width), bf16),
        ],
        scratch_shapes=[
            pltpu.VMEM((groups, part, width), bf16),
            pltpu.VMEM((groups, width, width), bf16),
            pltpu.VMEM((groups, width, width), bf16),
            pltpu.VMEM((groups, rows, width), bf16),
            pltpu.VMEM((groups, rows, width), bf16),
            pltpu.VMEM((groups, rows, width), f32),
            pltpu.SemaphoreType.DMA((groups + 2, groups)),
        ],
        compiler_params=pltpu.CompilerParams(vmem_limit_bytes=56 * 2**20),
        cost_estimate=pl.CostEstimate(
            flops=36 * rows * width * width * groups // 3 * 2,
            bytes_accessed=24 * 2**20,
            transcendentals=2 * rows * width * groups,
        ),
        name="layer_dense",
    )(places, *mixed_pieces, tokens, cotangent, small, inner_bias, *inner_pieces, *outer_pieces)

def gather_kernel(place_ref, p0, p1, p2, p3, wide_ref, stat_ref, out_ref):
    rows, part = p0.shape
    lane = lax.broadcasted_iota(jnp.int32, (rows, 128), 1)
    slot = lax.broadcasted_iota(jnp.int32, (rows, HEAD_DIM), 1)
    for r, piece in enumerate((p0, p1, p2, p3)):
        here = pl.ds(pl.multiple_of(place_ref[r] * rows, rows), rows)
        tile = piece[...]
        product = tile.astype(f32) * wide_ref[here, :]
        pair, last = product[:, 0:128], product[:, 128:192]
        values = [stat_ref[here, h : h + 1] for h in range(3)] + [
            jnp.sum(jnp.where(lane < HEAD_DIM, pair, 0.0), axis=1, keepdims=True),
            jnp.sum(jnp.where(lane < HEAD_DIM, 0.0, pair), axis=1, keepdims=True),
            jnp.sum(last, axis=1, keepdims=True),
        ]
        tail = jnp.zeros((rows, HEAD_DIM), f32)
        for i, left in enumerate(values):
            for j in range(3):
                high = left.astype(bf16).astype(f32)
                tail = jnp.where(slot == 3 * i + j, high, tail)
                left = left - high
        out_ref[here, 0:192] = tile
        out_ref[here, 192:256] = tail.astype(bf16)


def gathered(places, pieces, wide, stats):
    block = wide.shape[0]
    vmem = pl.BlockSpec(memory_space=pltpu.VMEM)
    return pl.pallas_call(
        gather_kernel,
        in_specs=[pl.BlockSpec(memory_space=pltpu.SMEM)] + [vmem] * 6,
        out_specs=vmem,
        out_shape=jax.ShapeDtypeStruct((block, 256), bf16),
        compiler_params=pltpu.CompilerParams(vmem_limit_bytes=16 * 2**20),
        cost_estimate=pl.CostEstimate(flops=2**20, bytes_accessed=3 * 2**20, transcendentals=0),
        name="layer_gather",
    )(places, *pieces, wide, stats)


def heads_kernel(place_ref, tokens_ref, query_ref, pair_ref, w0, w1, w2, w3, grad_ref, back_ref, weight, sem):
    groups, part = grad_ref.shape[0], w0.shape[0]
    rows = back_ref.shape[1]
    copies = []
    for r, piece in enumerate((w0, w1, w2, w3)):
        where = pl.multiple_of(place_ref[r] * part, part)
        copies.append(pltpu.make_async_copy(piece, weight.at[pl.ds(where, part), :], sem.at[r]))
        copies[-1].start()
    tokens = tokens_ref[...]
    pair_grad = rows_tn(tokens, pair_ref[...]).astype(bf16)
    query_grad = rows_tn(tokens, query_ref[...]).astype(bf16)
    for k in range(groups):
        here = slice(k * part, (k + 1) * part)
        grad_ref[k, :, 0 : 2 * part] = pair_grad[here]
        grad_ref[k, :, 2 * part : 3 * part] = query_grad[here]
    ones = jnp.ones((tokens.shape[0], HEAD_DIM), bf16)
    query_sum = rows_tn(query_ref[...], ones)
    value_sum = rows_tn(pair_ref[:, part:], ones)
    lane = lax.broadcasted_iota(jnp.int32, (part, HEAD_DIM), 1)
    sums = jnp.where(lane == 0, query_sum, jnp.where(lane == 1, value_sum, 0.0))
    grad_ref[:, :, 3 * part : 3 * part + HEAD_DIM] = jnp.zeros((groups, part, HEAD_DIM), bf16)
    grad_ref[place_ref[0], :, 3 * part : 3 * part + HEAD_DIM] = sums.astype(bf16)
    for copy in copies:
        copy.wait()
    for k in range(groups):
        here = slice(k * rows, (k + 1) * rows)
        made = rows_nt(pair_ref[here, :], weight[:, : 2 * part])
        made = made + rows_nt(query_ref[here, :], weight[:, 2 * part :])
        back_ref[k] = made.astype(bf16)


def head_grads(places, tokens, grad_query, grad_pair, weight_pieces):
    block, width = tokens.shape
    groups, part = len(weight_pieces), weight_pieces[0].shape[0]
    vmem = pl.BlockSpec(memory_space=pltpu.VMEM)
    return pl.pallas_call(
        heads_kernel,
        in_specs=[pl.BlockSpec(memory_space=pltpu.SMEM)]
        + [vmem] * 3
        + [pl.BlockSpec(memory_space=pl.ANY)] * groups,
        out_specs=[vmem] * 2,
        out_shape=[
            jax.ShapeDtypeStruct((groups, part, 3 * part + HEAD_DIM), bf16),
            jax.ShapeDtypeStruct((groups, block // groups, width), bf16),
        ],
        scratch_shapes=[pltpu.VMEM((width, 3 * part), bf16), pltpu.SemaphoreType.DMA((groups,))],
        compiler_params=pltpu.CompilerParams(vmem_limit_bytes=32 * 2**20),
        cost_estimate=pl.CostEstimate(
            flops=4 * block * width * 3 * part, bytes_accessed=8 * 2**20, transcendentals=0
        ),
        name="layer_heads",
    )(places, tokens, grad_query, grad_pair, *weight_pieces)


def both(left, right):
    return (left.astype(f32) + right.astype(f32)).astype(bf16)


def halves(block, bit, axis):
    size = block.shape[axis] // 2
    kept = lax.dynamic_slice_in_dim(block, bit * size, size, axis)
    sent = lax.dynamic_slice_in_dim(block, (1 - bit) * size, size, axis)
    return kept, sent


def scatter_sum(block, axis_name, order, axis):
    index = lax.axis_index(axis_name)
    for step in order:
        kept, sent = halves(block, (index // step) % 2, axis)
        block = both(kept, swapped(sent, axis_name, step))
    return block


def gather_back(block, axis_name, order, axis):
    index = lax.axis_index(axis_name)
    for step in reversed(order):
        other = swapped(block, axis_name, step)
        late = (index // step) % 2 == 1
        block = jnp.where(
            late,
            jnp.concatenate([other, block], axis),
            jnp.concatenate([block, other], axis),
        )
    return block


def on_device(
    tokens,
    doc_start,
    cotangent,
    query_weight,
    key_weight,
    value_weight,
    out_weight,
    query_bias,
    value_bias,
    out_bias,
    first_gain,
    first_shift,
    inner_weight,
    inner_bias,
    outer_weight,
    outer_bias,
    second_gain,
    second_shift,
):
    rows, width = tokens.shape
    cycle = lax.axis_size("ctx")
    shards = lax.axis_size("wt")
    block = rows * shards
    reach = (MAXDOC + block - 2) // block
    window = (2 * reach + 1) * block
    c = lax.axis_index("ctx")
    w = lax.axis_index("wt")
    part = width // shards
    places = jnp.stack([w ^ r for r in range(shards)]).astype(jnp.int32)

    def spread(own, near):
        far = swapped(own, "wt", 2)
        return [own, near, far, swapped(far, "wt", 1)]

    def columns(r):
        start = (w ^ r) * part
        return jnp.concatenate(
            [
                lax.dynamic_slice_in_dim(x, start, part, 1)
                for x in (key_weight, value_weight, query_weight)
            ],
            axis=1,
        )

    token_pieces = spread(tokens, swapped(tokens, "wt", 1))
    weight_pieces = [columns(0)] + [swapped(columns(r), "wt", r) for r in range(1, shards)]
    head_bias = jnp.concatenate([jnp.zeros((part,), f32), value_bias.astype(f32), query_bias.astype(f32)])
    head_bias = jnp.broadcast_to(head_bias[None], (8, 3 * part))

    pad = reach * block
    padded = jnp.pad(doc_start, (pad, pad), constant_values=-1)
    base = c * block - pad
    marks = lax.dynamic_slice_in_dim(padded, c * block, window)
    place = jnp.arange(window, dtype=jnp.int32)
    begins = jnp.where((marks == base + place) | (marks < 0), place, window)
    next_begin = lax.cummin(begins, axis=0, reverse=True)
    stops = jnp.concatenate([next_begin[1:], jnp.full((1,), window, jnp.int32)])
    starts = marks - base
    spans_row = jnp.stack([starts, stops] + [jnp.zeros_like(starts)] * 6)
    spans_column = spans_row[:, pad : pad + block].T
    own_starts = starts[pad : pad + block]
    own_stops = stops[pad : pad + block]

    def bounds_of(tile, span):
        lowest = own_starts.reshape(-1, tile)[:, 0] // 128 * 128
        highest = own_stops.reshape(-1, tile)[:, -1]
        count = (highest - lowest + span - 1) // span
        lowest = jnp.minimum(lowest, (window - count * span) // 128 * 128)
        return jnp.stack([lowest, count], axis=1).reshape(-1)

    query_bounds = bounds_of(TILE_Q, SPAN_K)
    key_bounds = bounds_of(TILE_K, SPAN_Q)

    block_tokens, queries, pair = project(places, token_pieces, weight_pieces, head_bias)

    distances = [d for d in range(reach, -reach - 1, -1)]

    def halo(own):
        return [own if d == 0 else shifted(own, "ctx", d) for d in distances]

    pairs = halo(pair)

    small_own = jnp.stack(
        [out_bias, first_gain, first_shift, outer_bias, second_gain, second_shift]
    )
    small_own = jnp.concatenate([small_own, inner_bias.reshape(-1, part)], axis=0)
    small_own = jnp.pad(small_own, ((0, 16 - small_own.shape[0]), (0, width - part)))
    outer_own = jnp.concatenate([outer_weight, out_weight, small_own], axis=0)
    inner_own, outer_own, _ = lax.optimization_barrier((inner_weight, outer_own, token_pieces[2]))
    inner_pieces = spread(inner_own, swapped(inner_own, "wt", 1))
    outer_pieces = spread(outer_own, swapped(outer_own, "wt", 1))
    small = jnp.stack([x[width + part :, :part] for x in outer_pieces]).astype(f32)
    small = [lax.dynamic_index_in_dim(small, w ^ k, 0, keepdims=False) for k in range(shards)]
    small_rows = jnp.concatenate([x[:8] for x in small], axis=1)
    inner_bias_rows = jnp.stack([x[6:10].reshape(-1) for x in small])

    mixed, mixed_wide, stat_columns = attention_forward(query_bounds, queries, spans_column, pairs)
    queries_sent, _ = lax.optimization_barrier((queries, pairs))
    query_halo = [
        queries if d == 0 else shifted(queries_sent, "ctx", d) for d in distances
    ]

    mixed_rows = mixed.reshape(shards, rows, part)
    mixed_pieces = [
        lax.dynamic_index_in_dim(mixed_rows, w ^ r, 0, keepdims=False) for r in range(shards)
    ]
    mixed_pieces = [mixed_pieces[0]] + [
        swapped(mixed_pieces[r], "wt", r) for r in range(1, shards)
    ]
    mixed_pieces, query_halo = lax.optimization_barrier((mixed_pieces, query_halo))
    layer_out, grad_one, back, outer_grad, inner_grad = dense(
        places,
        mixed_pieces,
        tokens,
        cotangent,
        small_rows,
        inner_bias_rows,
        inner_pieces,
        outer_pieces,
    )

    back_pieces = [back[0]] + [swapped(back[r], "wt", r) for r in range(1, shards)]

    def near_sum(grad):
        kept, sent = halves(grad.reshape((2, 2) + grad.shape[1:]), w % 2, 1)
        return both(kept, swapped(sent, "wt", 1))

    def far_sum(grad):
        kept, sent = halves(grad, w // 2, 0)
        return both(kept, swapped(sent, "wt", 2))[0, 0]

    outer_near = near_sum(outer_grad)
    inner_near = near_sum(inner_grad)
    grads = gathered(places, back_pieces, mixed_wide, stat_columns)
    grad_halo = halo(grads)
    outer_far = far_sum(outer_near)
    grad_query = attention_queries(
        query_bounds, queries, spans_column, grads, mixed_wide, stat_columns, pairs
    )
    grad_query, grad_halo, outer_far, inner_near = lax.optimization_barrier(
        (grad_query, grad_halo, outer_far, inner_near)
    )

    near_first = [1 << i for i in range(cycle.bit_length() - 1)]
    far_first = [2, 1] + near_first[2:]
    outer_part = scatter_sum(outer_far, "ctx", near_first[:1], 0)
    inner_far = far_sum(inner_near)
    grad_pair = attention_keys(key_bounds, pair, spans_row, query_halo, grad_halo)
    grad_pair, outer_part, inner_far = lax.optimization_barrier(
        (grad_pair, outer_part, inner_far)
    )

    head_grad, token_partial = head_grads(places, block_tokens, grad_query, grad_pair, weight_pieces)
    outer_part = scatter_sum(outer_part, "ctx", near_first[1:], 0)
    inner_part = scatter_sum(inner_far, "ctx", far_first, 0)
    head_part = scatter_sum(head_grad, "ctx", near_first, 1)
    token_sum = far_sum(near_sum(token_partial))
    outer_total = gather_back(outer_part, "ctx", near_first, 0)
    inner_total = gather_back(inner_part, "ctx", far_first, 0)
    head_pieces = [
        lax.dynamic_index_in_dim(head_part, w ^ r, 0, keepdims=False) for r in range(shards)
    ]
    head_pieces = [head_pieces[0]] + [swapped(head_pieces[r], "wt", r) for r in range(1, shards)]
    head_parts = jnp.stack(
        [
            lax.dynamic_index_in_dim(jnp.stack(head_pieces), w ^ k, 0, keepdims=False)
            for k in range(shards)
        ]
    )
    head_total = gather_back(head_parts, "ctx", near_first, 1)

    tokens_gradient = grad_one + token_sum.astype(f32)
    key_total, value_total, query_total = (
        jnp.concatenate(
            [head_total[k, :, i * part : (i + 1) * part] for k in range(shards)], axis=1
        ).astype(f32)
        for i in range(3)
    )
    own_total = lax.dynamic_index_in_dim(head_total, w, 0, keepdims=False)
    inner_rows = inner_total[:width].reshape(shards, part, width)
    inner_rows = jnp.concatenate([inner_rows[k] for k in range(shards)], axis=1).astype(f32)
    lines = inner_total[width + part : width + part + 16, :part].astype(f32)

    return (
        layer_out,
        tokens_gradient,
        query_total,
        key_total,
        value_total,
        inner_total[width : width + part].astype(f32),
        own_total[:, 3 * part].astype(f32),
        own_total[:, 3 * part + 1].astype(f32),
        lines[0],
        lines[1],
        lines[2],
        inner_rows,
        lines[6:10].reshape(-1),
        outer_total.astype(f32),
        lines[3],
        lines[4],
        lines[5],
    )


def solution(mesh):
    matrix, vector = P("wt", None), P("wt")
    stream = P(("ctx", "wt"), None)
    in_specs = (stream, P(), stream) + (matrix,) * 4 + (vector,) * 5
    in_specs += (matrix, vector, matrix, vector, vector, vector)
    out_specs = (stream, stream) + (matrix,) * 4 + (vector,) * 5
    out_specs += (matrix, vector, matrix, vector, vector, vector)
    return jax.shard_map(
        on_device, mesh=mesh, in_specs=in_specs, out_specs=out_specs, check_vma=False
    )
```

```python
import functools

import jax
import jax.numpy as jnp
from jax import lax
from jax.experimental import pallas as pl
from jax.experimental.pallas import tpu as pltpu
from jax.sharding import PartitionSpec as P

HEADS = 12
HEAD_DIM = 64
MAXDOC = 2048
TILE_Q = 256
SPAN_K = 768
TILE_K = 256
SPAN_Q = 768

masked_score = -1e30
epsilon = 1e-06
bf16 = jnp.bfloat16
f32 = jnp.float32


def swapped(block, axis, bit):
    count = lax.axis_size(axis)
    return lax.ppermute(block, axis, [(i, i ^ bit) for i in range(count)])


def shifted(block, axis, distance):
    count = lax.axis_size(axis)
    route = [(i, i + distance) for i in range(count) if 0 <= i + distance < count]
    return lax.ppermute(block, axis, route)


def rows_nt(left, right):
    return lax.dot_general(left, right, (((1,), (1,)), ((), ())), preferred_element_type=f32)


def rows_nn(left, right):
    return lax.dot_general(left, right, (((1,), (0,)), ((), ())), preferred_element_type=f32)


def load_window(pieces, target, sem, starts):
    copies = []
    for i, piece in enumerate(pieces):
        rows = pl.ds(pl.multiple_of(starts[i], 128), piece.shape[0])
        copies.append(pltpu.make_async_copy(piece, target.at[rows, :], sem.at[i]))
    for copy in copies:
        copy.start()
    return copies


def lanes_of(values, size):
    return jnp.tile(values, (1, size // 128))


def head_of(tile0, tile1, head):
    lane = lax.broadcasted_iota(jnp.int32, tile0.shape, 1)
    if head == 0:
        return jnp.where(lane < HEAD_DIM, tile0, jnp.zeros_like(tile0))
    if head == 1:
        return jnp.where(lane >= HEAD_DIM, tile0, jnp.zeros_like(tile0))
    return tile1


def forward_kernel(bounds, q_ref, span_ref, *rest):
    pieces, (out_ref, wide_ref, stat_ref, kv, top, total, accum, sem) = rest[:-8], rest[-8:]
    step = pl.program_id(0)

    @pl.when(step == 0)
    def _():
        for copy in load_window(pieces, kv, sem, [bounds[8 + i] for i in range(len(pieces))]):
            copy.wait()

    first = pl.multiple_of(step * TILE_Q, TILE_Q)
    here = pl.ds(first, TILE_Q)
    top[...] = jnp.full_like(top, masked_score)
    total[...] = jnp.zeros_like(total)
    accum[...] = jnp.zeros_like(accum)
    q_tile = q_ref[here, :]
    heads = [head_of(q_tile[:, :128], q_tile[:, 128:], h) for h in range(3)]
    lower, count = bounds[2 * step], bounds[2 * step + 1]

    def run(i, carry):
        begin = pl.multiple_of(lower + i * SPAN_K, 128)
        rows = pl.ds(begin, SPAN_K)
        keys = lax.broadcasted_iota(jnp.int32, (TILE_Q, SPAN_K), 1)
        allowed = (keys >= span_ref[here, 0:1] - begin) & (keys < span_ref[here, 1:2] - begin)
        scores = [rows_nt(heads[h], kv[rows, 0:128] if h < 2 else kv[rows, 128:192]) for h in range(3)]
        for h in range(3):
            score = scores[h]
            score = jnp.where(allowed, score, masked_score)
            before = top[h]
            newest = jnp.maximum(before, jnp.max(score, axis=1, keepdims=True))
            factor = jnp.exp(before - newest)
            weight = jnp.exp(score - lanes_of(newest, SPAN_K))
            part = weight[:, 0:128]
            for j in range(1, SPAN_K // 128):
                part = part + weight[:, 128 * j : 128 * j + 128]
            total[h] = total[h] * factor + part
            values = kv[rows, 128:256] if h == 0 else kv[rows, 256:384]
            accum[h] = accum[h] * factor + rows_nn(weight.astype(bf16), values)
            top[h] = newest
        return carry

    lax.fori_loop(0, count, run, 0)
    lane = lax.broadcasted_iota(jnp.int32, (TILE_Q, 128), 1)
    mixed, stats = [], jnp.zeros((TILE_Q, 128), f32)
    for h in range(3):
        mass = jnp.sum(total[h], axis=1, keepdims=True)
        mixed.append(pltpu.roll(accum[h] / mass, HEAD_DIM, 1))
        stats = jnp.where(lane == h, top[h] + jnp.log(mass), stats)
    pair = jnp.where(lane < HEAD_DIM, mixed[0], mixed[1])
    wide_ref[here, 0:128] = pair
    wide_ref[here, 128:192] = mixed[2][:, :HEAD_DIM]
    out_ref[here, 0:128] = pair.astype(bf16)
    out_ref[here, 128:192] = mixed[2][:, :HEAD_DIM].astype(bf16)
    stat_ref[here, :] = stats


def whole_spec(shape):
    return pl.BlockSpec(shape, lambda i, *_: (0,) * len(shape))


def attention_forward(bounds, queries, spans, pieces):
    block = queries.shape[0]
    window = sum(x.shape[0] for x in pieces)
    return pl.pallas_call(
        forward_kernel,
        grid_spec=pltpu.PrefetchScalarGridSpec(
            num_scalar_prefetch=1,
            grid=(block // TILE_Q,),
            in_specs=[whole_spec(queries.shape), whole_spec(spans.shape)]
            + [pl.BlockSpec(memory_space=pl.ANY)] * len(pieces),
            out_specs=[
                whole_spec((block, 192)),
                whole_spec((block, 192)),
                whole_spec((block, 128)),
            ],
            scratch_shapes=[
                pltpu.VMEM((window, 384), bf16),
                pltpu.VMEM((3, TILE_Q, 128), f32),
                pltpu.VMEM((3, TILE_Q, 128), f32),
                pltpu.VMEM((3, TILE_Q, 128), f32),
                pltpu.SemaphoreType.DMA((len(pieces),)),
            ],
        ),
        out_shape=[
            jax.ShapeDtypeStruct((block, 192), bf16),
            jax.ShapeDtypeStruct((block, 192), f32),
            jax.ShapeDtypeStruct((block, 128), f32),
        ],
        compiler_params=pltpu.CompilerParams(vmem_limit_bytes=40 * 2**20),
        cost_estimate=pl.CostEstimate(
            flops=4 * block * 2304 * 192, bytes_accessed=6 * 2**20, transcendentals=block * 2304 * 3
        ),
        name="attention_forward",
    )(bounds, queries, spans, *pieces)


def query_kernel(bounds, q_ref, span_ref, grad_ref, wide_ref, stat_ref, *rest):
    pieces, (out_ref, kv, accum, sem) = rest[:-4], rest[-4:]
    step = pl.program_id(0)

    @pl.when(step == 0)
    def _():
        for copy in load_window(pieces, kv, sem, [bounds[8 + i] for i in range(len(pieces))]):
            copy.wait()

    first = pl.multiple_of(step * TILE_Q, TILE_Q)
    here = pl.ds(first, TILE_Q)
    accum[...] = jnp.zeros_like(accum)
    q_tile = q_ref[here, :]
    heads = [head_of(q_tile[:, :128], q_tile[:, 128:], h) for h in range(3)]
    g_tile = grad_ref[here, :]
    lane = lax.broadcasted_iota(jnp.int32, (TILE_Q, 128), 1)
    g_pair = g_tile[:, :128]
    g_last = g_tile[:, 128:256]
    none = jnp.zeros((TILE_Q, 128), bf16)
    r_pair = pltpu.roll(g_pair.astype(f32), HEAD_DIM, 1).astype(bf16)
    r_last = pltpu.roll(g_last.astype(f32), HEAD_DIM, 1).astype(bf16)
    grads = [
        jnp.where(lane >= HEAD_DIM, r_pair, none),
        jnp.where(lane < HEAD_DIM, r_pair, none),
        jnp.where(lane >= HEAD_DIM, r_last, none),
    ]
    product_pair = g_pair.astype(f32) * wide_ref[here, 0:128]
    product_last = g_tile[:, 128:192].astype(f32) * wide_ref[here, 128:192]
    deltas = [
        jnp.sum(jnp.where(lane < HEAD_DIM, product_pair, 0.0), axis=1, keepdims=True),
        jnp.sum(jnp.where(lane < HEAD_DIM, 0.0, product_pair), axis=1, keepdims=True),
        jnp.sum(product_last, axis=1, keepdims=True),
    ]
    logs = [stat_ref[here, h : h + 1] for h in range(3)]
    lower, count = bounds[2 * step], bounds[2 * step + 1]

    def run(i, carry):
        begin = pl.multiple_of(lower + i * SPAN_K, 128)
        rows = pl.ds(begin, SPAN_K)
        keys = lax.broadcasted_iota(jnp.int32, (TILE_Q, SPAN_K), 1)
        allowed = (keys >= span_ref[here, 0:1] - begin) & (keys < span_ref[here, 1:2] - begin)
        S = [rows_nt(heads[h], kv[rows, 0:128] if h < 2 else kv[rows, 128:192]) for h in range(3)]
        B = [rows_nt(grads[h], kv[rows, 128:256] if h == 0 else kv[rows, 256:384]) for h in range(3)]
        for h in range(3):
            chance = jnp.exp(jnp.where(allowed, S[h] - logs[h], masked_score))
            change = (chance * (B[h] - deltas[h])).astype(bf16)
            accum[h] += rows_nn(change, kv[rows, 0:128] if h < 2 else kv[rows, 128:256])
        return carry

    lax.fori_loop(0, count, run, 0)
    out_ref[here, 0:128] = (jnp.where(lane < HEAD_DIM, accum[0], accum[1]) * 0.125).astype(bf16)
    out_ref[here, 128:192] = (accum[2][:, :HEAD_DIM] * 0.125).astype(bf16)


def attention_queries(bounds, queries, spans, grads, wide, stats, pieces):
    block = queries.shape[0]
    window = sum(x.shape[0] for x in pieces)
    return pl.pallas_call(
        query_kernel,
        grid_spec=pltpu.PrefetchScalarGridSpec(
            num_scalar_prefetch=1,
            grid=(block // TILE_Q,),
            in_specs=[whole_spec(x.shape) for x in (queries, spans, grads, wide, stats)]
            + [pl.BlockSpec(memory_space=pl.ANY)] * len(pieces),
            out_specs=whole_spec((block, 192)),
            scratch_shapes=[
                pltpu.VMEM((window, 384), bf16),
                pltpu.VMEM((3, TILE_Q, 128), f32),
                pltpu.SemaphoreType.DMA((len(pieces),)),
            ],
        ),
        out_shape=jax.ShapeDtypeStruct((block, 192), bf16),
        compiler_params=pltpu.CompilerParams(vmem_limit_bytes=40 * 2**20),
        cost_estimate=pl.CostEstimate(
            flops=6 * block * 2304 * 192, bytes_accessed=6 * 2**20, transcendentals=block * 2304 * 3
        ),
        name="attention_queries",
    )(bounds, queries, spans, grads, wide, stats, *pieces)


def key_kernel(reach, bounds, kv_ref, span_ref, *rest):
    window = 2 * reach + 1
    q_pieces, g_pieces = rest[:window], rest[window : 2 * window]
    out_ref, qs, gs, key_sum, value_sum, sem = rest[2 * window :]
    step = pl.program_id(0)
    block = q_pieces[0].shape[0]

    @pl.when(step == 0)
    def _():
        copies = load_window(q_pieces, qs, sem.at[0], [i * block for i in range(window)])
        copies += load_window(g_pieces, gs, sem.at[1], [i * block for i in range(window)])
        for copy in copies:
            copy.wait()

    first = pl.multiple_of(step * TILE_K, TILE_K)
    here = pl.ds(first, TILE_K)
    key_sum[...] = jnp.zeros_like(key_sum)
    value_sum[...] = jnp.zeros_like(value_sum)
    keys_pair = kv_ref[here, 0:128]
    keys = [head_of(keys_pair, kv_ref[here, 128:192], h) for h in range(3)]
    lane = lax.broadcasted_iota(jnp.int32, (TILE_K, 128), 1)
    zero = jnp.zeros((TILE_K, 128), f32)
    v_one = pltpu.roll(kv_ref[here, 128:256].astype(f32), HEAD_DIM, 1)
    v_two = pltpu.roll(kv_ref[here, 256:384].astype(f32), HEAD_DIM, 1)
    values = [
        jnp.where(lane < HEAD_DIM, v_one, zero).astype(bf16),
        jnp.where(lane < HEAD_DIM, zero, v_two).astype(bf16),
        v_two.astype(bf16)[:, :HEAD_DIM],
    ]
    line = lax.broadcasted_iota(jnp.int32, (16, HEAD_DIM), 0)
    slot = lax.broadcasted_iota(jnp.int32, (16, HEAD_DIM), 1)
    selector = jnp.where((slot // 3 == line) & (slot < 18), 1.0, 0.0).astype(bf16)
    lower, count = bounds[2 * step], bounds[2 * step + 1]

    def run(i, carry):
        begin = pl.multiple_of(lower + i * SPAN_Q, 128)
        columns = pl.ds(begin, SPAN_Q)
        place = reach * block + first + lax.broadcasted_iota(jnp.int32, (TILE_K, SPAN_Q), 0)
        allowed = (place >= span_ref[0:1, columns]) & (place < span_ref[1:2, columns])
        lanes = [slice(0, 128), slice(0, 128), slice(128, 192)]
        parts = gs[columns, 192:256]
        stats = rows_nt(selector, parts)
        S = [rows_nt(keys[h], qs[columns, lanes[h]]) for h in range(3)]
        B = [rows_nt(values[h], gs[columns, lanes[h]]) for h in range(3)]
        for h in range(3):
            score = S[h] - stats[h : h + 1, :]
            chance = jnp.exp(jnp.where(allowed, score, masked_score))
            change = (chance * (B[h] - stats[h + 3 : h + 4, :])).astype(bf16)
            size = 128 if h < 2 else HEAD_DIM
            key_sum[h, :, 0:size] += rows_nn(change, qs[columns, lanes[h]])
            value_sum[h, :, 0:size] += rows_nn(chance.astype(bf16), gs[columns, lanes[h]])
        return carry

    lax.fori_loop(0, count, run, 0)
    k_pair = jnp.where(lane < HEAD_DIM, key_sum[0], key_sum[1])
    v_pair = jnp.where(lane < HEAD_DIM, value_sum[0], value_sum[1])
    v_turn = pltpu.roll(v_pair, HEAD_DIM, 1)
    last_turn = pltpu.roll(value_sum[2], HEAD_DIM, 1)
    out_ref[here, 0:128] = k_pair.astype(bf16)
    out_ref[here, 128:256] = jnp.where(lane < HEAD_DIM, key_sum[2], v_turn).astype(bf16)
    out_ref[here, 256:384] = jnp.where(lane < HEAD_DIM, v_turn, last_turn).astype(bf16)


def attention_keys(bounds, pair, spans, q_pieces, g_pieces):
    block = pair.shape[0]
    count = len(q_pieces)
    return pl.pallas_call(
        functools.partial(key_kernel, count // 2),
        grid_spec=pltpu.PrefetchScalarGridSpec(
            num_scalar_prefetch=1,
            grid=(block // TILE_K,),
            in_specs=[whole_spec(x.shape) for x in (pair, spans)]
            + [pl.BlockSpec(memory_space=pl.ANY)] * (2 * count),
            out_specs=whole_spec((block, 384)),
            scratch_shapes=[
                pltpu.VMEM((count * block, 192), bf16),
                pltpu.VMEM((count * block, 256), bf16),
                pltpu.VMEM((3, TILE_K, 128), f32),
                pltpu.VMEM((3, TILE_K, 128), f32),
                pltpu.SemaphoreType.DMA((2, count)),
            ],
        ),
        out_shape=jax.ShapeDtypeStruct((block, 384), bf16),
        compiler_params=pltpu.CompilerParams(vmem_limit_bytes=40 * 2**20),
        cost_estimate=pl.CostEstimate(
            flops=8 * block * 2304 * 192, bytes_accessed=8 * 2**20, transcendentals=block * 2304 * 3
        ),
        name="attention_keys",
    )(bounds, pair, spans, *q_pieces, *g_pieces)


def projection_kernel(place_ref, own, near, far, corner, w_own, w_near, w_far, w_corner, bias_ref, *rest):
    tokens_ref, query_ref, pair_ref, weight, sem = rest
    rows, part = own.shape[0], w_own.shape[0]
    pieces = (w_own, w_near, w_far, w_corner)
    copies = []
    for r, piece in enumerate(pieces):
        where = pl.multiple_of(place_ref[r] * part, part)
        copies.append(pltpu.make_async_copy(piece, weight.at[pl.ds(where, part), :], sem.at[r]))
        copies[-1].start()
    for copy in copies:
        copy.wait()
    for r, piece in enumerate((own, near, far, corner)):
        here = pl.ds(pl.multiple_of(place_ref[r] * rows, rows), rows)
        tile = piece[...]
        tokens_ref[here, :] = tile
        made = rows_nn(tile, weight[...]) + bias_ref[0:1, :]
        pair_ref[here, :] = made[:, : 2 * part].astype(bf16)
        query_ref[here, :] = (made[:, 2 * part :].astype(bf16).astype(f32) * 0.125).astype(bf16)


def project(places, token_pieces, weight_pieces, bias):
    rows, width = token_pieces[0].shape
    part = weight_pieces[0].shape[0]
    block = rows * len(token_pieces)
    vmem = pl.BlockSpec(memory_space=pltpu.VMEM)
    return pl.pallas_call(
        projection_kernel,
        in_specs=[pl.BlockSpec(memory_space=pltpu.SMEM)]
        + [vmem] * 4
        + [pl.BlockSpec(memory_space=pl.ANY)] * 4
        + [vmem],
        out_specs=[vmem] * 3,
        out_shape=[
            jax.ShapeDtypeStruct((block, width), bf16),
            jax.ShapeDtypeStruct((block, part), bf16),
            jax.ShapeDtypeStruct((block, 2 * part), bf16),
        ],
        scratch_shapes=[pltpu.VMEM((width, 3 * part), bf16), pltpu.SemaphoreType.DMA((4,))],
        compiler_params=pltpu.CompilerParams(vmem_limit_bytes=32 * 2**20),
        cost_estimate=pl.CostEstimate(
            flops=2 * block * width * 3 * part, bytes_accessed=5 * 2**20, transcendentals=0
        ),
        name="layer_projection",
    )(places, *token_pieces, *weight_pieces, bias)


def normal_of(values):
    center = values - jnp.mean(values, axis=1, keepdims=True)
    inverse = lax.rsqrt(jnp.mean(center * center, axis=1, keepdims=True) + epsilon)
    return center * inverse, inverse


def normal_back(upstream, normal, inverse, gain):
    scaled = upstream * gain
    mean_scaled = jnp.mean(scaled, axis=1, keepdims=True)
    mean_product = jnp.mean(scaled * normal, axis=1, keepdims=True)
    return (scaled - mean_scaled - normal * mean_product) * inverse


def rows_tn(left, right):
    return lax.dot_general(left, right, (((0,), (0,)), ((), ())), preferred_element_type=f32)


def dense_kernel(place_ref, *refs):
    mixed = refs[0:4]
    tokens_ref, up_ref, small_ref, inner_bias_ref = refs[4:8]
    packs = refs[8:12]
    out_ref, grad_ref, back_ref = refs[12:15]
    outer_keep, outer_send, inner_keep, inner_send = refs[15:19]
    w_out, w_inner, w_outer, hidden, activated, slopes, inner_grad, sem = refs[19:]
    rows, width = tokens_ref.shape
    groups = w_inner.shape[0]
    part = width // groups
    copies = []
    for r in range(groups):
        copies.append(
            pltpu.make_async_copy(packs[r].at[pl.ds(width, part), :], w_out.at[r], sem.at[0, r])
        )
    for r in range(groups):
        here = pl.ds(pl.multiple_of(place_ref[r] * part, part), part)
        for g in range(groups):
            copies.append(
                pltpu.make_async_copy(
                    packs[r].at[pl.ds(width + part + 16 + g * part, part), :],
                    w_inner.at[g, here, :],
                    sem.at[1 + g, r],
                )
            )
    for r in range(groups):
        copies.append(
            pltpu.make_async_copy(
                packs[r].at[pl.ds(0, width), :], w_outer.at[place_ref[r]], sem.at[1 + groups, r]
            )
        )
    for copy in copies:
        copy.start()

    out_bias, gain_one, shift_one = small_ref[0:1], small_ref[1:2], small_ref[2:3]
    outer_bias, gain_two, shift_two = small_ref[3:4], small_ref[4:5], small_ref[5:6]

    for copy in copies[:groups]:
        copy.wait()
    residual = tokens_ref[...].astype(f32) + out_bias
    for r in range(groups):
        residual = residual + rows_nn(mixed[r][...], w_out[r])
    normal_one, inverse_one = normal_of(residual)
    first = normal_one * gain_one + shift_one
    first_low = first.astype(bf16)
    for copy in copies[groups:]:
        copy.wait()

    def ahead(g, total):
        value = rows_nn(first_low, w_inner[g]) + inner_bias_ref[pl.ds(g, 1), :]
        chance = 0.5 * (1.0 + lax.erf(value * (2.0**-0.5)))
        density = jnp.exp(-0.5 * value * value) * (2.0 * jnp.pi) ** -0.5
        slopes[g] = chance + value * density
        low = (value * chance).astype(bf16)
        activated[g] = low
        return total + rows_nn(low, w_outer[g])

    residual = lax.fori_loop(0, groups, ahead, first + outer_bias)
    normal_two, inverse_two = normal_of(residual)
    out_ref[...] = (normal_two * gain_two + shift_two).astype(bf16)
    upstream = up_ref[...].astype(f32)
    grad_two = normal_back(upstream, normal_two, inverse_two, gain_two)
    grad_two_low = grad_two.astype(bf16)
    shift_two_sum = jnp.sum(upstream, axis=0, keepdims=True)
    gain_two_sum = jnp.sum(upstream * normal_two, axis=0, keepdims=True)
    outer_bias_sum = jnp.sum(grad_two_low.astype(f32), axis=0, keepdims=True)

    def behind(g, total):
        made = rows_tn(activated[g], grad_two_low).astype(bf16)
        r = place_ref[g]

        @pl.when(r % 2 == 0)
        def _():
            outer_keep[r // 2] = made

        @pl.when(r % 2 == 1)
        def _():
            outer_send[r // 2] = made

        value = (rows_nt(grad_two_low, w_outer[g]) * slopes[g]).astype(bf16)
        hidden[g] = value
        return total + rows_nt(value, w_inner[g])

    grad_first = lax.fori_loop(0, groups, behind, grad_two)
    grad_one = normal_back(grad_first, normal_one, inverse_one, gain_one)
    grad_ref[...] = grad_one
    grad_one_low = grad_one.astype(bf16)
    for r in range(groups):
        back_ref[r] = rows_nt(grad_one_low, w_out[r]).astype(bf16)

    for g in range(groups):
        made = rows_tn(first_low, hidden[g]).astype(bf16)
        for k in range(groups):
            inner_grad[place_ref[k], g * part : (g + 1) * part, :] = made[k * part : (k + 1) * part, :]
    for r in range(groups):
        made = rows_tn(mixed[r][...], grad_one_low).astype(bf16)
        inner_grad[r, width : width + part, :] = made

    sums = [
        jnp.sum(grad_one_low.astype(f32), axis=0, keepdims=True),
        jnp.sum(grad_first * normal_one, axis=0, keepdims=True),
        jnp.sum(grad_first, axis=0, keepdims=True),
        outer_bias_sum,
        gain_two_sum,
        shift_two_sum,
    ]
    line = lax.broadcasted_iota(jnp.int32, (16, part), 0)
    inner_grad[:, width + part : width + part + 64, :] = jnp.zeros((groups, 64, width), bf16)
    for k in range(groups):
        tail = jnp.zeros((16, part), f32)
        for i, line_sum in enumerate(sums):
            tail = jnp.where(line == i, line_sum[:, k * part : (k + 1) * part], tail)
        bias_sum = jnp.sum(hidden[k].astype(f32), axis=0, keepdims=True)
        for i in range(groups):
            tail = jnp.where(
                line == len(sums) + i, bias_sum[:, i * part : (i + 1) * part], tail
            )
        inner_grad[place_ref[k], width + part : width + part + 16, 0:part] = tail.astype(bf16)
    for i in range(groups // 2):
        inner_keep[i] = inner_grad[2 * i]
        inner_send[i] = inner_grad[2 * i + 1]


def dense(places, mixed_pieces, tokens, cotangent, small, inner_bias, packs):
    rows, width = tokens.shape
    groups = len(packs)
    part = width // groups
    vmem = pl.BlockSpec(memory_space=pltpu.VMEM)
    hbm = pl.BlockSpec(memory_space=pl.ANY)
    return pl.pallas_call(
        dense_kernel,
        in_specs=[pl.BlockSpec(memory_space=pltpu.SMEM)] + [vmem] * (groups + 4) + [hbm] * groups,
        out_specs=[vmem] * 7,
        out_shape=[
            jax.ShapeDtypeStruct((rows, width), bf16),
            jax.ShapeDtypeStruct((rows, width), f32),
            jax.ShapeDtypeStruct((groups, rows, part), bf16),
        ]
        + [jax.ShapeDtypeStruct((groups // 2, width, width), bf16)] * 2
        + [jax.ShapeDtypeStruct((groups // 2, width + part + 64, width), bf16)] * 2,
        scratch_shapes=[
            pltpu.VMEM((groups, part, width), bf16),
            pltpu.VMEM((groups, width, width), bf16),
            pltpu.VMEM((groups, width, width), bf16),
            pltpu.VMEM((groups, rows, width), bf16),
            pltpu.VMEM((groups, rows, width), bf16),
            pltpu.VMEM((groups, rows, width), f32),
            pltpu.VMEM((groups, width + part + 64, width), bf16),
            pltpu.SemaphoreType.DMA((groups + 2, groups)),
        ],
        compiler_params=pltpu.CompilerParams(vmem_limit_bytes=56 * 2**20),
        cost_estimate=pl.CostEstimate(
            flops=36 * rows * width * width * groups // 3 * 2,
            bytes_accessed=24 * 2**20,
            transcendentals=2 * rows * width * groups,
        ),
        name="layer_dense",
    )(places, *mixed_pieces, tokens, cotangent, small, inner_bias, *packs)

def gather_kernel(place_ref, p0, p1, p2, p3, wide_ref, stat_ref, out_ref):
    rows, part = p0.shape
    lane = lax.broadcasted_iota(jnp.int32, (rows, 128), 1)
    slot = lax.broadcasted_iota(jnp.int32, (rows, HEAD_DIM), 1)
    for r, piece in enumerate((p0, p1, p2, p3)):
        here = pl.ds(pl.multiple_of(place_ref[r] * rows, rows), rows)
        tile = piece[...]
        product = tile.astype(f32) * wide_ref[here, :]
        pair, last = product[:, 0:128], product[:, 128:192]
        values = [stat_ref[here, h : h + 1] for h in range(3)] + [
            jnp.sum(jnp.where(lane < HEAD_DIM, pair, 0.0), axis=1, keepdims=True),
            jnp.sum(jnp.where(lane < HEAD_DIM, 0.0, pair), axis=1, keepdims=True),
            jnp.sum(last, axis=1, keepdims=True),
        ]
        tail = jnp.zeros((rows, HEAD_DIM), f32)
        for i, left in enumerate(values):
            for j in range(3):
                high = left.astype(bf16).astype(f32)
                tail = jnp.where(slot == 3 * i + j, high, tail)
                left = left - high
        out_ref[here, 0:192] = tile
        out_ref[here, 192:256] = tail.astype(bf16)


def gathered(places, pieces, wide, stats):
    block = wide.shape[0]
    vmem = pl.BlockSpec(memory_space=pltpu.VMEM)
    return pl.pallas_call(
        gather_kernel,
        in_specs=[pl.BlockSpec(memory_space=pltpu.SMEM)] + [vmem] * 6,
        out_specs=vmem,
        out_shape=jax.ShapeDtypeStruct((block, 256), bf16),
        compiler_params=pltpu.CompilerParams(vmem_limit_bytes=16 * 2**20),
        cost_estimate=pl.CostEstimate(flops=2**20, bytes_accessed=3 * 2**20, transcendentals=0),
        name="layer_gather",
    )(places, *pieces, wide, stats)


def heads_kernel(place_ref, tokens_ref, query_ref, pair_ref, w0, w1, w2, w3, grad_ref, back_ref, weight, sem):
    groups, part = grad_ref.shape[0], w0.shape[0]
    rows = back_ref.shape[1]
    copies = []
    for r, piece in enumerate((w0, w1, w2, w3)):
        where = pl.multiple_of(place_ref[r] * part, part)
        copies.append(pltpu.make_async_copy(piece, weight.at[pl.ds(where, part), :], sem.at[r]))
        copies[-1].start()
    tokens = tokens_ref[...]
    pair_grad = rows_tn(tokens, pair_ref[...]).astype(bf16)
    query_grad = rows_tn(tokens, query_ref[...]).astype(bf16)
    for k in range(groups):
        here = slice(k * part, (k + 1) * part)
        grad_ref[k, :, 0 : 2 * part] = pair_grad[here]
        grad_ref[k, :, 2 * part : 3 * part] = query_grad[here]
    ones = jnp.ones((tokens.shape[0], HEAD_DIM), bf16)
    query_sum = rows_tn(query_ref[...], ones)
    value_sum = rows_tn(pair_ref[:, part:], ones)
    lane = lax.broadcasted_iota(jnp.int32, (part, HEAD_DIM), 1)
    sums = jnp.where(lane == 0, query_sum, jnp.where(lane == 1, value_sum, 0.0))
    grad_ref[:, :, 3 * part : 3 * part + HEAD_DIM] = jnp.zeros((groups, part, HEAD_DIM), bf16)
    grad_ref[place_ref[0], :, 3 * part : 3 * part + HEAD_DIM] = sums.astype(bf16)
    for copy in copies:
        copy.wait()
    for k in range(groups):
        here = slice(k * rows, (k + 1) * rows)
        made = rows_nt(pair_ref[here, :], weight[:, : 2 * part])
        made = made + rows_nt(query_ref[here, :], weight[:, 2 * part :])
        back_ref[place_ref[k]] = made.astype(bf16)


def head_grads(places, tokens, grad_query, grad_pair, weight_pieces):
    block, width = tokens.shape
    groups, part = len(weight_pieces), weight_pieces[0].shape[0]
    vmem = pl.BlockSpec(memory_space=pltpu.VMEM)
    return pl.pallas_call(
        heads_kernel,
        in_specs=[pl.BlockSpec(memory_space=pltpu.SMEM)]
        + [vmem] * 3
        + [pl.BlockSpec(memory_space=pl.ANY)] * groups,
        out_specs=[vmem] * 2,
        out_shape=[
            jax.ShapeDtypeStruct((groups, part, 3 * part + HEAD_DIM), bf16),
            jax.ShapeDtypeStruct((groups, block // groups, width), bf16),
        ],
        scratch_shapes=[pltpu.VMEM((width, 3 * part), bf16), pltpu.SemaphoreType.DMA((groups,))],
        compiler_params=pltpu.CompilerParams(vmem_limit_bytes=32 * 2**20),
        cost_estimate=pl.CostEstimate(
            flops=4 * block * width * 3 * part, bytes_accessed=8 * 2**20, transcendentals=0
        ),
        name="layer_heads",
    )(places, tokens, grad_query, grad_pair, *weight_pieces)


def both(left, right):
    return (left.astype(f32) + right.astype(f32)).astype(bf16)


def half_of(block, bit, axis):
    size = block.shape[axis] // 2
    return lax.dynamic_slice_in_dim(block, bit * size, size, axis)


def scatter_sum(terms, axis_name, order, axis):
    index = lax.axis_index(axis_name)
    for step in order:
        bit = (index // step) % 2
        sent = functools.reduce(both, [half_of(x, 1 - bit, axis) for x in terms])
        kept = functools.reduce(both, [half_of(x, bit, axis) for x in terms])
        terms = [kept, swapped(sent, axis_name, step)]
    return terms


def gather_back(block, axis_name, order, axis):
    index = lax.axis_index(axis_name)
    for step in reversed(order):
        other = swapped(block, axis_name, step)
        late = (index // step) % 2 == 1
        block = jnp.where(
            late,
            jnp.concatenate([other, block], axis),
            jnp.concatenate([block, other], axis),
        )
    return block


def on_device(
    tokens,
    doc_start,
    cotangent,
    query_weight,
    key_weight,
    value_weight,
    out_weight,
    query_bias,
    value_bias,
    out_bias,
    first_gain,
    first_shift,
    inner_weight,
    inner_bias,
    outer_weight,
    outer_bias,
    second_gain,
    second_shift,
):
    rows, width = tokens.shape
    cycle = lax.axis_size("ctx")
    shards = lax.axis_size("wt")
    block = rows * shards
    reach = (MAXDOC + block - 2) // block
    window = (2 * reach + 1) * block
    c = lax.axis_index("ctx")
    w = lax.axis_index("wt")
    part = width // shards
    places = jnp.stack([w ^ r for r in range(shards)]).astype(jnp.int32)

    def spread(own, near):
        far = swapped(own, "wt", 2)
        return [own, near, far, swapped(far, "wt", 1)]

    def columns(r):
        start = (w ^ r) * part
        return jnp.concatenate(
            [
                lax.dynamic_slice_in_dim(x, start, part, 1)
                for x in (key_weight, value_weight, query_weight)
            ],
            axis=1,
        )

    token_pieces = spread(tokens, swapped(tokens, "wt", 1))
    weight_pieces = [columns(0)] + [swapped(columns(r), "wt", r) for r in range(1, shards)]
    head_bias = jnp.concatenate([jnp.zeros((part,), f32), value_bias.astype(f32), query_bias.astype(f32)])
    head_bias = jnp.broadcast_to(head_bias[None], (8, 3 * part))

    pad = reach * block
    padded = jnp.pad(doc_start, (pad, pad), constant_values=-1)
    base = c * block - pad
    marks = lax.dynamic_slice_in_dim(padded, c * block, window)
    place = jnp.arange(window, dtype=jnp.int32)
    begins = jnp.where((marks == base + place) | (marks < 0), place, window)
    next_begin = lax.cummin(begins, axis=0, reverse=True)
    stops = jnp.concatenate([next_begin[1:], jnp.full((1,), window, jnp.int32)])
    starts = marks - base
    spans_row = jnp.stack([starts, stops] + [jnp.zeros_like(starts)] * 6)
    spans_column = spans_row[:, pad : pad + block].T
    own_starts = starts[pad : pad + block]
    own_stops = stops[pad : pad + block]

    def bounds_of(tile, span):
        lowest = own_starts.reshape(-1, tile)[:, 0] // 128 * 128
        highest = own_stops.reshape(-1, tile)[:, -1]
        count = (highest - lowest + span - 1) // span
        lowest = jnp.minimum(lowest, (window - count * span) // 128 * 128)
        return jnp.stack([lowest, count], axis=1).reshape(-1)

    query_bounds = bounds_of(TILE_Q, SPAN_K)
    key_bounds = bounds_of(TILE_K, SPAN_Q)

    block_tokens, queries, pair = project(places, token_pieces, weight_pieces, head_bias)

    distances = [d for d in range(reach, -reach - 1, -1)]

    def halo(own):
        return [own if d == 0 else shifted(own, "ctx", d) for d in distances]

    even = c % 2 == 0
    beside = swapped(pair, "ctx", 1)
    before, after = shifted(pair, "ctx", 2), shifted(pair, "ctx", -2)
    half = block // 2
    route = [(i, i + 2 if i % 2 == 0 else i - 2) for i in range(cycle)]
    route = [(i, j) for i, j in route if 0 <= j < cycle]
    upper = swapped(jnp.where(even, after[:half], before[:half]), "ctx", 1)
    lower = lax.ppermute(beside[half:], "ctx", route)
    pairs = [before, after, pair, beside, upper, lower]
    beside_at = jnp.where(even, reach + 1, reach - 1) * block
    missing_at = jnp.where(even, reach - 1, reach + 1) * block
    load_at = jnp.stack(
        [0 * missing_at, 2 * reach * block + 0 * missing_at, reach * block + 0 * missing_at]
        + [beside_at, missing_at, missing_at + half]
    )
    query_bounds = jnp.concatenate([query_bounds, load_at]).astype(jnp.int32)

    small_own = jnp.stack(
        [out_bias, first_gain, first_shift, outer_bias, second_gain, second_shift]
    )
    small_own = jnp.concatenate([small_own, inner_bias.reshape(-1, part)], axis=0)
    small_own = jnp.pad(small_own, ((0, 16 - small_own.shape[0]), (0, width - part)))
    inner_parts = [inner_weight[:, i * width : (i + 1) * width] for i in range(shards)]
    pack = jnp.concatenate([outer_weight, out_weight, small_own] + inner_parts, axis=0)
    pack, _ = lax.optimization_barrier((pack, token_pieces[2:] + weight_pieces[1:]))
    pack_near, pack_far = swapped(pack, "wt", 1), swapped(pack, "wt", 2)
    mixed, mixed_wide, stat_columns = attention_forward(query_bounds, queries, spans_column, pairs)
    ready, _ = lax.optimization_barrier((queries, pairs))
    query_halo = [queries if d == 0 else shifted(ready, "ctx", d) if d * d == 1 else None for d in distances]
    close = [x for x, d in zip(query_halo, distances) if d * d == 1]
    mixed, mixed_wide, stat_columns, close, pack_far = lax.optimization_barrier(
        (mixed, mixed_wide, stat_columns, close, pack_far)
    )
    packs = [pack, pack_near, pack_far, swapped(pack_far, "wt", 1)]
    small = jnp.stack([x[width + part : width + part + 16, :part] for x in packs]).astype(f32)
    small = [lax.dynamic_index_in_dim(small, w ^ k, 0, keepdims=False) for k in range(shards)]
    small_rows = jnp.concatenate([x[:8] for x in small], axis=1)
    inner_bias_rows = jnp.stack([x[6:10].reshape(-1) for x in small])

    mixed_rows = mixed.reshape(shards, rows, part)
    mixed_pieces = [
        lax.dynamic_index_in_dim(mixed_rows, w ^ r, 0, keepdims=False) for r in range(shards)
    ]
    mixed_pieces = [mixed_pieces[0]] + [
        swapped(mixed_pieces[r], "wt", r) for r in range(1, shards)
    ]
    far_ready, mixed_pieces = lax.optimization_barrier((queries, mixed_pieces))
    results = dense(
        places, mixed_pieces, tokens, cotangent, small_rows, inner_bias_rows, packs
    )
    remote = [shifted(far_ready, "ctx", d) for d in distances if d * d > 1]
    results, remote = lax.optimization_barrier((results, remote))
    layer_out, grad_one, back, outer_keep, outer_send, inner_keep, inner_send = results
    query_halo = [remote[0], close[0], queries, close[1], remote[1]]

    back_pieces = [back[0]] + [swapped(back[r], "wt", r) for r in range(1, shards)]
    outer_got = swapped(outer_send, "wt", 1)
    inner_got = swapped(inner_send, "wt", 1)
    grads = gathered(places, back_pieces, mixed_wide, stat_columns)
    grads, outer_got, inner_got = lax.optimization_barrier((grads, outer_got, inner_got))

    def far_terms(keep, got):
        return [both(keep[0], got[0]), swapped(both(keep[1], got[1]), "wt", 2)]

    grad_halo = halo(grads)
    outer_terms = far_terms(outer_keep, outer_got)
    grad_query = attention_queries(
        query_bounds, queries, spans_column, grads, mixed_wide, stat_columns, pairs
    )
    grad_query, grad_halo, outer_terms, inner_keep, inner_got = lax.optimization_barrier(
        (grad_query, grad_halo, outer_terms, inner_keep, inner_got)
    )

    near_first = [1 << i for i in range(cycle.bit_length() - 1)]
    outer_terms = scatter_sum(outer_terms, "ctx", near_first[:1], 0)
    inner_terms = far_terms(inner_keep, inner_got)
    grad_pair = attention_keys(key_bounds, pair, spans_row, query_halo, grad_halo)
    grad_pair, outer_terms, inner_terms = lax.optimization_barrier(
        (grad_pair, outer_terms, inner_terms)
    )

    head_grad, token_partial = head_grads(places, block_tokens, grad_query, grad_pair, weight_pieces)
    outer_part = both(*scatter_sum(outer_terms, "ctx", near_first[1:], 0))
    inner_part = both(*scatter_sum(inner_terms, "ctx", near_first, 0))
    head_part = both(*scatter_sum([head_grad], "ctx", near_first, 1))
    token_got = swapped(token_partial[1::2], "wt", 1)
    token_sum = both(*far_terms(token_partial[0::2], token_got))
    outer_total = gather_back(outer_part, "ctx", near_first, 0)
    inner_total = gather_back(inner_part, "ctx", near_first, 0)
    head_pieces = [
        lax.dynamic_index_in_dim(head_part, w ^ r, 0, keepdims=False) for r in range(shards)
    ]
    head_pieces = [head_pieces[0]] + [swapped(head_pieces[r], "wt", r) for r in range(1, shards)]
    head_parts = jnp.stack(
        [
            lax.dynamic_index_in_dim(jnp.stack(head_pieces), w ^ k, 0, keepdims=False)
            for k in range(shards)
        ]
    )
    head_total = gather_back(head_parts, "ctx", near_first, 1)

    tokens_gradient = grad_one + token_sum.astype(f32)
    key_total, value_total, query_total = (
        jnp.concatenate(
            [head_total[k, :, i * part : (i + 1) * part] for k in range(shards)], axis=1
        ).astype(f32)
        for i in range(3)
    )
    own_total = lax.dynamic_index_in_dim(head_total, w, 0, keepdims=False)
    inner_rows = inner_total[:width].reshape(shards, part, width)
    inner_rows = jnp.concatenate([inner_rows[k] for k in range(shards)], axis=1).astype(f32)
    lines = inner_total[width + part : width + part + 16, :part].astype(f32)

    return (
        layer_out,
        tokens_gradient,
        query_total,
        key_total,
        value_total,
        inner_total[width : width + part].astype(f32),
        own_total[:, 3 * part].astype(f32),
        own_total[:, 3 * part + 1].astype(f32),
        lines[0],
        lines[1],
        lines[2],
        inner_rows,
        lines[6:10].reshape(-1),
        outer_total.astype(f32),
        lines[3],
        lines[4],
        lines[5],
    )


def solution(mesh):
    matrix, vector = P("wt", None), P("wt")
    stream = P(("ctx", "wt"), None)
    in_specs = (stream, P(), stream) + (matrix,) * 4 + (vector,) * 5
    in_specs += (matrix, vector, matrix, vector, vector, vector)
    out_specs = (stream, stream) + (matrix,) * 4 + (vector,) * 5
    out_specs += (matrix, vector, matrix, vector, vector, vector)
    return jax.shard_map(
        on_device, mesh=mesh, in_specs=in_specs, out_specs=out_specs, check_vma=False
    )
```

```python
import functools

import jax
import jax.numpy as jnp
from jax import lax
from jax.experimental import pallas as pl
from jax.experimental.pallas import tpu as pltpu
from jax.sharding import PartitionSpec as P

HEADS = 12
HEAD_DIM = 64
MAXDOC = 2048
TILE_Q = 256
SPAN_K = 768
TILE_K = 256
SPAN_Q = 768

masked_score = -1e30
epsilon = 1e-06
bf16 = jnp.bfloat16
f32 = jnp.float32


def swapped(block, axis, bit):
    count = lax.axis_size(axis)
    return lax.ppermute(block, axis, [(i, i ^ bit) for i in range(count)])


def shifted(block, axis, distance):
    count = lax.axis_size(axis)
    route = [(i, i + distance) for i in range(count) if 0 <= i + distance < count]
    return lax.ppermute(block, axis, route)


def rows_nt(left, right):
    return lax.dot_general(left, right, (((1,), (1,)), ((), ())), preferred_element_type=f32)


def rows_nn(left, right):
    return lax.dot_general(left, right, (((1,), (0,)), ((), ())), preferred_element_type=f32)


def load_window(pieces, target, sem, starts):
    copies = []
    for i, piece in enumerate(pieces):
        rows = pl.ds(pl.multiple_of(starts[i], 128), piece.shape[0])
        copies.append(pltpu.make_async_copy(piece, target.at[rows, :], sem.at[i]))
    for copy in copies:
        copy.start()
    return copies


def lanes_of(values, size):
    return jnp.tile(values, (1, size // 128))


def head_of(tile0, tile1, head):
    lane = lax.broadcasted_iota(jnp.int32, tile0.shape, 1)
    if head == 0:
        return jnp.where(lane < HEAD_DIM, tile0, jnp.zeros_like(tile0))
    if head == 1:
        return jnp.where(lane >= HEAD_DIM, tile0, jnp.zeros_like(tile0))
    return tile1


def forward_kernel(bounds, q_ref, span_ref, *rest):
    pieces, (out_ref, wide_ref, stat_ref, kv, top, total, accum, sem) = rest[:-8], rest[-8:]
    step = pl.program_id(0)

    @pl.when(step == 0)
    def _():
        for copy in load_window(pieces, kv, sem, [bounds[8 + i] for i in range(len(pieces))]):
            copy.wait()

    first = pl.multiple_of(step * TILE_Q, TILE_Q)
    here = pl.ds(first, TILE_Q)
    top[...] = jnp.full_like(top, masked_score)
    total[...] = jnp.zeros_like(total)
    accum[...] = jnp.zeros_like(accum)
    q_tile = q_ref[here, :]
    heads = [head_of(q_tile[:, :128], q_tile[:, 128:], h) for h in range(3)]
    lower, count = bounds[2 * step], bounds[2 * step + 1]

    def run(i, carry):
        begin = pl.multiple_of(lower + i * SPAN_K, 128)
        rows = pl.ds(begin, SPAN_K)
        keys = lax.broadcasted_iota(jnp.int32, (TILE_Q, SPAN_K), 1)
        allowed = (keys >= span_ref[here, 0:1] - begin) & (keys < span_ref[here, 1:2] - begin)
        scores = [rows_nt(heads[h], kv[rows, 0:128] if h < 2 else kv[rows, 128:192]) for h in range(3)]
        for h in range(3):
            score = scores[h]
            score = jnp.where(allowed, score, masked_score)
            before = top[h]
            newest = jnp.maximum(before, jnp.max(score, axis=1, keepdims=True))
            factor = jnp.exp(before - newest)
            weight = jnp.exp(score - lanes_of(newest, SPAN_K))
            part = weight[:, 0:128]
            for j in range(1, SPAN_K // 128):
                part = part + weight[:, 128 * j : 128 * j + 128]
            total[h] = total[h] * factor + part
            values = kv[rows, 128:256] if h == 0 else kv[rows, 256:384]
            accum[h] = accum[h] * factor + rows_nn(weight.astype(bf16), values)
            top[h] = newest
        return carry

    lax.fori_loop(0, count, run, 0)
    lane = lax.broadcasted_iota(jnp.int32, (TILE_Q, 128), 1)
    mixed, stats = [], jnp.zeros((TILE_Q, 128), f32)
    for h in range(3):
        mass = jnp.sum(total[h], axis=1, keepdims=True)
        mixed.append(pltpu.roll(accum[h] / mass, HEAD_DIM, 1))
        stats = jnp.where(lane == h, top[h] + jnp.log(mass), stats)
    pair = jnp.where(lane < HEAD_DIM, mixed[0], mixed[1])
    wide_ref[here, 0:128] = pair
    wide_ref[here, 128:192] = mixed[2][:, :HEAD_DIM]
    out_ref[here, 0:128] = pair.astype(bf16)
    out_ref[here, 128:192] = mixed[2][:, :HEAD_DIM].astype(bf16)
    stat_ref[here, :] = stats


def whole_spec(shape):
    return pl.BlockSpec(shape, lambda i, *_: (0,) * len(shape))


def attention_forward(bounds, queries, spans, pieces):
    block = queries.shape[0]
    window = sum(x.shape[0] for x in pieces)
    return pl.pallas_call(
        forward_kernel,
        grid_spec=pltpu.PrefetchScalarGridSpec(
            num_scalar_prefetch=1,
            grid=(block // TILE_Q,),
            in_specs=[whole_spec(queries.shape), whole_spec(spans.shape)]
            + [pl.BlockSpec(memory_space=pl.ANY)] * len(pieces),
            out_specs=[
                whole_spec((block, 192)),
                whole_spec((block, 192)),
                whole_spec((block, 128)),
            ],
            scratch_shapes=[
                pltpu.VMEM((window, 384), bf16),
                pltpu.VMEM((3, TILE_Q, 128), f32),
                pltpu.VMEM((3, TILE_Q, 128), f32),
                pltpu.VMEM((3, TILE_Q, 128), f32),
                pltpu.SemaphoreType.DMA((len(pieces),)),
            ],
        ),
        out_shape=[
            jax.ShapeDtypeStruct((block, 192), bf16),
            jax.ShapeDtypeStruct((block, 192), f32),
            jax.ShapeDtypeStruct((block, 128), f32),
        ],
        compiler_params=pltpu.CompilerParams(vmem_limit_bytes=60 * 2**20),
        cost_estimate=pl.CostEstimate(
            flops=4 * block * 2304 * 192, bytes_accessed=6 * 2**20, transcendentals=block * 2304 * 3
        ),
        name="attention_forward",
    )(bounds, queries, spans, *pieces)


def query_kernel(bounds, q_ref, span_ref, grad_ref, wide_ref, stat_ref, *rest):
    pieces, (out_ref, kv, accum, sem) = rest[:-4], rest[-4:]
    step = pl.program_id(0)

    @pl.when(step == 0)
    def _():
        for copy in load_window(pieces, kv, sem, [bounds[8 + i] for i in range(len(pieces))]):
            copy.wait()

    first = pl.multiple_of(step * TILE_Q, TILE_Q)
    here = pl.ds(first, TILE_Q)
    accum[...] = jnp.zeros_like(accum)
    q_tile = q_ref[here, :]
    heads = [head_of(q_tile[:, :128], q_tile[:, 128:], h) for h in range(3)]
    g_tile = grad_ref[here, :]
    lane = lax.broadcasted_iota(jnp.int32, (TILE_Q, 128), 1)
    g_pair = g_tile[:, :128]
    g_last = g_tile[:, 128:256]
    none = jnp.zeros((TILE_Q, 128), bf16)
    r_pair = pltpu.roll(g_pair.astype(f32), HEAD_DIM, 1).astype(bf16)
    r_last = pltpu.roll(g_last.astype(f32), HEAD_DIM, 1).astype(bf16)
    grads = [
        jnp.where(lane >= HEAD_DIM, r_pair, none),
        jnp.where(lane < HEAD_DIM, r_pair, none),
        jnp.where(lane >= HEAD_DIM, r_last, none),
    ]
    product_pair = g_pair.astype(f32) * wide_ref[here, 0:128]
    product_last = g_tile[:, 128:192].astype(f32) * wide_ref[here, 128:192]
    deltas = [
        jnp.sum(jnp.where(lane < HEAD_DIM, product_pair, 0.0), axis=1, keepdims=True),
        jnp.sum(jnp.where(lane < HEAD_DIM, 0.0, product_pair), axis=1, keepdims=True),
        jnp.sum(product_last, axis=1, keepdims=True),
    ]
    logs = [stat_ref[here, h : h + 1] for h in range(3)]
    lower, count = bounds[2 * step], bounds[2 * step + 1]

    def run(i, carry):
        begin = pl.multiple_of(lower + i * SPAN_K, 128)
        rows = pl.ds(begin, SPAN_K)
        keys = lax.broadcasted_iota(jnp.int32, (TILE_Q, SPAN_K), 1)
        allowed = (keys >= span_ref[here, 0:1] - begin) & (keys < span_ref[here, 1:2] - begin)
        S = [rows_nt(heads[h], kv[rows, 0:128] if h < 2 else kv[rows, 128:192]) for h in range(3)]
        B = [rows_nt(grads[h], kv[rows, 128:256] if h == 0 else kv[rows, 256:384]) for h in range(3)]
        for h in range(3):
            chance = jnp.exp(jnp.where(allowed, S[h] - logs[h], masked_score))
            change = (chance * (B[h] - deltas[h])).astype(bf16)
            accum[h] += rows_nn(change, kv[rows, 0:128] if h < 2 else kv[rows, 128:256])
        return carry

    lax.fori_loop(0, count, run, 0)
    out_ref[here, 0:128] = (jnp.where(lane < HEAD_DIM, accum[0], accum[1]) * 0.125).astype(bf16)
    out_ref[here, 128:192] = (accum[2][:, :HEAD_DIM] * 0.125).astype(bf16)


def attention_queries(bounds, queries, spans, grads, wide, stats, pieces):
    block = queries.shape[0]
    window = sum(x.shape[0] for x in pieces)
    return pl.pallas_call(
        query_kernel,
        grid_spec=pltpu.PrefetchScalarGridSpec(
            num_scalar_prefetch=1,
            grid=(block // TILE_Q,),
            in_specs=[whole_spec(x.shape) for x in (queries, spans, grads, wide, stats)]
            + [pl.BlockSpec(memory_space=pl.ANY)] * len(pieces),
            out_specs=whole_spec((block, 192)),
            scratch_shapes=[
                pltpu.VMEM((window, 384), bf16),
                pltpu.VMEM((3, TILE_Q, 128), f32),
                pltpu.SemaphoreType.DMA((len(pieces),)),
            ],
        ),
        out_shape=jax.ShapeDtypeStruct((block, 192), bf16),
        compiler_params=pltpu.CompilerParams(vmem_limit_bytes=60 * 2**20),
        cost_estimate=pl.CostEstimate(
            flops=6 * block * 2304 * 192, bytes_accessed=6 * 2**20, transcendentals=block * 2304 * 3
        ),
        name="attention_queries",
    )(bounds, queries, spans, grads, wide, stats, *pieces)


def key_kernel(reach, bounds, kv_ref, span_ref, *rest):
    window = 2 * reach + 1
    q_pieces, g_pieces = rest[:window], rest[window : 2 * window]
    out_ref, qs, gs, key_sum, value_sum, sem = rest[2 * window :]
    step = pl.program_id(0)
    block = q_pieces[0].shape[0]

    @pl.when(step == 0)
    def _():
        copies = load_window(q_pieces, qs, sem.at[0], [i * block for i in range(window)])
        copies += load_window(g_pieces, gs, sem.at[1], [i * block for i in range(window)])
        for copy in copies:
            copy.wait()

    first = pl.multiple_of(step * TILE_K, TILE_K)
    here = pl.ds(first, TILE_K)
    key_sum[...] = jnp.zeros_like(key_sum)
    value_sum[...] = jnp.zeros_like(value_sum)
    keys_pair = kv_ref[here, 0:128]
    keys = [head_of(keys_pair, kv_ref[here, 128:192], h) for h in range(3)]
    lane = lax.broadcasted_iota(jnp.int32, (TILE_K, 128), 1)
    zero = jnp.zeros((TILE_K, 128), f32)
    v_one = pltpu.roll(kv_ref[here, 128:256].astype(f32), HEAD_DIM, 1)
    v_two = pltpu.roll(kv_ref[here, 256:384].astype(f32), HEAD_DIM, 1)
    values = [
        jnp.where(lane < HEAD_DIM, v_one, zero).astype(bf16),
        jnp.where(lane < HEAD_DIM, zero, v_two).astype(bf16),
        v_two.astype(bf16)[:, :HEAD_DIM],
    ]
    line = lax.broadcasted_iota(jnp.int32, (16, HEAD_DIM), 0)
    slot = lax.broadcasted_iota(jnp.int32, (16, HEAD_DIM), 1)
    selector = jnp.where((slot // 3 == line) & (slot < 18), 1.0, 0.0).astype(bf16)
    lower, count = bounds[2 * step], bounds[2 * step + 1]

    def run(i, carry):
        begin = pl.multiple_of(lower + i * SPAN_Q, 128)
        columns = pl.ds(begin, SPAN_Q)
        place = reach * block + first + lax.broadcasted_iota(jnp.int32, (TILE_K, SPAN_Q), 0)
        allowed = (place >= span_ref[0:1, columns]) & (place < span_ref[1:2, columns])
        lanes = [slice(0, 128), slice(0, 128), slice(128, 192)]
        parts = gs[columns, 192:256]
        stats = rows_nt(selector, parts)
        S = [rows_nt(keys[h], qs[columns, lanes[h]]) for h in range(3)]
        B = [rows_nt(values[h], gs[columns, lanes[h]]) for h in range(3)]
        for h in range(3):
            score = S[h] - stats[h : h + 1, :]
            chance = jnp.exp(jnp.where(allowed, score, masked_score))
            change = (chance * (B[h] - stats[h + 3 : h + 4, :])).astype(bf16)
            size = 128 if h < 2 else HEAD_DIM
            key_sum[h, :, 0:size] += rows_nn(change, qs[columns, lanes[h]])
            value_sum[h, :, 0:size] += rows_nn(chance.astype(bf16), gs[columns, lanes[h]])
        return carry

    lax.fori_loop(0, count, run, 0)
    k_pair = jnp.where(lane < HEAD_DIM, key_sum[0], key_sum[1])
    v_pair = jnp.where(lane < HEAD_DIM, value_sum[0], value_sum[1])
    v_turn = pltpu.roll(v_pair, HEAD_DIM, 1)
    last_turn = pltpu.roll(value_sum[2], HEAD_DIM, 1)
    out_ref[here, 0:128] = k_pair.astype(bf16)
    out_ref[here, 128:256] = jnp.where(lane < HEAD_DIM, key_sum[2], v_turn).astype(bf16)
    out_ref[here, 256:384] = jnp.where(lane < HEAD_DIM, v_turn, last_turn).astype(bf16)


def attention_keys(bounds, pair, spans, q_pieces, g_pieces):
    block = pair.shape[0]
    count = len(q_pieces)
    return pl.pallas_call(
        functools.partial(key_kernel, count // 2),
        grid_spec=pltpu.PrefetchScalarGridSpec(
            num_scalar_prefetch=1,
            grid=(block // TILE_K,),
            in_specs=[whole_spec(x.shape) for x in (pair, spans)]
            + [pl.BlockSpec(memory_space=pl.ANY)] * (2 * count),
            out_specs=whole_spec((block, 384)),
            scratch_shapes=[
                pltpu.VMEM((count * block, 192), bf16),
                pltpu.VMEM((count * block, 256), bf16),
                pltpu.VMEM((3, TILE_K, 128), f32),
                pltpu.VMEM((3, TILE_K, 128), f32),
                pltpu.SemaphoreType.DMA((2, count)),
            ],
        ),
        out_shape=jax.ShapeDtypeStruct((block, 384), bf16),
        compiler_params=pltpu.CompilerParams(vmem_limit_bytes=60 * 2**20),
        cost_estimate=pl.CostEstimate(
            flops=8 * block * 2304 * 192, bytes_accessed=8 * 2**20, transcendentals=block * 2304 * 3
        ),
        name="attention_keys",
    )(bounds, pair, spans, *q_pieces, *g_pieces)


def projection_kernel(place_ref, own, near, far, corner, w_own, w_near, w_far, w_corner, bias_ref, *rest):
    tokens_ref, query_ref, pair_ref, weight, sem = rest
    rows, part = own.shape[0], w_own.shape[0]
    pieces = (w_own, w_near, w_far, w_corner)
    copies = []
    for r, piece in enumerate(pieces):
        where = pl.multiple_of(place_ref[r] * part, part)
        copies.append(pltpu.make_async_copy(piece, weight.at[pl.ds(where, part), :], sem.at[r]))
        copies[-1].start()
    for copy in copies:
        copy.wait()
    for r, piece in enumerate((own, near, far, corner)):
        here = pl.ds(pl.multiple_of(place_ref[r] * rows, rows), rows)
        tile = piece[...]
        tokens_ref[here, :] = tile
        made = rows_nn(tile, weight[...]) + bias_ref[0:1, :]
        pair_ref[here, :] = made[:, : 2 * part].astype(bf16)
        query_ref[here, :] = (made[:, 2 * part :].astype(bf16).astype(f32) * 0.125).astype(bf16)


def project(places, token_pieces, weight_pieces, bias):
    rows, width = token_pieces[0].shape
    part = weight_pieces[0].shape[0]
    block = rows * len(token_pieces)
    vmem = pl.BlockSpec(memory_space=pltpu.VMEM)
    return pl.pallas_call(
        projection_kernel,
        in_specs=[pl.BlockSpec(memory_space=pltpu.SMEM)]
        + [vmem] * 4
        + [pl.BlockSpec(memory_space=pl.ANY)] * 4
        + [vmem],
        out_specs=[vmem] * 3,
        out_shape=[
            jax.ShapeDtypeStruct((block, width), bf16),
            jax.ShapeDtypeStruct((block, part), bf16),
            jax.ShapeDtypeStruct((block, 2 * part), bf16),
        ],
        scratch_shapes=[pltpu.VMEM((width, 3 * part), bf16), pltpu.SemaphoreType.DMA((4,))],
        compiler_params=pltpu.CompilerParams(vmem_limit_bytes=32 * 2**20),
        cost_estimate=pl.CostEstimate(
            flops=2 * block * width * 3 * part, bytes_accessed=5 * 2**20, transcendentals=0
        ),
        name="layer_projection",
    )(places, *token_pieces, *weight_pieces, bias)


def normal_of(values):
    center = values - jnp.mean(values, axis=1, keepdims=True)
    inverse = lax.rsqrt(jnp.mean(center * center, axis=1, keepdims=True) + epsilon)
    return center * inverse, inverse


def normal_back(upstream, normal, inverse, gain):
    scaled = upstream * gain
    mean_scaled = jnp.mean(scaled, axis=1, keepdims=True)
    mean_product = jnp.mean(scaled * normal, axis=1, keepdims=True)
    return (scaled - mean_scaled - normal * mean_product) * inverse


def rows_tn(left, right):
    return lax.dot_general(left, right, (((0,), (0,)), ((), ())), preferred_element_type=f32)


def dense_kernel(place_ref, *refs):
    mixed = refs[0:4]
    tokens_ref, up_ref, small_ref, inner_bias_ref = refs[4:8]
    packs = refs[8:12]
    out_ref, grad_ref, back_ref = refs[12:15]
    outer_keep, outer_send, inner_keep, inner_send = refs[15:19]
    w_out, w_inner, w_outer, hidden, activated, slopes, inner_grad, sem = refs[19:]
    rows, width = tokens_ref.shape
    groups = w_inner.shape[0]
    part = width // groups
    copies = []
    for r in range(groups):
        copies.append(
            pltpu.make_async_copy(packs[r].at[pl.ds(width, part), :], w_out.at[r], sem.at[0, r])
        )
    for r in range(groups):
        here = pl.ds(pl.multiple_of(place_ref[r] * part, part), part)
        for g in range(groups):
            copies.append(
                pltpu.make_async_copy(
                    packs[r].at[pl.ds(width + part + 16 + g * part, part), :],
                    w_inner.at[g, here, :],
                    sem.at[1 + g, r],
                )
            )
    for r in range(groups):
        copies.append(
            pltpu.make_async_copy(
                packs[r].at[pl.ds(0, width), :], w_outer.at[place_ref[r]], sem.at[1 + groups, r]
            )
        )
    for copy in copies:
        copy.start()

    out_bias, gain_one, shift_one = small_ref[0:1], small_ref[1:2], small_ref[2:3]
    outer_bias, gain_two, shift_two = small_ref[3:4], small_ref[4:5], small_ref[5:6]

    for copy in copies[:groups]:
        copy.wait()
    residual = tokens_ref[...].astype(f32) + out_bias
    for r in range(groups):
        residual = residual + rows_nn(mixed[r][...], w_out[r])
    normal_one, inverse_one = normal_of(residual)
    first = normal_one * gain_one + shift_one
    first_low = first.astype(bf16)
    for copy in copies[groups:]:
        copy.wait()

    def ahead(g, total):
        value = rows_nn(first_low, w_inner[g]) + inner_bias_ref[pl.ds(g, 1), :]
        chance = 0.5 * (1.0 + lax.erf(value * (2.0**-0.5)))
        density = jnp.exp(-0.5 * value * value) * (2.0 * jnp.pi) ** -0.5
        slopes[g] = chance + value * density
        low = (value * chance).astype(bf16)
        activated[g] = low
        return total + rows_nn(low, w_outer[g])

    residual = lax.fori_loop(0, groups, ahead, first + outer_bias)
    normal_two, inverse_two = normal_of(residual)
    out_ref[...] = (normal_two * gain_two + shift_two).astype(bf16)
    upstream = up_ref[...].astype(f32)
    grad_two = normal_back(upstream, normal_two, inverse_two, gain_two)
    grad_two_low = grad_two.astype(bf16)
    shift_two_sum = jnp.sum(upstream, axis=0, keepdims=True)
    gain_two_sum = jnp.sum(upstream * normal_two, axis=0, keepdims=True)
    outer_bias_sum = jnp.sum(grad_two_low.astype(f32), axis=0, keepdims=True)

    def behind(g, total):
        made = rows_tn(activated[g], grad_two_low).astype(bf16)
        r = place_ref[g]

        @pl.when(r % 2 == 0)
        def _():
            outer_keep[r // 2] = made

        @pl.when(r % 2 == 1)
        def _():
            outer_send[r // 2] = made

        value = (rows_nt(grad_two_low, w_outer[g]) * slopes[g]).astype(bf16)
        hidden[g] = value
        return total + rows_nt(value, w_inner[g])

    grad_first = lax.fori_loop(0, groups, behind, grad_two)
    grad_one = normal_back(grad_first, normal_one, inverse_one, gain_one)
    grad_ref[...] = grad_one
    grad_one_low = grad_one.astype(bf16)
    for r in range(groups):
        back_ref[r] = rows_nt(grad_one_low, w_out[r]).astype(bf16)

    for g in range(groups):
        made = rows_tn(first_low, hidden[g]).astype(bf16)
        for k in range(groups):
            inner_grad[place_ref[k], g * part : (g + 1) * part, :] = made[k * part : (k + 1) * part, :]
    for r in range(groups):
        made = rows_tn(mixed[r][...], grad_one_low).astype(bf16)
        inner_grad[r, width : width + part, :] = made

    sums = [
        jnp.sum(grad_one_low.astype(f32), axis=0, keepdims=True),
        jnp.sum(grad_first * normal_one, axis=0, keepdims=True),
        jnp.sum(grad_first, axis=0, keepdims=True),
        outer_bias_sum,
        gain_two_sum,
        shift_two_sum,
    ]
    line = lax.broadcasted_iota(jnp.int32, (16, part), 0)
    inner_grad[:, width + part : width + part + 64, :] = jnp.zeros((groups, 64, width), bf16)
    for k in range(groups):
        tail = jnp.zeros((16, part), f32)
        for i, line_sum in enumerate(sums):
            tail = jnp.where(line == i, line_sum[:, k * part : (k + 1) * part], tail)
        bias_sum = jnp.sum(hidden[k].astype(f32), axis=0, keepdims=True)
        for i in range(groups):
            tail = jnp.where(
                line == len(sums) + i, bias_sum[:, i * part : (i + 1) * part], tail
            )
        inner_grad[place_ref[k], width + part : width + part + 16, 0:part] = tail.astype(bf16)
    for i in range(groups // 2):
        inner_keep[i] = inner_grad[2 * i]
        inner_send[i] = inner_grad[2 * i + 1]


def dense(places, mixed_pieces, tokens, cotangent, small, inner_bias, packs):
    rows, width = tokens.shape
    groups = len(packs)
    part = width // groups
    vmem = pl.BlockSpec(memory_space=pltpu.VMEM)
    hbm = pl.BlockSpec(memory_space=pl.ANY)
    return pl.pallas_call(
        dense_kernel,
        in_specs=[pl.BlockSpec(memory_space=pltpu.SMEM)] + [vmem] * (groups + 4) + [hbm] * groups,
        out_specs=[vmem] * 7,
        out_shape=[
            jax.ShapeDtypeStruct((rows, width), bf16),
            jax.ShapeDtypeStruct((rows, width), f32),
            jax.ShapeDtypeStruct((groups, rows, part), bf16),
        ]
        + [jax.ShapeDtypeStruct((groups // 2, width, width), bf16)] * 2
        + [jax.ShapeDtypeStruct((groups // 2, width + part + 64, width), bf16)] * 2,
        scratch_shapes=[
            pltpu.VMEM((groups, part, width), bf16),
            pltpu.VMEM((groups, width, width), bf16),
            pltpu.VMEM((groups, width, width), bf16),
            pltpu.VMEM((groups, rows, width), bf16),
            pltpu.VMEM((groups, rows, width), bf16),
            pltpu.VMEM((groups, rows, width), f32),
            pltpu.VMEM((groups, width + part + 64, width), bf16),
            pltpu.SemaphoreType.DMA((groups + 2, groups)),
        ],
        compiler_params=pltpu.CompilerParams(vmem_limit_bytes=56 * 2**20),
        cost_estimate=pl.CostEstimate(
            flops=36 * rows * width * width * groups // 3 * 2,
            bytes_accessed=24 * 2**20,
            transcendentals=2 * rows * width * groups,
        ),
        name="layer_dense",
    )(places, *mixed_pieces, tokens, cotangent, small, inner_bias, *packs)

def gather_kernel(place_ref, p0, p1, p2, p3, wide_ref, stat_ref, out_ref):
    rows, part = p0.shape
    lane = lax.broadcasted_iota(jnp.int32, (rows, 128), 1)
    slot = lax.broadcasted_iota(jnp.int32, (rows, HEAD_DIM), 1)
    for r, piece in enumerate((p0, p1, p2, p3)):
        here = pl.ds(pl.multiple_of(place_ref[r] * rows, rows), rows)
        tile = piece[...]
        product = tile.astype(f32) * wide_ref[here, :]
        pair, last = product[:, 0:128], product[:, 128:192]
        values = [stat_ref[here, h : h + 1] for h in range(3)] + [
            jnp.sum(jnp.where(lane < HEAD_DIM, pair, 0.0), axis=1, keepdims=True),
            jnp.sum(jnp.where(lane < HEAD_DIM, 0.0, pair), axis=1, keepdims=True),
            jnp.sum(last, axis=1, keepdims=True),
        ]
        tail = jnp.zeros((rows, HEAD_DIM), f32)
        for i, left in enumerate(values):
            for j in range(3):
                high = left.astype(bf16).astype(f32)
                tail = jnp.where(slot == 3 * i + j, high, tail)
                left = left - high
        out_ref[here, 0:192] = tile
        out_ref[here, 192:256] = tail.astype(bf16)


def gathered(places, pieces, wide, stats):
    block = wide.shape[0]
    vmem = pl.BlockSpec(memory_space=pltpu.VMEM)
    return pl.pallas_call(
        gather_kernel,
        in_specs=[pl.BlockSpec(memory_space=pltpu.SMEM)] + [vmem] * 6,
        out_specs=vmem,
        out_shape=jax.ShapeDtypeStruct((block, 256), bf16),
        compiler_params=pltpu.CompilerParams(vmem_limit_bytes=16 * 2**20),
        cost_estimate=pl.CostEstimate(flops=2**20, bytes_accessed=3 * 2**20, transcendentals=0),
        name="layer_gather",
    )(places, *pieces, wide, stats)


def heads_kernel(place_ref, tokens_ref, query_ref, pair_ref, w0, w1, w2, w3, grad_ref, back_ref, weight, sem):
    groups, part = grad_ref.shape[0], w0.shape[0]
    rows = back_ref.shape[1]
    copies = []
    for r, piece in enumerate((w0, w1, w2, w3)):
        where = pl.multiple_of(place_ref[r] * part, part)
        copies.append(pltpu.make_async_copy(piece, weight.at[pl.ds(where, part), :], sem.at[r]))
        copies[-1].start()
    tokens = tokens_ref[...]
    pair_grad = rows_tn(tokens, pair_ref[...]).astype(bf16)
    query_grad = rows_tn(tokens, query_ref[...]).astype(bf16)
    for k in range(groups):
        here = slice(k * part, (k + 1) * part)
        grad_ref[k, :, 0 : 2 * part] = pair_grad[here]
        grad_ref[k, :, 2 * part : 3 * part] = query_grad[here]
    ones = jnp.ones((tokens.shape[0], HEAD_DIM), bf16)
    query_sum = rows_tn(query_ref[...], ones)
    value_sum = rows_tn(pair_ref[:, part:], ones)
    lane = lax.broadcasted_iota(jnp.int32, (part, HEAD_DIM), 1)
    sums = jnp.where(lane == 0, query_sum, jnp.where(lane == 1, value_sum, 0.0))
    grad_ref[:, :, 3 * part : 3 * part + HEAD_DIM] = jnp.zeros((groups, part, HEAD_DIM), bf16)
    grad_ref[place_ref[0], :, 3 * part : 3 * part + HEAD_DIM] = sums.astype(bf16)
    for copy in copies:
        copy.wait()
    for k in range(groups):
        here = slice(k * rows, (k + 1) * rows)
        made = rows_nt(pair_ref[here, :], weight[:, : 2 * part])
        made = made + rows_nt(query_ref[here, :], weight[:, 2 * part :])
        back_ref[place_ref[k]] = made.astype(bf16)


def head_grads(places, tokens, grad_query, grad_pair, weight_pieces):
    block, width = tokens.shape
    groups, part = len(weight_pieces), weight_pieces[0].shape[0]
    vmem = pl.BlockSpec(memory_space=pltpu.VMEM)
    return pl.pallas_call(
        heads_kernel,
        in_specs=[pl.BlockSpec(memory_space=pltpu.SMEM)]
        + [vmem] * 3
        + [pl.BlockSpec(memory_space=pl.ANY)] * groups,
        out_specs=[vmem] * 2,
        out_shape=[
            jax.ShapeDtypeStruct((groups, part, 3 * part + HEAD_DIM), bf16),
            jax.ShapeDtypeStruct((groups, block // groups, width), bf16),
        ],
        scratch_shapes=[pltpu.VMEM((width, 3 * part), bf16), pltpu.SemaphoreType.DMA((groups,))],
        compiler_params=pltpu.CompilerParams(vmem_limit_bytes=32 * 2**20),
        cost_estimate=pl.CostEstimate(
            flops=4 * block * width * 3 * part, bytes_accessed=8 * 2**20, transcendentals=0
        ),
        name="layer_heads",
    )(places, tokens, grad_query, grad_pair, *weight_pieces)


def both(left, right):
    return (left.astype(f32) + right.astype(f32)).astype(bf16)


def half_of(block, bit, axis):
    size = block.shape[axis] // 2
    return lax.dynamic_slice_in_dim(block, bit * size, size, axis)


def scatter_sum(terms, axis_name, order, axis):
    index = lax.axis_index(axis_name)
    for step in order:
        bit = (index // step) % 2
        sent = functools.reduce(both, [half_of(x, 1 - bit, axis) for x in terms])
        kept = functools.reduce(both, [half_of(x, bit, axis) for x in terms])
        terms = [kept, swapped(sent, axis_name, step)]
    return terms


def gather_back(block, axis_name, order, axis):
    index = lax.axis_index(axis_name)
    for step in reversed(order):
        other = swapped(block, axis_name, step)
        late = (index // step) % 2 == 1
        block = jnp.where(
            late,
            jnp.concatenate([other, block], axis),
            jnp.concatenate([block, other], axis),
        )
    return block


def on_device(
    tokens,
    doc_start,
    cotangent,
    query_weight,
    key_weight,
    value_weight,
    out_weight,
    query_bias,
    value_bias,
    out_bias,
    first_gain,
    first_shift,
    inner_weight,
    inner_bias,
    outer_weight,
    outer_bias,
    second_gain,
    second_shift,
):
    rows, width = tokens.shape
    cycle = lax.axis_size("ctx")
    shards = lax.axis_size("wt")
    block = rows * shards
    reach = (MAXDOC + block - 2) // block
    window = (2 * reach + 1) * block
    c = lax.axis_index("ctx")
    w = lax.axis_index("wt")
    part = width // shards
    places = jnp.stack([w ^ r for r in range(shards)]).astype(jnp.int32)

    def spread(own, near):
        far = swapped(own, "wt", 2)
        return [own, near, far, swapped(far, "wt", 1)]

    def columns(r):
        start = (w ^ r) * part
        return jnp.concatenate(
            [
                lax.dynamic_slice_in_dim(x, start, part, 1)
                for x in (key_weight, value_weight, query_weight)
            ],
            axis=1,
        )

    token_pieces = spread(tokens, swapped(tokens, "wt", 1))
    weight_pieces = [columns(0)] + [swapped(columns(r), "wt", r) for r in range(1, shards)]
    head_bias = jnp.concatenate([jnp.zeros((part,), f32), value_bias.astype(f32), query_bias.astype(f32)])
    head_bias = jnp.broadcast_to(head_bias[None], (8, 3 * part))

    pad = reach * block
    padded = jnp.pad(doc_start, (pad, pad), constant_values=-1)
    base = c * block - pad
    marks = lax.dynamic_slice_in_dim(padded, c * block, window)
    place = jnp.arange(window, dtype=jnp.int32)
    begins = jnp.where((marks == base + place) | (marks < 0), place, window)
    next_begin = lax.cummin(begins, axis=0, reverse=True)
    stops = jnp.concatenate([next_begin[1:], jnp.full((1,), window, jnp.int32)])
    starts = marks - base
    spans_row = jnp.stack([starts, stops] + [jnp.zeros_like(starts)] * 6)
    spans_column = spans_row[:, pad : pad + block].T
    own_starts = starts[pad : pad + block]
    own_stops = stops[pad : pad + block]

    def bounds_of(tile, span):
        lowest = own_starts.reshape(-1, tile)[:, 0] // 128 * 128
        highest = own_stops.reshape(-1, tile)[:, -1]
        count = (highest - lowest + span - 1) // span
        lowest = jnp.minimum(lowest, (window - count * span) // 128 * 128)
        return jnp.stack([lowest, count], axis=1).reshape(-1)

    query_bounds = bounds_of(TILE_Q, SPAN_K)
    key_bounds = bounds_of(TILE_K, SPAN_Q)

    block_tokens, queries, pair = project(places, token_pieces, weight_pieces, head_bias)

    distances = [d for d in range(reach, -reach - 1, -1)]

    def halo(own):
        return [own if d == 0 else shifted(own, "ctx", d) for d in distances]

    even = c % 2 == 0
    beside = swapped(pair, "ctx", 1)
    before, after = shifted(pair, "ctx", 2), shifted(pair, "ctx", -2)
    half = block // 2
    route = [(i, i + 2 if i % 2 == 0 else i - 2) for i in range(cycle)]
    route = [(i, j) for i, j in route if 0 <= j < cycle]
    upper = swapped(jnp.where(even, after[:half], before[:half]), "ctx", 1)
    lower = lax.ppermute(beside[half:], "ctx", route)
    pairs = [before, after, pair, beside, upper, lower]
    beside_at = jnp.where(even, reach + 1, reach - 1) * block
    missing_at = jnp.where(even, reach - 1, reach + 1) * block
    load_at = jnp.stack(
        [0 * missing_at, 2 * reach * block + 0 * missing_at, reach * block + 0 * missing_at]
        + [beside_at, missing_at, missing_at + half]
    )
    query_bounds = jnp.concatenate([query_bounds, load_at]).astype(jnp.int32)

    small_own = jnp.stack(
        [out_bias, first_gain, first_shift, outer_bias, second_gain, second_shift]
    )
    small_own = jnp.concatenate([small_own, inner_bias.reshape(-1, part)], axis=0)
    small_own = jnp.pad(small_own, ((0, 16 - small_own.shape[0]), (0, width - part)))
    inner_parts = [inner_weight[:, i * width : (i + 1) * width] for i in range(shards)]
    pack = jnp.concatenate([outer_weight, out_weight, small_own] + inner_parts, axis=0)
    pack, _ = lax.optimization_barrier((pack, token_pieces[2:] + weight_pieces[1:]))
    pack_near, pack_far = swapped(pack, "wt", 1), swapped(pack, "wt", 2)
    mixed, mixed_wide, stat_columns = attention_forward(query_bounds, queries, spans_column, pairs)
    ready, _ = lax.optimization_barrier((queries, pairs))
    query_halo = [queries if d == 0 else shifted(ready, "ctx", d) if d * d == 1 else None for d in distances]
    close = [x for x, d in zip(query_halo, distances) if d * d == 1]
    mixed, mixed_wide, stat_columns, close, pack_far = lax.optimization_barrier(
        (mixed, mixed_wide, stat_columns, close, pack_far)
    )
    packs = [pack, pack_near, pack_far, swapped(pack_far, "wt", 1)]
    small = jnp.stack([x[width + part : width + part + 16, :part] for x in packs]).astype(f32)
    small = [lax.dynamic_index_in_dim(small, w ^ k, 0, keepdims=False) for k in range(shards)]
    small_rows = jnp.concatenate([x[:8] for x in small], axis=1)
    inner_bias_rows = jnp.stack([x[6:10].reshape(-1) for x in small])

    mixed_rows = mixed.reshape(shards, rows, part)
    mixed_pieces = [
        lax.dynamic_index_in_dim(mixed_rows, w ^ r, 0, keepdims=False) for r in range(shards)
    ]
    mixed_pieces = [mixed_pieces[0]] + [
        swapped(mixed_pieces[r], "wt", r) for r in range(1, shards)
    ]
    far_ready, mixed_pieces = lax.optimization_barrier((queries, mixed_pieces))
    results = dense(
        places, mixed_pieces, tokens, cotangent, small_rows, inner_bias_rows, packs
    )
    remote = [shifted(far_ready, "ctx", d) for d in distances if d * d > 1]
    results, remote = lax.optimization_barrier((results, remote))
    layer_out, grad_one, back, outer_keep, outer_send, inner_keep, inner_send = results
    query_halo = [remote[0], close[0], queries, close[1], remote[1]]

    back_pieces = [back[0]] + [swapped(back[r], "wt", r) for r in range(1, shards)]
    outer_got = swapped(outer_send, "wt", 1)
    inner_got = swapped(inner_send, "wt", 1)
    grads = gathered(places, back_pieces, mixed_wide, stat_columns)
    grads, outer_got, inner_got = lax.optimization_barrier((grads, outer_got, inner_got))

    def far_terms(keep, got):
        return [both(keep[0], got[0]), swapped(both(keep[1], got[1]), "wt", 2)]

    grad_halo = halo(grads)
    inner_terms = far_terms(inner_keep, inner_got)
    grad_query = attention_queries(
        query_bounds, queries, spans_column, grads, mixed_wide, stat_columns, pairs
    )
    grad_query, grad_halo, inner_terms, outer_keep, outer_got = lax.optimization_barrier(
        (grad_query, grad_halo, inner_terms, outer_keep, outer_got)
    )

    near_first = [1 << i for i in range(cycle.bit_length() - 1)]
    inner_terms = scatter_sum(inner_terms, "ctx", near_first[:1], 0)
    outer_terms = far_terms(outer_keep, outer_got)
    grad_pair = attention_keys(key_bounds, pair, spans_row, query_halo, grad_halo)
    grad_pair, inner_terms, outer_terms = lax.optimization_barrier(
        (grad_pair, inner_terms, outer_terms)
    )

    head_grad, token_partial = head_grads(places, block_tokens, grad_query, grad_pair, weight_pieces)
    inner_part = both(*scatter_sum(inner_terms, "ctx", near_first[1:], 0))
    outer_part = both(*scatter_sum(outer_terms, "ctx", near_first, 0))
    head_part = both(*scatter_sum([head_grad], "ctx", near_first, 1))
    token_got = swapped(token_partial[1::2], "wt", 1)
    token_sum = both(*far_terms(token_partial[0::2], token_got))
    inner_total = gather_back(inner_part, "ctx", near_first, 0)
    outer_total = gather_back(outer_part, "ctx", near_first, 0)
    head_pieces = [
        lax.dynamic_index_in_dim(head_part, w ^ r, 0, keepdims=False) for r in range(shards)
    ]
    head_pieces = [head_pieces[0]] + [swapped(head_pieces[r], "wt", r) for r in range(1, shards)]
    head_parts = jnp.stack(
        [
            lax.dynamic_index_in_dim(jnp.stack(head_pieces), w ^ k, 0, keepdims=False)
            for k in range(shards)
        ]
    )
    head_total = gather_back(head_parts, "ctx", near_first, 1)

    tokens_gradient = grad_one + token_sum.astype(f32)
    key_total, value_total, query_total = (
        jnp.concatenate(
            [head_total[k, :, i * part : (i + 1) * part] for k in range(shards)], axis=1
        ).astype(f32)
        for i in range(3)
    )
    own_total = lax.dynamic_index_in_dim(head_total, w, 0, keepdims=False)
    inner_rows = inner_total[:width].reshape(shards, part, width)
    inner_rows = jnp.concatenate([inner_rows[k] for k in range(shards)], axis=1).astype(f32)
    lines = inner_total[width + part : width + part + 16, :part].astype(f32)

    return (
        layer_out,
        tokens_gradient,
        query_total,
        key_total,
        value_total,
        inner_total[width : width + part].astype(f32),
        own_total[:, 3 * part].astype(f32),
        own_total[:, 3 * part + 1].astype(f32),
        lines[0],
        lines[1],
        lines[2],
        inner_rows,
        lines[6:10].reshape(-1),
        outer_total.astype(f32),
        lines[3],
        lines[4],
        lines[5],
    )


def solution(mesh):
    matrix, vector = P("wt", None), P("wt")
    stream = P(("ctx", "wt"), None)
    in_specs = (stream, P(), stream) + (matrix,) * 4 + (vector,) * 5
    in_specs += (matrix, vector, matrix, vector, vector, vector)
    out_specs = (stream, stream) + (matrix,) * 4 + (vector,) * 5
    out_specs += (matrix, vector, matrix, vector, vector, vector)
    return jax.shard_map(
        on_device, mesh=mesh, in_specs=in_specs, out_specs=out_specs, check_vma=False
    )
```

```python
import functools

import jax
import jax.numpy as jnp
from jax import lax
from jax.experimental import pallas as pl
from jax.experimental.pallas import tpu as pltpu
from jax.sharding import PartitionSpec as P

HEADS = 12
HEAD_DIM = 64
MAXDOC = 2048
TILE_Q = 256
SPAN_K = 768
TILE_K = 256
SPAN_Q = 768

masked_score = -1e30
epsilon = 1e-06
bf16 = jnp.bfloat16
f32 = jnp.float32


def swapped(block, axis, bit):
    count = lax.axis_size(axis)
    return lax.ppermute(block, axis, [(i, i ^ bit) for i in range(count)])


def shifted(block, axis, distance):
    count = lax.axis_size(axis)
    route = [(i, i + distance) for i in range(count) if 0 <= i + distance < count]
    return lax.ppermute(block, axis, route)


def rows_nt(left, right):
    return lax.dot_general(left, right, (((1,), (1,)), ((), ())), preferred_element_type=f32)


def rows_nn(left, right):
    return lax.dot_general(left, right, (((1,), (0,)), ((), ())), preferred_element_type=f32)


def load_window(pieces, target, sem, starts):
    copies = []
    for i, piece in enumerate(pieces):
        rows = pl.ds(pl.multiple_of(starts[i], 128), piece.shape[0])
        copies.append(pltpu.make_async_copy(piece, target.at[rows, :], sem.at[i]))
    for copy in copies:
        copy.start()
    return copies


def lanes_of(values, size):
    return jnp.tile(values, (1, size // 128))


def head_of(tile0, tile1, head):
    lane = lax.broadcasted_iota(jnp.int32, tile0.shape, 1)
    if head == 0:
        return jnp.where(lane < HEAD_DIM, tile0, jnp.zeros_like(tile0))
    if head == 1:
        return jnp.where(lane >= HEAD_DIM, tile0, jnp.zeros_like(tile0))
    return tile1


def forward_kernel(bounds, q_ref, span_ref, *rest):
    pieces, rest = rest[:-11], rest[-11:]
    outs, (wide_ref, stat_ref, kv, top, total, accum, sem) = rest[:4], rest[4:]
    step = pl.program_id(0)

    @pl.when(step == 0)
    def _():
        for copy in load_window(pieces, kv, sem, [bounds[8 + i] for i in range(len(pieces))]):
            copy.wait()

    first = pl.multiple_of(step * TILE_Q, TILE_Q)
    here = pl.ds(first, TILE_Q)
    top[...] = jnp.full_like(top, masked_score)
    total[...] = jnp.zeros_like(total)
    accum[...] = jnp.zeros_like(accum)
    q_tile = q_ref[here, :]
    heads = [head_of(q_tile[:, :128], q_tile[:, 128:], h) for h in range(3)]
    lower, count = bounds[2 * step], bounds[2 * step + 1]

    def run(i, carry):
        begin = pl.multiple_of(lower + i * SPAN_K, 128)
        rows = pl.ds(begin, SPAN_K)
        keys = lax.broadcasted_iota(jnp.int32, (TILE_Q, SPAN_K), 1)
        allowed = (keys >= span_ref[here, 0:1] - begin) & (keys < span_ref[here, 1:2] - begin)
        scores = [rows_nt(heads[h], kv[rows, 0:128] if h < 2 else kv[rows, 128:192]) for h in range(3)]
        for h in range(3):
            score = scores[h]
            score = jnp.where(allowed, score, masked_score)
            before = top[h]
            newest = jnp.maximum(before, jnp.max(score, axis=1, keepdims=True))
            factor = jnp.exp(before - newest)
            weight = jnp.exp(score - lanes_of(newest, SPAN_K))
            part = weight[:, 0:128]
            for j in range(1, SPAN_K // 128):
                part = part + weight[:, 128 * j : 128 * j + 128]
            total[h] = total[h] * factor + part
            values = kv[rows, 128:256] if h == 0 else kv[rows, 256:384]
            accum[h] = accum[h] * factor + rows_nn(weight.astype(bf16), values)
            top[h] = newest
        return carry

    lax.fori_loop(0, count, run, 0)
    lane = lax.broadcasted_iota(jnp.int32, (TILE_Q, 128), 1)
    mixed, stats = [], jnp.zeros((TILE_Q, 128), f32)
    for h in range(3):
        mass = jnp.sum(total[h], axis=1, keepdims=True)
        mixed.append(pltpu.roll(accum[h] / mass, HEAD_DIM, 1))
        stats = jnp.where(lane == h, top[h] + jnp.log(mass), stats)
    pair = jnp.where(lane < HEAD_DIM, mixed[0], mixed[1])
    wide_ref[here, 0:128] = pair
    wide_ref[here, 128:192] = mixed[2][:, :HEAD_DIM]
    stat_ref[here, :] = stats
    for r, out_ref in enumerate(outs):

        @pl.when(bounds[14 + step] == r)
        def _(out_ref=out_ref):
            out_ref[:, 0:128] = pair.astype(bf16)
            out_ref[:, 128:192] = mixed[2][:, :HEAD_DIM].astype(bf16)


def whole_spec(shape):
    return pl.BlockSpec(shape, lambda i, *_: (0,) * len(shape))


def attention_forward(bounds, queries, spans, pieces):
    block = queries.shape[0]
    window = sum(x.shape[0] for x in pieces)
    return pl.pallas_call(
        forward_kernel,
        grid_spec=pltpu.PrefetchScalarGridSpec(
            num_scalar_prefetch=1,
            grid=(block // TILE_Q,),
            in_specs=[whole_spec(queries.shape), whole_spec(spans.shape)]
            + [pl.BlockSpec(memory_space=pl.ANY)] * len(pieces),
            out_specs=[whole_spec((TILE_Q, 192))] * 4
            + [whole_spec((block, 192)), whole_spec((block, 128))],
            scratch_shapes=[
                pltpu.VMEM((window, 384), bf16),
                pltpu.VMEM((3, TILE_Q, 128), f32),
                pltpu.VMEM((3, TILE_Q, 128), f32),
                pltpu.VMEM((3, TILE_Q, 128), f32),
                pltpu.SemaphoreType.DMA((len(pieces),)),
            ],
        ),
        out_shape=[jax.ShapeDtypeStruct((TILE_Q, 192), bf16)] * 4
        + [jax.ShapeDtypeStruct((block, 192), f32), jax.ShapeDtypeStruct((block, 128), f32)],
        compiler_params=pltpu.CompilerParams(vmem_limit_bytes=40 * 2**20),
        cost_estimate=pl.CostEstimate(
            flops=4 * block * 2304 * 192, bytes_accessed=6 * 2**20, transcendentals=block * 2304 * 3
        ),
        name="attention_forward",
    )(bounds, queries, spans, *pieces)


def query_kernel(bounds, q_ref, span_ref, grad_ref, wide_ref, stat_ref, *rest):
    pieces, (out_ref, kv, accum, sem) = rest[:-4], rest[-4:]
    step = pl.program_id(0)

    @pl.when(step == 0)
    def _():
        for copy in load_window(pieces, kv, sem, [bounds[8 + i] for i in range(len(pieces))]):
            copy.wait()

    first = pl.multiple_of(step * TILE_Q, TILE_Q)
    here = pl.ds(first, TILE_Q)
    accum[...] = jnp.zeros_like(accum)
    q_tile = q_ref[here, :]
    heads = [head_of(q_tile[:, :128], q_tile[:, 128:], h) for h in range(3)]
    g_tile = grad_ref[here, :]
    lane = lax.broadcasted_iota(jnp.int32, (TILE_Q, 128), 1)
    g_pair = g_tile[:, :128]
    g_last = g_tile[:, 128:256]
    none = jnp.zeros((TILE_Q, 128), bf16)
    r_pair = pltpu.roll(g_pair.astype(f32), HEAD_DIM, 1).astype(bf16)
    r_last = pltpu.roll(g_last.astype(f32), HEAD_DIM, 1).astype(bf16)
    grads = [
        jnp.where(lane >= HEAD_DIM, r_pair, none),
        jnp.where(lane < HEAD_DIM, r_pair, none),
        jnp.where(lane >= HEAD_DIM, r_last, none),
    ]
    product_pair = g_pair.astype(f32) * wide_ref[here, 0:128]
    product_last = g_tile[:, 128:192].astype(f32) * wide_ref[here, 128:192]
    deltas = [
        jnp.sum(jnp.where(lane < HEAD_DIM, product_pair, 0.0), axis=1, keepdims=True),
        jnp.sum(jnp.where(lane < HEAD_DIM, 0.0, product_pair), axis=1, keepdims=True),
        jnp.sum(product_last, axis=1, keepdims=True),
    ]
    logs = [stat_ref[here, h : h + 1] for h in range(3)]
    lower, count = bounds[2 * step], bounds[2 * step + 1]

    def run(i, carry):
        begin = pl.multiple_of(lower + i * SPAN_K, 128)
        rows = pl.ds(begin, SPAN_K)
        keys = lax.broadcasted_iota(jnp.int32, (TILE_Q, SPAN_K), 1)
        allowed = (keys >= span_ref[here, 0:1] - begin) & (keys < span_ref[here, 1:2] - begin)
        S = [rows_nt(heads[h], kv[rows, 0:128] if h < 2 else kv[rows, 128:192]) for h in range(3)]
        B = [rows_nt(grads[h], kv[rows, 128:256] if h == 0 else kv[rows, 256:384]) for h in range(3)]
        for h in range(3):
            chance = jnp.exp(jnp.where(allowed, S[h] - logs[h], masked_score))
            change = (chance * (B[h] - deltas[h])).astype(bf16)
            accum[h] += rows_nn(change, kv[rows, 0:128] if h < 2 else kv[rows, 128:256])
        return carry

    lax.fori_loop(0, count, run, 0)
    out_ref[here, 0:128] = (jnp.where(lane < HEAD_DIM, accum[0], accum[1]) * 0.125).astype(bf16)
    out_ref[here, 128:192] = (accum[2][:, :HEAD_DIM] * 0.125).astype(bf16)


def attention_queries(bounds, queries, spans, grads, wide, stats, pieces):
    block = queries.shape[0]
    window = sum(x.shape[0] for x in pieces)
    return pl.pallas_call(
        query_kernel,
        grid_spec=pltpu.PrefetchScalarGridSpec(
            num_scalar_prefetch=1,
            grid=(block // TILE_Q,),
            in_specs=[whole_spec(x.shape) for x in (queries, spans, grads, wide, stats)]
            + [pl.BlockSpec(memory_space=pl.ANY)] * len(pieces),
            out_specs=whole_spec((block, 192)),
            scratch_shapes=[
                pltpu.VMEM((window, 384), bf16),
                pltpu.VMEM((3, TILE_Q, 128), f32),
                pltpu.SemaphoreType.DMA((len(pieces),)),
            ],
        ),
        out_shape=jax.ShapeDtypeStruct((block, 192), bf16),
        compiler_params=pltpu.CompilerParams(vmem_limit_bytes=40 * 2**20),
        cost_estimate=pl.CostEstimate(
            flops=6 * block * 2304 * 192, bytes_accessed=6 * 2**20, transcendentals=block * 2304 * 3
        ),
        name="attention_queries",
    )(bounds, queries, spans, grads, wide, stats, *pieces)


def key_kernel(reach, bounds, kv_ref, span_ref, *rest):
    window = 2 * reach + 1
    q_pieces, g_pieces = rest[:window], rest[window : 2 * window]
    out_ref, qs, gs, key_sum, value_sum, sem = rest[2 * window :]
    step = pl.program_id(0)
    block = q_pieces[0].shape[0]

    @pl.when(step == 0)
    def _():
        copies = load_window(q_pieces, qs, sem.at[0], [i * block for i in range(window)])
        copies += load_window(g_pieces, gs, sem.at[1], [i * block for i in range(window)])
        for copy in copies:
            copy.wait()

    first = pl.multiple_of(step * TILE_K, TILE_K)
    here = pl.ds(first, TILE_K)
    key_sum[...] = jnp.zeros_like(key_sum)
    value_sum[...] = jnp.zeros_like(value_sum)
    keys_pair = kv_ref[here, 0:128]
    keys = [head_of(keys_pair, kv_ref[here, 128:192], h) for h in range(3)]
    lane = lax.broadcasted_iota(jnp.int32, (TILE_K, 128), 1)
    zero = jnp.zeros((TILE_K, 128), f32)
    v_one = pltpu.roll(kv_ref[here, 128:256].astype(f32), HEAD_DIM, 1)
    v_two = pltpu.roll(kv_ref[here, 256:384].astype(f32), HEAD_DIM, 1)
    values = [
        jnp.where(lane < HEAD_DIM, v_one, zero).astype(bf16),
        jnp.where(lane < HEAD_DIM, zero, v_two).astype(bf16),
        v_two.astype(bf16)[:, :HEAD_DIM],
    ]
    line = lax.broadcasted_iota(jnp.int32, (16, HEAD_DIM), 0)
    slot = lax.broadcasted_iota(jnp.int32, (16, HEAD_DIM), 1)
    selector = jnp.where((slot // 3 == line) & (slot < 18), 1.0, 0.0).astype(bf16)
    lower, count = bounds[2 * step], bounds[2 * step + 1]

    def run(i, carry):
        begin = pl.multiple_of(lower + i * SPAN_Q, 128)
        columns = pl.ds(begin, SPAN_Q)
        place = reach * block + first + lax.broadcasted_iota(jnp.int32, (TILE_K, SPAN_Q), 0)
        allowed = (place >= span_ref[0:1, columns]) & (place < span_ref[1:2, columns])
        lanes = [slice(0, 128), slice(0, 128), slice(128, 192)]
        parts = gs[columns, 192:256]
        stats = rows_nt(selector, parts)
        S = [rows_nt(keys[h], qs[columns, lanes[h]]) for h in range(3)]
        B = [rows_nt(values[h], gs[columns, lanes[h]]) for h in range(3)]
        for h in range(3):
            score = S[h] - stats[h : h + 1, :]
            chance = jnp.exp(jnp.where(allowed, score, masked_score))
            change = (chance * (B[h] - stats[h + 3 : h + 4, :])).astype(bf16)
            size = 128 if h < 2 else HEAD_DIM
            key_sum[h, :, 0:size] += rows_nn(change, qs[columns, lanes[h]])
            value_sum[h, :, 0:size] += rows_nn(chance.astype(bf16), gs[columns, lanes[h]])
        return carry

    lax.fori_loop(0, count, run, 0)
    k_pair = jnp.where(lane < HEAD_DIM, key_sum[0], key_sum[1])
    v_pair = jnp.where(lane < HEAD_DIM, value_sum[0], value_sum[1])
    v_turn = pltpu.roll(v_pair, HEAD_DIM, 1)
    last_turn = pltpu.roll(value_sum[2], HEAD_DIM, 1)
    out_ref[here, 0:128] = k_pair.astype(bf16)
    out_ref[here, 128:256] = jnp.where(lane < HEAD_DIM, key_sum[2], v_turn).astype(bf16)
    out_ref[here, 256:384] = jnp.where(lane < HEAD_DIM, v_turn, last_turn).astype(bf16)


def attention_keys(bounds, pair, spans, q_pieces, g_pieces):
    block = pair.shape[0]
    count = len(q_pieces)
    return pl.pallas_call(
        functools.partial(key_kernel, count // 2),
        grid_spec=pltpu.PrefetchScalarGridSpec(
            num_scalar_prefetch=1,
            grid=(block // TILE_K,),
            in_specs=[whole_spec(x.shape) for x in (pair, spans)]
            + [pl.BlockSpec(memory_space=pl.ANY)] * (2 * count),
            out_specs=whole_spec((block, 384)),
            scratch_shapes=[
                pltpu.VMEM((count * block, 192), bf16),
                pltpu.VMEM((count * block, 256), bf16),
                pltpu.VMEM((3, TILE_K, 128), f32),
                pltpu.VMEM((3, TILE_K, 128), f32),
                pltpu.SemaphoreType.DMA((2, count)),
            ],
        ),
        out_shape=jax.ShapeDtypeStruct((block, 384), bf16),
        compiler_params=pltpu.CompilerParams(vmem_limit_bytes=40 * 2**20),
        cost_estimate=pl.CostEstimate(
            flops=8 * block * 2304 * 192, bytes_accessed=8 * 2**20, transcendentals=block * 2304 * 3
        ),
        name="attention_keys",
    )(bounds, pair, spans, *q_pieces, *g_pieces)


def projection_kernel(place_ref, own, near, far, corner, w_own, w_near, w_far, w_corner, bias_ref, *rest):
    tokens_ref, query_ref, pair_ref, weight, sem = rest
    rows, part = own.shape[0], w_own.shape[0]
    pieces = (w_own, w_near, w_far, w_corner)
    copies = []
    for r, piece in enumerate(pieces):
        where = pl.multiple_of(place_ref[r] * part, part)
        copies.append(pltpu.make_async_copy(piece, weight.at[pl.ds(where, part), :], sem.at[r]))
        copies[-1].start()
    for copy in copies:
        copy.wait()
    for r, piece in enumerate((own, near, far, corner)):
        here = pl.ds(pl.multiple_of(place_ref[r] * rows, rows), rows)
        tile = piece[...]
        tokens_ref[here, :] = tile
        made = rows_nn(tile, weight[...]) + bias_ref[0:1, :]
        pair_ref[here, :] = made[:, : 2 * part].astype(bf16)
        query_ref[here, :] = (made[:, 2 * part :].astype(bf16).astype(f32) * 0.125).astype(bf16)


def project(places, token_pieces, weight_pieces, bias):
    rows, width = token_pieces[0].shape
    part = weight_pieces[0].shape[0]
    block = rows * len(token_pieces)
    vmem = pl.BlockSpec(memory_space=pltpu.VMEM)
    return pl.pallas_call(
        projection_kernel,
        in_specs=[pl.BlockSpec(memory_space=pltpu.SMEM)]
        + [vmem] * 4
        + [pl.BlockSpec(memory_space=pl.ANY)] * 4
        + [vmem],
        out_specs=[vmem] * 3,
        out_shape=[
            jax.ShapeDtypeStruct((block, width), bf16),
            jax.ShapeDtypeStruct((block, part), bf16),
            jax.ShapeDtypeStruct((block, 2 * part), bf16),
        ],
        scratch_shapes=[pltpu.VMEM((width, 3 * part), bf16), pltpu.SemaphoreType.DMA((4,))],
        compiler_params=pltpu.CompilerParams(vmem_limit_bytes=32 * 2**20),
        cost_estimate=pl.CostEstimate(
            flops=2 * block * width * 3 * part, bytes_accessed=5 * 2**20, transcendentals=0
        ),
        name="layer_projection",
    )(places, *token_pieces, *weight_pieces, bias)


def normal_of(values):
    center = values - jnp.mean(values, axis=1, keepdims=True)
    inverse = lax.rsqrt(jnp.mean(center * center, axis=1, keepdims=True) + epsilon)
    return center * inverse, inverse


def normal_back(upstream, normal, inverse, gain):
    scaled = upstream * gain
    mean_scaled = jnp.mean(scaled, axis=1, keepdims=True)
    mean_product = jnp.mean(scaled * normal, axis=1, keepdims=True)
    return (scaled - mean_scaled - normal * mean_product) * inverse


def rows_tn(left, right):
    return lax.dot_general(left, right, (((0,), (0,)), ((), ())), preferred_element_type=f32)


def dense_kernel(place_ref, *refs):
    mixed = refs[0:4]
    tokens_ref, up_ref, small_ref, inner_bias_ref = refs[4:8]
    packs = refs[8:12]
    out_ref, grad_ref = refs[12:14]
    back_refs = refs[14:18]
    outer_refs, inner_refs = refs[18:20], refs[20:22]
    w_out, w_inner, w_outer, hidden, activated, slopes = refs[22:28]
    outer_made, inner_made, tail_made, sem, sent = refs[28:]
    rows, width = tokens_ref.shape
    groups = w_inner.shape[0]
    part = width // groups

    def inner_copies(g):
        return [
            pltpu.make_async_copy(
                packs[r].at[pl.ds(pl.multiple_of(width + part + 16 + g * part, 16), part), :],
                w_inner.at[g, pl.ds(pl.multiple_of(place_ref[r] * part, part), part), :],
                sem.at[1 + g, r],
            )
            for r in range(groups)
        ]

    out_copies = [
        pltpu.make_async_copy(packs[r].at[pl.ds(width, part), :], w_out.at[r], sem.at[0, r])
        for r in range(groups)
    ]
    outer_copies = [
        pltpu.make_async_copy(
            packs[r].at[pl.ds(0, width), :], w_outer.at[place_ref[r]], sem.at[1 + groups, r]
        )
        for r in range(groups)
    ]
    for copy in out_copies + [x for g in range(groups) for x in inner_copies(g)] + outer_copies:
        copy.start()

    out_bias, gain_one, shift_one = small_ref[0:1], small_ref[1:2], small_ref[2:3]
    outer_bias, gain_two, shift_two = small_ref[3:4], small_ref[4:5], small_ref[5:6]

    for copy in out_copies:
        copy.wait()
    residual = tokens_ref[...].astype(f32) + out_bias
    for r in range(groups):
        residual = residual + rows_nn(mixed[r][...], w_out[r])
    normal_one, inverse_one = normal_of(residual)
    first = normal_one * gain_one + shift_one
    first_low = first.astype(bf16)

    def ahead(g, carry):
        for copy in inner_copies(g):
            copy.wait()
        value = rows_nn(first_low, w_inner[g]) + inner_bias_ref[pl.ds(g, 1), :]
        chance = 0.5 * (1.0 + lax.erf(value * (2.0**-0.5)))
        density = jnp.exp(-0.5 * value * value) * (2.0 * jnp.pi) ** -0.5
        slopes[g] = chance + value * density
        activated[g] = (value * chance).astype(bf16)
        return carry

    lax.fori_loop(0, groups, ahead, 0)
    for copy in outer_copies:
        copy.wait()

    def combine(g, total):
        return total + rows_nn(activated[g], w_outer[g])

    residual = lax.fori_loop(0, groups, combine, first + outer_bias)
    normal_two, inverse_two = normal_of(residual)
    out_ref[...] = (normal_two * gain_two + shift_two).astype(bf16)
    upstream = up_ref[...].astype(f32)
    grad_two = normal_back(upstream, normal_two, inverse_two, gain_two)
    grad_two_low = grad_two.astype(bf16)
    shift_two_sum = jnp.sum(upstream, axis=0, keepdims=True)
    gain_two_sum = jnp.sum(upstream * normal_two, axis=0, keepdims=True)
    outer_bias_sum = jnp.sum(grad_two_low.astype(f32), axis=0, keepdims=True)

    def outer_copy(i, odd):
        r = 2 * i + odd
        return pltpu.make_async_copy(outer_made.at[r], outer_refs[odd].at[i], sent.at[0, r])

    def behind(i, total):
        for odd in range(2):
            g = place_ref[2 * i + odd]
            outer_made[2 * i + odd] = rows_tn(activated[g], grad_two_low).astype(bf16)
            outer_copy(i, odd).start()
            value = (rows_nt(grad_two_low, w_outer[g]) * slopes[g]).astype(bf16)
            hidden[g] = value
            total = total + rows_nt(value, w_inner[g])
        return total

    grad_first = lax.fori_loop(0, groups // 2, behind, grad_two)
    grad_one = normal_back(grad_first, normal_one, inverse_one, gain_one)
    grad_ref[...] = grad_one
    grad_one_low = grad_one.astype(bf16)
    for r in range(groups):
        back_refs[r][...] = rows_nt(grad_one_low, w_out[r]).astype(bf16)

    def inner_sends(g):
        return [
            pltpu.make_async_copy(
                inner_made.at[g, pl.ds(pl.multiple_of(place_ref[r] * part, part), part), :],
                inner_refs[r % 2].at[r // 2, pl.ds(pl.multiple_of(g * part, part), part), :],
                sent.at[1 + g, r],
            )
            for r in range(groups)
        ]

    def weigh(g, carry):
        inner_made[g] = rows_tn(first_low, hidden[g]).astype(bf16)
        for copy in inner_sends(g):
            copy.start()
        return carry

    lax.fori_loop(0, groups, weigh, 0)
    sums = [
        jnp.sum(grad_one_low.astype(f32), axis=0, keepdims=True),
        jnp.sum(grad_first * normal_one, axis=0, keepdims=True),
        jnp.sum(grad_first, axis=0, keepdims=True),
        outer_bias_sum,
        gain_two_sum,
        shift_two_sum,
    ]
    line = lax.broadcasted_iota(jnp.int32, (16, part), 0)
    tail_made[:, part:, :] = jnp.zeros((groups, 64, width), bf16)
    for r in range(groups):
        tail_made[r, 0:part, :] = rows_tn(mixed[r][...], grad_one_low).astype(bf16)
    for k in range(groups):
        tail = jnp.zeros((16, part), f32)
        for i, line_sum in enumerate(sums):
            tail = jnp.where(line == i, line_sum[:, k * part : (k + 1) * part], tail)
        bias_sum = jnp.sum(hidden[k].astype(f32), axis=0, keepdims=True)
        for i in range(groups):
            tail = jnp.where(
                line == len(sums) + i, bias_sum[:, i * part : (i + 1) * part], tail
            )
        tail_made[place_ref[k], part : part + 16, 0:part] = tail.astype(bf16)
    tail_copies = [
        pltpu.make_async_copy(
            tail_made.at[r], inner_refs[r % 2].at[r // 2, pl.ds(width, part + 64), :], sent.at[1 + groups, r]
        )
        for r in range(groups)
    ]
    for copy in tail_copies:
        copy.start()
    for i in range(groups // 2):
        for odd in range(2):
            outer_copy(i, odd).wait()
    for g in range(groups):
        for copy in inner_sends(g):
            copy.wait()
    for copy in tail_copies:
        copy.wait()


def dense(places, mixed_pieces, tokens, cotangent, small, inner_bias, packs):
    rows, width = tokens.shape
    groups = len(packs)
    part = width // groups
    vmem = pl.BlockSpec(memory_space=pltpu.VMEM)
    hbm = pl.BlockSpec(memory_space=pl.ANY)
    return pl.pallas_call(
        dense_kernel,
        in_specs=[pl.BlockSpec(memory_space=pltpu.SMEM)] + [vmem] * (groups + 4) + [hbm] * groups,
        out_specs=[vmem] * (2 + groups) + [hbm] * 4,
        out_shape=[
            jax.ShapeDtypeStruct((rows, width), bf16),
            jax.ShapeDtypeStruct((rows, width), f32),
        ]
        + [jax.ShapeDtypeStruct((rows, part), bf16)] * groups
        + [jax.ShapeDtypeStruct((groups // 2, width, width), bf16)] * 2
        + [jax.ShapeDtypeStruct((groups // 2, width + part + 64, width), bf16)] * 2,
        scratch_shapes=[
            pltpu.VMEM((groups, part, width), bf16),
            pltpu.VMEM((groups, width, width), bf16),
            pltpu.VMEM((groups, width, width), bf16),
            pltpu.VMEM((groups, rows, width), bf16),
            pltpu.VMEM((groups, rows, width), bf16),
            pltpu.VMEM((groups, rows, width), f32),
            pltpu.VMEM((groups, width, width), bf16),
            pltpu.VMEM((groups, width, width), bf16),
            pltpu.VMEM((groups, part + 64, width), bf16),
            pltpu.SemaphoreType.DMA((groups + 2, groups)),
            pltpu.SemaphoreType.DMA((groups + 2, groups)),
        ],
        compiler_params=pltpu.CompilerParams(vmem_limit_bytes=48 * 2**20),
        cost_estimate=pl.CostEstimate(
            flops=24 * rows * width * width * groups,
            bytes_accessed=24 * 2**20,
            transcendentals=2 * rows * width * groups,
        ),
        name="layer_dense",
    )(places, *mixed_pieces, tokens, cotangent, small, inner_bias, *packs)


def gather_kernel(place_ref, p0, p1, p2, p3, wide_ref, stat_ref, out_ref):
    rows, part = p0.shape
    lane = lax.broadcasted_iota(jnp.int32, (rows, 128), 1)
    slot = lax.broadcasted_iota(jnp.int32, (rows, HEAD_DIM), 1)
    for r, piece in enumerate((p0, p1, p2, p3)):
        here = pl.ds(pl.multiple_of(place_ref[r] * rows, rows), rows)
        tile = piece[...]
        product = tile.astype(f32) * wide_ref[here, :]
        pair, last = product[:, 0:128], product[:, 128:192]
        values = [stat_ref[here, h : h + 1] for h in range(3)] + [
            jnp.sum(jnp.where(lane < HEAD_DIM, pair, 0.0), axis=1, keepdims=True),
            jnp.sum(jnp.where(lane < HEAD_DIM, 0.0, pair), axis=1, keepdims=True),
            jnp.sum(last, axis=1, keepdims=True),
        ]
        tail = jnp.zeros((rows, HEAD_DIM), f32)
        for i, left in enumerate(values):
            for j in range(3):
                high = left.astype(bf16).astype(f32)
                tail = jnp.where(slot == 3 * i + j, high, tail)
                left = left - high
        out_ref[here, 0:192] = tile
        out_ref[here, 192:256] = tail.astype(bf16)


def gathered(places, pieces, wide, stats):
    block = wide.shape[0]
    vmem = pl.BlockSpec(memory_space=pltpu.VMEM)
    return pl.pallas_call(
        gather_kernel,
        in_specs=[pl.BlockSpec(memory_space=pltpu.SMEM)] + [vmem] * 6,
        out_specs=vmem,
        out_shape=jax.ShapeDtypeStruct((block, 256), bf16),
        compiler_params=pltpu.CompilerParams(vmem_limit_bytes=16 * 2**20),
        cost_estimate=pl.CostEstimate(flops=2**20, bytes_accessed=3 * 2**20, transcendentals=0),
        name="layer_gather",
    )(places, *pieces, wide, stats)


def heads_kernel(place_ref, tokens_ref, query_ref, pair_ref, w0, w1, w2, w3, grad_ref, back_ref, weight, sem):
    groups, part = grad_ref.shape[0], w0.shape[0]
    rows = back_ref.shape[1]
    copies = []
    for r, piece in enumerate((w0, w1, w2, w3)):
        where = pl.multiple_of(place_ref[r] * part, part)
        copies.append(pltpu.make_async_copy(piece, weight.at[pl.ds(where, part), :], sem.at[r]))
        copies[-1].start()
    tokens = tokens_ref[...]
    pair_grad = rows_tn(tokens, pair_ref[...]).astype(bf16)
    query_grad = rows_tn(tokens, query_ref[...]).astype(bf16)
    for k in range(groups):
        here = slice(k * part, (k + 1) * part)
        grad_ref[k, :, 0 : 2 * part] = pair_grad[here]
        grad_ref[k, :, 2 * part : 3 * part] = query_grad[here]
    ones = jnp.ones((tokens.shape[0], HEAD_DIM), bf16)
    query_sum = rows_tn(query_ref[...], ones)
    value_sum = rows_tn(pair_ref[:, part:], ones)
    lane = lax.broadcasted_iota(jnp.int32, (part, HEAD_DIM), 1)
    sums = jnp.where(lane == 0, query_sum, jnp.where(lane == 1, value_sum, 0.0))
    grad_ref[:, :, 3 * part : 3 * part + HEAD_DIM] = jnp.zeros((groups, part, HEAD_DIM), bf16)
    grad_ref[place_ref[0], :, 3 * part : 3 * part + HEAD_DIM] = sums.astype(bf16)
    for copy in copies:
        copy.wait()
    for k in range(groups):
        here = slice(k * rows, (k + 1) * rows)
        made = rows_nt(pair_ref[here, :], weight[:, : 2 * part])
        made = made + rows_nt(query_ref[here, :], weight[:, 2 * part :])
        back_ref[place_ref[k]] = made.astype(bf16)


def head_grads(places, tokens, grad_query, grad_pair, weight_pieces):
    block, width = tokens.shape
    groups, part = len(weight_pieces), weight_pieces[0].shape[0]
    vmem = pl.BlockSpec(memory_space=pltpu.VMEM)
    return pl.pallas_call(
        heads_kernel,
        in_specs=[pl.BlockSpec(memory_space=pltpu.SMEM)]
        + [vmem] * 3
        + [pl.BlockSpec(memory_space=pl.ANY)] * groups,
        out_specs=[vmem] * 2,
        out_shape=[
            jax.ShapeDtypeStruct((groups, part, 3 * part + HEAD_DIM), bf16),
            jax.ShapeDtypeStruct((groups, block // groups, width), bf16),
        ],
        scratch_shapes=[pltpu.VMEM((width, 3 * part), bf16), pltpu.SemaphoreType.DMA((groups,))],
        compiler_params=pltpu.CompilerParams(vmem_limit_bytes=32 * 2**20),
        cost_estimate=pl.CostEstimate(
            flops=4 * block * width * 3 * part, bytes_accessed=8 * 2**20, transcendentals=0
        ),
        name="layer_heads",
    )(places, tokens, grad_query, grad_pair, *weight_pieces)


def both(left, right):
    return (left.astype(f32) + right.astype(f32)).astype(bf16)


def half_of(block, bit, axis):
    size = block.shape[axis] // 2
    return lax.dynamic_slice_in_dim(block, bit * size, size, axis)


def scatter_sum(terms, axis_name, order, axis):
    index = lax.axis_index(axis_name)
    for step in order:
        bit = (index // step) % 2
        sent = functools.reduce(both, [half_of(x, 1 - bit, axis) for x in terms])
        kept = functools.reduce(both, [half_of(x, bit, axis) for x in terms])
        terms = [kept, swapped(sent, axis_name, step)]
    return terms


def full_sum(terms, axis_name, step):
    block = functools.reduce(both, terms)
    return both(block, swapped(block, axis_name, step))


def gather_back(block, axis_name, order, axis):
    index = lax.axis_index(axis_name)
    for step in reversed(order):
        other = swapped(block, axis_name, step)
        late = (index // step) % 2 == 1
        block = jnp.where(
            late,
            jnp.concatenate([other, block], axis),
            jnp.concatenate([block, other], axis),
        )
    return block


def on_device(
    tokens,
    doc_start,
    cotangent,
    query_weight,
    key_weight,
    value_weight,
    out_weight,
    query_bias,
    value_bias,
    out_bias,
    first_gain,
    first_shift,
    inner_weight,
    inner_bias,
    outer_weight,
    outer_bias,
    second_gain,
    second_shift,
):
    rows, width = tokens.shape
    cycle = lax.axis_size("ctx")
    shards = lax.axis_size("wt")
    block = rows * shards
    reach = (MAXDOC + block - 2) // block
    window = (2 * reach + 1) * block
    c = lax.axis_index("ctx")
    w = lax.axis_index("wt")
    part = width // shards
    places = jnp.stack([w ^ r for r in range(shards)]).astype(jnp.int32)

    def spread(own, near):
        far = swapped(own, "wt", 2)
        return [own, near, far, swapped(far, "wt", 1)]

    def columns(r):
        start = (w ^ r) * part
        return jnp.concatenate(
            [
                lax.dynamic_slice_in_dim(x, start, part, 1)
                for x in (key_weight, value_weight, query_weight)
            ],
            axis=1,
        )

    token_pieces = spread(tokens, swapped(tokens, "wt", 1))
    weight_pieces = [columns(0)] + [swapped(columns(r), "wt", r) for r in range(1, shards)]
    head_bias = jnp.concatenate([jnp.zeros((part,), f32), value_bias.astype(f32), query_bias.astype(f32)])
    head_bias = jnp.broadcast_to(head_bias[None], (8, 3 * part))

    pad = reach * block
    padded = jnp.pad(doc_start, (pad, pad), constant_values=-1)
    base = c * block - pad
    marks = lax.dynamic_slice_in_dim(padded, c * block, window)
    place = jnp.arange(window, dtype=jnp.int32)
    begins = jnp.where((marks == base + place) | (marks < 0), place, window)
    next_begin = lax.cummin(begins, axis=0, reverse=True)
    stops = jnp.concatenate([next_begin[1:], jnp.full((1,), window, jnp.int32)])
    starts = marks - base
    spans_row = jnp.stack([starts, stops] + [jnp.zeros_like(starts)] * 6)
    spans_column = spans_row[:, pad : pad + block].T
    own_starts = starts[pad : pad + block]
    own_stops = stops[pad : pad + block]

    def bounds_of(tile, span):
        lowest = own_starts.reshape(-1, tile)[:, 0] // 128 * 128
        highest = own_stops.reshape(-1, tile)[:, -1]
        count = (highest - lowest + span - 1) // span
        lowest = jnp.minimum(lowest, (window - count * span) // 128 * 128)
        return jnp.stack([lowest, count], axis=1).reshape(-1)

    query_bounds = bounds_of(TILE_Q, SPAN_K)
    key_bounds = bounds_of(TILE_K, SPAN_Q)

    block_tokens, queries, pair = project(places, token_pieces, weight_pieces, head_bias)

    distances = [d for d in range(reach, -reach - 1, -1)]

    def halo(own):
        return [own if d == 0 else shifted(own, "ctx", d) for d in distances]

    even = c % 2 == 0
    beside = swapped(pair, "ctx", 1)
    before, after = shifted(pair, "ctx", 2), shifted(pair, "ctx", -2)
    half = block // 2
    route = [(i, i + 2 if i % 2 == 0 else i - 2) for i in range(cycle)]
    route = [(i, j) for i, j in route if 0 <= j < cycle]
    upper = swapped(jnp.where(even, after[:half], before[:half]), "ctx", 1)
    lower = lax.ppermute(beside[half:], "ctx", route)
    pairs = [before, after, pair, beside, upper, lower]
    beside_at = jnp.where(even, reach + 1, reach - 1) * block
    missing_at = jnp.where(even, reach - 1, reach + 1) * block
    load_at = jnp.stack(
        [0 * missing_at, 2 * reach * block + 0 * missing_at, reach * block + 0 * missing_at]
        + [beside_at, missing_at, missing_at + half]
    )
    query_bounds = jnp.concatenate([query_bounds, load_at, places]).astype(jnp.int32)

    small_own = jnp.stack(
        [out_bias, first_gain, first_shift, outer_bias, second_gain, second_shift]
    )
    small_own = jnp.concatenate([small_own, inner_bias.reshape(-1, part)], axis=0)
    small_own = jnp.pad(small_own, ((0, 16 - small_own.shape[0]), (0, width - part)))
    inner_parts = [inner_weight[:, i * width : (i + 1) * width] for i in range(shards)]
    pack = jnp.concatenate([outer_weight, out_weight, small_own] + inner_parts, axis=0)
    pack, _ = lax.optimization_barrier((pack, token_pieces[2:] + weight_pieces[1:]))
    pack_near, pack_far = swapped(pack, "wt", 1), swapped(pack, "wt", 2)
    *mixed_pieces, mixed_wide, stat_columns = attention_forward(
        query_bounds, queries, spans_column, pairs
    )
    ready, _ = lax.optimization_barrier((queries, pairs))
    query_halo = [queries if d == 0 else shifted(ready, "ctx", d) if d * d == 1 else None for d in distances]
    close = [x for x, d in zip(query_halo, distances) if d * d == 1]
    mixed_pieces, mixed_wide, stat_columns, close, pack_far = lax.optimization_barrier(
        (mixed_pieces, mixed_wide, stat_columns, close, pack_far)
    )
    packs = [pack, pack_near, pack_far, swapped(pack_far, "wt", 1)]
    small = jnp.stack([x[width + part : width + part + 16, :part] for x in packs]).astype(f32)
    small = [lax.dynamic_index_in_dim(small, w ^ k, 0, keepdims=False) for k in range(shards)]
    small_rows = jnp.concatenate([x[:8] for x in small], axis=1)
    inner_bias_rows = jnp.stack([x[6:10].reshape(-1) for x in small])

    mixed_pieces = [mixed_pieces[0]] + [
        swapped(mixed_pieces[r], "wt", r) for r in range(1, shards)
    ]
    far_ready, mixed_pieces = lax.optimization_barrier((queries, mixed_pieces))
    results = dense(
        places, mixed_pieces, tokens, cotangent, small_rows, inner_bias_rows, packs
    )
    remote = [shifted(far_ready, "ctx", d) for d in distances if d * d > 1]
    results, remote = lax.optimization_barrier((results, remote))
    layer_out, grad_one, *back = results[: 2 + shards]
    outer_keep, outer_send, inner_keep, inner_send = results[2 + shards :]
    query_halo = [remote[0], close[0], queries, close[1], remote[1]]

    back_pieces = [back[0]] + [swapped(back[r], "wt", r) for r in range(1, shards)]
    outer_got = swapped(outer_send, "wt", 1)
    inner_got = swapped(inner_send, "wt", 1)
    grads = gathered(places, back_pieces, mixed_wide, stat_columns)
    outer_got, _ = lax.optimization_barrier((outer_got, back_pieces[1:]))
    grads, inner_got = lax.optimization_barrier((grads, inner_got))

    def far_terms(keep, got):
        return [both(keep[0], got[0]), swapped(both(keep[1], got[1]), "wt", 2)]

    grad_halo = halo(grads)
    outer_terms = far_terms(outer_keep, outer_got)
    grad_query = attention_queries(
        query_bounds, queries, spans_column, grads, mixed_wide, stat_columns, pairs
    )
    grad_query, grad_halo, outer_terms, inner_keep, inner_got = lax.optimization_barrier(
        (grad_query, grad_halo, outer_terms, inner_keep, inner_got)
    )

    near_first = [1 << i for i in range(cycle.bit_length() - 1)]
    outer_terms = scatter_sum(outer_terms, "ctx", near_first[:1], 0)
    inner_terms = far_terms(inner_keep, inner_got)
    grad_pair = attention_keys(key_bounds, pair, spans_row, query_halo, grad_halo)
    grad_pair, outer_terms, inner_terms = lax.optimization_barrier(
        (grad_pair, outer_terms, inner_terms)
    )

    head_grad, token_partial = head_grads(places, block_tokens, grad_query, grad_pair, weight_pieces)
    halved, last = near_first[:-1], near_first[-1]
    outer_part = full_sum(scatter_sum(outer_terms, "ctx", halved[1:], 0), "ctx", last)
    inner_part = full_sum(scatter_sum(inner_terms, "ctx", halved, 0), "ctx", last)
    head_part = full_sum(scatter_sum([head_grad], "ctx", halved, 1), "ctx", last)
    token_got = swapped(token_partial[1::2], "wt", 1)
    token_sum = both(*far_terms(token_partial[0::2], token_got))
    outer_total = gather_back(outer_part, "ctx", halved, 0)
    inner_total = gather_back(inner_part, "ctx", halved, 0)
    head_pieces = [
        lax.dynamic_index_in_dim(head_part, w ^ r, 0, keepdims=False) for r in range(shards)
    ]
    head_pieces = [head_pieces[0]] + [swapped(head_pieces[r], "wt", r) for r in range(1, shards)]
    head_parts = jnp.stack(
        [
            lax.dynamic_index_in_dim(jnp.stack(head_pieces), w ^ k, 0, keepdims=False)
            for k in range(shards)
        ]
    )
    head_total = gather_back(head_parts, "ctx", halved, 1)

    tokens_gradient = grad_one + token_sum.astype(f32)
    key_total, value_total, query_total = (
        jnp.concatenate(
            [head_total[k, :, i * part : (i + 1) * part] for k in range(shards)], axis=1
        ).astype(f32)
        for i in range(3)
    )
    own_total = lax.dynamic_index_in_dim(head_total, w, 0, keepdims=False)
    inner_rows = inner_total[:width].reshape(shards, part, width)
    inner_rows = jnp.concatenate([inner_rows[k] for k in range(shards)], axis=1).astype(f32)
    lines = inner_total[width + part : width + part + 16, :part].astype(f32)

    return (
        layer_out,
        tokens_gradient,
        query_total,
        key_total,
        value_total,
        inner_total[width : width + part].astype(f32),
        own_total[:, 3 * part].astype(f32),
        own_total[:, 3 * part + 1].astype(f32),
        lines[0],
        lines[1],
        lines[2],
        inner_rows,
        lines[6:10].reshape(-1),
        outer_total.astype(f32),
        lines[3],
        lines[4],
        lines[5],
    )


def solution(mesh):
    matrix, vector = P("wt", None), P("wt")
    stream = P(("ctx", "wt"), None)
    in_specs = (stream, P(), stream) + (matrix,) * 4 + (vector,) * 5
    in_specs += (matrix, vector, matrix, vector, vector, vector)
    out_specs = (stream, stream) + (matrix,) * 4 + (vector,) * 5
    out_specs += (matrix, vector, matrix, vector, vector, vector)
    return jax.shard_map(
        on_device, mesh=mesh, in_specs=in_specs, out_specs=out_specs, check_vma=False
    )
```

```python
import functools

import jax
import jax.numpy as jnp
from jax import lax
from jax.experimental import pallas as pl
from jax.experimental.pallas import tpu as pltpu
from jax.sharding import PartitionSpec as P

HEADS = 12
HEAD_DIM = 64
MAXDOC = 2048
TILE_Q = 256
SPAN_K = 768
TILE_K = 256
SPAN_Q = 768
CHUNK = 256

masked_score = -1e30
epsilon = 1e-06
bf16 = jnp.bfloat16
f32 = jnp.float32


def swapped(block, axis, bit):
    count = lax.axis_size(axis)
    return lax.ppermute(block, axis, [(i, i ^ bit) for i in range(count)])


def shifted(block, axis, distance):
    count = lax.axis_size(axis)
    route = [(i, i + distance) for i in range(count) if 0 <= i + distance < count]
    return lax.ppermute(block, axis, route)


def rows_nt(left, right):
    return lax.dot_general(left, right, (((1,), (1,)), ((), ())), preferred_element_type=f32)


def rows_nn(left, right):
    return lax.dot_general(left, right, (((1,), (0,)), ((), ())), preferred_element_type=f32)


def load_window(pieces, target, sem, starts):
    copies = []
    for i, piece in enumerate(pieces):
        rows = pl.ds(pl.multiple_of(starts[i], 128), piece.shape[0])
        copies.append(pltpu.make_async_copy(piece, target.at[rows, :], sem.at[i]))
    for copy in copies:
        copy.start()
    return copies


def head_of(tile0, tile1, head):
    lane = lax.broadcasted_iota(jnp.int32, tile0.shape, 1)
    if head == 0:
        return jnp.where(lane < HEAD_DIM, tile0, jnp.zeros_like(tile0))
    if head == 1:
        return jnp.where(lane >= HEAD_DIM, tile0, jnp.zeros_like(tile0))
    return tile1


def turned(source, target, lanes, low, high):
    def turn(i, carry):
        rows = pl.ds(pl.multiple_of(i * 256, 256), 256)
        target[:, rows] = source[rows, lanes].T
        return carry

    lax.fori_loop(low, high, turn, 0)


def inside(span_ref, first, begin, rows):
    own = pl.ds(first, TILE_Q)
    place = begin + lax.broadcasted_iota(jnp.int32, (rows, TILE_Q), 0)
    return (place >= span_ref[0:1, own]) & (place < span_ref[1:2, own])


def forward_kernel(bounds, q_ref, span_ref, *rest):
    pieces, rest = rest[:-10], rest[-10:]
    outs, (wide_ref, row_ref, stat_ref, kv, vt, sem) = rest[:4], rest[4:]
    step = pl.program_id(0)

    @pl.when(step == 0)
    def _():
        for copy in load_window(pieces, kv, sem, [bounds[10 + i] for i in range(len(pieces))]):
            copy.wait()
        turned(kv, vt, slice(192, 384), bounds[8], bounds[9])

    first = pl.multiple_of(step * TILE_Q, TILE_Q)
    here = pl.ds(first, TILE_Q)
    q_tile = q_ref[here, :]
    heads = [head_of(q_tile[:, :128], q_tile[:, 128:], h) for h in range(3)]
    lower, count = bounds[2 * step], bounds[2 * step + 1]

    def run(i, carry):
        begin = pl.multiple_of(lower + i * SPAN_K, 128)
        rows = pl.ds(begin, SPAN_K)
        allowed = inside(span_ref, first, begin, SPAN_K)
        after = []

        def ahead(h):
            score = rows_nt(kv[rows, 0:128] if h < 2 else kv[rows, 128:192], heads[h])
            return jnp.where(allowed, score, masked_score)

        coming = ahead(0)
        for h in range(3):
            score = coming
            if h < 2:
                coming = ahead(h + 1)
            before, total, accum = carry[3 * h : 3 * h + 3]
            newest = jnp.maximum(before, jnp.max(score, axis=0, keepdims=True))
            factor = jnp.exp(before - newest)
            weight = jnp.exp(score - newest)
            total = total * factor + jnp.sum(weight, axis=0, keepdims=True)
            made = rows_nn(vt[h * HEAD_DIM : (h + 1) * HEAD_DIM, rows], weight.astype(bf16))
            after += [newest, total, accum * factor + made]
        return tuple(after)

    start = (
        jnp.full((1, TILE_Q), masked_score, f32),
        jnp.zeros((1, TILE_Q), f32),
        jnp.zeros((HEAD_DIM, TILE_Q), f32),
    )
    state = lax.fori_loop(0, count, run, start * 3)
    mixed = jnp.concatenate([state[3 * h + 2] / state[3 * h + 1] for h in range(3)], axis=0).T
    line = lax.broadcasted_iota(jnp.int32, (128, TILE_Q), 0)
    stats = jnp.zeros((128, TILE_Q), f32)
    for h in range(3):
        stats = jnp.where(line == h, state[3 * h] + jnp.log(state[3 * h + 1]), stats)
    wide_ref[here, :] = mixed
    row_ref[:, here] = stats[0:8, :]
    stat_ref[here, :] = stats.T
    low = mixed.astype(bf16)
    for r, out_ref in enumerate(outs):

        @pl.when(bounds[16 + step] == r)
        def _(out_ref=out_ref):
            out_ref[...] = low


def whole_spec(shape):
    return pl.BlockSpec(shape, lambda i, *_: (0,) * len(shape))


def attention_forward(bounds, queries, spans, pieces):
    block = queries.shape[0]
    window = sum(x.shape[0] for x in pieces)
    return pl.pallas_call(
        forward_kernel,
        grid_spec=pltpu.PrefetchScalarGridSpec(
            num_scalar_prefetch=1,
            grid=(block // TILE_Q,),
            in_specs=[whole_spec(queries.shape), whole_spec(spans.shape)]
            + [pl.BlockSpec(memory_space=pl.ANY)] * len(pieces),
            out_specs=[whole_spec((TILE_Q, 192))] * 4
            + [whole_spec((block, 192)), whole_spec((8, block)), whole_spec((block, 128))],
            scratch_shapes=[
                pltpu.VMEM((window, 384), bf16),
                pltpu.VMEM((192, window), bf16),
                pltpu.SemaphoreType.DMA((len(pieces),)),
            ],
        ),
        out_shape=[jax.ShapeDtypeStruct((TILE_Q, 192), bf16)] * 4
        + [
            jax.ShapeDtypeStruct((block, 192), f32),
            jax.ShapeDtypeStruct((8, block), f32),
            jax.ShapeDtypeStruct((block, 128), f32),
        ],
        compiler_params=pltpu.CompilerParams(vmem_limit_bytes=60 * 2**20),
        cost_estimate=pl.CostEstimate(
            flops=4 * block * 2304 * 192, bytes_accessed=6 * 2**20, transcendentals=block * 2304 * 3
        ),
        name="attention_forward",
    )(bounds, queries, spans, *pieces)


def query_kernel(bounds, q_ref, span_ref, grad_ref, wide_ref, row_ref, *rest):
    pieces, (out_ref, kv, kt, sem) = rest[:-4], rest[-4:]
    step = pl.program_id(0)

    @pl.when(step == 0)
    def _():
        for copy in load_window(pieces, kv, sem, [bounds[10 + i] for i in range(len(pieces))]):
            copy.wait()
        turned(kv, kt, slice(0, 192), bounds[8], bounds[9])

    first = pl.multiple_of(step * TILE_Q, TILE_Q)
    here = pl.ds(first, TILE_Q)
    q_tile = q_ref[here, :]
    heads = [head_of(q_tile[:, :128], q_tile[:, 128:], h) for h in range(3)]
    g_tile = grad_ref[here, :]
    lane = lax.broadcasted_iota(jnp.int32, (TILE_Q, 128), 1)
    none = jnp.zeros((TILE_Q, 128), bf16)
    r_pair = pltpu.roll(g_tile[:, :128].astype(f32), HEAD_DIM, 1).astype(bf16)
    r_last = pltpu.roll(g_tile[:, 128:256].astype(f32), HEAD_DIM, 1).astype(bf16)
    grads = [
        jnp.where(lane >= HEAD_DIM, r_pair, none),
        jnp.where(lane < HEAD_DIM, r_pair, none),
        jnp.where(lane >= HEAD_DIM, r_last, none),
    ]
    product = (g_tile[:, 0:192].astype(f32) * wide_ref[here, :]).T
    deltas = [
        jnp.sum(product[h * HEAD_DIM : (h + 1) * HEAD_DIM], axis=0, keepdims=True) for h in range(3)
    ]
    logs = [row_ref[h : h + 1, here] for h in range(3)]
    lower, count = bounds[2 * step], bounds[2 * step + 1]

    def run(i, carry):
        begin = pl.multiple_of(lower + i * SPAN_K, 128)
        rows = pl.ds(begin, SPAN_K)
        allowed = inside(span_ref, first, begin, SPAN_K)
        after = []

        def ahead(h):
            score = rows_nt(kv[rows, 0:128] if h < 2 else kv[rows, 128:192], heads[h])
            return score, rows_nt(kv[rows, 128:256] if h == 0 else kv[rows, 256:384], grads[h])

        coming = ahead(0)
        for h in range(3):
            score, back = coming
            if h < 2:
                coming = ahead(h + 1)
            chance = jnp.exp(jnp.where(allowed, score - logs[h], masked_score))
            change = (chance * (back - deltas[h])).astype(bf16)
            after.append(carry[h] + rows_nn(kt[h * HEAD_DIM : (h + 1) * HEAD_DIM, rows], change))
        return tuple(after)

    sums = lax.fori_loop(0, count, run, (jnp.zeros((HEAD_DIM, TILE_Q), f32),) * 3)
    out_ref[here, :] = (jnp.concatenate(sums, axis=0).T * 0.125).astype(bf16)


def attention_queries(bounds, queries, spans, grads, wide, stats, pieces):
    block = queries.shape[0]
    window = sum(x.shape[0] for x in pieces)
    return pl.pallas_call(
        query_kernel,
        grid_spec=pltpu.PrefetchScalarGridSpec(
            num_scalar_prefetch=1,
            grid=(block // TILE_Q,),
            in_specs=[whole_spec(x.shape) for x in (queries, spans, grads, wide, stats)]
            + [pl.BlockSpec(memory_space=pl.ANY)] * len(pieces),
            out_specs=whole_spec((block, 192)),
            scratch_shapes=[
                pltpu.VMEM((window, 384), bf16),
                pltpu.VMEM((192, window), bf16),
                pltpu.SemaphoreType.DMA((len(pieces),)),
            ],
        ),
        out_shape=jax.ShapeDtypeStruct((block, 192), bf16),
        compiler_params=pltpu.CompilerParams(vmem_limit_bytes=40 * 2**20),
        cost_estimate=pl.CostEstimate(
            flops=6 * block * 2304 * 192, bytes_accessed=6 * 2**20, transcendentals=block * 2304 * 3
        ),
        name="attention_queries",
    )(bounds, queries, spans, grads, wide, stats, *pieces)


def key_kernel(reach, bounds, kv_ref, span_ref, *rest):
    window = 2 * reach + 1
    q_pieces, g_pieces = rest[:window], rest[window : 2 * window]
    out_ref, qs, gs, key_sum, value_sum, sem = rest[2 * window :]
    step = pl.program_id(0)
    block = q_pieces[0].shape[0]

    @pl.when(step == 0)
    def _():
        copies = load_window(q_pieces, qs, sem.at[0], [i * block for i in range(window)])
        copies += load_window(g_pieces, gs, sem.at[1], [i * block for i in range(window)])
        for copy in copies:
            copy.wait()

    first = pl.multiple_of(step * TILE_K, TILE_K)
    here = pl.ds(first, TILE_K)
    key_sum[...] = jnp.zeros_like(key_sum)
    value_sum[...] = jnp.zeros_like(value_sum)
    keys_pair = kv_ref[here, 0:128]
    keys = [head_of(keys_pair, kv_ref[here, 128:192], h) for h in range(3)]
    lane = lax.broadcasted_iota(jnp.int32, (TILE_K, 128), 1)
    zero = jnp.zeros((TILE_K, 128), f32)
    v_one = pltpu.roll(kv_ref[here, 128:256].astype(f32), HEAD_DIM, 1)
    v_two = pltpu.roll(kv_ref[here, 256:384].astype(f32), HEAD_DIM, 1)
    values = [
        jnp.where(lane < HEAD_DIM, v_one, zero).astype(bf16),
        jnp.where(lane < HEAD_DIM, zero, v_two).astype(bf16),
        v_two.astype(bf16)[:, :HEAD_DIM],
    ]
    line = lax.broadcasted_iota(jnp.int32, (16, HEAD_DIM), 0)
    slot = lax.broadcasted_iota(jnp.int32, (16, HEAD_DIM), 1)
    selector = jnp.where((slot // 3 == line) & (slot < 18), 1.0, 0.0).astype(bf16)
    lower, count = bounds[2 * step], bounds[2 * step + 1]

    def run(i, carry):
        begin = pl.multiple_of(lower + i * SPAN_Q, 128)
        columns = pl.ds(begin, SPAN_Q)
        place = reach * block + first + lax.broadcasted_iota(jnp.int32, (TILE_K, SPAN_Q), 0)
        allowed = (place >= span_ref[0:1, columns]) & (place < span_ref[1:2, columns])
        lanes = [slice(0, 128), slice(0, 128), slice(128, 192)]
        stats = rows_nt(selector, gs[columns, 192:256])
        items = [(h, ch) for h in range(3) for ch in range(SPAN_Q // CHUNK)]

        def ahead(item):
            h, ch = item
            here = pl.ds(pl.multiple_of(begin + ch * CHUNK, 128), CHUNK)
            q_tile, g_tile = qs[here, lanes[h]], gs[here, lanes[h]]
            return q_tile, g_tile, rows_nt(keys[h], q_tile), rows_nt(values[h], g_tile)

        coming = ahead(items[0])
        for n, (h, ch) in enumerate(items):
            q_tile, g_tile, score, back = coming
            if n + 1 < len(items):
                coming = ahead(items[n + 1])
            cols = slice(ch * CHUNK, (ch + 1) * CHUNK)
            score = jnp.where(allowed[:, cols], score - stats[h : h + 1, cols], masked_score)
            chance = jnp.exp(score)
            change = (chance * (back - stats[h + 3 : h + 4, cols])).astype(bf16)
            size = 128 if h < 2 else HEAD_DIM
            key_sum[h, :, 0:size] += rows_nn(change, q_tile)
            value_sum[h, :, 0:size] += rows_nn(chance.astype(bf16), g_tile)
        return carry

    lax.fori_loop(0, count, run, 0)
    k_pair = jnp.where(lane < HEAD_DIM, key_sum[0], key_sum[1])
    v_pair = jnp.where(lane < HEAD_DIM, value_sum[0], value_sum[1])
    v_turn = pltpu.roll(v_pair, HEAD_DIM, 1)
    last_turn = pltpu.roll(value_sum[2], HEAD_DIM, 1)
    out_ref[here, 0:128] = k_pair.astype(bf16)
    out_ref[here, 128:256] = jnp.where(lane < HEAD_DIM, key_sum[2], v_turn).astype(bf16)
    out_ref[here, 256:384] = jnp.where(lane < HEAD_DIM, v_turn, last_turn).astype(bf16)


def attention_keys(bounds, pair, spans, q_pieces, g_pieces):
    block = pair.shape[0]
    count = len(q_pieces)
    return pl.pallas_call(
        functools.partial(key_kernel, count // 2),
        grid_spec=pltpu.PrefetchScalarGridSpec(
            num_scalar_prefetch=1,
            grid=(block // TILE_K,),
            in_specs=[whole_spec(x.shape) for x in (pair, spans)]
            + [pl.BlockSpec(memory_space=pl.ANY)] * (2 * count),
            out_specs=whole_spec((block, 384)),
            scratch_shapes=[
                pltpu.VMEM((count * block, 192), bf16),
                pltpu.VMEM((count * block, 256), bf16),
                pltpu.VMEM((3, TILE_K, 128), f32),
                pltpu.VMEM((3, TILE_K, 128), f32),
                pltpu.SemaphoreType.DMA((2, count)),
            ],
        ),
        out_shape=jax.ShapeDtypeStruct((block, 384), bf16),
        compiler_params=pltpu.CompilerParams(vmem_limit_bytes=40 * 2**20),
        cost_estimate=pl.CostEstimate(
            flops=8 * block * 2304 * 192, bytes_accessed=8 * 2**20, transcendentals=block * 2304 * 3
        ),
        name="attention_keys",
    )(bounds, pair, spans, *q_pieces, *g_pieces)


def projection_kernel(place_ref, own, near, far, corner, w_own, w_near, w_far, w_corner, bias_ref, *rest):
    tokens_ref, query_ref, pair_ref, weight, sem = rest
    rows, part = own.shape[0], w_own.shape[0]
    pieces = (w_own, w_near, w_far, w_corner)
    copies = []
    for r, piece in enumerate(pieces):
        where = pl.multiple_of(place_ref[r] * part, part)
        copies.append(pltpu.make_async_copy(piece, weight.at[pl.ds(where, part), :], sem.at[r]))
        copies[-1].start()
    for copy in copies:
        copy.wait()
    for r, piece in enumerate((own, near, far, corner)):
        here = pl.ds(pl.multiple_of(place_ref[r] * rows, rows), rows)
        tile = piece[...]
        tokens_ref[here, :] = tile
        made = rows_nn(tile, weight[...]) + bias_ref[0:1, :]
        pair_ref[here, :] = made[:, : 2 * part].astype(bf16)
        query_ref[here, :] = (made[:, 2 * part :].astype(bf16).astype(f32) * 0.125).astype(bf16)


def project(places, token_pieces, weight_pieces, bias):
    rows, width = token_pieces[0].shape
    part = weight_pieces[0].shape[0]
    block = rows * len(token_pieces)
    vmem = pl.BlockSpec(memory_space=pltpu.VMEM)
    return pl.pallas_call(
        projection_kernel,
        in_specs=[pl.BlockSpec(memory_space=pltpu.SMEM)]
        + [vmem] * 4
        + [pl.BlockSpec(memory_space=pl.ANY)] * 4
        + [vmem],
        out_specs=[vmem] * 3,
        out_shape=[
            jax.ShapeDtypeStruct((block, width), bf16),
            jax.ShapeDtypeStruct((block, part), bf16),
            jax.ShapeDtypeStruct((block, 2 * part), bf16),
        ],
        scratch_shapes=[pltpu.VMEM((width, 3 * part), bf16), pltpu.SemaphoreType.DMA((4,))],
        compiler_params=pltpu.CompilerParams(vmem_limit_bytes=32 * 2**20),
        cost_estimate=pl.CostEstimate(
            flops=2 * block * width * 3 * part, bytes_accessed=5 * 2**20, transcendentals=0
        ),
        name="layer_projection",
    )(places, *token_pieces, *weight_pieces, bias)


def normal_of(values):
    center = values - jnp.mean(values, axis=1, keepdims=True)
    inverse = lax.rsqrt(jnp.mean(center * center, axis=1, keepdims=True) + epsilon)
    return center * inverse, inverse


def normal_back(upstream, normal, inverse, gain):
    scaled = upstream * gain
    mean_scaled = jnp.mean(scaled, axis=1, keepdims=True)
    mean_product = jnp.mean(scaled * normal, axis=1, keepdims=True)
    return (scaled - mean_scaled - normal * mean_product) * inverse


def rows_tn(left, right):
    return lax.dot_general(left, right, (((0,), (0,)), ((), ())), preferred_element_type=f32)


def dense_kernel(place_ref, *refs):
    mixed = refs[0:4]
    tokens_ref, up_ref = refs[4:6]
    packs = refs[6:10]
    out_ref, grad_ref = refs[10:12]
    back_refs = refs[12:16]
    outer_refs, inner_refs = refs[16:18], refs[18:20]
    w_out, w_inner, w_outer, hidden, activated, slopes = refs[20:26]
    outer_made, inner_made, tail_made, lines, bias_rows, sem, sent = refs[26:]
    rows, width = tokens_ref.shape
    groups = w_inner.shape[0]
    part = width // groups

    def inner_copies(g):
        return [
            pltpu.make_async_copy(
                packs[r].at[pl.ds(pl.multiple_of(width + part + 16 + g * part, 16), part), :],
                w_inner.at[g, pl.ds(pl.multiple_of(place_ref[r] * part, part), part), :],
                sem.at[1 + g, r],
            )
            for r in range(groups)
        ]

    out_copies = [
        pltpu.make_async_copy(packs[r].at[pl.ds(width, part), :], w_out.at[r], sem.at[0, r])
        for r in range(groups)
    ]
    outer_copies = [
        pltpu.make_async_copy(
            packs[r].at[pl.ds(0, width), :], w_outer.at[place_ref[r]], sem.at[1 + groups, r]
        )
        for r in range(groups)
    ]
    line_copies = [
        pltpu.make_async_copy(
            packs[r].at[pl.ds(width + part, 16), :], lines.at[place_ref[r]], sem.at[2 + groups, r]
        )
        for r in range(groups)
    ]
    for copy in line_copies + out_copies + [x for g in range(groups) for x in inner_copies(g)] + outer_copies:
        copy.start()

    for copy in line_copies:
        copy.wait()
    small = [lines[k][:, 0:part].astype(f32) for k in range(groups)]
    out_bias, gain_one, shift_one, outer_bias, gain_two, shift_two = (
        jnp.concatenate([x[i : i + 1] for x in small], axis=1) for i in range(6)
    )
    for k in range(groups):
        bias_rows[k : k + 1, :] = jnp.concatenate(
            [small[k][6 + i : 7 + i] for i in range(groups)], axis=1
        )
    for copy in out_copies:
        copy.wait()
    residual = tokens_ref[...].astype(f32) + out_bias
    for r in range(groups):
        residual = residual + rows_nn(mixed[r][...], w_out[r])
    normal_one, inverse_one = normal_of(residual)
    first = normal_one * gain_one + shift_one
    first_low = first.astype(bf16)

    def ahead(g, carry):
        for copy in inner_copies(g):
            copy.wait()
        value = rows_nn(first_low, w_inner[g]) + bias_rows[pl.ds(g, 1), :]
        chance = 0.5 * (1.0 + lax.erf(value * (2.0**-0.5)))
        density = jnp.exp(-0.5 * value * value) * (2.0 * jnp.pi) ** -0.5
        slopes[g] = chance + value * density
        activated[g] = (value * chance).astype(bf16)
        return carry

    lax.fori_loop(0, groups, ahead, 0)
    for copy in outer_copies:
        copy.wait()

    def combine(g, total):
        return total + rows_nn(activated[g], w_outer[g])

    residual = lax.fori_loop(0, groups, combine, first + outer_bias)
    normal_two, inverse_two = normal_of(residual)
    out_ref[...] = (normal_two * gain_two + shift_two).astype(bf16)
    upstream = up_ref[...].astype(f32)
    grad_two = normal_back(upstream, normal_two, inverse_two, gain_two)
    grad_two_low = grad_two.astype(bf16)
    shift_two_sum = jnp.sum(upstream, axis=0, keepdims=True)
    gain_two_sum = jnp.sum(upstream * normal_two, axis=0, keepdims=True)
    outer_bias_sum = jnp.sum(grad_two_low.astype(f32), axis=0, keepdims=True)

    def outer_copy(i, odd):
        r = 2 * i + odd
        return pltpu.make_async_copy(outer_made.at[r], outer_refs[odd].at[i], sent.at[0, r])

    def behind(i, total):
        for odd in range(2):
            g = place_ref[2 * i + odd]
            outer_made[2 * i + odd] = rows_tn(activated[g], grad_two_low).astype(bf16)
            outer_copy(i, odd).start()
            value = (rows_nt(grad_two_low, w_outer[g]) * slopes[g]).astype(bf16)
            hidden[g] = value
            total = total + rows_nt(value, w_inner[g])
        return total

    grad_first = lax.fori_loop(0, groups // 2, behind, grad_two)
    grad_one = normal_back(grad_first, normal_one, inverse_one, gain_one)
    grad_ref[...] = grad_one
    grad_one_low = grad_one.astype(bf16)
    for r in range(groups):
        back_refs[r][...] = rows_nt(grad_one_low, w_out[r]).astype(bf16)

    def inner_sends(g):
        return [
            pltpu.make_async_copy(
                inner_made.at[g, pl.ds(pl.multiple_of(place_ref[r] * part, part), part), :],
                inner_refs[r % 2].at[r // 2, pl.ds(pl.multiple_of(g * part, part), part), :],
                sent.at[1 + g, r],
            )
            for r in range(groups)
        ]

    def weigh(g, carry):
        inner_made[g] = rows_tn(first_low, hidden[g]).astype(bf16)
        for copy in inner_sends(g):
            copy.start()
        return carry

    lax.fori_loop(0, groups, weigh, 0)
    sums = [
        jnp.sum(grad_one_low.astype(f32), axis=0, keepdims=True),
        jnp.sum(grad_first * normal_one, axis=0, keepdims=True),
        jnp.sum(grad_first, axis=0, keepdims=True),
        outer_bias_sum,
        gain_two_sum,
        shift_two_sum,
    ]
    line = lax.broadcasted_iota(jnp.int32, (16, part), 0)
    tail_made[:, part:, :] = jnp.zeros((groups, 64, width), bf16)
    for r in range(groups):
        tail_made[r, 0:part, :] = rows_tn(mixed[r][...], grad_one_low).astype(bf16)
    for k in range(groups):
        tail = jnp.zeros((16, part), f32)
        for i, line_sum in enumerate(sums):
            tail = jnp.where(line == i, line_sum[:, k * part : (k + 1) * part], tail)
        bias_sum = jnp.sum(hidden[k].astype(f32), axis=0, keepdims=True)
        for i in range(groups):
            tail = jnp.where(
                line == len(sums) + i, bias_sum[:, i * part : (i + 1) * part], tail
            )
        tail_made[place_ref[k], part : part + 16, 0:part] = tail.astype(bf16)
    tail_copies = [
        pltpu.make_async_copy(
            tail_made.at[r], inner_refs[r % 2].at[r // 2, pl.ds(width, part + 64), :], sent.at[1 + groups, r]
        )
        for r in range(groups)
    ]
    for copy in tail_copies:
        copy.start()
    for i in range(groups // 2):
        for odd in range(2):
            outer_copy(i, odd).wait()
    for g in range(groups):
        for copy in inner_sends(g):
            copy.wait()
    for copy in tail_copies:
        copy.wait()


def dense(places, mixed_pieces, tokens, cotangent, packs):
    rows, width = tokens.shape
    groups = len(packs)
    part = width // groups
    vmem = pl.BlockSpec(memory_space=pltpu.VMEM)
    hbm = pl.BlockSpec(memory_space=pl.ANY)
    return pl.pallas_call(
        dense_kernel,
        in_specs=[pl.BlockSpec(memory_space=pltpu.SMEM)] + [vmem] * (groups + 2) + [hbm] * groups,
        out_specs=[vmem] * (2 + groups) + [hbm] * 4,
        out_shape=[
            jax.ShapeDtypeStruct((rows, width), bf16),
            jax.ShapeDtypeStruct((rows, width), f32),
        ]
        + [jax.ShapeDtypeStruct((rows, part), bf16)] * groups
        + [jax.ShapeDtypeStruct((groups // 2, width, width), bf16)] * 2
        + [jax.ShapeDtypeStruct((groups // 2, width + part + 64, width), bf16)] * 2,
        scratch_shapes=[
            pltpu.VMEM((groups, part, width), bf16),
            pltpu.VMEM((groups, width, width), bf16),
            pltpu.VMEM((groups, width, width), bf16),
            pltpu.VMEM((groups, rows, width), bf16),
            pltpu.VMEM((groups, rows, width), bf16),
            pltpu.VMEM((groups, rows, width), f32),
            pltpu.VMEM((groups, width, width), bf16),
            pltpu.VMEM((groups, width, width), bf16),
            pltpu.VMEM((groups, part + 64, width), bf16),
            pltpu.VMEM((groups, 16, width), bf16),
            pltpu.VMEM((8, width), f32),
            pltpu.SemaphoreType.DMA((groups + 3, groups)),
            pltpu.SemaphoreType.DMA((groups + 2, groups)),
        ],
        compiler_params=pltpu.CompilerParams(vmem_limit_bytes=48 * 2**20),
        cost_estimate=pl.CostEstimate(
            flops=24 * rows * width * width * groups,
            bytes_accessed=24 * 2**20,
            transcendentals=2 * rows * width * groups,
        ),
        name="layer_dense",
    )(places, *mixed_pieces, tokens, cotangent, *packs)


def gather_kernel(place_ref, p0, p1, p2, p3, wide_ref, stat_ref, out_ref):
    rows, part = p0.shape
    lane = lax.broadcasted_iota(jnp.int32, (rows, 128), 1)
    slot = lax.broadcasted_iota(jnp.int32, (rows, HEAD_DIM), 1)
    for r, piece in enumerate((p0, p1, p2, p3)):
        here = pl.ds(pl.multiple_of(place_ref[r] * rows, rows), rows)
        tile = piece[...]
        product = tile.astype(f32) * wide_ref[here, :]
        pair, last = product[:, 0:128], product[:, 128:192]
        values = [stat_ref[here, h : h + 1] for h in range(3)] + [
            jnp.sum(jnp.where(lane < HEAD_DIM, pair, 0.0), axis=1, keepdims=True),
            jnp.sum(jnp.where(lane < HEAD_DIM, 0.0, pair), axis=1, keepdims=True),
            jnp.sum(last, axis=1, keepdims=True),
        ]
        tail = jnp.zeros((rows, HEAD_DIM), f32)
        for i, left in enumerate(values):
            for j in range(3):
                high = left.astype(bf16).astype(f32)
                tail = jnp.where(slot == 3 * i + j, high, tail)
                left = left - high
        out_ref[here, 0:192] = tile
        out_ref[here, 192:256] = tail.astype(bf16)


def gathered(places, pieces, wide, stats):
    block = wide.shape[0]
    vmem = pl.BlockSpec(memory_space=pltpu.VMEM)
    return pl.pallas_call(
        gather_kernel,
        in_specs=[pl.BlockSpec(memory_space=pltpu.SMEM)] + [vmem] * 6,
        out_specs=vmem,
        out_shape=jax.ShapeDtypeStruct((block, 256), bf16),
        compiler_params=pltpu.CompilerParams(vmem_limit_bytes=16 * 2**20),
        cost_estimate=pl.CostEstimate(flops=2**20, bytes_accessed=3 * 2**20, transcendentals=0),
        name="layer_gather",
    )(places, *pieces, wide, stats)


def heads_kernel(place_ref, tokens_ref, query_ref, pair_ref, w0, w1, w2, w3, grad_ref, back_ref, weight, sem):
    groups, part = grad_ref.shape[0], w0.shape[0]
    rows = back_ref.shape[1]
    copies = []
    for r, piece in enumerate((w0, w1, w2, w3)):
        where = pl.multiple_of(place_ref[r] * part, part)
        copies.append(pltpu.make_async_copy(piece, weight.at[pl.ds(where, part), :], sem.at[r]))
        copies[-1].start()
    tokens = tokens_ref[...]
    pair_grad = rows_tn(tokens, pair_ref[...]).astype(bf16)
    query_grad = rows_tn(tokens, query_ref[...]).astype(bf16)
    for k in range(groups):
        here = slice(k * part, (k + 1) * part)
        grad_ref[k, :, 0 : 2 * part] = pair_grad[here]
        grad_ref[k, :, 2 * part : 3 * part] = query_grad[here]
    ones = jnp.ones((tokens.shape[0], HEAD_DIM), bf16)
    query_sum = rows_tn(query_ref[...], ones)
    value_sum = rows_tn(pair_ref[:, part:], ones)
    lane = lax.broadcasted_iota(jnp.int32, (part, HEAD_DIM), 1)
    sums = jnp.where(lane == 0, query_sum, jnp.where(lane == 1, value_sum, 0.0))
    grad_ref[:, :, 3 * part : 3 * part + HEAD_DIM] = jnp.zeros((groups, part, HEAD_DIM), bf16)
    grad_ref[place_ref[0], :, 3 * part : 3 * part + HEAD_DIM] = sums.astype(bf16)
    for copy in copies:
        copy.wait()
    for k in range(groups):
        here = slice(k * rows, (k + 1) * rows)
        made = rows_nt(pair_ref[here, :], weight[:, : 2 * part])
        made = made + rows_nt(query_ref[here, :], weight[:, 2 * part :])
        back_ref[place_ref[k]] = made.astype(bf16)


def head_grads(places, tokens, grad_query, grad_pair, weight_pieces):
    block, width = tokens.shape
    groups, part = len(weight_pieces), weight_pieces[0].shape[0]
    vmem = pl.BlockSpec(memory_space=pltpu.VMEM)
    return pl.pallas_call(
        heads_kernel,
        in_specs=[pl.BlockSpec(memory_space=pltpu.SMEM)]
        + [vmem] * 3
        + [pl.BlockSpec(memory_space=pl.ANY)] * groups,
        out_specs=[vmem] * 2,
        out_shape=[
            jax.ShapeDtypeStruct((groups, part, 3 * part + HEAD_DIM), bf16),
            jax.ShapeDtypeStruct((groups, block // groups, width), bf16),
        ],
        scratch_shapes=[pltpu.VMEM((width, 3 * part), bf16), pltpu.SemaphoreType.DMA((groups,))],
        compiler_params=pltpu.CompilerParams(vmem_limit_bytes=32 * 2**20),
        cost_estimate=pl.CostEstimate(
            flops=4 * block * width * 3 * part, bytes_accessed=8 * 2**20, transcendentals=0
        ),
        name="layer_heads",
    )(places, tokens, grad_query, grad_pair, *weight_pieces)


def both(left, right):
    return (left.astype(f32) + right.astype(f32)).astype(bf16)


def half_of(block, bit, axis):
    size = block.shape[axis] // 2
    return lax.dynamic_slice_in_dim(block, bit * size, size, axis)


def scatter_sum(terms, axis_name, order, axis):
    index = lax.axis_index(axis_name)
    for step in order:
        bit = (index // step) % 2
        sent = functools.reduce(both, [half_of(x, 1 - bit, axis) for x in terms])
        kept = functools.reduce(both, [half_of(x, bit, axis) for x in terms])
        terms = [kept, swapped(sent, axis_name, step)]
    return terms


def gather_back(block, axis_name, order, axis):
    index = lax.axis_index(axis_name)
    for step in reversed(order):
        other = swapped(block, axis_name, step)
        late = (index // step) % 2 == 1
        block = jnp.where(
            late,
            jnp.concatenate([other, block], axis),
            jnp.concatenate([block, other], axis),
        )
    return block


def on_device(
    tokens,
    doc_start,
    cotangent,
    query_weight,
    key_weight,
    value_weight,
    out_weight,
    query_bias,
    value_bias,
    out_bias,
    first_gain,
    first_shift,
    inner_weight,
    inner_bias,
    outer_weight,
    outer_bias,
    second_gain,
    second_shift,
):
    rows, width = tokens.shape
    cycle = lax.axis_size("ctx")
    shards = lax.axis_size("wt")
    block = rows * shards
    reach = (MAXDOC + block - 2) // block
    window = (2 * reach + 1) * block
    c = lax.axis_index("ctx")
    w = lax.axis_index("wt")
    part = width // shards
    places = jnp.stack([w ^ r for r in range(shards)]).astype(jnp.int32)

    def spread(own, near):
        far = swapped(own, "wt", 2)
        return [own, near, far, swapped(far, "wt", 1)]

    def columns(r):
        start = (w ^ r) * part
        return jnp.concatenate(
            [
                lax.dynamic_slice_in_dim(x, start, part, 1)
                for x in (key_weight, value_weight, query_weight)
            ],
            axis=1,
        )

    token_pieces = spread(tokens, swapped(tokens, "wt", 1))
    weight_pieces = [columns(0)] + [swapped(columns(r), "wt", r) for r in range(1, shards)]
    head_bias = jnp.concatenate([jnp.zeros((part,), f32), value_bias.astype(f32), query_bias.astype(f32)])
    head_bias = jnp.broadcast_to(head_bias[None], (8, 3 * part))

    pad = reach * block
    padded = jnp.pad(doc_start, (pad, pad), constant_values=-1)
    base = c * block - pad
    marks = lax.dynamic_slice_in_dim(padded, c * block, window)
    place = jnp.arange(window, dtype=jnp.int32)
    begins = jnp.where((marks == base + place) | (marks < 0), place, window)
    next_begin = lax.cummin(begins, axis=0, reverse=True)
    stops = jnp.concatenate([next_begin[1:], jnp.full((1,), window, jnp.int32)])
    starts = marks - base
    own_starts = starts[pad : pad + block]
    own_stops = stops[pad : pad + block]
    spans_row = jnp.stack([starts, stops] + [jnp.zeros_like(starts)] * 6)
    spans = spans_row[:, pad : pad + block]
    lowest = own_starts.reshape(-1, TILE_Q)[:, 0] // 128 * 128
    highest = own_stops.reshape(-1, TILE_Q)[:, -1]
    count = (highest - lowest + SPAN_K - 1) // SPAN_K
    lowest = jnp.minimum(lowest, (window - count * SPAN_K) // 128 * 128)
    reached = jnp.stack([jnp.min(lowest) // 256, (jnp.max(lowest + count * SPAN_K) + 255) // 256])
    bounds = jnp.concatenate([jnp.stack([lowest, count], axis=1).reshape(-1), reached])

    block_tokens, queries, pair = project(places, token_pieces, weight_pieces, head_bias)

    distances = [d for d in range(reach, -reach - 1, -1)]

    def halo(own):
        return [own if d == 0 else shifted(own, "ctx", d) for d in distances]

    even = c % 2 == 0
    beside_at = jnp.where(even, reach + 1, reach - 1) * block
    missing_at = jnp.where(even, reach - 1, reach + 1) * block
    load_at = jnp.stack(
        [0 * missing_at, 2 * reach * block + 0 * missing_at, reach * block + 0 * missing_at]
        + [beside_at, missing_at, missing_at + block // 2]
    )
    bounds = jnp.concatenate([bounds, load_at, places]).astype(jnp.int32)
    beside = swapped(pair, "ctx", 1)
    before, after = shifted(pair, "ctx", 2), shifted(pair, "ctx", -2)
    half = block // 2
    before, after, bounds, spans, spans_row = lax.optimization_barrier(
        (before, after, bounds, spans, spans_row)
    )
    route = [(i, i + 2 if i % 2 == 0 else i - 2) for i in range(cycle)]
    route = [(i, j) for i, j in route if 0 <= j < cycle]
    upper = swapped(jnp.where(even, after[:half], before[:half]), "ctx", 1)
    lower = lax.ppermute(beside[half:], "ctx", route)
    pairs = [before, after, pair, beside, upper, lower]
    small_own = jnp.stack(
        [out_bias, first_gain, first_shift, outer_bias, second_gain, second_shift]
    )
    small_own = jnp.concatenate([small_own, inner_bias.reshape(-1, part)], axis=0)
    small_own = jnp.pad(small_own, ((0, 16 - small_own.shape[0]), (0, width - part)))
    inner_parts = [inner_weight[:, i * width : (i + 1) * width] for i in range(shards)]
    pack = jnp.concatenate([outer_weight, out_weight, small_own] + inner_parts, axis=0)
    pack, _ = lax.optimization_barrier((pack, token_pieces[2:] + weight_pieces[1:]))
    pack_near, pack_far = swapped(pack, "wt", 1), swapped(pack, "wt", 2)
    *mixed_pieces, mixed_wide, stat_rows, stat_columns = attention_forward(
        bounds, queries, spans, pairs
    )
    ready, _ = lax.optimization_barrier((queries, pairs))
    query_halo = [queries if d == 0 else shifted(ready, "ctx", d) if d * d == 1 else None for d in distances]
    close = [x for x, d in zip(query_halo, distances) if d * d == 1]
    mixed_pieces, mixed_wide, stat_columns, close, pack_far = lax.optimization_barrier(
        (mixed_pieces, mixed_wide, stat_columns, close, pack_far)
    )
    packs = [pack, pack_near, pack_far, swapped(pack_far, "wt", 1)]

    mixed_pieces = [mixed_pieces[0]] + [
        swapped(mixed_pieces[r], "wt", r) for r in range(1, shards)
    ]
    far_ready, mixed_pieces = lax.optimization_barrier((queries, mixed_pieces))
    results = dense(
        places, mixed_pieces, tokens, cotangent, packs
    )
    remote = [shifted(far_ready, "ctx", d) for d in distances if d * d > 1]
    results, remote = lax.optimization_barrier((results, remote))
    layer_out, grad_one, *back = results[: 2 + shards]
    outer_keep, outer_send, inner_keep, inner_send = results[2 + shards :]
    query_halo = [remote[0], close[0], queries, close[1], remote[1]]

    back_pieces = [back[0]] + [swapped(back[r], "wt", r) for r in range(1, shards)]
    outer_got = swapped(outer_send, "wt", 1)
    inner_got = swapped(inner_send, "wt", 1)
    grads = gathered(places, back_pieces, mixed_wide, stat_columns)
    outer_got, _ = lax.optimization_barrier((outer_got, back_pieces[1:]))
    grads, inner_got = lax.optimization_barrier((grads, inner_got))

    def far_terms(keep, got):
        return [both(keep[0], got[0]), swapped(both(keep[1], got[1]), "wt", 2)]

    grad_halo = halo(grads)
    outer_terms = far_terms(outer_keep, outer_got)
    grad_query = attention_queries(
        bounds, queries, spans, grads, mixed_wide, stat_rows, pairs
    )
    grad_query, grad_halo, outer_terms, inner_keep, inner_got = lax.optimization_barrier(
        (grad_query, grad_halo, outer_terms, inner_keep, inner_got)
    )

    near_first = [1 << i for i in range(cycle.bit_length() - 1)]
    outer_terms = scatter_sum(outer_terms, "ctx", near_first[:1], 0)
    inner_terms = far_terms(inner_keep, inner_got)
    grad_pair = attention_keys(bounds, pair, spans_row, query_halo, grad_halo)
    grad_pair, outer_terms, inner_terms = lax.optimization_barrier(
        (grad_pair, outer_terms, inner_terms)
    )

    head_grad, token_partial = head_grads(places, block_tokens, grad_query, grad_pair, weight_pieces)
    outer_part = both(*scatter_sum(outer_terms, "ctx", near_first[1:], 0))
    inner_part = both(*scatter_sum(inner_terms, "ctx", near_first, 0))
    head_part = both(*scatter_sum([head_grad], "ctx", near_first, 1))
    token_got = swapped(token_partial[1::2], "wt", 1)
    token_sum = both(*far_terms(token_partial[0::2], token_got))
    outer_total = gather_back(outer_part, "ctx", near_first, 0)
    inner_total = gather_back(inner_part, "ctx", near_first, 0)
    head_pieces = [
        lax.dynamic_index_in_dim(head_part, w ^ r, 0, keepdims=False) for r in range(shards)
    ]
    head_pieces = [head_pieces[0]] + [swapped(head_pieces[r], "wt", r) for r in range(1, shards)]
    head_parts = jnp.stack(
        [
            lax.dynamic_index_in_dim(jnp.stack(head_pieces), w ^ k, 0, keepdims=False)
            for k in range(shards)
        ]
    )
    head_total = gather_back(head_parts, "ctx", near_first, 1)

    tokens_gradient = grad_one + token_sum.astype(f32)
    key_total, value_total, query_total = (
        jnp.concatenate(
            [head_total[k, :, i * part : (i + 1) * part] for k in range(shards)], axis=1
        ).astype(f32)
        for i in range(3)
    )
    own_total = lax.dynamic_index_in_dim(head_total, w, 0, keepdims=False)
    inner_rows = inner_total[:width].reshape(shards, part, width)
    inner_rows = jnp.concatenate([inner_rows[k] for k in range(shards)], axis=1).astype(f32)
    lines = inner_total[width + part : width + part + 16, :part].astype(f32)

    return (
        layer_out,
        tokens_gradient,
        query_total,
        key_total,
        value_total,
        inner_total[width : width + part].astype(f32),
        own_total[:, 3 * part].astype(f32),
        own_total[:, 3 * part + 1].astype(f32),
        lines[0],
        lines[1],
        lines[2],
        inner_rows,
        lines[6:10].reshape(-1),
        outer_total.astype(f32),
        lines[3],
        lines[4],
        lines[5],
    )


def solution(mesh):
    matrix, vector = P("wt", None), P("wt")
    stream = P(("ctx", "wt"), None)
    in_specs = (stream, P(), stream) + (matrix,) * 4 + (vector,) * 5
    in_specs += (matrix, vector, matrix, vector, vector, vector)
    out_specs = (stream, stream) + (matrix,) * 4 + (vector,) * 5
    out_specs += (matrix, vector, matrix, vector, vector, vector)
    return jax.shard_map(
        on_device, mesh=mesh, in_specs=in_specs, out_specs=out_specs, check_vma=False
    )
```

```python
import functools

import jax
import jax.numpy as jnp
from jax import lax
from jax.experimental import pallas as pl
from jax.experimental.pallas import tpu as pltpu
from jax.sharding import PartitionSpec as P

HEADS = 12
HEAD_DIM = 64
MAXDOC = 2048
TILE_Q = 256
SPAN_K = 768
TILE_K = 256
SPAN_Q = 768
CHUNK = 256

masked_score = -1e30
epsilon = 1e-06
bf16 = jnp.bfloat16
f32 = jnp.float32


def swapped(block, axis, bit):
    count = lax.axis_size(axis)
    return lax.ppermute(block, axis, [(i, i ^ bit) for i in range(count)])


def shifted(block, axis, distance):
    count = lax.axis_size(axis)
    route = [(i, i + distance) for i in range(count) if 0 <= i + distance < count]
    return lax.ppermute(block, axis, route)


def rows_nt(left, right):
    return lax.dot_general(left, right, (((1,), (1,)), ((), ())), preferred_element_type=f32)


def rows_nn(left, right):
    return lax.dot_general(left, right, (((1,), (0,)), ((), ())), preferred_element_type=f32)


def load_window(pieces, target, sem, starts):
    copies = []
    for i, piece in enumerate(pieces):
        rows = pl.ds(pl.multiple_of(starts[i], 128), piece.shape[0])
        copies.append(pltpu.make_async_copy(piece, target.at[rows, :], sem.at[i]))
    for copy in copies:
        copy.start()
    return copies


def head_of(tile0, tile1, head):
    lane = lax.broadcasted_iota(jnp.int32, tile0.shape, 1)
    if head == 0:
        return jnp.where(lane < HEAD_DIM, tile0, jnp.zeros_like(tile0))
    if head == 1:
        return jnp.where(lane >= HEAD_DIM, tile0, jnp.zeros_like(tile0))
    return tile1


def turned(source, target, lanes, low, high):
    def turn(i, carry):
        rows = pl.ds(pl.multiple_of(i * 256, 256), 256)
        target[:, rows] = source[rows, lanes].T
        return carry

    lax.fori_loop(low, high, turn, 0)


def inside(span_ref, first, begin, rows):
    own = pl.ds(first, TILE_Q)
    place = begin + lax.broadcasted_iota(jnp.int32, (rows, TILE_Q), 0)
    return (place >= span_ref[0:1, own]) & (place < span_ref[1:2, own])


def forward_kernel(bounds, q_ref, span_ref, *rest):
    pieces, rest = rest[:-10], rest[-10:]
    outs, (wide_ref, row_ref, stat_ref, kv, vt, sem) = rest[:4], rest[4:]
    step = pl.program_id(0)

    @pl.when(step == 0)
    def _():
        for copy in load_window(pieces, kv, sem, [bounds[10 + i] for i in range(len(pieces))]):
            copy.wait()
        turned(kv, vt, slice(192, 384), bounds[8], bounds[9])

    first = pl.multiple_of(step * TILE_Q, TILE_Q)
    here = pl.ds(first, TILE_Q)
    q_tile = q_ref[here, :]
    heads = [head_of(q_tile[:, :128], q_tile[:, 128:], h) for h in range(3)]
    lower, count = bounds[2 * step], bounds[2 * step + 1]

    def run(i, carry):
        begin = pl.multiple_of(lower + i * SPAN_K, 128)
        rows = pl.ds(begin, SPAN_K)
        allowed = inside(span_ref, first, begin, SPAN_K)
        after = []

        def ahead(h):
            score = rows_nt(kv[rows, 0:128] if h < 2 else kv[rows, 128:192], heads[h])
            return jnp.where(allowed, score, masked_score)

        coming = ahead(0)
        for h in range(3):
            score = coming
            if h < 2:
                coming = ahead(h + 1)
            before, total, accum = carry[3 * h : 3 * h + 3]
            newest = jnp.maximum(before, jnp.max(score, axis=0, keepdims=True))
            factor = jnp.exp(before - newest)
            weight = jnp.exp(score - newest)
            total = total * factor + jnp.sum(weight, axis=0, keepdims=True)
            made = rows_nn(vt[h * HEAD_DIM : (h + 1) * HEAD_DIM, rows], weight.astype(bf16))
            after += [newest, total, accum * factor + made]
        return tuple(after)

    start = (
        jnp.full((1, TILE_Q), masked_score, f32),
        jnp.zeros((1, TILE_Q), f32),
        jnp.zeros((HEAD_DIM, TILE_Q), f32),
    )
    state = lax.fori_loop(0, count, run, start * 3)
    mixed = jnp.concatenate([state[3 * h + 2] / state[3 * h + 1] for h in range(3)], axis=0).T
    line = lax.broadcasted_iota(jnp.int32, (128, TILE_Q), 0)
    stats = jnp.zeros((128, TILE_Q), f32)
    for h in range(3):
        stats = jnp.where(line == h, state[3 * h] + jnp.log(state[3 * h + 1]), stats)
    wide_ref[here, :] = mixed
    row_ref[:, here] = stats[0:8, :]
    stat_ref[here, :] = stats.T
    low = mixed.astype(bf16)
    for r, out_ref in enumerate(outs):

        @pl.when(bounds[16 + step] == r)
        def _(out_ref=out_ref):
            out_ref[...] = low


def whole_spec(shape):
    return pl.BlockSpec(shape, lambda i, *_: (0,) * len(shape))


def attention_forward(bounds, queries, spans, pieces):
    block = queries.shape[0]
    window = sum(x.shape[0] for x in pieces)
    return pl.pallas_call(
        forward_kernel,
        grid_spec=pltpu.PrefetchScalarGridSpec(
            num_scalar_prefetch=1,
            grid=(block // TILE_Q,),
            in_specs=[whole_spec(queries.shape), whole_spec(spans.shape)]
            + [pl.BlockSpec(memory_space=pl.ANY)] * len(pieces),
            out_specs=[whole_spec((TILE_Q, 192))] * 4
            + [whole_spec((block, 192)), whole_spec((8, block)), whole_spec((block, 128))],
            scratch_shapes=[
                pltpu.VMEM((window, 384), bf16),
                pltpu.VMEM((192, window), bf16),
                pltpu.SemaphoreType.DMA((len(pieces),)),
            ],
        ),
        out_shape=[jax.ShapeDtypeStruct((TILE_Q, 192), bf16)] * 4
        + [
            jax.ShapeDtypeStruct((block, 192), f32),
            jax.ShapeDtypeStruct((8, block), f32),
            jax.ShapeDtypeStruct((block, 128), f32),
        ],
        compiler_params=pltpu.CompilerParams(vmem_limit_bytes=60 * 2**20),
        cost_estimate=pl.CostEstimate(
            flops=4 * block * 2304 * 192, bytes_accessed=6 * 2**20, transcendentals=block * 2304 * 3
        ),
        name="attention_forward",
    )(bounds, queries, spans, *pieces)


def query_kernel(bounds, q_ref, span_ref, grad_ref, wide_ref, row_ref, *rest):
    pieces, (out_ref, kv, kt, sem) = rest[:-4], rest[-4:]
    step = pl.program_id(0)

    @pl.when(step == 0)
    def _():
        for copy in load_window(pieces, kv, sem, [bounds[10 + i] for i in range(len(pieces))]):
            copy.wait()
        turned(kv, kt, slice(0, 192), bounds[8], bounds[9])

    first = pl.multiple_of(step * TILE_Q, TILE_Q)
    here = pl.ds(first, TILE_Q)
    q_tile = q_ref[here, :]
    heads = [head_of(q_tile[:, :128], q_tile[:, 128:], h) for h in range(3)]
    g_tile = grad_ref[here, :]
    lane = lax.broadcasted_iota(jnp.int32, (TILE_Q, 128), 1)
    none = jnp.zeros((TILE_Q, 128), bf16)
    r_pair = pltpu.roll(g_tile[:, :128].astype(f32), HEAD_DIM, 1).astype(bf16)
    r_last = pltpu.roll(g_tile[:, 128:256].astype(f32), HEAD_DIM, 1).astype(bf16)
    grads = [
        jnp.where(lane >= HEAD_DIM, r_pair, none),
        jnp.where(lane < HEAD_DIM, r_pair, none),
        jnp.where(lane >= HEAD_DIM, r_last, none),
    ]
    product = (g_tile[:, 0:192].astype(f32) * wide_ref[here, :]).T
    deltas = [
        jnp.sum(product[h * HEAD_DIM : (h + 1) * HEAD_DIM], axis=0, keepdims=True) for h in range(3)
    ]
    logs = [row_ref[h : h + 1, here] for h in range(3)]
    lower, count = bounds[2 * step], bounds[2 * step + 1]

    def run(i, carry):
        begin = pl.multiple_of(lower + i * SPAN_K, 128)
        rows = pl.ds(begin, SPAN_K)
        allowed = inside(span_ref, first, begin, SPAN_K)
        after = []

        def ahead(h):
            score = rows_nt(kv[rows, 0:128] if h < 2 else kv[rows, 128:192], heads[h])
            return score, rows_nt(kv[rows, 128:256] if h == 0 else kv[rows, 256:384], grads[h])

        coming = ahead(0)
        for h in range(3):
            score, back = coming
            if h < 2:
                coming = ahead(h + 1)
            chance = jnp.exp(jnp.where(allowed, score - logs[h], masked_score))
            change = (chance * (back - deltas[h])).astype(bf16)
            after.append(carry[h] + rows_nn(kt[h * HEAD_DIM : (h + 1) * HEAD_DIM, rows], change))
        return tuple(after)

    sums = lax.fori_loop(0, count, run, (jnp.zeros((HEAD_DIM, TILE_Q), f32),) * 3)
    out_ref[here, :] = (jnp.concatenate(sums, axis=0).T * 0.125).astype(bf16)


def attention_queries(bounds, queries, spans, grads, wide, stats, pieces):
    block = queries.shape[0]
    window = sum(x.shape[0] for x in pieces)
    return pl.pallas_call(
        query_kernel,
        grid_spec=pltpu.PrefetchScalarGridSpec(
            num_scalar_prefetch=1,
            grid=(block // TILE_Q,),
            in_specs=[whole_spec(x.shape) for x in (queries, spans, grads, wide, stats)]
            + [pl.BlockSpec(memory_space=pl.ANY)] * len(pieces),
            out_specs=whole_spec((block, 192)),
            scratch_shapes=[
                pltpu.VMEM((window, 384), bf16),
                pltpu.VMEM((192, window), bf16),
                pltpu.SemaphoreType.DMA((len(pieces),)),
            ],
        ),
        out_shape=jax.ShapeDtypeStruct((block, 192), bf16),
        compiler_params=pltpu.CompilerParams(vmem_limit_bytes=40 * 2**20),
        cost_estimate=pl.CostEstimate(
            flops=6 * block * 2304 * 192, bytes_accessed=6 * 2**20, transcendentals=block * 2304 * 3
        ),
        name="attention_queries",
    )(bounds, queries, spans, grads, wide, stats, *pieces)


def weight_copies(bounds, pieces, weight, sem):
    part = pieces[0].shape[0]
    copies = []
    for r, piece in enumerate(pieces):
        where = pl.ds(pl.multiple_of(bounds[16 + r] * part, part), part)
        copies.append(pltpu.make_async_copy(piece, weight.at[where, :], sem.at[r]))
    return copies


def head_terms(bounds, tokens_ref, query_ref, pair_ref, weight, grad_ref, back_ref):
    groups, part = grad_ref.shape[0], grad_ref.shape[1]
    rows = back_ref.shape[1]
    tokens = tokens_ref[...]
    pair_grad = rows_tn(tokens, pair_ref[...]).astype(bf16)
    query_grad = rows_tn(tokens, query_ref[...]).astype(bf16)
    for k in range(groups):
        here = slice(k * part, (k + 1) * part)
        grad_ref[k, :, 0 : 2 * part] = pair_grad[here]
        grad_ref[k, :, 2 * part : 3 * part] = query_grad[here]
    ones = jnp.ones((tokens.shape[0], HEAD_DIM), bf16)
    query_sum = rows_tn(query_ref[...], ones)
    value_sum = rows_tn(pair_ref[:, part:], ones)
    lane = lax.broadcasted_iota(jnp.int32, (part, HEAD_DIM), 1)
    sums = jnp.where(lane == 0, query_sum, jnp.where(lane == 1, value_sum, 0.0))
    grad_ref[:, :, 3 * part : 3 * part + HEAD_DIM] = jnp.zeros((groups, part, HEAD_DIM), bf16)
    grad_ref[bounds[16], :, 3 * part : 3 * part + HEAD_DIM] = sums.astype(bf16)
    for k in range(groups):
        here = slice(k * rows, (k + 1) * rows)
        made = rows_nt(pair_ref[here, :], weight[:, : 2 * part])
        made = made + rows_nt(query_ref[here, :], weight[:, 2 * part :])
        back_ref[bounds[16 + k]] = made.astype(bf16)


def key_kernel(reach, bounds, kv_ref, span_ref, tokens_ref, query_ref, *rest):
    window = 2 * reach + 1
    w_pieces, rest = rest[:4], rest[4:]
    q_pieces, g_pieces = rest[:window], rest[window : 2 * window]
    grad_ref, back_ref, qs, gs, key_sum, value_sum, out_ref, weight, sem, w_sem = rest[2 * window :]
    step = pl.program_id(0)
    block = q_pieces[0].shape[0]

    @pl.when(step == 0)
    def _():
        copies = load_window(q_pieces, qs, sem.at[0], [i * block for i in range(window)])
        copies += load_window(g_pieces, gs, sem.at[1], [i * block for i in range(window)])
        for copy in weight_copies(bounds, w_pieces, weight, w_sem):
            copy.start()
        for copy in copies:
            copy.wait()

    first = pl.multiple_of(step * TILE_K, TILE_K)
    here = pl.ds(first, TILE_K)
    key_sum[...] = jnp.zeros_like(key_sum)
    value_sum[...] = jnp.zeros_like(value_sum)
    keys_pair = kv_ref[here, 0:128]
    keys = [head_of(keys_pair, kv_ref[here, 128:192], h) for h in range(3)]
    lane = lax.broadcasted_iota(jnp.int32, (TILE_K, 128), 1)
    zero = jnp.zeros((TILE_K, 128), f32)
    v_one = pltpu.roll(kv_ref[here, 128:256].astype(f32), HEAD_DIM, 1)
    v_two = pltpu.roll(kv_ref[here, 256:384].astype(f32), HEAD_DIM, 1)
    values = [
        jnp.where(lane < HEAD_DIM, v_one, zero).astype(bf16),
        jnp.where(lane < HEAD_DIM, zero, v_two).astype(bf16),
        v_two.astype(bf16)[:, :HEAD_DIM],
    ]
    line = lax.broadcasted_iota(jnp.int32, (16, HEAD_DIM), 0)
    slot = lax.broadcasted_iota(jnp.int32, (16, HEAD_DIM), 1)
    selector = jnp.where((slot // 3 == line) & (slot < 18), 1.0, 0.0).astype(bf16)
    lower, count = bounds[2 * step], bounds[2 * step + 1]

    def run(i, carry):
        begin = pl.multiple_of(lower + i * SPAN_Q, 128)
        columns = pl.ds(begin, SPAN_Q)
        place = reach * block + first + lax.broadcasted_iota(jnp.int32, (TILE_K, SPAN_Q), 0)
        allowed = (place >= span_ref[0:1, columns]) & (place < span_ref[1:2, columns])
        lanes = [slice(0, 128), slice(0, 128), slice(128, 192)]
        stats = rows_nt(selector, gs[columns, 192:256])
        items = [(h, ch) for h in range(3) for ch in range(SPAN_Q // CHUNK)]

        def ahead(item):
            h, ch = item
            here = pl.ds(pl.multiple_of(begin + ch * CHUNK, 128), CHUNK)
            q_tile, g_tile = qs[here, lanes[h]], gs[here, lanes[h]]
            return q_tile, g_tile, rows_nt(keys[h], q_tile), rows_nt(values[h], g_tile)

        coming = ahead(items[0])
        for n, (h, ch) in enumerate(items):
            q_tile, g_tile, score, back = coming
            if n + 1 < len(items):
                coming = ahead(items[n + 1])
            cols = slice(ch * CHUNK, (ch + 1) * CHUNK)
            score = jnp.where(allowed[:, cols], score - stats[h : h + 1, cols], masked_score)
            chance = jnp.exp(score)
            change = (chance * (back - stats[h + 3 : h + 4, cols])).astype(bf16)
            size = 128 if h < 2 else HEAD_DIM
            key_sum[h, :, 0:size] += rows_nn(change, q_tile)
            value_sum[h, :, 0:size] += rows_nn(chance.astype(bf16), g_tile)
        return carry

    lax.fori_loop(0, count, run, 0)
    k_pair = jnp.where(lane < HEAD_DIM, key_sum[0], key_sum[1])
    v_pair = jnp.where(lane < HEAD_DIM, value_sum[0], value_sum[1])
    v_turn = pltpu.roll(v_pair, HEAD_DIM, 1)
    last_turn = pltpu.roll(value_sum[2], HEAD_DIM, 1)
    out_ref[here, 0:128] = k_pair.astype(bf16)
    out_ref[here, 128:256] = jnp.where(lane < HEAD_DIM, key_sum[2], v_turn).astype(bf16)
    out_ref[here, 256:384] = jnp.where(lane < HEAD_DIM, v_turn, last_turn).astype(bf16)

    @pl.when(step == pl.num_programs(0) - 1)
    def _():
        for copy in weight_copies(bounds, w_pieces, weight, w_sem):
            copy.wait()
        head_terms(bounds, tokens_ref, query_ref, out_ref, weight, grad_ref, back_ref)


def attention_keys(bounds, pair, spans, tokens, grad_query, weight_pieces, q_pieces, g_pieces):
    block, width = tokens.shape
    count = len(q_pieces)
    groups, part = len(weight_pieces), weight_pieces[0].shape[0]
    return pl.pallas_call(
        functools.partial(key_kernel, count // 2),
        grid_spec=pltpu.PrefetchScalarGridSpec(
            num_scalar_prefetch=1,
            grid=(block // TILE_K,),
            in_specs=[whole_spec(x.shape) for x in (pair, spans, tokens, grad_query)]
            + [pl.BlockSpec(memory_space=pl.ANY)] * (groups + 2 * count),
            out_specs=[
                whole_spec((groups, part, 3 * part + HEAD_DIM)),
                whole_spec((groups, block // groups, width)),
            ],
            scratch_shapes=[
                pltpu.VMEM((count * block, 192), bf16),
                pltpu.VMEM((count * block, 256), bf16),
                pltpu.VMEM((3, TILE_K, 128), f32),
                pltpu.VMEM((3, TILE_K, 128), f32),
                pltpu.VMEM((block, 384), bf16),
                pltpu.VMEM((width, 3 * part), bf16),
                pltpu.SemaphoreType.DMA((2, count)),
                pltpu.SemaphoreType.DMA((groups,)),
            ],
        ),
        out_shape=[
            jax.ShapeDtypeStruct((groups, part, 3 * part + HEAD_DIM), bf16),
            jax.ShapeDtypeStruct((groups, block // groups, width), bf16),
        ],
        compiler_params=pltpu.CompilerParams(vmem_limit_bytes=60 * 2**20),
        cost_estimate=pl.CostEstimate(
            flops=10 * block * 2304 * 192, bytes_accessed=12 * 2**20, transcendentals=block * 2304 * 3
        ),
        name="attention_keys",
    )(bounds, pair, spans, tokens, grad_query, *weight_pieces, *q_pieces, *g_pieces)


def projection_kernel(place_ref, own, near, far, corner, w_own, w_near, w_far, w_corner, bias_ref, *rest):
    tokens_ref, query_ref, pair_ref, weight, sem = rest
    rows, part = own.shape[0], w_own.shape[0]
    pieces = (w_own, w_near, w_far, w_corner)
    copies = []
    for r, piece in enumerate(pieces):
        where = pl.multiple_of(place_ref[r] * part, part)
        copies.append(pltpu.make_async_copy(piece, weight.at[pl.ds(where, part), :], sem.at[r]))
        copies[-1].start()
    for copy in copies:
        copy.wait()
    for r, piece in enumerate((own, near, far, corner)):
        here = pl.ds(pl.multiple_of(place_ref[r] * rows, rows), rows)
        tile = piece[...]
        tokens_ref[here, :] = tile
        made = rows_nn(tile, weight[...]) + bias_ref[0:1, :]
        pair_ref[here, :] = made[:, : 2 * part].astype(bf16)
        query_ref[here, :] = (made[:, 2 * part :].astype(bf16).astype(f32) * 0.125).astype(bf16)


def project(places, token_pieces, weight_pieces, bias):
    rows, width = token_pieces[0].shape
    part = weight_pieces[0].shape[0]
    block = rows * len(token_pieces)
    vmem = pl.BlockSpec(memory_space=pltpu.VMEM)
    return pl.pallas_call(
        projection_kernel,
        in_specs=[pl.BlockSpec(memory_space=pltpu.SMEM)]
        + [vmem] * 4
        + [pl.BlockSpec(memory_space=pl.ANY)] * 4
        + [vmem],
        out_specs=[vmem] * 3,
        out_shape=[
            jax.ShapeDtypeStruct((block, width), bf16),
            jax.ShapeDtypeStruct((block, part), bf16),
            jax.ShapeDtypeStruct((block, 2 * part), bf16),
        ],
        scratch_shapes=[pltpu.VMEM((width, 3 * part), bf16), pltpu.SemaphoreType.DMA((4,))],
        compiler_params=pltpu.CompilerParams(vmem_limit_bytes=32 * 2**20),
        cost_estimate=pl.CostEstimate(
            flops=2 * block * width * 3 * part, bytes_accessed=5 * 2**20, transcendentals=0
        ),
        name="layer_projection",
    )(places, *token_pieces, *weight_pieces, bias)


def normal_of(values):
    center = values - jnp.mean(values, axis=1, keepdims=True)
    inverse = lax.rsqrt(jnp.mean(center * center, axis=1, keepdims=True) + epsilon)
    return center * inverse, inverse


def normal_back(upstream, normal, inverse, gain):
    scaled = upstream * gain
    mean_scaled = jnp.mean(scaled, axis=1, keepdims=True)
    mean_product = jnp.mean(scaled * normal, axis=1, keepdims=True)
    return (scaled - mean_scaled - normal * mean_product) * inverse


def rows_tn(left, right):
    return lax.dot_general(left, right, (((0,), (0,)), ((), ())), preferred_element_type=f32)


def dense_kernel(place_ref, *refs):
    mixed = refs[0:4]
    tokens_ref, up_ref = refs[4:6]
    packs = refs[6:10]
    out_ref, grad_ref = refs[10:12]
    back_refs = refs[12:16]
    outer_refs, inner_refs = refs[16:18], refs[18:20]
    w_out, w_inner, w_outer, hidden, activated, slopes = refs[20:26]
    outer_made, inner_made, tail_made, lines, bias_rows, sem, sent = refs[26:]
    rows, width = tokens_ref.shape
    groups = w_inner.shape[0]
    part = width // groups

    def inner_copies(g):
        return [
            pltpu.make_async_copy(
                packs[r].at[pl.ds(pl.multiple_of(width + part + 16 + g * part, 16), part), :],
                w_inner.at[g, pl.ds(pl.multiple_of(place_ref[r] * part, part), part), :],
                sem.at[1 + g, r],
            )
            for r in range(groups)
        ]

    out_copies = [
        pltpu.make_async_copy(packs[r].at[pl.ds(width, part), :], w_out.at[r], sem.at[0, r])
        for r in range(groups)
    ]
    outer_copies = [
        pltpu.make_async_copy(
            packs[r].at[pl.ds(0, width), :], w_outer.at[place_ref[r]], sem.at[1 + groups, r]
        )
        for r in range(groups)
    ]
    line_copies = [
        pltpu.make_async_copy(
            packs[r].at[pl.ds(width + part, 16), :], lines.at[place_ref[r]], sem.at[2 + groups, r]
        )
        for r in range(groups)
    ]
    for copy in line_copies + out_copies + [x for g in range(groups) for x in inner_copies(g)] + outer_copies:
        copy.start()

    for copy in line_copies:
        copy.wait()
    small = [lines[k][:, 0:part].astype(f32) for k in range(groups)]
    out_bias, gain_one, shift_one, outer_bias, gain_two, shift_two = (
        jnp.concatenate([x[i : i + 1] for x in small], axis=1) for i in range(6)
    )
    for k in range(groups):
        bias_rows[k : k + 1, :] = jnp.concatenate(
            [small[k][6 + i : 7 + i] for i in range(groups)], axis=1
        )
    for copy in out_copies:
        copy.wait()
    residual = tokens_ref[...].astype(f32) + out_bias
    for r in range(groups):
        residual = residual + rows_nn(mixed[r][...], w_out[r])
    normal_one, inverse_one = normal_of(residual)
    first = normal_one * gain_one + shift_one
    first_low = first.astype(bf16)

    def ahead(g, carry):
        for copy in inner_copies(g):
            copy.wait()
        value = rows_nn(first_low, w_inner[g]) + bias_rows[pl.ds(g, 1), :]
        chance = 0.5 * (1.0 + lax.erf(value * (2.0**-0.5)))
        density = jnp.exp(-0.5 * value * value) * (2.0 * jnp.pi) ** -0.5
        slopes[g] = chance + value * density
        activated[g] = (value * chance).astype(bf16)
        return carry

    lax.fori_loop(0, groups, ahead, 0)
    for copy in outer_copies:
        copy.wait()

    def combine(g, total):
        return total + rows_nn(activated[g], w_outer[g])

    residual = lax.fori_loop(0, groups, combine, first + outer_bias)
    normal_two, inverse_two = normal_of(residual)
    out_ref[...] = (normal_two * gain_two + shift_two).astype(bf16)
    upstream = up_ref[...].astype(f32)
    grad_two = normal_back(upstream, normal_two, inverse_two, gain_two)
    grad_two_low = grad_two.astype(bf16)
    shift_two_sum = jnp.sum(upstream, axis=0, keepdims=True)
    gain_two_sum = jnp.sum(upstream * normal_two, axis=0, keepdims=True)
    outer_bias_sum = jnp.sum(grad_two_low.astype(f32), axis=0, keepdims=True)

    def outer_copy(i, odd):
        r = 2 * i + odd
        return pltpu.make_async_copy(outer_made.at[r], outer_refs[odd].at[i], sent.at[0, r])

    def behind(i, total):
        for odd in range(2):
            g = place_ref[2 * i + odd]
            outer_made[2 * i + odd] = rows_tn(activated[g], grad_two_low).astype(bf16)
            outer_copy(i, odd).start()
            value = (rows_nt(grad_two_low, w_outer[g]) * slopes[g]).astype(bf16)
            hidden[g] = value
            total = total + rows_nt(value, w_inner[g])
        return total

    grad_first = lax.fori_loop(0, groups // 2, behind, grad_two)
    grad_one = normal_back(grad_first, normal_one, inverse_one, gain_one)
    grad_ref[...] = grad_one
    grad_one_low = grad_one.astype(bf16)
    for r in range(groups):
        back_refs[r][...] = rows_nt(grad_one_low, w_out[r]).astype(bf16)

    def inner_sends(g):
        return [
            pltpu.make_async_copy(
                inner_made.at[g, pl.ds(pl.multiple_of(place_ref[r] * part, part), part), :],
                inner_refs[r % 2].at[r // 2, pl.ds(pl.multiple_of(g * part, part), part), :],
                sent.at[1 + g, r],
            )
            for r in range(groups)
        ]

    def weigh(g, carry):
        inner_made[g] = rows_tn(first_low, hidden[g]).astype(bf16)
        for copy in inner_sends(g):
            copy.start()
        return carry

    lax.fori_loop(0, groups, weigh, 0)
    sums = [
        jnp.sum(grad_one_low.astype(f32), axis=0, keepdims=True),
        jnp.sum(grad_first * normal_one, axis=0, keepdims=True),
        jnp.sum(grad_first, axis=0, keepdims=True),
        outer_bias_sum,
        gain_two_sum,
        shift_two_sum,
    ]
    line = lax.broadcasted_iota(jnp.int32, (16, part), 0)
    tail_made[:, part:, :] = jnp.zeros((groups, 64, width), bf16)
    for r in range(groups):
        tail_made[r, 0:part, :] = rows_tn(mixed[r][...], grad_one_low).astype(bf16)
    for k in range(groups):
        tail = jnp.zeros((16, part), f32)
        for i, line_sum in enumerate(sums):
            tail = jnp.where(line == i, line_sum[:, k * part : (k + 1) * part], tail)
        bias_sum = jnp.sum(hidden[k].astype(f32), axis=0, keepdims=True)
        for i in range(groups):
            tail = jnp.where(
                line == len(sums) + i, bias_sum[:, i * part : (i + 1) * part], tail
            )
        tail_made[place_ref[k], part : part + 16, 0:part] = tail.astype(bf16)
    tail_copies = [
        pltpu.make_async_copy(
            tail_made.at[r], inner_refs[r % 2].at[r // 2, pl.ds(width, part + 64), :], sent.at[1 + groups, r]
        )
        for r in range(groups)
    ]
    for copy in tail_copies:
        copy.start()
    for i in range(groups // 2):
        for odd in range(2):
            outer_copy(i, odd).wait()
    for g in range(groups):
        for copy in inner_sends(g):
            copy.wait()
    for copy in tail_copies:
        copy.wait()


def dense(places, mixed_pieces, tokens, cotangent, packs):
    rows, width = tokens.shape
    groups = len(packs)
    part = width // groups
    vmem = pl.BlockSpec(memory_space=pltpu.VMEM)
    hbm = pl.BlockSpec(memory_space=pl.ANY)
    return pl.pallas_call(
        dense_kernel,
        in_specs=[pl.BlockSpec(memory_space=pltpu.SMEM)] + [vmem] * (groups + 2) + [hbm] * groups,
        out_specs=[vmem] * (2 + groups) + [hbm] * 4,
        out_shape=[
            jax.ShapeDtypeStruct((rows, width), bf16),
            jax.ShapeDtypeStruct((rows, width), f32),
        ]
        + [jax.ShapeDtypeStruct((rows, part), bf16)] * groups
        + [jax.ShapeDtypeStruct((groups // 2, width, width), bf16)] * 2
        + [jax.ShapeDtypeStruct((groups // 2, width + part + 64, width), bf16)] * 2,
        scratch_shapes=[
            pltpu.VMEM((groups, part, width), bf16),
            pltpu.VMEM((groups, width, width), bf16),
            pltpu.VMEM((groups, width, width), bf16),
            pltpu.VMEM((groups, rows, width), bf16),
            pltpu.VMEM((groups, rows, width), bf16),
            pltpu.VMEM((groups, rows, width), f32),
            pltpu.VMEM((groups, width, width), bf16),
            pltpu.VMEM((groups, width, width), bf16),
            pltpu.VMEM((groups, part + 64, width), bf16),
            pltpu.VMEM((groups, 16, width), bf16),
            pltpu.VMEM((8, width), f32),
            pltpu.SemaphoreType.DMA((groups + 3, groups)),
            pltpu.SemaphoreType.DMA((groups + 2, groups)),
        ],
        compiler_params=pltpu.CompilerParams(vmem_limit_bytes=48 * 2**20),
        cost_estimate=pl.CostEstimate(
            flops=24 * rows * width * width * groups,
            bytes_accessed=24 * 2**20,
            transcendentals=2 * rows * width * groups,
        ),
        name="layer_dense",
    )(places, *mixed_pieces, tokens, cotangent, *packs)


def gather_kernel(place_ref, p0, p1, p2, p3, wide_ref, stat_ref, out_ref):
    rows, part = p0.shape
    lane = lax.broadcasted_iota(jnp.int32, (rows, 128), 1)
    slot = lax.broadcasted_iota(jnp.int32, (rows, HEAD_DIM), 1)
    for r, piece in enumerate((p0, p1, p2, p3)):
        here = pl.ds(pl.multiple_of(place_ref[r] * rows, rows), rows)
        tile = piece[...]
        product = tile.astype(f32) * wide_ref[here, :]
        pair, last = product[:, 0:128], product[:, 128:192]
        values = [stat_ref[here, h : h + 1] for h in range(3)] + [
            jnp.sum(jnp.where(lane < HEAD_DIM, pair, 0.0), axis=1, keepdims=True),
            jnp.sum(jnp.where(lane < HEAD_DIM, 0.0, pair), axis=1, keepdims=True),
            jnp.sum(last, axis=1, keepdims=True),
        ]
        tail = jnp.zeros((rows, HEAD_DIM), f32)
        for i, left in enumerate(values):
            for j in range(3):
                high = left.astype(bf16).astype(f32)
                tail = jnp.where(slot == 3 * i + j, high, tail)
                left = left - high
        out_ref[here, 0:192] = tile
        out_ref[here, 192:256] = tail.astype(bf16)


def gathered(places, pieces, wide, stats):
    block = wide.shape[0]
    vmem = pl.BlockSpec(memory_space=pltpu.VMEM)
    return pl.pallas_call(
        gather_kernel,
        in_specs=[pl.BlockSpec(memory_space=pltpu.SMEM)] + [vmem] * 6,
        out_specs=vmem,
        out_shape=jax.ShapeDtypeStruct((block, 256), bf16),
        compiler_params=pltpu.CompilerParams(vmem_limit_bytes=16 * 2**20),
        cost_estimate=pl.CostEstimate(flops=2**20, bytes_accessed=3 * 2**20, transcendentals=0),
        name="layer_gather",
    )(places, *pieces, wide, stats)


def both(left, right):
    return (left.astype(f32) + right.astype(f32)).astype(bf16)


def half_of(block, bit, axis):
    size = block.shape[axis] // 2
    return lax.dynamic_slice_in_dim(block, bit * size, size, axis)


def scatter_sum(terms, axis_name, order, axis):
    index = lax.axis_index(axis_name)
    for step in order:
        bit = (index // step) % 2
        sent = functools.reduce(both, [half_of(x, 1 - bit, axis) for x in terms])
        kept = functools.reduce(both, [half_of(x, bit, axis) for x in terms])
        terms = [kept, swapped(sent, axis_name, step)]
    return terms


def gather_back(block, axis_name, order, axis):
    index = lax.axis_index(axis_name)
    for step in reversed(order):
        other = swapped(block, axis_name, step)
        late = (index // step) % 2 == 1
        block = jnp.where(
            late,
            jnp.concatenate([other, block], axis),
            jnp.concatenate([block, other], axis),
        )
    return block


def on_device(
    tokens,
    doc_start,
    cotangent,
    query_weight,
    key_weight,
    value_weight,
    out_weight,
    query_bias,
    value_bias,
    out_bias,
    first_gain,
    first_shift,
    inner_weight,
    inner_bias,
    outer_weight,
    outer_bias,
    second_gain,
    second_shift,
):
    rows, width = tokens.shape
    cycle = lax.axis_size("ctx")
    shards = lax.axis_size("wt")
    block = rows * shards
    reach = (MAXDOC + block - 2) // block
    window = (2 * reach + 1) * block
    c = lax.axis_index("ctx")
    w = lax.axis_index("wt")
    part = width // shards
    places = jnp.stack([w ^ r for r in range(shards)]).astype(jnp.int32)

    def spread(own, near):
        far = swapped(own, "wt", 2)
        return [own, near, far, swapped(far, "wt", 1)]

    def columns(r):
        start = (w ^ r) * part
        return jnp.concatenate(
            [
                lax.dynamic_slice_in_dim(x, start, part, 1)
                for x in (key_weight, value_weight, query_weight)
            ],
            axis=1,
        )

    token_pieces = spread(tokens, swapped(tokens, "wt", 1))
    weight_pieces = [columns(0)] + [swapped(columns(r), "wt", r) for r in range(1, shards)]
    head_bias = jnp.concatenate([jnp.zeros((part,), f32), value_bias.astype(f32), query_bias.astype(f32)])
    head_bias = jnp.broadcast_to(head_bias[None], (8, 3 * part))

    pad = reach * block
    padded = jnp.pad(doc_start, (pad, pad), constant_values=-1)
    base = c * block - pad
    marks = lax.dynamic_slice_in_dim(padded, c * block, window)
    place = jnp.arange(window, dtype=jnp.int32)
    begins = jnp.where((marks == base + place) | (marks < 0), place, window)
    next_begin = lax.cummin(begins, axis=0, reverse=True)
    stops = jnp.concatenate([next_begin[1:], jnp.full((1,), window, jnp.int32)])
    starts = marks - base
    own_starts = starts[pad : pad + block]
    own_stops = stops[pad : pad + block]
    spans_row = jnp.stack([starts, stops] + [jnp.zeros_like(starts)] * 6)
    spans = spans_row[:, pad : pad + block]
    lowest = own_starts.reshape(-1, TILE_Q)[:, 0] // 128 * 128
    highest = own_stops.reshape(-1, TILE_Q)[:, -1]
    count = (highest - lowest + SPAN_K - 1) // SPAN_K
    lowest = jnp.minimum(lowest, (window - count * SPAN_K) // 128 * 128)
    reached = jnp.stack([jnp.min(lowest) // 256, (jnp.max(lowest + count * SPAN_K) + 255) // 256])
    bounds = jnp.concatenate([jnp.stack([lowest, count], axis=1).reshape(-1), reached])

    block_tokens, queries, pair = project(places, token_pieces, weight_pieces, head_bias)

    distances = [d for d in range(reach, -reach - 1, -1)]

    def halo(own):
        return [own if d == 0 else shifted(own, "ctx", d) for d in distances]

    even = c % 2 == 0
    beside_at = jnp.where(even, reach + 1, reach - 1) * block
    missing_at = jnp.where(even, reach - 1, reach + 1) * block
    load_at = jnp.stack(
        [0 * missing_at, 2 * reach * block + 0 * missing_at, reach * block + 0 * missing_at]
        + [beside_at, missing_at, missing_at + block // 2]
    )
    bounds = jnp.concatenate([bounds, load_at, places]).astype(jnp.int32)
    beside = swapped(pair, "ctx", 1)
    before, after = shifted(pair, "ctx", 2), shifted(pair, "ctx", -2)
    half = block // 2
    before, after, bounds, spans, spans_row = lax.optimization_barrier(
        (before, after, bounds, spans, spans_row)
    )
    route = [(i, i + 2 if i % 2 == 0 else i - 2) for i in range(cycle)]
    route = [(i, j) for i, j in route if 0 <= j < cycle]
    upper = swapped(jnp.where(even, after[:half], before[:half]), "ctx", 1)
    lower = lax.ppermute(beside[half:], "ctx", route)
    pairs = [before, after, pair, beside, upper, lower]
    small_own = jnp.stack(
        [out_bias, first_gain, first_shift, outer_bias, second_gain, second_shift]
    )
    small_own = jnp.concatenate([small_own, inner_bias.reshape(-1, part)], axis=0)
    small_own = jnp.pad(small_own, ((0, 16 - small_own.shape[0]), (0, width - part)))
    inner_parts = [inner_weight[:, i * width : (i + 1) * width] for i in range(shards)]
    pack = jnp.concatenate([outer_weight, out_weight, small_own] + inner_parts, axis=0)
    pack, _ = lax.optimization_barrier((pack, token_pieces[2:] + weight_pieces[1:]))
    pack_near, pack_far = swapped(pack, "wt", 1), swapped(pack, "wt", 2)
    *mixed_pieces, mixed_wide, stat_rows, stat_columns = attention_forward(
        bounds, queries, spans, pairs
    )
    ready, _ = lax.optimization_barrier((queries, pairs))
    query_halo = [queries if d == 0 else shifted(ready, "ctx", d) if d * d == 1 else None for d in distances]
    close = [x for x, d in zip(query_halo, distances) if d * d == 1]
    mixed_pieces, mixed_wide, stat_columns, close, pack_far = lax.optimization_barrier(
        (mixed_pieces, mixed_wide, stat_columns, close, pack_far)
    )
    packs = [pack, pack_near, pack_far, swapped(pack_far, "wt", 1)]

    mixed_pieces = [mixed_pieces[0]] + [
        swapped(mixed_pieces[r], "wt", r) for r in range(1, shards)
    ]
    far_ready, mixed_pieces = lax.optimization_barrier((queries, mixed_pieces))
    results = dense(
        places, mixed_pieces, tokens, cotangent, packs
    )
    remote = [shifted(far_ready, "ctx", d) for d in distances if d * d > 1]
    results, remote = lax.optimization_barrier((results, remote))
    layer_out, grad_one, *back = results[: 2 + shards]
    outer_keep, outer_send, inner_keep, inner_send = results[2 + shards :]
    query_halo = [remote[0], close[0], queries, close[1], remote[1]]

    back_pieces = [back[0]] + [swapped(back[r], "wt", r) for r in range(1, shards)]
    outer_got = swapped(outer_send, "wt", 1)
    inner_got = swapped(inner_send, "wt", 1)
    grads = gathered(places, back_pieces, mixed_wide, stat_columns)
    outer_got, _ = lax.optimization_barrier((outer_got, back_pieces[1:]))
    grads, inner_got = lax.optimization_barrier((grads, inner_got))

    def far_terms(keep, got):
        return [both(keep[0], got[0]), swapped(both(keep[1], got[1]), "wt", 2)]

    grad_halo = halo(grads)
    outer_terms = far_terms(outer_keep, outer_got)
    grad_query = attention_queries(
        bounds, queries, spans, grads, mixed_wide, stat_rows, pairs
    )
    grad_query, grad_halo, outer_terms, inner_keep, inner_got = lax.optimization_barrier(
        (grad_query, grad_halo, outer_terms, inner_keep, inner_got)
    )

    near_first = [1 << i for i in range(cycle.bit_length() - 1)]
    outer_terms = scatter_sum(outer_terms, "ctx", near_first[:1], 0)
    inner_terms = far_terms(inner_keep, inner_got)
    head_grad, token_partial = attention_keys(
        bounds, pair, spans_row, block_tokens, grad_query, weight_pieces, query_halo, grad_halo
    )
    head_grad, token_partial, outer_terms, inner_terms = lax.optimization_barrier(
        (head_grad, token_partial, outer_terms, inner_terms)
    )

    outer_part = both(*scatter_sum(outer_terms, "ctx", near_first[1:], 0))
    inner_part = both(*scatter_sum(inner_terms, "ctx", near_first, 0))
    head_part = both(*scatter_sum([head_grad], "ctx", near_first, 1))
    token_got = swapped(token_partial[1::2], "wt", 1)
    token_sum = both(*far_terms(token_partial[0::2], token_got))
    outer_total = gather_back(outer_part, "ctx", near_first, 0)
    inner_total = gather_back(inner_part, "ctx", near_first, 0)
    head_pieces = [
        lax.dynamic_index_in_dim(head_part, w ^ r, 0, keepdims=False) for r in range(shards)
    ]
    head_pieces = [head_pieces[0]] + [swapped(head_pieces[r], "wt", r) for r in range(1, shards)]
    head_parts = jnp.stack(
        [
            lax.dynamic_index_in_dim(jnp.stack(head_pieces), w ^ k, 0, keepdims=False)
            for k in range(shards)
        ]
    )
    head_total = gather_back(head_parts, "ctx", near_first, 1)

    tokens_gradient = grad_one + token_sum.astype(f32)
    key_total, value_total, query_total = (
        jnp.concatenate(
            [head_total[k, :, i * part : (i + 1) * part] for k in range(shards)], axis=1
        ).astype(f32)
        for i in range(3)
    )
    own_total = lax.dynamic_index_in_dim(head_total, w, 0, keepdims=False)
    inner_rows = inner_total[:width].reshape(shards, part, width)
    inner_rows = jnp.concatenate([inner_rows[k] for k in range(shards)], axis=1).astype(f32)
    lines = inner_total[width + part : width + part + 16, :part].astype(f32)

    return (
        layer_out,
        tokens_gradient,
        query_total,
        key_total,
        value_total,
        inner_total[width : width + part].astype(f32),
        own_total[:, 3 * part].astype(f32),
        own_total[:, 3 * part + 1].astype(f32),
        lines[0],
        lines[1],
        lines[2],
        inner_rows,
        lines[6:10].reshape(-1),
        outer_total.astype(f32),
        lines[3],
        lines[4],
        lines[5],
    )


def solution(mesh):
    matrix, vector = P("wt", None), P("wt")
    stream = P(("ctx", "wt"), None)
    in_specs = (stream, P(), stream) + (matrix,) * 4 + (vector,) * 5
    in_specs += (matrix, vector, matrix, vector, vector, vector)
    out_specs = (stream, stream) + (matrix,) * 4 + (vector,) * 5
    out_specs += (matrix, vector, matrix, vector, vector, vector)
    return jax.shard_map(
        on_device, mesh=mesh, in_specs=in_specs, out_specs=out_specs, check_vma=False
    )
```

```python
import functools

import jax
import jax.numpy as jnp
from jax import lax
from jax.experimental import pallas as pl
from jax.experimental.pallas import tpu as pltpu
from jax.sharding import PartitionSpec as P

HEADS = 12
HEAD_DIM = 64
MAXDOC = 2048
TILE_Q = 256
SPAN_K = 768
TILE_K = 256
SPAN_Q = 768
CHUNK = 256

masked_score = -1e30
epsilon = 1e-06
bf16 = jnp.bfloat16
f32 = jnp.float32


def swapped(block, axis, bit):
    count = lax.axis_size(axis)
    return lax.ppermute(block, axis, [(i, i ^ bit) for i in range(count)])


def shifted(block, axis, distance):
    count = lax.axis_size(axis)
    route = [(i, i + distance) for i in range(count) if 0 <= i + distance < count]
    return lax.ppermute(block, axis, route)


def rows_nt(left, right):
    return lax.dot_general(left, right, (((1,), (1,)), ((), ())), preferred_element_type=f32)


def rows_nn(left, right):
    return lax.dot_general(left, right, (((1,), (0,)), ((), ())), preferred_element_type=f32)


def load_window(pieces, target, sem, starts):
    copies = []
    for i, piece in enumerate(pieces):
        rows = pl.ds(pl.multiple_of(starts[i], 128), piece.shape[0])
        copies.append(pltpu.make_async_copy(piece, target.at[rows, :], sem.at[i]))
    for copy in copies:
        copy.start()
    return copies


def head_of(tile0, tile1, head):
    lane = lax.broadcasted_iota(jnp.int32, tile0.shape, 1)
    if head == 0:
        return jnp.where(lane < HEAD_DIM, tile0, jnp.zeros_like(tile0))
    if head == 1:
        return jnp.where(lane >= HEAD_DIM, tile0, jnp.zeros_like(tile0))
    return tile1


def turned(source, target, lanes, low, high):
    def turn(i, carry):
        rows = pl.ds(pl.multiple_of(i * 256, 256), 256)
        target[:, rows] = source[rows, lanes].T
        return carry

    lax.fori_loop(low, high, turn, 0)


def inside(span_ref, first, begin, rows):
    own = pl.ds(first, TILE_Q)
    place = begin + lax.broadcasted_iota(jnp.int32, (rows, TILE_Q), 0)
    return (place >= span_ref[0:1, own]) & (place < span_ref[1:2, own])


def forward_kernel(bounds, q_ref, span_ref, *rest):
    pieces, rest = rest[:-10], rest[-10:]
    outs, (wide_ref, row_ref, stat_ref, kv, vt, sem) = rest[:4], rest[4:]
    step = pl.program_id(0)

    @pl.when(step == 0)
    def _():
        for copy in load_window(pieces, kv, sem, [bounds[10 + i] for i in range(len(pieces))]):
            copy.wait()
        turned(kv, vt, slice(192, 384), bounds[8], bounds[9])

    first = pl.multiple_of(step * TILE_Q, TILE_Q)
    here = pl.ds(first, TILE_Q)
    q_tile = q_ref[here, :]
    heads = [head_of(q_tile[:, :128], q_tile[:, 128:], h) for h in range(3)]
    lower, count = bounds[2 * step], bounds[2 * step + 1]

    def run(i, carry):
        begin = pl.multiple_of(lower + i * SPAN_K, 128)
        rows = pl.ds(begin, SPAN_K)
        allowed = inside(span_ref, first, begin, SPAN_K)
        after = []

        def ahead(h):
            score = rows_nt(kv[rows, 0:128] if h < 2 else kv[rows, 128:192], heads[h])
            return jnp.where(allowed, score, masked_score)

        coming = ahead(0)
        for h in range(3):
            score = coming
            if h < 2:
                coming = ahead(h + 1)
            before, total, accum = carry[3 * h : 3 * h + 3]
            newest = jnp.maximum(before, jnp.max(score, axis=0, keepdims=True))
            factor = jnp.exp(before - newest)
            weight = jnp.exp(score - newest)
            total = total * factor + jnp.sum(weight, axis=0, keepdims=True)
            made = rows_nn(vt[h * HEAD_DIM : (h + 1) * HEAD_DIM, rows], weight.astype(bf16))
            after += [newest, total, accum * factor + made]
        return tuple(after)

    start = (
        jnp.full((1, TILE_Q), masked_score, f32),
        jnp.zeros((1, TILE_Q), f32),
        jnp.zeros((HEAD_DIM, TILE_Q), f32),
    )
    state = lax.fori_loop(0, count, run, start * 3)
    mixed = jnp.concatenate([state[3 * h + 2] / state[3 * h + 1] for h in range(3)], axis=0).T
    line = lax.broadcasted_iota(jnp.int32, (128, TILE_Q), 0)
    stats = jnp.zeros((128, TILE_Q), f32)
    for h in range(3):
        stats = jnp.where(line == h, state[3 * h] + jnp.log(state[3 * h + 1]), stats)
    wide_ref[here, :] = mixed
    row_ref[:, here] = stats[0:8, :]
    stat_ref[here, :] = stats.T
    low = mixed.astype(bf16)
    for r, out_ref in enumerate(outs):

        @pl.when(bounds[16 + step] == r)
        def _(out_ref=out_ref):
            out_ref[...] = low


def whole_spec(shape):
    return pl.BlockSpec(shape, lambda i, *_: (0,) * len(shape))


def attention_forward(bounds, queries, spans, pieces):
    block = queries.shape[0]
    window = sum(x.shape[0] for x in pieces)
    return pl.pallas_call(
        forward_kernel,
        grid_spec=pltpu.PrefetchScalarGridSpec(
            num_scalar_prefetch=1,
            grid=(block // TILE_Q,),
            in_specs=[whole_spec(queries.shape), whole_spec(spans.shape)]
            + [pl.BlockSpec(memory_space=pl.ANY)] * len(pieces),
            out_specs=[whole_spec((TILE_Q, 192))] * 4
            + [whole_spec((block, 192)), whole_spec((8, block)), whole_spec((block, 128))],
            scratch_shapes=[
                pltpu.VMEM((window, 384), bf16),
                pltpu.VMEM((192, window), bf16),
                pltpu.SemaphoreType.DMA((len(pieces),)),
            ],
        ),
        out_shape=[jax.ShapeDtypeStruct((TILE_Q, 192), bf16)] * 4
        + [
            jax.ShapeDtypeStruct((block, 192), f32),
            jax.ShapeDtypeStruct((8, block), f32),
            jax.ShapeDtypeStruct((block, 128), f32),
        ],
        compiler_params=pltpu.CompilerParams(vmem_limit_bytes=60 * 2**20),
        cost_estimate=pl.CostEstimate(
            flops=4 * block * 2304 * 192, bytes_accessed=6 * 2**20, transcendentals=block * 2304 * 3
        ),
        name="attention_forward",
    )(bounds, queries, spans, *pieces)


def query_kernel(bounds, q_ref, span_ref, grad_ref, wide_ref, row_ref, *rest):
    pieces, (out_ref, kv, kt, sem) = rest[:-4], rest[-4:]
    step = pl.program_id(0)

    @pl.when(step == 0)
    def _():
        for copy in load_window(pieces, kv, sem, [bounds[10 + i] for i in range(len(pieces))]):
            copy.wait()
        turned(kv, kt, slice(0, 192), bounds[8], bounds[9])

    first = pl.multiple_of(step * TILE_Q, TILE_Q)
    here = pl.ds(first, TILE_Q)
    q_tile = q_ref[here, :]
    heads = [head_of(q_tile[:, :128], q_tile[:, 128:], h) for h in range(3)]
    g_tile = grad_ref[here, :]
    lane = lax.broadcasted_iota(jnp.int32, (TILE_Q, 128), 1)
    none = jnp.zeros((TILE_Q, 128), bf16)
    r_pair = pltpu.roll(g_tile[:, :128].astype(f32), HEAD_DIM, 1).astype(bf16)
    r_last = pltpu.roll(g_tile[:, 128:256].astype(f32), HEAD_DIM, 1).astype(bf16)
    grads = [
        jnp.where(lane >= HEAD_DIM, r_pair, none),
        jnp.where(lane < HEAD_DIM, r_pair, none),
        jnp.where(lane >= HEAD_DIM, r_last, none),
    ]
    product = (g_tile[:, 0:192].astype(f32) * wide_ref[here, :]).T
    deltas = [
        jnp.sum(product[h * HEAD_DIM : (h + 1) * HEAD_DIM], axis=0, keepdims=True) for h in range(3)
    ]
    logs = [row_ref[h : h + 1, here] for h in range(3)]
    lower, count = bounds[2 * step], bounds[2 * step + 1]

    def run(i, carry):
        begin = pl.multiple_of(lower + i * SPAN_K, 128)
        rows = pl.ds(begin, SPAN_K)
        allowed = inside(span_ref, first, begin, SPAN_K)
        after = []

        def ahead(h):
            score = rows_nt(kv[rows, 0:128] if h < 2 else kv[rows, 128:192], heads[h])
            return score, rows_nt(kv[rows, 128:256] if h == 0 else kv[rows, 256:384], grads[h])

        coming = ahead(0)
        for h in range(3):
            score, back = coming
            if h < 2:
                coming = ahead(h + 1)
            chance = jnp.exp(jnp.where(allowed, score - logs[h], masked_score))
            change = (chance * (back - deltas[h])).astype(bf16)
            after.append(carry[h] + rows_nn(kt[h * HEAD_DIM : (h + 1) * HEAD_DIM, rows], change))
        return tuple(after)

    sums = lax.fori_loop(0, count, run, (jnp.zeros((HEAD_DIM, TILE_Q), f32),) * 3)
    out_ref[here, :] = (jnp.concatenate(sums, axis=0).T * 0.125).astype(bf16)


def attention_queries(bounds, queries, spans, grads, wide, stats, pieces):
    block = queries.shape[0]
    window = sum(x.shape[0] for x in pieces)
    return pl.pallas_call(
        query_kernel,
        grid_spec=pltpu.PrefetchScalarGridSpec(
            num_scalar_prefetch=1,
            grid=(block // TILE_Q,),
            in_specs=[whole_spec(x.shape) for x in (queries, spans, grads, wide, stats)]
            + [pl.BlockSpec(memory_space=pl.ANY)] * len(pieces),
            out_specs=whole_spec((block, 192)),
            scratch_shapes=[
                pltpu.VMEM((window, 384), bf16),
                pltpu.VMEM((192, window), bf16),
                pltpu.SemaphoreType.DMA((len(pieces),)),
            ],
        ),
        out_shape=jax.ShapeDtypeStruct((block, 192), bf16),
        compiler_params=pltpu.CompilerParams(vmem_limit_bytes=40 * 2**20),
        cost_estimate=pl.CostEstimate(
            flops=6 * block * 2304 * 192, bytes_accessed=6 * 2**20, transcendentals=block * 2304 * 3
        ),
        name="attention_queries",
    )(bounds, queries, spans, grads, wide, stats, *pieces)


def weight_copies(bounds, pieces, weight, sem):
    part = pieces[0].shape[0]
    copies = []
    for r, piece in enumerate(pieces):
        where = pl.ds(pl.multiple_of(bounds[16 + r] * part, part), part)
        copies.append(pltpu.make_async_copy(piece, weight.at[where, :], sem.at[r]))
    return copies


def head_terms(bounds, tokens_ref, query_ref, pair_ref, weight, grad_ref, back_ref):
    groups, part = grad_ref.shape[0], grad_ref.shape[1]
    rows = back_ref.shape[1]
    tokens = tokens_ref[...]
    pair_grad = rows_tn(tokens, pair_ref[...]).astype(bf16)
    query_grad = rows_tn(tokens, query_ref[...]).astype(bf16)
    for k in range(groups):
        here = slice(k * part, (k + 1) * part)
        grad_ref[k, :, 0 : 2 * part] = pair_grad[here]
        grad_ref[k, :, 2 * part : 3 * part] = query_grad[here]
    ones = jnp.ones((tokens.shape[0], HEAD_DIM), bf16)
    query_sum = rows_tn(query_ref[...], ones)
    value_sum = rows_tn(pair_ref[:, part:], ones)
    lane = lax.broadcasted_iota(jnp.int32, (part, HEAD_DIM), 1)
    sums = jnp.where(lane == 0, query_sum, jnp.where(lane == 1, value_sum, 0.0))
    grad_ref[:, :, 3 * part : 3 * part + HEAD_DIM] = jnp.zeros((groups, part, HEAD_DIM), bf16)
    grad_ref[bounds[16], :, 3 * part : 3 * part + HEAD_DIM] = sums.astype(bf16)
    for k in range(groups):
        here = slice(k * rows, (k + 1) * rows)
        made = rows_nt(pair_ref[here, :], weight[:, : 2 * part])
        made = made + rows_nt(query_ref[here, :], weight[:, 2 * part :])
        back_ref[bounds[16 + k]] = made.astype(bf16)


def key_kernel(reach, bounds, kv_ref, span_ref, tokens_ref, query_ref, *rest):
    window = 2 * reach + 1
    w_pieces, rest = rest[:4], rest[4:]
    q_pieces, g_pieces = rest[:window], rest[window : 2 * window]
    grad_ref, back_ref, qs, gs, key_sum, value_sum, out_ref, weight, sem, w_sem = rest[2 * window :]
    step = pl.program_id(0)
    block = q_pieces[0].shape[0]

    @pl.when(step == 0)
    def _():
        copies = load_window(q_pieces, qs, sem.at[0], [i * block for i in range(window)])
        copies += load_window(g_pieces, gs, sem.at[1], [i * block for i in range(window)])
        for copy in weight_copies(bounds, w_pieces, weight, w_sem):
            copy.start()
        for copy in copies:
            copy.wait()

    first = pl.multiple_of(step * TILE_K, TILE_K)
    here = pl.ds(first, TILE_K)
    key_sum[...] = jnp.zeros_like(key_sum)
    value_sum[...] = jnp.zeros_like(value_sum)
    keys_pair = kv_ref[here, 0:128]
    keys = [head_of(keys_pair, kv_ref[here, 128:192], h) for h in range(3)]
    lane = lax.broadcasted_iota(jnp.int32, (TILE_K, 128), 1)
    zero = jnp.zeros((TILE_K, 128), f32)
    v_one = pltpu.roll(kv_ref[here, 128:256].astype(f32), HEAD_DIM, 1)
    v_two = pltpu.roll(kv_ref[here, 256:384].astype(f32), HEAD_DIM, 1)
    values = [
        jnp.where(lane < HEAD_DIM, v_one, zero).astype(bf16),
        jnp.where(lane < HEAD_DIM, zero, v_two).astype(bf16),
        v_two.astype(bf16)[:, :HEAD_DIM],
    ]
    line = lax.broadcasted_iota(jnp.int32, (16, HEAD_DIM), 0)
    slot = lax.broadcasted_iota(jnp.int32, (16, HEAD_DIM), 1)
    selector = jnp.where((slot // 3 == line) & (slot < 18), 1.0, 0.0).astype(bf16)
    lower, count = bounds[2 * step], bounds[2 * step + 1]

    def run(i, carry):
        begin = pl.multiple_of(lower + i * SPAN_Q, 128)
        columns = pl.ds(begin, SPAN_Q)
        place = reach * block + first + lax.broadcasted_iota(jnp.int32, (TILE_K, SPAN_Q), 0)
        allowed = (place >= span_ref[0:1, columns]) & (place < span_ref[1:2, columns])
        lanes = [slice(0, 128), slice(0, 128), slice(128, 192)]
        stats = rows_nt(selector, gs[columns, 192:256])
        items = [(h, ch) for h in range(3) for ch in range(SPAN_Q // CHUNK)]

        def ahead(item):
            h, ch = item
            here = pl.ds(pl.multiple_of(begin + ch * CHUNK, 128), CHUNK)
            q_tile, g_tile = qs[here, lanes[h]], gs[here, lanes[h]]
            return q_tile, g_tile, rows_nt(keys[h], q_tile), rows_nt(values[h], g_tile)

        coming = ahead(items[0])
        for n, (h, ch) in enumerate(items):
            q_tile, g_tile, score, back = coming
            if n + 1 < len(items):
                coming = ahead(items[n + 1])
            cols = slice(ch * CHUNK, (ch + 1) * CHUNK)
            score = jnp.where(allowed[:, cols], score - stats[h : h + 1, cols], masked_score)
            chance = jnp.exp(score)
            change = (chance * (back - stats[h + 3 : h + 4, cols])).astype(bf16)
            size = 128 if h < 2 else HEAD_DIM
            key_sum[h, :, 0:size] += rows_nn(change, q_tile)
            value_sum[h, :, 0:size] += rows_nn(chance.astype(bf16), g_tile)
        return carry

    lax.fori_loop(0, count, run, 0)
    k_pair = jnp.where(lane < HEAD_DIM, key_sum[0], key_sum[1])
    v_pair = jnp.where(lane < HEAD_DIM, value_sum[0], value_sum[1])
    v_turn = pltpu.roll(v_pair, HEAD_DIM, 1)
    last_turn = pltpu.roll(value_sum[2], HEAD_DIM, 1)
    out_ref[here, 0:128] = k_pair.astype(bf16)
    out_ref[here, 128:256] = jnp.where(lane < HEAD_DIM, key_sum[2], v_turn).astype(bf16)
    out_ref[here, 256:384] = jnp.where(lane < HEAD_DIM, v_turn, last_turn).astype(bf16)

    @pl.when(step == pl.num_programs(0) - 1)
    def _():
        for copy in weight_copies(bounds, w_pieces, weight, w_sem):
            copy.wait()
        head_terms(bounds, tokens_ref, query_ref, out_ref, weight, grad_ref, back_ref)


def attention_keys(bounds, pair, spans, tokens, grad_query, weight_pieces, q_pieces, g_pieces):
    block, width = tokens.shape
    count = len(q_pieces)
    groups, part = len(weight_pieces), weight_pieces[0].shape[0]
    return pl.pallas_call(
        functools.partial(key_kernel, count // 2),
        grid_spec=pltpu.PrefetchScalarGridSpec(
            num_scalar_prefetch=1,
            grid=(block // TILE_K,),
            in_specs=[whole_spec(x.shape) for x in (pair, spans, tokens, grad_query)]
            + [pl.BlockSpec(memory_space=pl.ANY)] * (groups + 2 * count),
            out_specs=[
                whole_spec((groups, part, 3 * part + HEAD_DIM)),
                whole_spec((groups, block // groups, width)),
            ],
            scratch_shapes=[
                pltpu.VMEM((count * block, 192), bf16),
                pltpu.VMEM((count * block, 256), bf16),
                pltpu.VMEM((3, TILE_K, 128), f32),
                pltpu.VMEM((3, TILE_K, 128), f32),
                pltpu.VMEM((block, 384), bf16),
                pltpu.VMEM((width, 3 * part), bf16),
                pltpu.SemaphoreType.DMA((2, count)),
                pltpu.SemaphoreType.DMA((groups,)),
            ],
        ),
        out_shape=[
            jax.ShapeDtypeStruct((groups, part, 3 * part + HEAD_DIM), bf16),
            jax.ShapeDtypeStruct((groups, block // groups, width), bf16),
        ],
        compiler_params=pltpu.CompilerParams(vmem_limit_bytes=60 * 2**20),
        cost_estimate=pl.CostEstimate(
            flops=10 * block * 2304 * 192, bytes_accessed=12 * 2**20, transcendentals=block * 2304 * 3
        ),
        name="attention_keys",
    )(bounds, pair, spans, tokens, grad_query, *weight_pieces, *q_pieces, *g_pieces)


def projection_kernel(place_ref, own, near, far, corner, w_own, w_near, w_far, w_corner, bias_ref, *rest):
    tokens_ref, query_ref, pair_ref, weight, sem = rest
    rows, part = own.shape[0], w_own.shape[0]
    pieces = (w_own, w_near, w_far, w_corner)
    copies = []
    for r, piece in enumerate(pieces):
        where = pl.multiple_of(place_ref[r] * part, part)
        copies.append(pltpu.make_async_copy(piece, weight.at[pl.ds(where, part), :], sem.at[r]))
        copies[-1].start()
    for copy in copies:
        copy.wait()
    for r, piece in enumerate((own, near, far, corner)):
        here = pl.ds(pl.multiple_of(place_ref[r] * rows, rows), rows)
        tile = piece[...]
        tokens_ref[here, :] = tile
        made = rows_nn(tile, weight[...]) + bias_ref[0:1, :]
        pair_ref[here, :] = made[:, : 2 * part].astype(bf16)
        query_ref[here, :] = (made[:, 2 * part :].astype(bf16).astype(f32) * 0.125).astype(bf16)


def project(places, token_pieces, weight_pieces, bias):
    rows, width = token_pieces[0].shape
    part = weight_pieces[0].shape[0]
    block = rows * len(token_pieces)
    vmem = pl.BlockSpec(memory_space=pltpu.VMEM)
    return pl.pallas_call(
        projection_kernel,
        in_specs=[pl.BlockSpec(memory_space=pltpu.SMEM)]
        + [vmem] * 4
        + [pl.BlockSpec(memory_space=pl.ANY)] * 4
        + [vmem],
        out_specs=[vmem] * 3,
        out_shape=[
            jax.ShapeDtypeStruct((block, width), bf16),
            jax.ShapeDtypeStruct((block, part), bf16),
            jax.ShapeDtypeStruct((block, 2 * part), bf16),
        ],
        scratch_shapes=[pltpu.VMEM((width, 3 * part), bf16), pltpu.SemaphoreType.DMA((4,))],
        compiler_params=pltpu.CompilerParams(vmem_limit_bytes=32 * 2**20),
        cost_estimate=pl.CostEstimate(
            flops=2 * block * width * 3 * part, bytes_accessed=5 * 2**20, transcendentals=0
        ),
        name="layer_projection",
    )(places, *token_pieces, *weight_pieces, bias)


def normal_of(values):
    center = values - jnp.mean(values, axis=1, keepdims=True)
    inverse = lax.rsqrt(jnp.mean(center * center, axis=1, keepdims=True) + epsilon)
    return center * inverse, inverse


def normal_back(upstream, normal, inverse, gain):
    scaled = upstream * gain
    mean_scaled = jnp.mean(scaled, axis=1, keepdims=True)
    mean_product = jnp.mean(scaled * normal, axis=1, keepdims=True)
    return (scaled - mean_scaled - normal * mean_product) * inverse


def rows_tn(left, right):
    return lax.dot_general(left, right, (((0,), (0,)), ((), ())), preferred_element_type=f32)


def dense_kernel(place_ref, *refs):
    mixed = refs[0:4]
    tokens_ref, up_ref = refs[4:6]
    packs = refs[6:10]
    out_ref, grad_ref = refs[10:12]
    back_refs = refs[12:16]
    outer_refs, inner_refs = refs[16:18], refs[18:20]
    w_out, w_inner, w_outer, hidden, activated, slopes = refs[20:26]
    outer_made, inner_made, tail_made, lines, bias_rows, sem, sent = refs[26:]
    rows, width = tokens_ref.shape
    groups = w_inner.shape[0]
    part = width // groups

    def inner_copies(g):
        return [
            pltpu.make_async_copy(
                packs[r].at[pl.ds(pl.multiple_of(width + part + 16 + g * part, 16), part), :],
                w_inner.at[g, pl.ds(pl.multiple_of(place_ref[r] * part, part), part), :],
                sem.at[1 + g, r],
            )
            for r in range(groups)
        ]

    out_copies = [
        pltpu.make_async_copy(packs[r].at[pl.ds(width, part), :], w_out.at[r], sem.at[0, r])
        for r in range(groups)
    ]
    outer_copies = [
        pltpu.make_async_copy(
            packs[r].at[pl.ds(0, width), :], w_outer.at[place_ref[r]], sem.at[1 + groups, r]
        )
        for r in range(groups)
    ]
    line_copies = [
        pltpu.make_async_copy(
            packs[r].at[pl.ds(width + part, 16), :], lines.at[place_ref[r]], sem.at[2 + groups, r]
        )
        for r in range(groups)
    ]
    for copy in line_copies + out_copies + [x for g in range(groups) for x in inner_copies(g)] + outer_copies:
        copy.start()

    for copy in line_copies:
        copy.wait()
    small = [lines[k][:, 0:part].astype(f32) for k in range(groups)]
    out_bias, gain_one, shift_one, outer_bias, gain_two, shift_two = (
        jnp.concatenate([x[i : i + 1] for x in small], axis=1) for i in range(6)
    )
    for k in range(groups):
        bias_rows[k : k + 1, :] = jnp.concatenate(
            [small[k][6 + i : 7 + i] for i in range(groups)], axis=1
        )
    for copy in out_copies:
        copy.wait()
    residual = tokens_ref[...].astype(f32) + out_bias
    for r in range(groups):
        residual = residual + rows_nn(mixed[r][...], w_out[r])
    normal_one, inverse_one = normal_of(residual)
    first = normal_one * gain_one + shift_one
    first_low = first.astype(bf16)

    def ahead(g, carry):
        for copy in inner_copies(g):
            copy.wait()
        value = rows_nn(first_low, w_inner[g]) + bias_rows[pl.ds(g, 1), :]
        chance = 0.5 * (1.0 + lax.erf(value * (2.0**-0.5)))
        density = jnp.exp(-0.5 * value * value) * (2.0 * jnp.pi) ** -0.5
        slopes[g] = chance + value * density
        activated[g] = (value * chance).astype(bf16)
        return carry

    lax.fori_loop(0, groups, ahead, 0)
    for copy in outer_copies:
        copy.wait()

    def combine(g, total):
        return total + rows_nn(activated[g], w_outer[g])

    residual = lax.fori_loop(0, groups, combine, first + outer_bias)
    normal_two, inverse_two = normal_of(residual)
    out_ref[...] = (normal_two * gain_two + shift_two).astype(bf16)
    upstream = up_ref[...].astype(f32)
    grad_two = normal_back(upstream, normal_two, inverse_two, gain_two)
    grad_two_low = grad_two.astype(bf16)
    shift_two_sum = jnp.sum(upstream, axis=0, keepdims=True)
    gain_two_sum = jnp.sum(upstream * normal_two, axis=0, keepdims=True)
    outer_bias_sum = jnp.sum(grad_two_low.astype(f32), axis=0, keepdims=True)

    def outer_copy(i, odd):
        r = 2 * i + odd
        return pltpu.make_async_copy(outer_made.at[r], outer_refs[odd].at[i], sent.at[0, r])

    def behind(i, total):
        for odd in range(2):
            g = place_ref[2 * i + odd]
            outer_made[2 * i + odd] = rows_tn(activated[g], grad_two_low).astype(bf16)
            outer_copy(i, odd).start()
            value = (rows_nt(grad_two_low, w_outer[g]) * slopes[g]).astype(bf16)
            hidden[g] = value
            total = total + rows_nt(value, w_inner[g])
        return total

    grad_first = lax.fori_loop(0, groups // 2, behind, grad_two)
    grad_one = normal_back(grad_first, normal_one, inverse_one, gain_one)
    grad_ref[...] = grad_one
    grad_one_low = grad_one.astype(bf16)
    for r in range(groups):
        back_refs[r][...] = rows_nt(grad_one_low, w_out[r]).astype(bf16)

    def inner_sends(g):
        return [
            pltpu.make_async_copy(
                inner_made.at[g, pl.ds(pl.multiple_of(place_ref[r] * part, part), part), :],
                inner_refs[r % 2].at[r // 2, pl.ds(pl.multiple_of(g * part, part), part), :],
                sent.at[1 + g, r],
            )
            for r in range(groups)
        ]

    def weigh(g, carry):
        inner_made[g] = rows_tn(first_low, hidden[g]).astype(bf16)
        for copy in inner_sends(g):
            copy.start()
        return carry

    lax.fori_loop(0, groups, weigh, 0)
    sums = [
        jnp.sum(grad_one_low.astype(f32), axis=0, keepdims=True),
        jnp.sum(grad_first * normal_one, axis=0, keepdims=True),
        jnp.sum(grad_first, axis=0, keepdims=True),
        outer_bias_sum,
        gain_two_sum,
        shift_two_sum,
    ]
    line = lax.broadcasted_iota(jnp.int32, (16, part), 0)
    tail_made[:, part:, :] = jnp.zeros((groups, 64, width), bf16)
    for r in range(groups):
        tail_made[r, 0:part, :] = rows_tn(mixed[r][...], grad_one_low).astype(bf16)
    for k in range(groups):
        tail = jnp.zeros((16, part), f32)
        for i, line_sum in enumerate(sums):
            tail = jnp.where(line == i, line_sum[:, k * part : (k + 1) * part], tail)
        bias_sum = jnp.sum(hidden[k].astype(f32), axis=0, keepdims=True)
        for i in range(groups):
            tail = jnp.where(
                line == len(sums) + i, bias_sum[:, i * part : (i + 1) * part], tail
            )
        tail_made[place_ref[k], part : part + 16, 0:part] = tail.astype(bf16)
    tail_copies = [
        pltpu.make_async_copy(
            tail_made.at[r], inner_refs[r % 2].at[r // 2, pl.ds(width, part + 64), :], sent.at[1 + groups, r]
        )
        for r in range(groups)
    ]
    for copy in tail_copies:
        copy.start()
    for i in range(groups // 2):
        for odd in range(2):
            outer_copy(i, odd).wait()
    for g in range(groups):
        for copy in inner_sends(g):
            copy.wait()
    for copy in tail_copies:
        copy.wait()


def dense(places, mixed_pieces, tokens, cotangent, packs):
    rows, width = tokens.shape
    groups = len(packs)
    part = width // groups
    vmem = pl.BlockSpec(memory_space=pltpu.VMEM)
    hbm = pl.BlockSpec(memory_space=pl.ANY)
    return pl.pallas_call(
        dense_kernel,
        in_specs=[pl.BlockSpec(memory_space=pltpu.SMEM)] + [vmem] * (groups + 2) + [hbm] * groups,
        out_specs=[vmem] * (2 + groups) + [hbm] * 4,
        out_shape=[
            jax.ShapeDtypeStruct((rows, width), bf16),
            jax.ShapeDtypeStruct((rows, width), f32),
        ]
        + [jax.ShapeDtypeStruct((rows, part), bf16)] * groups
        + [jax.ShapeDtypeStruct((groups // 2, width, width), bf16)] * 2
        + [jax.ShapeDtypeStruct((groups // 2, width + part + 64, width), bf16)] * 2,
        scratch_shapes=[
            pltpu.VMEM((groups, part, width), bf16),
            pltpu.VMEM((groups, width, width), bf16),
            pltpu.VMEM((groups, width, width), bf16),
            pltpu.VMEM((groups, rows, width), bf16),
            pltpu.VMEM((groups, rows, width), bf16),
            pltpu.VMEM((groups, rows, width), f32),
            pltpu.VMEM((groups, width, width), bf16),
            pltpu.VMEM((groups, width, width), bf16),
            pltpu.VMEM((groups, part + 64, width), bf16),
            pltpu.VMEM((groups, 16, width), bf16),
            pltpu.VMEM((8, width), f32),
            pltpu.SemaphoreType.DMA((groups + 3, groups)),
            pltpu.SemaphoreType.DMA((groups + 2, groups)),
        ],
        compiler_params=pltpu.CompilerParams(vmem_limit_bytes=48 * 2**20),
        cost_estimate=pl.CostEstimate(
            flops=24 * rows * width * width * groups,
            bytes_accessed=24 * 2**20,
            transcendentals=2 * rows * width * groups,
        ),
        name="layer_dense",
    )(places, *mixed_pieces, tokens, cotangent, *packs)


def gather_kernel(place_ref, p0, p1, p2, p3, wide_ref, stat_ref, out_ref):
    rows, part = p0.shape
    lane = lax.broadcasted_iota(jnp.int32, (rows, 128), 1)
    slot = lax.broadcasted_iota(jnp.int32, (rows, HEAD_DIM), 1)
    for r, piece in enumerate((p0, p1, p2, p3)):
        here = pl.ds(pl.multiple_of(place_ref[r] * rows, rows), rows)
        tile = piece[...]
        product = tile.astype(f32) * wide_ref[here, :]
        pair, last = product[:, 0:128], product[:, 128:192]
        values = [stat_ref[here, h : h + 1] for h in range(3)] + [
            jnp.sum(jnp.where(lane < HEAD_DIM, pair, 0.0), axis=1, keepdims=True),
            jnp.sum(jnp.where(lane < HEAD_DIM, 0.0, pair), axis=1, keepdims=True),
            jnp.sum(last, axis=1, keepdims=True),
        ]
        tail = jnp.zeros((rows, HEAD_DIM), f32)
        for i, left in enumerate(values):
            for j in range(3):
                high = left.astype(bf16).astype(f32)
                tail = jnp.where(slot == 3 * i + j, high, tail)
                left = left - high
        out_ref[here, 0:192] = tile
        out_ref[here, 192:256] = tail.astype(bf16)


def gathered(places, pieces, wide, stats):
    block = wide.shape[0]
    vmem = pl.BlockSpec(memory_space=pltpu.VMEM)
    return pl.pallas_call(
        gather_kernel,
        in_specs=[pl.BlockSpec(memory_space=pltpu.SMEM)] + [vmem] * 6,
        out_specs=vmem,
        out_shape=jax.ShapeDtypeStruct((block, 256), bf16),
        compiler_params=pltpu.CompilerParams(vmem_limit_bytes=16 * 2**20),
        cost_estimate=pl.CostEstimate(flops=2**20, bytes_accessed=3 * 2**20, transcendentals=0),
        name="layer_gather",
    )(places, *pieces, wide, stats)


def both(left, right):
    return (left.astype(f32) + right.astype(f32)).astype(bf16)


def half_of(block, bit, axis):
    size = block.shape[axis] // 2
    return lax.dynamic_slice_in_dim(block, bit * size, size, axis)


def scatter_sum(terms, axis_name, order, axis):
    index = lax.axis_index(axis_name)
    for step in order:
        bit = (index // step) % 2
        sent = functools.reduce(both, [half_of(x, 1 - bit, axis) for x in terms])
        kept = functools.reduce(both, [half_of(x, bit, axis) for x in terms])
        terms = [kept, swapped(sent, axis_name, step)]
    return terms


def gather_back(block, axis_name, order, axis):
    index = lax.axis_index(axis_name)
    for step in reversed(order):
        other = swapped(block, axis_name, step)
        late = (index // step) % 2 == 1
        block = jnp.where(
            late,
            jnp.concatenate([other, block], axis),
            jnp.concatenate([block, other], axis),
        )
    return block


def gather_square(block, axis_name):
    index = lax.axis_index(axis_name)
    rows, width = block.shape
    first, second = block[: rows // 2], block[rows // 2 :]
    first_got = swapped(first, axis_name, 1)
    second_got = swapped(second, axis_name, 2)
    first_got, second_got = lax.optimization_barrier((first_got, second_got))
    first_far = swapped(jnp.concatenate([first, first_got]), axis_name, 2)
    second_far = swapped(jnp.concatenate([second, second_got]), axis_name, 1)
    size = rows // 2
    ours = [
        (first, second),
        (first_far[:size], second_got),
        (first_got, second_far[:size]),
        (first_far[size:], second_far[size:]),
    ]
    low, high = index % 2 == 1, (index // 2) % 2 == 1
    placed = []
    for x in range(2):
        for z in range(2):
            for half in range(2):
                near = jnp.where(high, ours[2 * x + 1 - z][half], ours[2 * x + z][half])
                across = jnp.where(
                    high, ours[2 * (1 - x) + 1 - z][half], ours[2 * (1 - x) + z][half]
                )
                placed.append(jnp.where(low, across, near))
    return jnp.concatenate(placed, axis=0)


def on_device(
    tokens,
    doc_start,
    cotangent,
    query_weight,
    key_weight,
    value_weight,
    out_weight,
    query_bias,
    value_bias,
    out_bias,
    first_gain,
    first_shift,
    inner_weight,
    inner_bias,
    outer_weight,
    outer_bias,
    second_gain,
    second_shift,
):
    rows, width = tokens.shape
    cycle = lax.axis_size("ctx")
    shards = lax.axis_size("wt")
    block = rows * shards
    reach = (MAXDOC + block - 2) // block
    window = (2 * reach + 1) * block
    c = lax.axis_index("ctx")
    w = lax.axis_index("wt")
    part = width // shards
    places = jnp.stack([w ^ r for r in range(shards)]).astype(jnp.int32)

    def spread(own, near):
        far = swapped(own, "wt", 2)
        return [own, near, far, swapped(far, "wt", 1)]

    def columns(r):
        start = (w ^ r) * part
        return jnp.concatenate(
            [
                lax.dynamic_slice_in_dim(x, start, part, 1)
                for x in (key_weight, value_weight, query_weight)
            ],
            axis=1,
        )

    token_pieces = spread(tokens, swapped(tokens, "wt", 1))
    weight_pieces = [columns(0)] + [swapped(columns(r), "wt", r) for r in range(1, shards)]
    head_bias = jnp.concatenate([jnp.zeros((part,), f32), value_bias.astype(f32), query_bias.astype(f32)])
    head_bias = jnp.broadcast_to(head_bias[None], (8, 3 * part))

    pad = reach * block
    padded = jnp.pad(doc_start, (pad, pad), constant_values=-1)
    base = c * block - pad
    marks = lax.dynamic_slice_in_dim(padded, c * block, window)
    place = jnp.arange(window, dtype=jnp.int32)
    begins = jnp.where((marks == base + place) | (marks < 0), place, window)
    next_begin = lax.cummin(begins, axis=0, reverse=True)
    stops = jnp.concatenate([next_begin[1:], jnp.full((1,), window, jnp.int32)])
    starts = marks - base
    own_starts = starts[pad : pad + block]
    own_stops = stops[pad : pad + block]
    spans_row = jnp.stack([starts, stops] + [jnp.zeros_like(starts)] * 6)
    spans = spans_row[:, pad : pad + block]
    lowest = own_starts.reshape(-1, TILE_Q)[:, 0] // 128 * 128
    highest = own_stops.reshape(-1, TILE_Q)[:, -1]
    count = (highest - lowest + SPAN_K - 1) // SPAN_K
    lowest = jnp.minimum(lowest, (window - count * SPAN_K) // 128 * 128)
    reached = jnp.stack([jnp.min(lowest) // 256, (jnp.max(lowest + count * SPAN_K) + 255) // 256])
    bounds = jnp.concatenate([jnp.stack([lowest, count], axis=1).reshape(-1), reached])

    block_tokens, queries, pair = project(places, token_pieces, weight_pieces, head_bias)

    distances = [d for d in range(reach, -reach - 1, -1)]

    def halo(own):
        return [own if d == 0 else shifted(own, "ctx", d) for d in distances]

    even = c % 2 == 0
    beside_at = jnp.where(even, reach + 1, reach - 1) * block
    missing_at = jnp.where(even, reach - 1, reach + 1) * block
    load_at = jnp.stack(
        [0 * missing_at, 2 * reach * block + 0 * missing_at, reach * block + 0 * missing_at]
        + [beside_at, missing_at, missing_at + block // 2]
    )
    bounds = jnp.concatenate([bounds, load_at, places]).astype(jnp.int32)
    beside = swapped(pair, "ctx", 1)
    before, after = shifted(pair, "ctx", 2), shifted(pair, "ctx", -2)
    half = block // 2
    before, after, bounds, spans, spans_row = lax.optimization_barrier(
        (before, after, bounds, spans, spans_row)
    )
    route = [(i, i + 2 if i % 2 == 0 else i - 2) for i in range(cycle)]
    route = [(i, j) for i, j in route if 0 <= j < cycle]
    upper = swapped(jnp.where(even, after[:half], before[:half]), "ctx", 1)
    lower = lax.ppermute(beside[half:], "ctx", route)
    pairs = [before, after, pair, beside, upper, lower]
    small_own = jnp.stack(
        [out_bias, first_gain, first_shift, outer_bias, second_gain, second_shift]
    )
    small_own = jnp.concatenate([small_own, inner_bias.reshape(-1, part)], axis=0)
    small_own = jnp.pad(small_own, ((0, 16 - small_own.shape[0]), (0, width - part)))
    inner_parts = [inner_weight[:, i * width : (i + 1) * width] for i in range(shards)]
    pack = jnp.concatenate([outer_weight, out_weight, small_own] + inner_parts, axis=0)
    pack, _ = lax.optimization_barrier((pack, token_pieces[2:] + weight_pieces[1:]))
    pack_near, pack_far = swapped(pack, "wt", 1), swapped(pack, "wt", 2)
    *mixed_pieces, mixed_wide, stat_rows, stat_columns = attention_forward(
        bounds, queries, spans, pairs
    )
    ready, _ = lax.optimization_barrier((queries, pairs))
    query_halo = [queries if d == 0 else shifted(ready, "ctx", d) if d * d == 1 else None for d in distances]
    close = [x for x, d in zip(query_halo, distances) if d * d == 1]
    mixed_pieces, mixed_wide, stat_columns, close, pack_far = lax.optimization_barrier(
        (mixed_pieces, mixed_wide, stat_columns, close, pack_far)
    )
    packs = [pack, pack_near, pack_far, swapped(pack_far, "wt", 1)]

    mixed_pieces = [mixed_pieces[0]] + [
        swapped(mixed_pieces[r], "wt", r) for r in range(1, shards)
    ]
    far_ready, mixed_pieces = lax.optimization_barrier((queries, mixed_pieces))
    results = dense(
        places, mixed_pieces, tokens, cotangent, packs
    )
    remote = [shifted(far_ready, "ctx", d) for d in distances if d * d > 1]
    results, remote = lax.optimization_barrier((results, remote))
    layer_out, grad_one, *back = results[: 2 + shards]
    outer_keep, outer_send, inner_keep, inner_send = results[2 + shards :]
    query_halo = [remote[0], close[0], queries, close[1], remote[1]]

    back_pieces = [back[0]] + [swapped(back[r], "wt", r) for r in range(1, shards)]
    outer_got = swapped(outer_send, "wt", 1)
    inner_got = swapped(inner_send, "wt", 1)
    grads = gathered(places, back_pieces, mixed_wide, stat_columns)
    outer_got, _ = lax.optimization_barrier((outer_got, back_pieces[1:]))
    grads, inner_got = lax.optimization_barrier((grads, inner_got))

    def far_terms(keep, got):
        return [both(keep[0], got[0]), swapped(both(keep[1], got[1]), "wt", 2)]

    grad_halo = halo(grads)
    outer_terms = far_terms(outer_keep, outer_got)
    grad_query = attention_queries(
        bounds, queries, spans, grads, mixed_wide, stat_rows, pairs
    )
    grad_query, grad_halo, outer_terms, inner_keep, inner_got = lax.optimization_barrier(
        (grad_query, grad_halo, outer_terms, inner_keep, inner_got)
    )

    near_first = [1 << i for i in range(cycle.bit_length() - 1)]
    outer_terms = scatter_sum(outer_terms, "ctx", near_first[:1], 0)
    inner_terms = far_terms(inner_keep, inner_got)
    head_grad, token_partial = attention_keys(
        bounds, pair, spans_row, block_tokens, grad_query, weight_pieces, query_halo, grad_halo
    )
    head_grad, token_partial, outer_terms, inner_terms = lax.optimization_barrier(
        (head_grad, token_partial, outer_terms, inner_terms)
    )

    outer_part = both(*scatter_sum(outer_terms, "ctx", near_first[1:], 0))
    inner_part = both(*scatter_sum(inner_terms, "ctx", near_first, 0))
    head_part = both(*scatter_sum([head_grad], "ctx", near_first, 1))
    token_got = swapped(token_partial[1::2], "wt", 1)
    token_sum = both(*far_terms(token_partial[0::2], token_got))
    outer_total = gather_back(outer_part, "ctx", near_first, 0)
    inner_part = gather_back(inner_part, "ctx", near_first[2:], 0)
    inner_total = gather_square(inner_part, "ctx")
    head_pieces = [
        lax.dynamic_index_in_dim(head_part, w ^ r, 0, keepdims=False) for r in range(shards)
    ]
    head_pieces = [head_pieces[0]] + [swapped(head_pieces[r], "wt", r) for r in range(1, shards)]
    head_parts = jnp.stack(
        [
            lax.dynamic_index_in_dim(jnp.stack(head_pieces), w ^ k, 0, keepdims=False)
            for k in range(shards)
        ]
    )
    head_total = gather_back(head_parts, "ctx", near_first, 1)

    tokens_gradient = grad_one + token_sum.astype(f32)
    key_total, value_total, query_total = (
        jnp.concatenate(
            [head_total[k, :, i * part : (i + 1) * part] for k in range(shards)], axis=1
        ).astype(f32)
        for i in range(3)
    )
    own_total = lax.dynamic_index_in_dim(head_total, w, 0, keepdims=False)
    inner_rows = inner_total[:width].reshape(shards, part, width)
    inner_rows = jnp.concatenate([inner_rows[k] for k in range(shards)], axis=1).astype(f32)
    lines = inner_total[width + part : width + part + 16, :part].astype(f32)

    return (
        layer_out,
        tokens_gradient,
        query_total,
        key_total,
        value_total,
        inner_total[width : width + part].astype(f32),
        own_total[:, 3 * part].astype(f32),
        own_total[:, 3 * part + 1].astype(f32),
        lines[0],
        lines[1],
        lines[2],
        inner_rows,
        lines[6:10].reshape(-1),
        outer_total.astype(f32),
        lines[3],
        lines[4],
        lines[5],
    )


def solution(mesh):
    matrix, vector = P("wt", None), P("wt")
    stream = P(("ctx", "wt"), None)
    in_specs = (stream, P(), stream) + (matrix,) * 4 + (vector,) * 5
    in_specs += (matrix, vector, matrix, vector, vector, vector)
    out_specs = (stream, stream) + (matrix,) * 4 + (vector,) * 5
    out_specs += (matrix, vector, matrix, vector, vector, vector)
    return jax.shard_map(
        on_device, mesh=mesh, in_specs=in_specs, out_specs=out_specs, check_vma=False
    )
```

```python
import functools

import jax
import jax.numpy as jnp
from jax import lax
from jax.experimental import pallas as pl
from jax.experimental.pallas import tpu as pltpu
from jax.sharding import PartitionSpec as P

HEADS = 12
HEAD_DIM = 64
MAXDOC = 2048
TILE_Q = 256
SPAN_K = 768
TILE_K = 256
SPAN_Q = 768
CHUNK = 256

masked_score = -1e30
epsilon = 1e-06
bf16 = jnp.bfloat16
f32 = jnp.float32


def swapped(block, axis, bit):
    count = lax.axis_size(axis)
    return lax.ppermute(block, axis, [(i, i ^ bit) for i in range(count)])


def shifted(block, axis, distance):
    count = lax.axis_size(axis)
    route = [(i, i + distance) for i in range(count) if 0 <= i + distance < count]
    return lax.ppermute(block, axis, route)


def rows_nt(left, right):
    return lax.dot_general(left, right, (((1,), (1,)), ((), ())), preferred_element_type=f32)


def rows_nn(left, right):
    return lax.dot_general(left, right, (((1,), (0,)), ((), ())), preferred_element_type=f32)


def load_window(pieces, target, sem, starts):
    copies = []
    for i, piece in enumerate(pieces):
        rows = pl.ds(pl.multiple_of(starts[i], 128), piece.shape[0])
        copies.append(pltpu.make_async_copy(piece, target.at[rows, :], sem.at[i]))
    for copy in copies:
        copy.start()
    return copies


def head_of(tile0, tile1, head):
    lane = lax.broadcasted_iota(jnp.int32, tile0.shape, 1)
    if head == 0:
        return jnp.where(lane < HEAD_DIM, tile0, jnp.zeros_like(tile0))
    if head == 1:
        return jnp.where(lane >= HEAD_DIM, tile0, jnp.zeros_like(tile0))
    return tile1


def turned(source, target, lanes, low, high):
    def turn(i, carry):
        rows = pl.ds(pl.multiple_of(i * 256, 256), 256)
        target[:, rows] = source[rows, lanes].T
        return carry

    lax.fori_loop(low, high, turn, 0)


def inside(span_ref, first, begin, rows):
    own = pl.ds(first, TILE_Q)
    place = begin + lax.broadcasted_iota(jnp.int32, (rows, TILE_Q), 0)
    return (place >= span_ref[0:1, own]) & (place < span_ref[1:2, own])


def forward_kernel(bounds, q_ref, span_ref, *rest):
    pieces, rest = rest[:-10], rest[-10:]
    outs, (wide_ref, row_ref, stat_ref, kv, vt, sem) = rest[:4], rest[4:]
    step = pl.program_id(0)

    @pl.when(step == 0)
    def _():
        for copy in load_window(pieces, kv, sem, [bounds[10 + i] for i in range(len(pieces))]):
            copy.wait()
        turned(kv, vt, slice(192, 384), bounds[8], bounds[9])

    first = pl.multiple_of(step * TILE_Q, TILE_Q)
    here = pl.ds(first, TILE_Q)
    q_tile = q_ref[here, :]
    heads = [head_of(q_tile[:, :128], q_tile[:, 128:], h) for h in range(3)]
    lower, count = bounds[2 * step], bounds[2 * step + 1]

    def run(i, carry):
        begin = pl.multiple_of(lower + i * SPAN_K, 128)
        rows = pl.ds(begin, SPAN_K)
        allowed = inside(span_ref, first, begin, SPAN_K)
        after = []

        def ahead(h):
            score = rows_nt(kv[rows, 0:128] if h < 2 else kv[rows, 128:192], heads[h])
            return jnp.where(allowed, score, masked_score)

        coming = ahead(0)
        for h in range(3):
            score = coming
            if h < 2:
                coming = ahead(h + 1)
            before, total, accum = carry[3 * h : 3 * h + 3]
            newest = jnp.maximum(before, jnp.max(score, axis=0, keepdims=True))
            factor = jnp.exp(before - newest)
            weight = jnp.exp(score - newest)
            total = total * factor + jnp.sum(weight, axis=0, keepdims=True)
            made = rows_nn(vt[h * HEAD_DIM : (h + 1) * HEAD_DIM, rows], weight.astype(bf16))
            after += [newest, total, accum * factor + made]
        return tuple(after)

    start = (
        jnp.full((1, TILE_Q), masked_score, f32),
        jnp.zeros((1, TILE_Q), f32),
        jnp.zeros((HEAD_DIM, TILE_Q), f32),
    )
    state = lax.fori_loop(0, count, run, start * 3)
    mixed = jnp.concatenate([state[3 * h + 2] / state[3 * h + 1] for h in range(3)], axis=0).T
    line = lax.broadcasted_iota(jnp.int32, (128, TILE_Q), 0)
    stats = jnp.zeros((128, TILE_Q), f32)
    for h in range(3):
        stats = jnp.where(line == h, state[3 * h] + jnp.log(state[3 * h + 1]), stats)
    wide_ref[here, :] = mixed
    row_ref[:, here] = stats[0:8, :]
    stat_ref[here, :] = stats.T
    low = mixed.astype(bf16)
    for r, out_ref in enumerate(outs):

        @pl.when(bounds[16 + step] == r)
        def _(out_ref=out_ref):
            out_ref[...] = low


def whole_spec(shape):
    return pl.BlockSpec(shape, lambda i, *_: (0,) * len(shape))


def attention_forward(bounds, queries, spans, pieces):
    block = queries.shape[0]
    window = sum(x.shape[0] for x in pieces)
    return pl.pallas_call(
        forward_kernel,
        grid_spec=pltpu.PrefetchScalarGridSpec(
            num_scalar_prefetch=1,
            grid=(block // TILE_Q,),
            in_specs=[whole_spec(queries.shape), whole_spec(spans.shape)]
            + [pl.BlockSpec(memory_space=pl.ANY)] * len(pieces),
            out_specs=[whole_spec((TILE_Q, 192))] * 4
            + [whole_spec((block, 192)), whole_spec((8, block)), whole_spec((block, 128))],
            scratch_shapes=[
                pltpu.VMEM((window, 384), bf16),
                pltpu.VMEM((192, window), bf16),
                pltpu.SemaphoreType.DMA((len(pieces),)),
            ],
        ),
        out_shape=[jax.ShapeDtypeStruct((TILE_Q, 192), bf16)] * 4
        + [
            jax.ShapeDtypeStruct((block, 192), f32),
            jax.ShapeDtypeStruct((8, block), f32),
            jax.ShapeDtypeStruct((block, 128), f32),
        ],
        compiler_params=pltpu.CompilerParams(vmem_limit_bytes=60 * 2**20),
        cost_estimate=pl.CostEstimate(
            flops=4 * block * 2304 * 192, bytes_accessed=6 * 2**20, transcendentals=block * 2304 * 3
        ),
        name="attention_forward",
    )(bounds, queries, spans, *pieces)


def query_kernel(bounds, q_ref, span_ref, grad_ref, wide_ref, row_ref, *rest):
    pieces, (out_ref, kv, kt, sem) = rest[:-4], rest[-4:]
    step = pl.program_id(0)

    @pl.when(step == 0)
    def _():
        for copy in load_window(pieces, kv, sem, [bounds[10 + i] for i in range(len(pieces))]):
            copy.wait()
        turned(kv, kt, slice(0, 192), bounds[8], bounds[9])

    first = pl.multiple_of(step * TILE_Q, TILE_Q)
    here = pl.ds(first, TILE_Q)
    q_tile = q_ref[here, :]
    heads = [head_of(q_tile[:, :128], q_tile[:, 128:], h) for h in range(3)]
    g_tile = grad_ref[here, :]
    lane = lax.broadcasted_iota(jnp.int32, (TILE_Q, 128), 1)
    none = jnp.zeros((TILE_Q, 128), bf16)
    r_pair = pltpu.roll(g_tile[:, :128].astype(f32), HEAD_DIM, 1).astype(bf16)
    r_last = pltpu.roll(g_tile[:, 128:256].astype(f32), HEAD_DIM, 1).astype(bf16)
    grads = [
        jnp.where(lane >= HEAD_DIM, r_pair, none),
        jnp.where(lane < HEAD_DIM, r_pair, none),
        jnp.where(lane >= HEAD_DIM, r_last, none),
    ]
    product = (g_tile[:, 0:192].astype(f32) * wide_ref[here, :]).T
    deltas = [
        jnp.sum(product[h * HEAD_DIM : (h + 1) * HEAD_DIM], axis=0, keepdims=True) for h in range(3)
    ]
    logs = [row_ref[h : h + 1, here] for h in range(3)]
    lower, count = bounds[2 * step], bounds[2 * step + 1]

    def run(i, carry):
        begin = pl.multiple_of(lower + i * SPAN_K, 128)
        rows = pl.ds(begin, SPAN_K)
        allowed = inside(span_ref, first, begin, SPAN_K)
        after = []

        def ahead(h):
            score = rows_nt(kv[rows, 0:128] if h < 2 else kv[rows, 128:192], heads[h])
            return score, rows_nt(kv[rows, 128:256] if h == 0 else kv[rows, 256:384], grads[h])

        coming = ahead(0)
        for h in range(3):
            score, back = coming
            if h < 2:
                coming = ahead(h + 1)
            chance = jnp.exp(jnp.where(allowed, score - logs[h], masked_score))
            change = (chance * (back - deltas[h])).astype(bf16)
            after.append(carry[h] + rows_nn(kt[h * HEAD_DIM : (h + 1) * HEAD_DIM, rows], change))
        return tuple(after)

    sums = lax.fori_loop(0, count, run, (jnp.zeros((HEAD_DIM, TILE_Q), f32),) * 3)
    out_ref[here, :] = (jnp.concatenate(sums, axis=0).T * 0.125).astype(bf16)


def attention_queries(bounds, queries, spans, grads, wide, stats, pieces):
    block = queries.shape[0]
    window = sum(x.shape[0] for x in pieces)
    return pl.pallas_call(
        query_kernel,
        grid_spec=pltpu.PrefetchScalarGridSpec(
            num_scalar_prefetch=1,
            grid=(block // TILE_Q,),
            in_specs=[whole_spec(x.shape) for x in (queries, spans, grads, wide, stats)]
            + [pl.BlockSpec(memory_space=pl.ANY)] * len(pieces),
            out_specs=whole_spec((block, 192)),
            scratch_shapes=[
                pltpu.VMEM((window, 384), bf16),
                pltpu.VMEM((192, window), bf16),
                pltpu.SemaphoreType.DMA((len(pieces),)),
            ],
        ),
        out_shape=jax.ShapeDtypeStruct((block, 192), bf16),
        compiler_params=pltpu.CompilerParams(vmem_limit_bytes=40 * 2**20),
        cost_estimate=pl.CostEstimate(
            flops=6 * block * 2304 * 192, bytes_accessed=6 * 2**20, transcendentals=block * 2304 * 3
        ),
        name="attention_queries",
    )(bounds, queries, spans, grads, wide, stats, *pieces)


def weight_copies(bounds, pieces, weight, sem):
    part = pieces[0].shape[0]
    copies = []
    for r, piece in enumerate(pieces):
        where = pl.ds(pl.multiple_of(bounds[16 + r] * part, part), part)
        copies.append(pltpu.make_async_copy(piece, weight.at[where, :], sem.at[r]))
    return copies


def head_terms(bounds, tokens_ref, query_ref, pair_ref, weight, grad_ref, back_ref):
    groups, part = grad_ref.shape[0], grad_ref.shape[1]
    rows = back_ref.shape[1]
    tokens = tokens_ref[...]
    pair_grad = rows_tn(tokens, pair_ref[...]).astype(bf16)
    query_grad = rows_tn(tokens, query_ref[...]).astype(bf16)
    for k in range(groups):
        here = slice(k * part, (k + 1) * part)
        grad_ref[k, :, 0 : 2 * part] = pair_grad[here]
        grad_ref[k, :, 2 * part : 3 * part] = query_grad[here]
    ones = jnp.ones((tokens.shape[0], HEAD_DIM), bf16)
    query_sum = rows_tn(query_ref[...], ones)
    value_sum = rows_tn(pair_ref[:, part:], ones)
    lane = lax.broadcasted_iota(jnp.int32, (part, HEAD_DIM), 1)
    sums = jnp.where(lane == 0, query_sum, jnp.where(lane == 1, value_sum, 0.0))
    grad_ref[:, :, 3 * part : 3 * part + HEAD_DIM] = jnp.zeros((groups, part, HEAD_DIM), bf16)
    grad_ref[bounds[16], :, 3 * part : 3 * part + HEAD_DIM] = sums.astype(bf16)
    for k in range(groups):
        here = slice(k * rows, (k + 1) * rows)
        made = rows_nt(pair_ref[here, :], weight[:, : 2 * part])
        made = made + rows_nt(query_ref[here, :], weight[:, 2 * part :])
        back_ref[bounds[16 + k]] = made.astype(bf16)


def key_kernel(reach, bounds, kv_ref, span_ref, tokens_ref, query_ref, *rest):
    window = 2 * reach + 1
    w_pieces, rest = rest[:4], rest[4:]
    q_pieces, g_pieces = rest[:window], rest[window : 2 * window]
    grad_ref, back_ref, qs, gs, key_sum, value_sum, out_ref, weight, sem, w_sem = rest[2 * window :]
    step = pl.program_id(0)
    block = q_pieces[0].shape[0]

    @pl.when(step == 0)
    def _():
        copies = load_window(q_pieces, qs, sem.at[0], [i * block for i in range(window)])
        copies += load_window(g_pieces, gs, sem.at[1], [i * block for i in range(window)])
        for copy in weight_copies(bounds, w_pieces, weight, w_sem):
            copy.start()
        for copy in copies:
            copy.wait()

    first = pl.multiple_of(step * TILE_K, TILE_K)
    here = pl.ds(first, TILE_K)
    key_sum[...] = jnp.zeros_like(key_sum)
    value_sum[...] = jnp.zeros_like(value_sum)
    keys_pair = kv_ref[here, 0:128]
    keys = [head_of(keys_pair, kv_ref[here, 128:192], h) for h in range(3)]
    lane = lax.broadcasted_iota(jnp.int32, (TILE_K, 128), 1)
    zero = jnp.zeros((TILE_K, 128), f32)
    v_one = pltpu.roll(kv_ref[here, 128:256].astype(f32), HEAD_DIM, 1)
    v_two = pltpu.roll(kv_ref[here, 256:384].astype(f32), HEAD_DIM, 1)
    values = [
        jnp.where(lane < HEAD_DIM, v_one, zero).astype(bf16),
        jnp.where(lane < HEAD_DIM, zero, v_two).astype(bf16),
        v_two.astype(bf16)[:, :HEAD_DIM],
    ]
    line = lax.broadcasted_iota(jnp.int32, (16, HEAD_DIM), 0)
    slot = lax.broadcasted_iota(jnp.int32, (16, HEAD_DIM), 1)
    selector = jnp.where((slot // 3 == line) & (slot < 18), 1.0, 0.0).astype(bf16)
    lower, count = bounds[2 * step], bounds[2 * step + 1]

    def run(i, carry):
        begin = pl.multiple_of(lower + i * SPAN_Q, 128)
        columns = pl.ds(begin, SPAN_Q)
        place = reach * block + first + lax.broadcasted_iota(jnp.int32, (TILE_K, SPAN_Q), 0)
        allowed = (place >= span_ref[0:1, columns]) & (place < span_ref[1:2, columns])
        lanes = [slice(0, 128), slice(0, 128), slice(128, 192)]
        stats = rows_nt(selector, gs[columns, 192:256])
        items = [(h, ch) for h in range(3) for ch in range(SPAN_Q // CHUNK)]

        def ahead(item):
            h, ch = item
            here = pl.ds(pl.multiple_of(begin + ch * CHUNK, 128), CHUNK)
            q_tile, g_tile = qs[here, lanes[h]], gs[here, lanes[h]]
            return q_tile, g_tile, rows_nt(keys[h], q_tile), rows_nt(values[h], g_tile)

        coming = ahead(items[0])
        for n, (h, ch) in enumerate(items):
            q_tile, g_tile, score, back = coming
            if n + 1 < len(items):
                coming = ahead(items[n + 1])
            cols = slice(ch * CHUNK, (ch + 1) * CHUNK)
            score = jnp.where(allowed[:, cols], score - stats[h : h + 1, cols], masked_score)
            chance = jnp.exp(score)
            change = (chance * (back - stats[h + 3 : h + 4, cols])).astype(bf16)
            size = 128 if h < 2 else HEAD_DIM
            key_sum[h, :, 0:size] += rows_nn(change, q_tile)
            value_sum[h, :, 0:size] += rows_nn(chance.astype(bf16), g_tile)
        return carry

    lax.fori_loop(0, count, run, 0)
    k_pair = jnp.where(lane < HEAD_DIM, key_sum[0], key_sum[1])
    v_pair = jnp.where(lane < HEAD_DIM, value_sum[0], value_sum[1])
    v_turn = pltpu.roll(v_pair, HEAD_DIM, 1)
    last_turn = pltpu.roll(value_sum[2], HEAD_DIM, 1)
    out_ref[here, 0:128] = k_pair.astype(bf16)
    out_ref[here, 128:256] = jnp.where(lane < HEAD_DIM, key_sum[2], v_turn).astype(bf16)
    out_ref[here, 256:384] = jnp.where(lane < HEAD_DIM, v_turn, last_turn).astype(bf16)

    @pl.when(step == pl.num_programs(0) - 1)
    def _():
        for copy in weight_copies(bounds, w_pieces, weight, w_sem):
            copy.wait()
        head_terms(bounds, tokens_ref, query_ref, out_ref, weight, grad_ref, back_ref)


def attention_keys(bounds, pair, spans, tokens, grad_query, weight_pieces, q_pieces, g_pieces):
    block, width = tokens.shape
    count = len(q_pieces)
    groups, part = len(weight_pieces), weight_pieces[0].shape[0]
    return pl.pallas_call(
        functools.partial(key_kernel, count // 2),
        grid_spec=pltpu.PrefetchScalarGridSpec(
            num_scalar_prefetch=1,
            grid=(block // TILE_K,),
            in_specs=[whole_spec(x.shape) for x in (pair, spans, tokens, grad_query)]
            + [pl.BlockSpec(memory_space=pl.ANY)] * (groups + 2 * count),
            out_specs=[
                whole_spec((groups, part, 3 * part + HEAD_DIM)),
                whole_spec((groups, block // groups, width)),
            ],
            scratch_shapes=[
                pltpu.VMEM((count * block, 192), bf16),
                pltpu.VMEM((count * block, 256), bf16),
                pltpu.VMEM((3, TILE_K, 128), f32),
                pltpu.VMEM((3, TILE_K, 128), f32),
                pltpu.VMEM((block, 384), bf16),
                pltpu.VMEM((width, 3 * part), bf16),
                pltpu.SemaphoreType.DMA((2, count)),
                pltpu.SemaphoreType.DMA((groups,)),
            ],
        ),
        out_shape=[
            jax.ShapeDtypeStruct((groups, part, 3 * part + HEAD_DIM), bf16),
            jax.ShapeDtypeStruct((groups, block // groups, width), bf16),
        ],
        compiler_params=pltpu.CompilerParams(vmem_limit_bytes=60 * 2**20),
        cost_estimate=pl.CostEstimate(
            flops=10 * block * 2304 * 192, bytes_accessed=12 * 2**20, transcendentals=block * 2304 * 3
        ),
        name="attention_keys",
    )(bounds, pair, spans, tokens, grad_query, *weight_pieces, *q_pieces, *g_pieces)


def projection_kernel(place_ref, own, near, far, corner, w_own, w_near, w_far, w_corner, bias_ref, *rest):
    tokens_ref, query_ref, pair_ref, weight, sem = rest
    rows, part = own.shape[0], w_own.shape[0]
    pieces = (w_own, w_near, w_far, w_corner)
    copies = []
    for r, piece in enumerate(pieces):
        where = pl.multiple_of(place_ref[r] * part, part)
        copies.append(pltpu.make_async_copy(piece, weight.at[pl.ds(where, part), :], sem.at[r]))
        copies[-1].start()
    for copy in copies:
        copy.wait()
    for r, piece in enumerate((own, near, far, corner)):
        here = pl.ds(pl.multiple_of(place_ref[r] * rows, rows), rows)
        tile = piece[...]
        tokens_ref[here, :] = tile
        made = rows_nn(tile, weight[...]) + bias_ref[0:1, :]
        pair_ref[here, :] = made[:, : 2 * part].astype(bf16)
        query_ref[here, :] = (made[:, 2 * part :].astype(bf16).astype(f32) * 0.125).astype(bf16)


def project(places, token_pieces, weight_pieces, bias):
    rows, width = token_pieces[0].shape
    part = weight_pieces[0].shape[0]
    block = rows * len(token_pieces)
    vmem = pl.BlockSpec(memory_space=pltpu.VMEM)
    return pl.pallas_call(
        projection_kernel,
        in_specs=[pl.BlockSpec(memory_space=pltpu.SMEM)]
        + [vmem] * 4
        + [pl.BlockSpec(memory_space=pl.ANY)] * 4
        + [vmem],
        out_specs=[vmem] * 3,
        out_shape=[
            jax.ShapeDtypeStruct((block, width), bf16),
            jax.ShapeDtypeStruct((block, part), bf16),
            jax.ShapeDtypeStruct((block, 2 * part), bf16),
        ],
        scratch_shapes=[pltpu.VMEM((width, 3 * part), bf16), pltpu.SemaphoreType.DMA((4,))],
        compiler_params=pltpu.CompilerParams(vmem_limit_bytes=32 * 2**20),
        cost_estimate=pl.CostEstimate(
            flops=2 * block * width * 3 * part, bytes_accessed=5 * 2**20, transcendentals=0
        ),
        name="layer_projection",
    )(places, *token_pieces, *weight_pieces, bias)


def normal_of(values):
    center = values - jnp.mean(values, axis=1, keepdims=True)
    inverse = lax.rsqrt(jnp.mean(center * center, axis=1, keepdims=True) + epsilon)
    return center * inverse, inverse


def normal_back(upstream, normal, inverse, gain):
    scaled = upstream * gain
    mean_scaled = jnp.mean(scaled, axis=1, keepdims=True)
    mean_product = jnp.mean(scaled * normal, axis=1, keepdims=True)
    return (scaled - mean_scaled - normal * mean_product) * inverse


def rows_tn(left, right):
    return lax.dot_general(left, right, (((0,), (0,)), ((), ())), preferred_element_type=f32)


def dense_kernel(place_ref, *refs):
    mixed = refs[0:4]
    tokens_ref, up_ref = refs[4:6]
    packs = refs[6:10]
    out_ref, grad_ref = refs[10:12]
    back_refs = refs[12:16]
    outer_refs, inner_refs = refs[16:18], refs[18:20]
    w_out, w_inner, w_outer, hidden, activated, slopes = refs[20:26]
    outer_made, inner_made, tail_made, lines, bias_rows, sem, sent = refs[26:]
    rows, width = tokens_ref.shape
    groups = w_inner.shape[0]
    part = width // groups

    def inner_copies(g):
        return [
            pltpu.make_async_copy(
                packs[r].at[pl.ds(pl.multiple_of(width + part + 16 + g * part, 16), part), :],
                w_inner.at[g, pl.ds(pl.multiple_of(place_ref[r] * part, part), part), :],
                sem.at[1 + g, r],
            )
            for r in range(groups)
        ]

    out_copies = [
        pltpu.make_async_copy(packs[r].at[pl.ds(width, part), :], w_out.at[r], sem.at[0, r])
        for r in range(groups)
    ]
    outer_copies = [
        pltpu.make_async_copy(
            packs[r].at[pl.ds(0, width), :], w_outer.at[place_ref[r]], sem.at[1 + groups, r]
        )
        for r in range(groups)
    ]
    line_copies = [
        pltpu.make_async_copy(
            packs[r].at[pl.ds(width + part, 16), :], lines.at[place_ref[r]], sem.at[2 + groups, r]
        )
        for r in range(groups)
    ]
    for copy in line_copies + out_copies + [x for g in range(groups) for x in inner_copies(g)] + outer_copies:
        copy.start()

    for copy in line_copies:
        copy.wait()
    small = [lines[k][:, 0:part].astype(f32) for k in range(groups)]
    out_bias, gain_one, shift_one, outer_bias, gain_two, shift_two = (
        jnp.concatenate([x[i : i + 1] for x in small], axis=1) for i in range(6)
    )
    for k in range(groups):
        bias_rows[k : k + 1, :] = jnp.concatenate(
            [small[k][6 + i : 7 + i] for i in range(groups)], axis=1
        )
    for copy in out_copies:
        copy.wait()
    residual = tokens_ref[...].astype(f32) + out_bias
    for r in range(groups):
        residual = residual + rows_nn(mixed[r][...], w_out[r])
    normal_one, inverse_one = normal_of(residual)
    first = normal_one * gain_one + shift_one
    first_low = first.astype(bf16)

    def ahead(g, carry):
        for copy in inner_copies(g):
            copy.wait()
        value = rows_nn(first_low, w_inner[g]) + bias_rows[pl.ds(g, 1), :]
        chance = 0.5 * (1.0 + lax.erf(value * (2.0**-0.5)))
        density = jnp.exp(-0.5 * value * value) * (2.0 * jnp.pi) ** -0.5
        slopes[g] = chance + value * density
        activated[g] = (value * chance).astype(bf16)
        return carry

    lax.fori_loop(0, groups, ahead, 0)
    for copy in outer_copies:
        copy.wait()

    def combine(g, total):
        return total + rows_nn(activated[g], w_outer[g])

    residual = lax.fori_loop(0, groups, combine, first + outer_bias)
    normal_two, inverse_two = normal_of(residual)
    out_ref[...] = (normal_two * gain_two + shift_two).astype(bf16)
    upstream = up_ref[...].astype(f32)
    grad_two = normal_back(upstream, normal_two, inverse_two, gain_two)
    grad_two_low = grad_two.astype(bf16)
    shift_two_sum = jnp.sum(upstream, axis=0, keepdims=True)
    gain_two_sum = jnp.sum(upstream * normal_two, axis=0, keepdims=True)
    outer_bias_sum = jnp.sum(grad_two_low.astype(f32), axis=0, keepdims=True)

    def outer_copy(i, odd):
        r = 2 * i + odd
        return pltpu.make_async_copy(outer_made.at[r], outer_refs[odd].at[i], sent.at[0, r])

    def behind(i, total):
        for odd in range(2):
            g = place_ref[2 * i + odd]
            outer_made[2 * i + odd] = rows_tn(activated[g], grad_two_low).astype(bf16)
            outer_copy(i, odd).start()
            value = (rows_nt(grad_two_low, w_outer[g]) * slopes[g]).astype(bf16)
            hidden[g] = value
            total = total + rows_nt(value, w_inner[g])
        return total

    grad_first = lax.fori_loop(0, groups // 2, behind, grad_two)
    grad_one = normal_back(grad_first, normal_one, inverse_one, gain_one)
    grad_ref[...] = grad_one
    grad_one_low = grad_one.astype(bf16)
    for r in range(groups):
        back_refs[r][...] = rows_nt(grad_one_low, w_out[r]).astype(bf16)

    def inner_sends(g):
        return [
            pltpu.make_async_copy(
                inner_made.at[g, pl.ds(pl.multiple_of(place_ref[r] * part, part), part), :],
                inner_refs[r % 2].at[r // 2, pl.ds(pl.multiple_of(g * part, part), part), :],
                sent.at[1 + g, r],
            )
            for r in range(groups)
        ]

    def weigh(g, carry):
        inner_made[g] = rows_tn(first_low, hidden[g]).astype(bf16)
        for copy in inner_sends(g):
            copy.start()
        return carry

    lax.fori_loop(0, groups, weigh, 0)
    sums = [
        jnp.sum(grad_one_low.astype(f32), axis=0, keepdims=True),
        jnp.sum(grad_first * normal_one, axis=0, keepdims=True),
        jnp.sum(grad_first, axis=0, keepdims=True),
        outer_bias_sum,
        gain_two_sum,
        shift_two_sum,
    ]
    line = lax.broadcasted_iota(jnp.int32, (16, part), 0)
    tail_made[:, part:, :] = jnp.zeros((groups, 64, width), bf16)
    for r in range(groups):
        tail_made[r, 0:part, :] = rows_tn(mixed[r][...], grad_one_low).astype(bf16)
    for k in range(groups):
        tail = jnp.zeros((16, part), f32)
        for i, line_sum in enumerate(sums):
            tail = jnp.where(line == i, line_sum[:, k * part : (k + 1) * part], tail)
        bias_sum = jnp.sum(hidden[k].astype(f32), axis=0, keepdims=True)
        for i in range(groups):
            tail = jnp.where(
                line == len(sums) + i, bias_sum[:, i * part : (i + 1) * part], tail
            )
        tail_made[place_ref[k], part : part + 16, 0:part] = tail.astype(bf16)
    tail_copies = [
        pltpu.make_async_copy(
            tail_made.at[r], inner_refs[r % 2].at[r // 2, pl.ds(width, part + 64), :], sent.at[1 + groups, r]
        )
        for r in range(groups)
    ]
    for copy in tail_copies:
        copy.start()
    for i in range(groups // 2):
        for odd in range(2):
            outer_copy(i, odd).wait()
    for g in range(groups):
        for copy in inner_sends(g):
            copy.wait()
    for copy in tail_copies:
        copy.wait()


def dense(places, mixed_pieces, tokens, cotangent, packs):
    rows, width = tokens.shape
    groups = len(packs)
    part = width // groups
    vmem = pl.BlockSpec(memory_space=pltpu.VMEM)
    hbm = pl.BlockSpec(memory_space=pl.ANY)
    return pl.pallas_call(
        dense_kernel,
        in_specs=[pl.BlockSpec(memory_space=pltpu.SMEM)] + [vmem] * (groups + 2) + [hbm] * groups,
        out_specs=[vmem] * (2 + groups) + [hbm] * 4,
        out_shape=[
            jax.ShapeDtypeStruct((rows, width), bf16),
            jax.ShapeDtypeStruct((rows, width), f32),
        ]
        + [jax.ShapeDtypeStruct((rows, part), bf16)] * groups
        + [jax.ShapeDtypeStruct((groups // 2, width, width), bf16)] * 2
        + [jax.ShapeDtypeStruct((groups // 2, width + part + 64, width), bf16)] * 2,
        scratch_shapes=[
            pltpu.VMEM((groups, part, width), bf16),
            pltpu.VMEM((groups, width, width), bf16),
            pltpu.VMEM((groups, width, width), bf16),
            pltpu.VMEM((groups, rows, width), bf16),
            pltpu.VMEM((groups, rows, width), bf16),
            pltpu.VMEM((groups, rows, width), f32),
            pltpu.VMEM((groups, width, width), bf16),
            pltpu.VMEM((groups, width, width), bf16),
            pltpu.VMEM((groups, part + 64, width), bf16),
            pltpu.VMEM((groups, 16, width), bf16),
            pltpu.VMEM((8, width), f32),
            pltpu.SemaphoreType.DMA((groups + 3, groups)),
            pltpu.SemaphoreType.DMA((groups + 2, groups)),
        ],
        compiler_params=pltpu.CompilerParams(vmem_limit_bytes=48 * 2**20),
        cost_estimate=pl.CostEstimate(
            flops=24 * rows * width * width * groups,
            bytes_accessed=24 * 2**20,
            transcendentals=2 * rows * width * groups,
        ),
        name="layer_dense",
    )(places, *mixed_pieces, tokens, cotangent, *packs)


def gather_kernel(place_ref, p0, p1, p2, p3, wide_ref, stat_ref, out_ref):
    rows, part = p0.shape
    lane = lax.broadcasted_iota(jnp.int32, (rows, 128), 1)
    slot = lax.broadcasted_iota(jnp.int32, (rows, HEAD_DIM), 1)
    for r, piece in enumerate((p0, p1, p2, p3)):
        here = pl.ds(pl.multiple_of(place_ref[r] * rows, rows), rows)
        tile = piece[...]
        product = tile.astype(f32) * wide_ref[here, :]
        pair, last = product[:, 0:128], product[:, 128:192]
        values = [stat_ref[here, h : h + 1] for h in range(3)] + [
            jnp.sum(jnp.where(lane < HEAD_DIM, pair, 0.0), axis=1, keepdims=True),
            jnp.sum(jnp.where(lane < HEAD_DIM, 0.0, pair), axis=1, keepdims=True),
            jnp.sum(last, axis=1, keepdims=True),
        ]
        tail = jnp.zeros((rows, HEAD_DIM), f32)
        for i, left in enumerate(values):
            for j in range(3):
                high = left.astype(bf16).astype(f32)
                tail = jnp.where(slot == 3 * i + j, high, tail)
                left = left - high
        out_ref[here, 0:192] = tile
        out_ref[here, 192:256] = tail.astype(bf16)


def gathered(places, pieces, wide, stats):
    block = wide.shape[0]
    vmem = pl.BlockSpec(memory_space=pltpu.VMEM)
    return pl.pallas_call(
        gather_kernel,
        in_specs=[pl.BlockSpec(memory_space=pltpu.SMEM)] + [vmem] * 6,
        out_specs=vmem,
        out_shape=jax.ShapeDtypeStruct((block, 256), bf16),
        compiler_params=pltpu.CompilerParams(vmem_limit_bytes=16 * 2**20),
        cost_estimate=pl.CostEstimate(flops=2**20, bytes_accessed=3 * 2**20, transcendentals=0),
        name="layer_gather",
    )(places, *pieces, wide, stats)


def both(left, right):
    return (left.astype(f32) + right.astype(f32)).astype(bf16)


def half_of(block, bit, axis):
    size = block.shape[axis] // 2
    return lax.dynamic_slice_in_dim(block, bit * size, size, axis)


def scatter_sum(terms, axis_name, order, axis):
    index = lax.axis_index(axis_name)
    for step in order:
        bit = (index // step) % 2
        sent = functools.reduce(both, [half_of(x, 1 - bit, axis) for x in terms])
        kept = functools.reduce(both, [half_of(x, bit, axis) for x in terms])
        terms = [kept, swapped(sent, axis_name, step)]
    return terms


def gather_back(block, axis_name, order, axis):
    index = lax.axis_index(axis_name)
    for step in reversed(order):
        other = swapped(block, axis_name, step)
        late = (index // step) % 2 == 1
        block = jnp.where(
            late,
            jnp.concatenate([other, block], axis),
            jnp.concatenate([block, other], axis),
        )
    return block


def gather_square(block, axis_name):
    index = lax.axis_index(axis_name)
    rows, width = block.shape
    first, second = block[: rows // 2], block[rows // 2 :]
    first_got = swapped(first, axis_name, 1)
    second_got = swapped(second, axis_name, 2)
    first_got, second_got = lax.optimization_barrier((first_got, second_got))
    first_far = swapped(jnp.concatenate([first, first_got]), axis_name, 2)
    second_far = swapped(jnp.concatenate([second, second_got]), axis_name, 1)
    size = rows // 2
    ours = [
        (first, second),
        (first_far[:size], second_got),
        (first_got, second_far[:size]),
        (first_far[size:], second_far[size:]),
    ]
    low, high = index % 2 == 1, (index // 2) % 2 == 1
    placed = []
    for x in range(2):
        for z in range(2):
            for half in range(2):
                near = jnp.where(high, ours[2 * x + 1 - z][half], ours[2 * x + z][half])
                across = jnp.where(
                    high, ours[2 * (1 - x) + 1 - z][half], ours[2 * (1 - x) + z][half]
                )
                placed.append(jnp.where(low, across, near))
    return jnp.concatenate(placed, axis=0)


def on_device(
    tokens,
    doc_start,
    cotangent,
    query_weight,
    key_weight,
    value_weight,
    out_weight,
    query_bias,
    value_bias,
    out_bias,
    first_gain,
    first_shift,
    inner_weight,
    inner_bias,
    outer_weight,
    outer_bias,
    second_gain,
    second_shift,
):
    rows, width = tokens.shape
    cycle = lax.axis_size("ctx")
    shards = lax.axis_size("wt")
    block = rows * shards
    reach = (MAXDOC + block - 2) // block
    window = (2 * reach + 1) * block
    c = lax.axis_index("ctx")
    w = lax.axis_index("wt")
    part = width // shards
    places = jnp.stack([w ^ r for r in range(shards)]).astype(jnp.int32)

    def spread(own, near):
        far = swapped(own, "wt", 2)
        return [own, near, far, swapped(far, "wt", 1)]

    def columns(r):
        start = (w ^ r) * part
        return jnp.concatenate(
            [
                lax.dynamic_slice_in_dim(x, start, part, 1)
                for x in (key_weight, value_weight, query_weight)
            ],
            axis=1,
        )

    token_pieces = spread(tokens, swapped(tokens, "wt", 1))
    weight_pieces = [columns(0)] + [swapped(columns(r), "wt", r) for r in range(1, shards)]
    head_bias = jnp.concatenate([jnp.zeros((part,), f32), value_bias.astype(f32), query_bias.astype(f32)])
    head_bias = jnp.broadcast_to(head_bias[None], (8, 3 * part))

    pad = reach * block
    padded = jnp.pad(doc_start, (pad, pad), constant_values=-1)
    base = c * block - pad
    marks = lax.dynamic_slice_in_dim(padded, c * block, window)
    place = jnp.arange(window, dtype=jnp.int32)
    begins = jnp.where((marks == base + place) | (marks < 0), place, window)
    next_begin = lax.cummin(begins, axis=0, reverse=True)
    stops = jnp.concatenate([next_begin[1:], jnp.full((1,), window, jnp.int32)])
    starts = marks - base
    own_starts = starts[pad : pad + block]
    own_stops = stops[pad : pad + block]
    spans_row = jnp.stack([starts, stops] + [jnp.zeros_like(starts)] * 6)
    spans = spans_row[:, pad : pad + block]
    lowest = own_starts.reshape(-1, TILE_Q)[:, 0] // 128 * 128
    highest = own_stops.reshape(-1, TILE_Q)[:, -1]
    count = (highest - lowest + SPAN_K - 1) // SPAN_K
    lowest = jnp.minimum(lowest, (window - count * SPAN_K) // 128 * 128)
    reached = jnp.stack([jnp.min(lowest) // 256, (jnp.max(lowest + count * SPAN_K) + 255) // 256])
    bounds = jnp.concatenate([jnp.stack([lowest, count], axis=1).reshape(-1), reached])

    block_tokens, queries, pair = project(places, token_pieces, weight_pieces, head_bias)

    distances = [d for d in range(reach, -reach - 1, -1)]

    def halo(own):
        return [own if d == 0 else shifted(own, "ctx", d) for d in distances]

    even = c % 2 == 0
    beside_at = jnp.where(even, reach + 1, reach - 1) * block
    missing_at = jnp.where(even, reach - 1, reach + 1) * block
    load_at = jnp.stack(
        [0 * missing_at, 2 * reach * block + 0 * missing_at, reach * block + 0 * missing_at]
        + [beside_at, missing_at, missing_at + block // 2]
    )
    bounds = jnp.concatenate([bounds, load_at, places]).astype(jnp.int32)
    beside = swapped(pair, "ctx", 1)
    before, after = shifted(pair, "ctx", 2), shifted(pair, "ctx", -2)
    half = block // 2
    before, after, bounds, spans, spans_row = lax.optimization_barrier(
        (before, after, bounds, spans, spans_row)
    )
    route = [(i, i + 2 if i % 2 == 0 else i - 2) for i in range(cycle)]
    route = [(i, j) for i, j in route if 0 <= j < cycle]
    upper = swapped(jnp.where(even, after[:half], before[:half]), "ctx", 1)
    lower = lax.ppermute(beside[half:], "ctx", route)
    pairs = [before, after, pair, beside, upper, lower]
    small_own = jnp.stack(
        [out_bias, first_gain, first_shift, outer_bias, second_gain, second_shift]
    )
    small_own = jnp.concatenate([small_own, inner_bias.reshape(-1, part)], axis=0)
    small_own = jnp.pad(small_own, ((0, 16 - small_own.shape[0]), (0, width - part)))
    inner_parts = [inner_weight[:, i * width : (i + 1) * width] for i in range(shards)]
    pack = jnp.concatenate([outer_weight, out_weight, small_own] + inner_parts, axis=0)
    pack, _ = lax.optimization_barrier((pack, token_pieces[2:] + weight_pieces[1:]))
    pack_near, pack_far = swapped(pack, "wt", 1), swapped(pack, "wt", 2)
    *mixed_pieces, mixed_wide, stat_rows, stat_columns = attention_forward(
        bounds, queries, spans, pairs
    )
    ready, _ = lax.optimization_barrier((queries, [before, after, beside]))
    query_halo = [queries if d == 0 else shifted(ready, "ctx", d) if d * d > 1 else None for d in distances]
    close = [x for x, d in zip(query_halo, distances) if d * d > 1]
    mixed_pieces, mixed_wide, stat_columns, close, pack_far = lax.optimization_barrier(
        (mixed_pieces, mixed_wide, stat_columns, close, pack_far)
    )
    packs = [pack, pack_near, pack_far, swapped(pack_far, "wt", 1)]

    mixed_pieces = [mixed_pieces[0]] + [
        swapped(mixed_pieces[r], "wt", r) for r in range(1, shards)
    ]
    far_ready, mixed_pieces = lax.optimization_barrier((queries, mixed_pieces))
    results = dense(
        places, mixed_pieces, tokens, cotangent, packs
    )
    remote = [shifted(far_ready, "ctx", d) for d in distances if d * d == 1]
    results, remote = lax.optimization_barrier((results, remote))
    layer_out, grad_one, *back = results[: 2 + shards]
    outer_keep, outer_send, inner_keep, inner_send = results[2 + shards :]
    query_halo = [close[0], remote[0], queries, remote[1], close[1]]

    back_pieces = [back[0]] + [swapped(back[r], "wt", r) for r in range(1, shards)]
    outer_got = swapped(outer_send, "wt", 1)
    inner_got = swapped(inner_send, "wt", 1)
    grads = gathered(places, back_pieces, mixed_wide, stat_columns)
    outer_got, _ = lax.optimization_barrier((outer_got, back_pieces[1:]))
    grads, inner_got = lax.optimization_barrier((grads, inner_got))

    def far_terms(keep, got):
        return [both(keep[0], got[0]), swapped(both(keep[1], got[1]), "wt", 2)]

    grad_halo = halo(grads)
    outer_terms = far_terms(outer_keep, outer_got)
    grad_query = attention_queries(
        bounds, queries, spans, grads, mixed_wide, stat_rows, pairs
    )
    grad_query, grad_halo, outer_terms, inner_keep, inner_got = lax.optimization_barrier(
        (grad_query, grad_halo, outer_terms, inner_keep, inner_got)
    )

    near_first = [1 << i for i in range(cycle.bit_length() - 1)]
    outer_terms = scatter_sum(outer_terms, "ctx", near_first[:1], 0)
    inner_terms = far_terms(inner_keep, inner_got)
    head_grad, token_partial = attention_keys(
        bounds, pair, spans_row, block_tokens, grad_query, weight_pieces, query_halo, grad_halo
    )
    head_grad, token_partial, outer_terms, inner_terms = lax.optimization_barrier(
        (head_grad, token_partial, outer_terms, inner_terms)
    )

    outer_part = both(*scatter_sum(outer_terms, "ctx", near_first[1:], 0))
    inner_part = both(*scatter_sum(inner_terms, "ctx", near_first, 0))
    head_part = both(*scatter_sum([head_grad], "ctx", near_first, 1))
    token_got = swapped(token_partial[1::2], "wt", 1)
    token_sum = both(*far_terms(token_partial[0::2], token_got))
    outer_total = gather_back(outer_part, "ctx", near_first, 0)
    inner_part = gather_back(inner_part, "ctx", near_first[2:], 0)
    inner_total = gather_square(inner_part, "ctx")
    head_pieces = [
        lax.dynamic_index_in_dim(head_part, w ^ r, 0, keepdims=False) for r in range(shards)
    ]
    head_pieces = [head_pieces[0]] + [swapped(head_pieces[r], "wt", r) for r in range(1, shards)]
    head_parts = jnp.stack(
        [
            lax.dynamic_index_in_dim(jnp.stack(head_pieces), w ^ k, 0, keepdims=False)
            for k in range(shards)
        ]
    )
    head_total = gather_back(head_parts, "ctx", near_first, 1)

    tokens_gradient = grad_one + token_sum.astype(f32)
    key_total, value_total, query_total = (
        jnp.concatenate(
            [head_total[k, :, i * part : (i + 1) * part] for k in range(shards)], axis=1
        ).astype(f32)
        for i in range(3)
    )
    own_total = lax.dynamic_index_in_dim(head_total, w, 0, keepdims=False)
    inner_rows = inner_total[:width].reshape(shards, part, width)
    inner_rows = jnp.concatenate([inner_rows[k] for k in range(shards)], axis=1).astype(f32)
    lines = inner_total[width + part : width + part + 16, :part].astype(f32)

    return (
        layer_out,
        tokens_gradient,
        query_total,
        key_total,
        value_total,
        inner_total[width : width + part].astype(f32),
        own_total[:, 3 * part].astype(f32),
        own_total[:, 3 * part + 1].astype(f32),
        lines[0],
        lines[1],
        lines[2],
        inner_rows,
        lines[6:10].reshape(-1),
        outer_total.astype(f32),
        lines[3],
        lines[4],
        lines[5],
    )


def solution(mesh):
    matrix, vector = P("wt", None), P("wt")
    stream = P(("ctx", "wt"), None)
    in_specs = (stream, P(), stream) + (matrix,) * 4 + (vector,) * 5
    in_specs += (matrix, vector, matrix, vector, vector, vector)
    out_specs = (stream, stream) + (matrix,) * 4 + (vector,) * 5
    out_specs += (matrix, vector, matrix, vector, vector, vector)
    return jax.shard_map(
        on_device, mesh=mesh, in_specs=in_specs, out_specs=out_specs, check_vma=False
    )
```

```python
import functools

import jax
import jax.numpy as jnp
from jax import lax
from jax.experimental import pallas as pl
from jax.experimental.pallas import tpu as pltpu
from jax.sharding import PartitionSpec as P

HEADS = 12
HEAD_DIM = 64
MAXDOC = 2048
TILE_Q = 256
SPAN_K = 768
TILE_K = 256
SPAN_Q = 768
CHUNK = 256

masked_score = -1e30
epsilon = 1e-06
bf16 = jnp.bfloat16
f32 = jnp.float32


def swapped(block, axis, bit):
    count = lax.axis_size(axis)
    return lax.ppermute(block, axis, [(i, i ^ bit) for i in range(count)])


def shifted(block, axis, distance):
    count = lax.axis_size(axis)
    route = [(i, i + distance) for i in range(count) if 0 <= i + distance < count]
    return lax.ppermute(block, axis, route)


def rows_nt(left, right):
    return lax.dot_general(left, right, (((1,), (1,)), ((), ())), preferred_element_type=f32)


def rows_nn(left, right):
    return lax.dot_general(left, right, (((1,), (0,)), ((), ())), preferred_element_type=f32)


def load_window(pieces, target, sem, starts):
    copies = []
    for i, piece in enumerate(pieces):
        rows = pl.ds(pl.multiple_of(starts[i], 128), piece.shape[0])
        copies.append(pltpu.make_async_copy(piece, target.at[rows, :], sem.at[i]))
    for copy in copies:
        copy.start()
    return copies


def head_of(tile0, tile1, head):
    lane = lax.broadcasted_iota(jnp.int32, tile0.shape, 1)
    if head == 0:
        return jnp.where(lane < HEAD_DIM, tile0, jnp.zeros_like(tile0))
    if head == 1:
        return jnp.where(lane >= HEAD_DIM, tile0, jnp.zeros_like(tile0))
    return tile1


def turned(source, target, lanes, low, high):
    def turn(i, carry):
        rows = pl.ds(pl.multiple_of(i * 256, 256), 256)
        target[:, rows] = source[rows, lanes].T
        return carry

    lax.fori_loop(low, high, turn, 0)


def inside(span_ref, first, begin, rows):
    own = pl.ds(first, TILE_Q)
    place = begin + lax.broadcasted_iota(jnp.int32, (rows, TILE_Q), 0)
    return (place >= span_ref[0:1, own]) & (place < span_ref[1:2, own])


def forward_kernel(bounds, q_ref, span_ref, *rest):
    pieces, rest = rest[:-10], rest[-10:]
    outs, (wide_ref, row_ref, stat_ref, kv, vt, sem) = rest[:4], rest[4:]
    step = pl.program_id(0)

    @pl.when(step == 0)
    def _():
        for copy in load_window(pieces, kv, sem, [bounds[10 + i] for i in range(len(pieces))]):
            copy.wait()
        turned(kv, vt, slice(192, 384), bounds[8], bounds[9])

    first = pl.multiple_of(step * TILE_Q, TILE_Q)
    here = pl.ds(first, TILE_Q)
    q_tile = q_ref[here, :]
    heads = [head_of(q_tile[:, :128], q_tile[:, 128:], h) for h in range(3)]
    lower, count = bounds[2 * step], bounds[2 * step + 1]

    def run(i, carry):
        begin = pl.multiple_of(lower + i * SPAN_K, 128)
        rows = pl.ds(begin, SPAN_K)
        allowed = inside(span_ref, first, begin, SPAN_K)
        after = []

        def ahead(h):
            score = rows_nt(kv[rows, 0:128] if h < 2 else kv[rows, 128:192], heads[h])
            return jnp.where(allowed, score, masked_score)

        coming = ahead(0)
        for h in range(3):
            score = coming
            if h < 2:
                coming = ahead(h + 1)
            before, total, accum = carry[3 * h : 3 * h + 3]
            newest = jnp.maximum(before, jnp.max(score, axis=0, keepdims=True))
            factor = jnp.exp(before - newest)
            weight = jnp.exp(score - newest)
            total = total * factor + jnp.sum(weight, axis=0, keepdims=True)
            made = rows_nn(vt[h * HEAD_DIM : (h + 1) * HEAD_DIM, rows], weight.astype(bf16))
            after += [newest, total, accum * factor + made]
        return tuple(after)

    start = (
        jnp.full((1, TILE_Q), masked_score, f32),
        jnp.zeros((1, TILE_Q), f32),
        jnp.zeros((HEAD_DIM, TILE_Q), f32),
    )
    state = lax.fori_loop(0, count, run, start * 3)
    mixed = jnp.concatenate([state[3 * h + 2] / state[3 * h + 1] for h in range(3)], axis=0).T
    line = lax.broadcasted_iota(jnp.int32, (128, TILE_Q), 0)
    stats = jnp.zeros((128, TILE_Q), f32)
    for h in range(3):
        stats = jnp.where(line == h, state[3 * h] + jnp.log(state[3 * h + 1]), stats)
    wide_ref[here, :] = mixed
    row_ref[:, here] = stats[0:8, :]
    stat_ref[here, :] = stats.T
    low = mixed.astype(bf16)
    for r, out_ref in enumerate(outs):

        @pl.when(bounds[16 + step] == r)
        def _(out_ref=out_ref):
            out_ref[...] = low


def whole_spec(shape):
    return pl.BlockSpec(shape, lambda i, *_: (0,) * len(shape))


def attention_forward(bounds, queries, spans, pieces):
    block = queries.shape[0]
    window = sum(x.shape[0] for x in pieces)
    return pl.pallas_call(
        forward_kernel,
        grid_spec=pltpu.PrefetchScalarGridSpec(
            num_scalar_prefetch=1,
            grid=(block // TILE_Q,),
            in_specs=[whole_spec(queries.shape), whole_spec(spans.shape)]
            + [pl.BlockSpec(memory_space=pl.ANY)] * len(pieces),
            out_specs=[whole_spec((TILE_Q, 192))] * 4
            + [whole_spec((block, 192)), whole_spec((8, block)), whole_spec((block, 128))],
            scratch_shapes=[
                pltpu.VMEM((window, 384), bf16),
                pltpu.VMEM((192, window), bf16),
                pltpu.SemaphoreType.DMA((len(pieces),)),
            ],
        ),
        out_shape=[jax.ShapeDtypeStruct((TILE_Q, 192), bf16)] * 4
        + [
            jax.ShapeDtypeStruct((block, 192), f32),
            jax.ShapeDtypeStruct((8, block), f32),
            jax.ShapeDtypeStruct((block, 128), f32),
        ],
        compiler_params=pltpu.CompilerParams(vmem_limit_bytes=60 * 2**20),
        cost_estimate=pl.CostEstimate(
            flops=4 * block * 2304 * 192, bytes_accessed=6 * 2**20, transcendentals=block * 2304 * 3
        ),
        name="attention_forward",
    )(bounds, queries, spans, *pieces)


def query_kernel(bounds, q_ref, span_ref, grad_ref, wide_ref, row_ref, *rest):
    pieces, (out_ref, kv, kt, sem) = rest[:-4], rest[-4:]
    step = pl.program_id(0)

    @pl.when(step == 0)
    def _():
        for copy in load_window(pieces, kv, sem, [bounds[10 + i] for i in range(len(pieces))]):
            copy.wait()
        turned(kv, kt, slice(0, 192), bounds[8], bounds[9])

    first = pl.multiple_of(step * TILE_Q, TILE_Q)
    here = pl.ds(first, TILE_Q)
    q_tile = q_ref[here, :]
    heads = [head_of(q_tile[:, :128], q_tile[:, 128:], h) for h in range(3)]
    g_tile = grad_ref[here, :]
    lane = lax.broadcasted_iota(jnp.int32, (TILE_Q, 128), 1)
    none = jnp.zeros((TILE_Q, 128), bf16)
    r_pair = pltpu.roll(g_tile[:, :128].astype(f32), HEAD_DIM, 1).astype(bf16)
    r_last = pltpu.roll(g_tile[:, 128:256].astype(f32), HEAD_DIM, 1).astype(bf16)
    grads = [
        jnp.where(lane >= HEAD_DIM, r_pair, none),
        jnp.where(lane < HEAD_DIM, r_pair, none),
        jnp.where(lane >= HEAD_DIM, r_last, none),
    ]
    product = (g_tile[:, 0:192].astype(f32) * wide_ref[here, :]).T
    deltas = [
        jnp.sum(product[h * HEAD_DIM : (h + 1) * HEAD_DIM], axis=0, keepdims=True) for h in range(3)
    ]
    logs = [row_ref[h : h + 1, here] for h in range(3)]
    lower, count = bounds[2 * step], bounds[2 * step + 1]

    def run(i, carry):
        begin = pl.multiple_of(lower + i * SPAN_K, 128)
        rows = pl.ds(begin, SPAN_K)
        allowed = inside(span_ref, first, begin, SPAN_K)
        after = []

        def ahead(h):
            score = rows_nt(kv[rows, 0:128] if h < 2 else kv[rows, 128:192], heads[h])
            return score, rows_nt(kv[rows, 128:256] if h == 0 else kv[rows, 256:384], grads[h])

        coming = ahead(0)
        for h in range(3):
            score, back = coming
            if h < 2:
                coming = ahead(h + 1)
            chance = jnp.exp(jnp.where(allowed, score - logs[h], masked_score))
            change = (chance * (back - deltas[h])).astype(bf16)
            after.append(carry[h] + rows_nn(kt[h * HEAD_DIM : (h + 1) * HEAD_DIM, rows], change))
        return tuple(after)

    sums = lax.fori_loop(0, count, run, (jnp.zeros((HEAD_DIM, TILE_Q), f32),) * 3)
    out_ref[here, :] = (jnp.concatenate(sums, axis=0).T * 0.125).astype(bf16)


def attention_queries(bounds, queries, spans, grads, wide, stats, pieces):
    block = queries.shape[0]
    window = sum(x.shape[0] for x in pieces)
    return pl.pallas_call(
        query_kernel,
        grid_spec=pltpu.PrefetchScalarGridSpec(
            num_scalar_prefetch=1,
            grid=(block // TILE_Q,),
            in_specs=[whole_spec(x.shape) for x in (queries, spans, grads, wide, stats)]
            + [pl.BlockSpec(memory_space=pl.ANY)] * len(pieces),
            out_specs=whole_spec((block, 192)),
            scratch_shapes=[
                pltpu.VMEM((window, 384), bf16),
                pltpu.VMEM((192, window), bf16),
                pltpu.SemaphoreType.DMA((len(pieces),)),
            ],
        ),
        out_shape=jax.ShapeDtypeStruct((block, 192), bf16),
        compiler_params=pltpu.CompilerParams(vmem_limit_bytes=40 * 2**20),
        cost_estimate=pl.CostEstimate(
            flops=6 * block * 2304 * 192, bytes_accessed=6 * 2**20, transcendentals=block * 2304 * 3
        ),
        name="attention_queries",
    )(bounds, queries, spans, grads, wide, stats, *pieces)


def weight_copies(bounds, pieces, weight, sem):
    part = pieces[0].shape[0]
    copies = []
    for r, piece in enumerate(pieces):
        where = pl.ds(pl.multiple_of(bounds[16 + r] * part, part), part)
        copies.append(pltpu.make_async_copy(piece, weight.at[where, :], sem.at[r]))
    return copies


def head_terms(bounds, tokens_ref, query_ref, pair_ref, weight, grad_ref, back_ref):
    groups, part = grad_ref.shape[0], grad_ref.shape[1]
    rows = back_ref.shape[1]
    tokens = tokens_ref[...]
    pair_grad = rows_tn(tokens, pair_ref[...]).astype(bf16)
    query_grad = rows_tn(tokens, query_ref[...]).astype(bf16)
    for k in range(groups):
        here = slice(k * part, (k + 1) * part)
        grad_ref[k, :, 0 : 2 * part] = pair_grad[here]
        grad_ref[k, :, 2 * part : 3 * part] = query_grad[here]
    ones = jnp.ones((tokens.shape[0], HEAD_DIM), bf16)
    query_sum = rows_tn(query_ref[...], ones)
    value_sum = rows_tn(pair_ref[:, part:], ones)
    lane = lax.broadcasted_iota(jnp.int32, (part, HEAD_DIM), 1)
    sums = jnp.where(lane == 0, query_sum, jnp.where(lane == 1, value_sum, 0.0))
    grad_ref[:, :, 3 * part : 3 * part + HEAD_DIM] = jnp.zeros((groups, part, HEAD_DIM), bf16)
    grad_ref[bounds[16], :, 3 * part : 3 * part + HEAD_DIM] = sums.astype(bf16)
    for k in range(groups):
        here = slice(k * rows, (k + 1) * rows)
        made = rows_nt(pair_ref[here, :], weight[:, : 2 * part])
        made = made + rows_nt(query_ref[here, :], weight[:, 2 * part :])
        back_ref[bounds[16 + k]] = made.astype(bf16)


def key_kernel(reach, bounds, kv_ref, span_ref, tokens_ref, query_ref, *rest):
    window = 2 * reach + 1
    w_pieces, rest = rest[:4], rest[4:]
    q_pieces, g_pieces = rest[:window], rest[window : 2 * window]
    grad_ref, back_ref, qs, gs, key_sum, value_sum, out_ref, weight, sem, w_sem = rest[2 * window :]
    step = pl.program_id(0)
    block = q_pieces[0].shape[0]

    @pl.when(step == 0)
    def _():
        copies = load_window(q_pieces, qs, sem.at[0], [i * block for i in range(window)])
        copies += load_window(g_pieces, gs, sem.at[1], [i * block for i in range(window)])
        for copy in weight_copies(bounds, w_pieces, weight, w_sem):
            copy.start()
        for copy in copies:
            copy.wait()

    first = pl.multiple_of(step * TILE_K, TILE_K)
    here = pl.ds(first, TILE_K)
    key_sum[...] = jnp.zeros_like(key_sum)
    value_sum[...] = jnp.zeros_like(value_sum)
    keys_pair = kv_ref[here, 0:128]
    keys = [head_of(keys_pair, kv_ref[here, 128:192], h) for h in range(3)]
    lane = lax.broadcasted_iota(jnp.int32, (TILE_K, 128), 1)
    zero = jnp.zeros((TILE_K, 128), f32)
    v_one = pltpu.roll(kv_ref[here, 128:256].astype(f32), HEAD_DIM, 1)
    v_two = pltpu.roll(kv_ref[here, 256:384].astype(f32), HEAD_DIM, 1)
    values = [
        jnp.where(lane < HEAD_DIM, v_one, zero).astype(bf16),
        jnp.where(lane < HEAD_DIM, zero, v_two).astype(bf16),
        v_two.astype(bf16)[:, :HEAD_DIM],
    ]
    line = lax.broadcasted_iota(jnp.int32, (16, HEAD_DIM), 0)
    slot = lax.broadcasted_iota(jnp.int32, (16, HEAD_DIM), 1)
    selector = jnp.where((slot // 3 == line) & (slot < 18), 1.0, 0.0).astype(bf16)
    lower, count = bounds[2 * step], bounds[2 * step + 1]

    def run(i, carry):
        begin = pl.multiple_of(lower + i * SPAN_Q, 128)
        columns = pl.ds(begin, SPAN_Q)
        place = reach * block + first + lax.broadcasted_iota(jnp.int32, (TILE_K, SPAN_Q), 0)
        allowed = (place >= span_ref[0:1, columns]) & (place < span_ref[1:2, columns])
        lanes = [slice(0, 128), slice(0, 128), slice(128, 192)]
        stats = rows_nt(selector, gs[columns, 192:256])
        items = [(h, ch) for h in range(3) for ch in range(SPAN_Q // CHUNK)]

        def ahead(item):
            h, ch = item
            here = pl.ds(pl.multiple_of(begin + ch * CHUNK, 128), CHUNK)
            q_tile, g_tile = qs[here, lanes[h]], gs[here, lanes[h]]
            return q_tile, g_tile, rows_nt(keys[h], q_tile), rows_nt(values[h], g_tile)

        coming = ahead(items[0])
        for n, (h, ch) in enumerate(items):
            q_tile, g_tile, score, back = coming
            if n + 1 < len(items):
                coming = ahead(items[n + 1])
            cols = slice(ch * CHUNK, (ch + 1) * CHUNK)
            score = jnp.where(allowed[:, cols], score - stats[h : h + 1, cols], masked_score)
            chance = jnp.exp(score)
            change = (chance * (back - stats[h + 3 : h + 4, cols])).astype(bf16)
            size = 128 if h < 2 else HEAD_DIM
            key_sum[h, :, 0:size] += rows_nn(change, q_tile)
            value_sum[h, :, 0:size] += rows_nn(chance.astype(bf16), g_tile)
        return carry

    lax.fori_loop(0, count, run, 0)
    k_pair = jnp.where(lane < HEAD_DIM, key_sum[0], key_sum[1])
    v_pair = jnp.where(lane < HEAD_DIM, value_sum[0], value_sum[1])
    v_turn = pltpu.roll(v_pair, HEAD_DIM, 1)
    last_turn = pltpu.roll(value_sum[2], HEAD_DIM, 1)
    out_ref[here, 0:128] = k_pair.astype(bf16)
    out_ref[here, 128:256] = jnp.where(lane < HEAD_DIM, key_sum[2], v_turn).astype(bf16)
    out_ref[here, 256:384] = jnp.where(lane < HEAD_DIM, v_turn, last_turn).astype(bf16)

    @pl.when(step == pl.num_programs(0) - 1)
    def _():
        for copy in weight_copies(bounds, w_pieces, weight, w_sem):
            copy.wait()
        head_terms(bounds, tokens_ref, query_ref, out_ref, weight, grad_ref, back_ref)


def attention_keys(bounds, pair, spans, tokens, grad_query, weight_pieces, q_pieces, g_pieces):
    block, width = tokens.shape
    count = len(q_pieces)
    groups, part = len(weight_pieces), weight_pieces[0].shape[0]
    return pl.pallas_call(
        functools.partial(key_kernel, count // 2),
        grid_spec=pltpu.PrefetchScalarGridSpec(
            num_scalar_prefetch=1,
            grid=(block // TILE_K,),
            in_specs=[whole_spec(x.shape) for x in (pair, spans, tokens, grad_query)]
            + [pl.BlockSpec(memory_space=pl.ANY)] * (groups + 2 * count),
            out_specs=[
                whole_spec((groups, part, 3 * part + HEAD_DIM)),
                whole_spec((groups, block // groups, width)),
            ],
            scratch_shapes=[
                pltpu.VMEM((count * block, 192), bf16),
                pltpu.VMEM((count * block, 256), bf16),
                pltpu.VMEM((3, TILE_K, 128), f32),
                pltpu.VMEM((3, TILE_K, 128), f32),
                pltpu.VMEM((block, 384), bf16),
                pltpu.VMEM((width, 3 * part), bf16),
                pltpu.SemaphoreType.DMA((2, count)),
                pltpu.SemaphoreType.DMA((groups,)),
            ],
        ),
        out_shape=[
            jax.ShapeDtypeStruct((groups, part, 3 * part + HEAD_DIM), bf16),
            jax.ShapeDtypeStruct((groups, block // groups, width), bf16),
        ],
        compiler_params=pltpu.CompilerParams(vmem_limit_bytes=60 * 2**20),
        cost_estimate=pl.CostEstimate(
            flops=10 * block * 2304 * 192, bytes_accessed=12 * 2**20, transcendentals=block * 2304 * 3
        ),
        name="attention_keys",
    )(bounds, pair, spans, tokens, grad_query, *weight_pieces, *q_pieces, *g_pieces)


def projection_kernel(place_ref, own, near, far, corner, w_own, w_near, w_far, w_corner, bias_ref, *rest):
    tokens_ref, query_ref, pair_ref, weight, sem = rest
    rows, part = own.shape[0], w_own.shape[0]
    pieces = (w_own, w_near, w_far, w_corner)
    copies = []
    for r, piece in enumerate(pieces):
        where = pl.multiple_of(place_ref[r] * part, part)
        copies.append(pltpu.make_async_copy(piece, weight.at[pl.ds(where, part), :], sem.at[r]))
        copies[-1].start()
    for copy in copies:
        copy.wait()
    for r, piece in enumerate((own, near, far, corner)):
        here = pl.ds(pl.multiple_of(place_ref[r] * rows, rows), rows)
        tile = piece[...]
        tokens_ref[here, :] = tile
        made = rows_nn(tile, weight[...]) + bias_ref[0:1, :]
        pair_ref[here, :] = made[:, : 2 * part].astype(bf16)
        query_ref[here, :] = (made[:, 2 * part :].astype(bf16).astype(f32) * 0.125).astype(bf16)


def project(places, token_pieces, weight_pieces, bias):
    rows, width = token_pieces[0].shape
    part = weight_pieces[0].shape[0]
    block = rows * len(token_pieces)
    vmem = pl.BlockSpec(memory_space=pltpu.VMEM)
    return pl.pallas_call(
        projection_kernel,
        in_specs=[pl.BlockSpec(memory_space=pltpu.SMEM)]
        + [vmem] * 4
        + [pl.BlockSpec(memory_space=pl.ANY)] * 4
        + [vmem],
        out_specs=[vmem] * 3,
        out_shape=[
            jax.ShapeDtypeStruct((block, width), bf16),
            jax.ShapeDtypeStruct((block, part), bf16),
            jax.ShapeDtypeStruct((block, 2 * part), bf16),
        ],
        scratch_shapes=[pltpu.VMEM((width, 3 * part), bf16), pltpu.SemaphoreType.DMA((4,))],
        compiler_params=pltpu.CompilerParams(vmem_limit_bytes=32 * 2**20),
        cost_estimate=pl.CostEstimate(
            flops=2 * block * width * 3 * part, bytes_accessed=5 * 2**20, transcendentals=0
        ),
        name="layer_projection",
    )(places, *token_pieces, *weight_pieces, bias)


def normal_of(values):
    center = values - jnp.mean(values, axis=1, keepdims=True)
    inverse = lax.rsqrt(jnp.mean(center * center, axis=1, keepdims=True) + epsilon)
    return center * inverse, inverse


def normal_back(upstream, normal, inverse, gain):
    scaled = upstream * gain
    mean_scaled = jnp.mean(scaled, axis=1, keepdims=True)
    mean_product = jnp.mean(scaled * normal, axis=1, keepdims=True)
    return (scaled - mean_scaled - normal * mean_product) * inverse


def rows_tn(left, right):
    return lax.dot_general(left, right, (((0,), (0,)), ((), ())), preferred_element_type=f32)


def dense_kernel(place_ref, *refs):
    mixed = refs[0:4]
    tokens_ref, up_ref = refs[4:6]
    packs = refs[6:10]
    out_ref, grad_ref = refs[10:12]
    back_refs = refs[12:16]
    outer_refs, inner_refs = refs[16:18], refs[18:20]
    w_out, w_inner, w_outer, hidden, activated, slopes = refs[20:26]
    outer_made, inner_made, tail_made, lines, bias_rows, sem, sent = refs[26:]
    rows, width = tokens_ref.shape
    groups = w_inner.shape[0]
    part = width // groups

    def inner_copies(g):
        return [
            pltpu.make_async_copy(
                packs[r].at[pl.ds(pl.multiple_of(width + part + 16 + g * part, 16), part), :],
                w_inner.at[g, pl.ds(pl.multiple_of(place_ref[r] * part, part), part), :],
                sem.at[1 + g, r],
            )
            for r in range(groups)
        ]

    out_copies = [
        pltpu.make_async_copy(packs[r].at[pl.ds(width, part), :], w_out.at[r], sem.at[0, r])
        for r in range(groups)
    ]
    outer_copies = [
        pltpu.make_async_copy(
            packs[r].at[pl.ds(0, width), :], w_outer.at[place_ref[r]], sem.at[1 + groups, r]
        )
        for r in range(groups)
    ]
    line_copies = [
        pltpu.make_async_copy(
            packs[r].at[pl.ds(width + part, 16), :], lines.at[place_ref[r]], sem.at[2 + groups, r]
        )
        for r in range(groups)
    ]
    for copy in line_copies + out_copies + [x for g in range(groups) for x in inner_copies(g)] + outer_copies:
        copy.start()

    for copy in line_copies:
        copy.wait()
    small = [lines[k][:, 0:part].astype(f32) for k in range(groups)]
    out_bias, gain_one, shift_one, outer_bias, gain_two, shift_two = (
        jnp.concatenate([x[i : i + 1] for x in small], axis=1) for i in range(6)
    )
    for k in range(groups):
        bias_rows[k : k + 1, :] = jnp.concatenate(
            [small[k][6 + i : 7 + i] for i in range(groups)], axis=1
        )
    for copy in out_copies:
        copy.wait()
    residual = tokens_ref[...].astype(f32) + out_bias
    for r in range(groups):
        residual = residual + rows_nn(mixed[r][...], w_out[r])
    normal_one, inverse_one = normal_of(residual)
    first = normal_one * gain_one + shift_one
    first_low = first.astype(bf16)

    def ahead(g, carry):
        for copy in inner_copies(g):
            copy.wait()
        value = rows_nn(first_low, w_inner[g]) + bias_rows[pl.ds(g, 1), :]
        chance = 0.5 * (1.0 + lax.erf(value * (2.0**-0.5)))
        density = jnp.exp(-0.5 * value * value) * (2.0 * jnp.pi) ** -0.5
        slopes[g] = chance + value * density
        activated[g] = (value * chance).astype(bf16)
        return carry

    lax.fori_loop(0, groups, ahead, 0)
    for copy in outer_copies:
        copy.wait()

    def combine(g, total):
        return total + rows_nn(activated[g], w_outer[g])

    residual = lax.fori_loop(0, groups, combine, first + outer_bias)
    normal_two, inverse_two = normal_of(residual)
    out_ref[...] = (normal_two * gain_two + shift_two).astype(bf16)
    upstream = up_ref[...].astype(f32)
    grad_two = normal_back(upstream, normal_two, inverse_two, gain_two)
    grad_two_low = grad_two.astype(bf16)
    shift_two_sum = jnp.sum(upstream, axis=0, keepdims=True)
    gain_two_sum = jnp.sum(upstream * normal_two, axis=0, keepdims=True)
    outer_bias_sum = jnp.sum(grad_two_low.astype(f32), axis=0, keepdims=True)

    def outer_copy(i, odd):
        r = 2 * i + odd
        return pltpu.make_async_copy(outer_made.at[r], outer_refs[odd].at[i], sent.at[0, r])

    def behind(i, total):
        for odd in range(2):
            g = place_ref[2 * i + odd]
            outer_made[2 * i + odd] = rows_tn(activated[g], grad_two_low).astype(bf16)
            outer_copy(i, odd).start()
            value = (rows_nt(grad_two_low, w_outer[g]) * slopes[g]).astype(bf16)
            hidden[g] = value
            total = total + rows_nt(value, w_inner[g])
        return total

    grad_first = lax.fori_loop(0, groups // 2, behind, grad_two)
    grad_one = normal_back(grad_first, normal_one, inverse_one, gain_one)
    grad_ref[...] = grad_one
    grad_one_low = grad_one.astype(bf16)
    for r in range(groups):
        back_refs[r][...] = rows_nt(grad_one_low, w_out[r]).astype(bf16)

    def inner_sends(g):
        return [
            pltpu.make_async_copy(
                inner_made.at[g, pl.ds(pl.multiple_of(place_ref[r] * part, part), part), :],
                inner_refs[r % 2].at[r // 2, pl.ds(pl.multiple_of(g * part, part), part), :],
                sent.at[1 + g, r],
            )
            for r in range(groups)
        ]

    def weigh(g, carry):
        inner_made[g] = rows_tn(first_low, hidden[g]).astype(bf16)
        for copy in inner_sends(g):
            copy.start()
        return carry

    lax.fori_loop(0, groups, weigh, 0)
    sums = [
        jnp.sum(grad_one_low.astype(f32), axis=0, keepdims=True),
        jnp.sum(grad_first * normal_one, axis=0, keepdims=True),
        jnp.sum(grad_first, axis=0, keepdims=True),
        outer_bias_sum,
        gain_two_sum,
        shift_two_sum,
    ]
    line = lax.broadcasted_iota(jnp.int32, (16, part), 0)
    tail_made[:, part:, :] = jnp.zeros((groups, 64, width), bf16)
    for r in range(groups):
        tail_made[r, 0:part, :] = rows_tn(mixed[r][...], grad_one_low).astype(bf16)
    for k in range(groups):
        tail = jnp.zeros((16, part), f32)
        for i, line_sum in enumerate(sums):
            tail = jnp.where(line == i, line_sum[:, k * part : (k + 1) * part], tail)
        bias_sum = jnp.sum(hidden[k].astype(f32), axis=0, keepdims=True)
        for i in range(groups):
            tail = jnp.where(
                line == len(sums) + i, bias_sum[:, i * part : (i + 1) * part], tail
            )
        tail_made[place_ref[k], part : part + 16, 0:part] = tail.astype(bf16)
    tail_copies = [
        pltpu.make_async_copy(
            tail_made.at[r], inner_refs[r % 2].at[r // 2, pl.ds(width, part + 64), :], sent.at[1 + groups, r]
        )
        for r in range(groups)
    ]
    for copy in tail_copies:
        copy.start()
    for i in range(groups // 2):
        for odd in range(2):
            outer_copy(i, odd).wait()
    for g in range(groups):
        for copy in inner_sends(g):
            copy.wait()
    for copy in tail_copies:
        copy.wait()


def dense(places, mixed_pieces, tokens, cotangent, packs):
    rows, width = tokens.shape
    groups = len(packs)
    part = width // groups
    vmem = pl.BlockSpec(memory_space=pltpu.VMEM)
    hbm = pl.BlockSpec(memory_space=pl.ANY)
    return pl.pallas_call(
        dense_kernel,
        in_specs=[pl.BlockSpec(memory_space=pltpu.SMEM)] + [vmem] * (groups + 2) + [hbm] * groups,
        out_specs=[vmem] * (2 + groups) + [hbm] * 4,
        out_shape=[
            jax.ShapeDtypeStruct((rows, width), bf16),
            jax.ShapeDtypeStruct((rows, width), f32),
        ]
        + [jax.ShapeDtypeStruct((rows, part), bf16)] * groups
        + [jax.ShapeDtypeStruct((groups // 2, width, width), bf16)] * 2
        + [jax.ShapeDtypeStruct((groups // 2, width + part + 64, width), bf16)] * 2,
        scratch_shapes=[
            pltpu.VMEM((groups, part, width), bf16),
            pltpu.VMEM((groups, width, width), bf16),
            pltpu.VMEM((groups, width, width), bf16),
            pltpu.VMEM((groups, rows, width), bf16),
            pltpu.VMEM((groups, rows, width), bf16),
            pltpu.VMEM((groups, rows, width), f32),
            pltpu.VMEM((groups, width, width), bf16),
            pltpu.VMEM((groups, width, width), bf16),
            pltpu.VMEM((groups, part + 64, width), bf16),
            pltpu.VMEM((groups, 16, width), bf16),
            pltpu.VMEM((8, width), f32),
            pltpu.SemaphoreType.DMA((groups + 3, groups)),
            pltpu.SemaphoreType.DMA((groups + 2, groups)),
        ],
        compiler_params=pltpu.CompilerParams(vmem_limit_bytes=40 * 2**20),
        cost_estimate=pl.CostEstimate(
            flops=24 * rows * width * width * groups,
            bytes_accessed=24 * 2**20,
            transcendentals=2 * rows * width * groups,
        ),
        name="layer_dense",
    )(places, *mixed_pieces, tokens, cotangent, *packs)


def gather_kernel(place_ref, p0, p1, p2, p3, wide_ref, stat_ref, out_ref):
    rows, part = p0.shape
    lane = lax.broadcasted_iota(jnp.int32, (rows, 128), 1)
    slot = lax.broadcasted_iota(jnp.int32, (rows, HEAD_DIM), 1)
    for r, piece in enumerate((p0, p1, p2, p3)):
        here = pl.ds(pl.multiple_of(place_ref[r] * rows, rows), rows)
        tile = piece[...]
        product = tile.astype(f32) * wide_ref[here, :]
        pair, last = product[:, 0:128], product[:, 128:192]
        values = [stat_ref[here, h : h + 1] for h in range(3)] + [
            jnp.sum(jnp.where(lane < HEAD_DIM, pair, 0.0), axis=1, keepdims=True),
            jnp.sum(jnp.where(lane < HEAD_DIM, 0.0, pair), axis=1, keepdims=True),
            jnp.sum(last, axis=1, keepdims=True),
        ]
        tail = jnp.zeros((rows, HEAD_DIM), f32)
        for i, left in enumerate(values):
            for j in range(3):
                high = left.astype(bf16).astype(f32)
                tail = jnp.where(slot == 3 * i + j, high, tail)
                left = left - high
        out_ref[here, 0:192] = tile
        out_ref[here, 192:256] = tail.astype(bf16)


def gathered(places, pieces, wide, stats):
    block = wide.shape[0]
    vmem = pl.BlockSpec(memory_space=pltpu.VMEM)
    return pl.pallas_call(
        gather_kernel,
        in_specs=[pl.BlockSpec(memory_space=pltpu.SMEM)] + [vmem] * 6,
        out_specs=vmem,
        out_shape=jax.ShapeDtypeStruct((block, 256), bf16),
        compiler_params=pltpu.CompilerParams(vmem_limit_bytes=16 * 2**20),
        cost_estimate=pl.CostEstimate(flops=2**20, bytes_accessed=3 * 2**20, transcendentals=0),
        name="layer_gather",
    )(places, *pieces, wide, stats)


def both(left, right):
    return (left.astype(f32) + right.astype(f32)).astype(bf16)


def half_of(block, bit, axis):
    size = block.shape[axis] // 2
    return lax.dynamic_slice_in_dim(block, bit * size, size, axis)


def scatter_sum(terms, axis_name, order, axis):
    index = lax.axis_index(axis_name)
    for step in order:
        bit = (index // step) % 2
        sent = functools.reduce(both, [half_of(x, 1 - bit, axis) for x in terms])
        kept = functools.reduce(both, [half_of(x, bit, axis) for x in terms])
        terms = [kept, swapped(sent, axis_name, step)]
    return terms


def gather_back(block, axis_name, order, axis):
    index = lax.axis_index(axis_name)
    for step in reversed(order):
        other = swapped(block, axis_name, step)
        late = (index // step) % 2 == 1
        block = jnp.where(
            late,
            jnp.concatenate([other, block], axis),
            jnp.concatenate([block, other], axis),
        )
    return block


def gather_square(block, axis_name):
    index = lax.axis_index(axis_name)
    rows, width = block.shape
    first, second = block[: rows // 2], block[rows // 2 :]
    first_got = swapped(first, axis_name, 1)
    second_got = swapped(second, axis_name, 2)
    first_got, second_got = lax.optimization_barrier((first_got, second_got))
    first_far = swapped(jnp.concatenate([first, first_got]), axis_name, 2)
    second_far = swapped(jnp.concatenate([second, second_got]), axis_name, 1)
    size = rows // 2
    ours = [
        (first, second),
        (first_far[:size], second_got),
        (first_got, second_far[:size]),
        (first_far[size:], second_far[size:]),
    ]
    low, high = index % 2 == 1, (index // 2) % 2 == 1
    placed = []
    for x in range(2):
        for z in range(2):
            for half in range(2):
                near = jnp.where(high, ours[2 * x + 1 - z][half], ours[2 * x + z][half])
                across = jnp.where(
                    high, ours[2 * (1 - x) + 1 - z][half], ours[2 * (1 - x) + z][half]
                )
                placed.append(jnp.where(low, across, near))
    return jnp.concatenate(placed, axis=0)


def on_device(
    tokens,
    doc_start,
    cotangent,
    query_weight,
    key_weight,
    value_weight,
    out_weight,
    query_bias,
    value_bias,
    out_bias,
    first_gain,
    first_shift,
    inner_weight,
    inner_bias,
    outer_weight,
    outer_bias,
    second_gain,
    second_shift,
):
    rows, width = tokens.shape
    cycle = lax.axis_size("ctx")
    shards = lax.axis_size("wt")
    block = rows * shards
    reach = (MAXDOC + block - 2) // block
    window = (2 * reach + 1) * block
    c = lax.axis_index("ctx")
    w = lax.axis_index("wt")
    part = width // shards
    places = jnp.stack([w ^ r for r in range(shards)]).astype(jnp.int32)

    def spread(own, near):
        far = swapped(own, "wt", 2)
        return [own, near, far, swapped(far, "wt", 1)]

    def columns(r):
        start = (w ^ r) * part
        return jnp.concatenate(
            [
                lax.dynamic_slice_in_dim(x, start, part, 1)
                for x in (key_weight, value_weight, query_weight)
            ],
            axis=1,
        )

    token_pieces = spread(tokens, swapped(tokens, "wt", 1))
    weight_pieces = [columns(0)] + [swapped(columns(r), "wt", r) for r in range(1, shards)]
    head_bias = jnp.concatenate([jnp.zeros((part,), f32), value_bias.astype(f32), query_bias.astype(f32)])
    head_bias = jnp.broadcast_to(head_bias[None], (8, 3 * part))

    pad = reach * block
    padded = jnp.pad(doc_start, (pad, pad), constant_values=-1)
    base = c * block - pad
    marks = lax.dynamic_slice_in_dim(padded, c * block, window)
    place = jnp.arange(window, dtype=jnp.int32)
    begins = jnp.where((marks == base + place) | (marks < 0), place, window)
    next_begin = lax.cummin(begins, axis=0, reverse=True)
    stops = jnp.concatenate([next_begin[1:], jnp.full((1,), window, jnp.int32)])
    starts = marks - base
    own_starts = starts[pad : pad + block]
    own_stops = stops[pad : pad + block]
    spans_row = jnp.stack([starts, stops] + [jnp.zeros_like(starts)] * 6)
    spans = spans_row[:, pad : pad + block]
    lowest = own_starts.reshape(-1, TILE_Q)[:, 0] // 128 * 128
    highest = own_stops.reshape(-1, TILE_Q)[:, -1]
    count = (highest - lowest + SPAN_K - 1) // SPAN_K
    lowest = jnp.minimum(lowest, (window - count * SPAN_K) // 128 * 128)
    reached = jnp.stack([jnp.min(lowest) // 256, (jnp.max(lowest + count * SPAN_K) + 255) // 256])
    bounds = jnp.concatenate([jnp.stack([lowest, count], axis=1).reshape(-1), reached])

    block_tokens, queries, pair = project(places, token_pieces, weight_pieces, head_bias)

    distances = [d for d in range(reach, -reach - 1, -1)]

    def halo(own):
        return [own if d == 0 else shifted(own, "ctx", d) for d in distances]

    even = c % 2 == 0
    beside_at = jnp.where(even, reach + 1, reach - 1) * block
    missing_at = jnp.where(even, reach - 1, reach + 1) * block
    load_at = jnp.stack(
        [0 * missing_at, 2 * reach * block + 0 * missing_at, reach * block + 0 * missing_at]
        + [beside_at, missing_at, missing_at + block // 2]
    )
    bounds = jnp.concatenate([bounds, load_at, places]).astype(jnp.int32)
    beside = swapped(pair, "ctx", 1)
    before, after = shifted(pair, "ctx", 2), shifted(pair, "ctx", -2)
    half = block // 2
    before, after, bounds, spans, spans_row = lax.optimization_barrier(
        (before, after, bounds, spans, spans_row)
    )
    route = [(i, i + 2 if i % 2 == 0 else i - 2) for i in range(cycle)]
    route = [(i, j) for i, j in route if 0 <= j < cycle]
    upper = swapped(jnp.where(even, after[:half], before[:half]), "ctx", 1)
    lower = lax.ppermute(beside[half:], "ctx", route)
    pairs = [before, after, pair, beside, upper, lower]
    small_own = jnp.stack(
        [out_bias, first_gain, first_shift, outer_bias, second_gain, second_shift]
    )
    small_own = jnp.concatenate([small_own, inner_bias.reshape(-1, part)], axis=0)
    small_own = jnp.pad(small_own, ((0, 16 - small_own.shape[0]), (0, width - part)))
    inner_parts = [inner_weight[:, i * width : (i + 1) * width] for i in range(shards)]
    pack = jnp.concatenate([outer_weight, out_weight, small_own] + inner_parts, axis=0)
    pack, _ = lax.optimization_barrier((pack, token_pieces[2:] + weight_pieces[1:]))
    pack_near, pack_far = swapped(pack, "wt", 1), swapped(pack, "wt", 2)
    *mixed_pieces, mixed_wide, stat_rows, stat_columns = attention_forward(
        bounds, queries, spans, pairs
    )
    ready, _ = lax.optimization_barrier((queries, [before, after, beside]))
    query_halo = [queries if d == 0 else shifted(ready, "ctx", d) if d * d > 1 else None for d in distances]
    close = [x for x, d in zip(query_halo, distances) if d * d > 1]
    mixed_pieces, mixed_wide, stat_columns, close, pack_far = lax.optimization_barrier(
        (mixed_pieces, mixed_wide, stat_columns, close, pack_far)
    )
    packs = [pack, pack_near, pack_far, swapped(pack_far, "wt", 1)]

    mixed_pieces = [mixed_pieces[0]] + [
        swapped(mixed_pieces[r], "wt", r) for r in range(1, shards)
    ]
    far_ready, mixed_pieces = lax.optimization_barrier((queries, mixed_pieces))
    results = dense(
        places, mixed_pieces, tokens, cotangent, packs
    )
    remote = [shifted(far_ready, "ctx", d) for d in distances if d * d == 1]
    results, remote = lax.optimization_barrier((results, remote))
    layer_out, grad_one, *back = results[: 2 + shards]
    outer_keep, outer_send, inner_keep, inner_send = results[2 + shards :]
    query_halo = [close[0], remote[0], queries, remote[1], close[1]]

    back_pieces = [back[0]] + [swapped(back[r], "wt", r) for r in range(1, shards)]
    outer_got = swapped(outer_send, "wt", 1)
    inner_got = swapped(inner_send, "wt", 1)
    grads = gathered(places, back_pieces, mixed_wide, stat_columns)
    outer_got, _ = lax.optimization_barrier((outer_got, back_pieces[1:]))
    grads, inner_got = lax.optimization_barrier((grads, inner_got))

    def far_terms(keep, got):
        return [both(keep[0], got[0]), swapped(both(keep[1], got[1]), "wt", 2)]

    grad_halo = halo(grads)
    outer_terms = far_terms(outer_keep, outer_got)
    grad_query = attention_queries(
        bounds, queries, spans, grads, mixed_wide, stat_rows, pairs
    )
    grad_query, grad_halo, outer_terms, inner_keep, inner_got = lax.optimization_barrier(
        (grad_query, grad_halo, outer_terms, inner_keep, inner_got)
    )

    near_first = [1 << i for i in range(cycle.bit_length() - 1)]
    outer_terms = scatter_sum(outer_terms, "ctx", near_first[:1], 0)
    inner_terms = far_terms(inner_keep, inner_got)
    head_grad, token_partial = attention_keys(
        bounds, pair, spans_row, block_tokens, grad_query, weight_pieces, query_halo, grad_halo
    )
    head_grad, token_partial, outer_terms, inner_terms = lax.optimization_barrier(
        (head_grad, token_partial, outer_terms, inner_terms)
    )

    outer_part = both(*scatter_sum(outer_terms, "ctx", near_first[1:], 0))
    inner_part = both(*scatter_sum(inner_terms, "ctx", near_first, 0))
    head_part = both(*scatter_sum([head_grad], "ctx", near_first, 1))
    token_got = swapped(token_partial[1::2], "wt", 1)
    token_sum = both(*far_terms(token_partial[0::2], token_got))
    outer_total = gather_back(outer_part, "ctx", near_first, 0)
    inner_part = gather_back(inner_part, "ctx", near_first[2:], 0)
    inner_total = gather_square(inner_part, "ctx")
    head_pieces = [
        lax.dynamic_index_in_dim(head_part, w ^ r, 0, keepdims=False) for r in range(shards)
    ]
    head_pieces = [head_pieces[0]] + [swapped(head_pieces[r], "wt", r) for r in range(1, shards)]
    head_parts = jnp.stack(
        [
            lax.dynamic_index_in_dim(jnp.stack(head_pieces), w ^ k, 0, keepdims=False)
            for k in range(shards)
        ]
    )
    head_total = gather_back(head_parts, "ctx", near_first, 1)

    tokens_gradient = grad_one + token_sum.astype(f32)
    key_total, value_total, query_total = (
        jnp.concatenate(
            [head_total[k, :, i * part : (i + 1) * part] for k in range(shards)], axis=1
        ).astype(f32)
        for i in range(3)
    )
    own_total = lax.dynamic_index_in_dim(head_total, w, 0, keepdims=False)
    inner_rows = inner_total[:width].reshape(shards, part, width)
    inner_rows = jnp.concatenate([inner_rows[k] for k in range(shards)], axis=1).astype(f32)
    lines = inner_total[width + part : width + part + 16, :part].astype(f32)

    return (
        layer_out,
        tokens_gradient,
        query_total,
        key_total,
        value_total,
        inner_total[width : width + part].astype(f32),
        own_total[:, 3 * part].astype(f32),
        own_total[:, 3 * part + 1].astype(f32),
        lines[0],
        lines[1],
        lines[2],
        inner_rows,
        lines[6:10].reshape(-1),
        outer_total.astype(f32),
        lines[3],
        lines[4],
        lines[5],
    )


def solution(mesh):
    matrix, vector = P("wt", None), P("wt")
    stream = P(("ctx", "wt"), None)
    in_specs = (stream, P(), stream) + (matrix,) * 4 + (vector,) * 5
    in_specs += (matrix, vector, matrix, vector, vector, vector)
    out_specs = (stream, stream) + (matrix,) * 4 + (vector,) * 5
    out_specs += (matrix, vector, matrix, vector, vector, vector)
    return jax.shard_map(
        on_device, mesh=mesh, in_specs=in_specs, out_specs=out_specs, check_vma=False
    )
```
